32 devices in a mesh: blk: 4 (over x, core), uly: 8 (over z, y).
Axes of the slice: x: 2, y: 2, z: 4, core: 2. Of those that a mesh axis runs over, the one named last changes fastest.
Arguments:
- residual: bfloat16 [2, 2048, 1024], P(None, ('uly', 'blk')), may hold values from -6 to 6
- cotangent: bfloat16 [2, 2048, 1024], P(None, ('uly', 'blk')), may hold values from -6 to 6
- lengths: int32 [2], replicated, may hold values from 512 to 2048, as said below
- positions: int32 [2, 2048], P(None, ('uly', 'blk')), may hold values from 0 to 2047, as said below
- masters: float32 [12596224], P(('blk', 'uly')), may hold values from -2 to 2
- momenta: float32 [12596224], P(('blk', 'uly')), may hold values from -102.4 to 102.4
- averages: float32 [12596224], P(('blk', 'uly')), may hold values from -2 to 2
Outputs:
- block_output: bfloat16 [2, 2048, 1024], P(None, ('uly', 'blk'))
- input_gradient: bfloat16 [2, 2048, 1024], P(None, ('uly', 'blk'))
- gradients: float32 [12596224], P(('blk', 'uly'))
- updated_masters: float32 [12596224], P(('blk', 'uly'))
- updated_momenta: float32 [12596224], P(('blk', 'uly'))
- updated_averages: float32 [12596224], P(('blk', 'uly'))
The draws below stay inside these ranges and needn't reach their ends.
Inputs may be any that keep to these rules, and one draw needn't show every extreme that they name: `lengths`: in every draw some slot is live over all 2048 positions; tokens at or past a slot's length are padding. Each slot's positions start at 0, restart at 0 at the first token of each packed document, and otherwise rise by one per token; the first slot holds a single document, every other slot two or more.
All inputs are finite; a program needn't handle non-finite values.
Results may differ from the reference program's by a relative error of at most 0.014.
The reference program's roundings to bfloat16 on the way count: a program that leaves them out, or rounds other values in their place, can miss the bound.
Values may be sent and summed in bfloat16 or wider, within the bound.
No kernel may reach another device: no remote copies, remote signals or barrier semaphores. Data moves between devices by JAX's collectives and lax.ppermute only.
A program may use at most 256 MiB of HBM per device.

```python
import math
import jax
import jax.numpy as jnp
from jax import lax

D = 1024
H = 16
HD = 64
ROT = 16
FF = 4096
SEQS = 2
SEQ = 2048
NPARAM = 12596224


def segment_law():
    return [(D, 1.0, 0.2), (D, 0.0, 0.3), (D, 1.0, 0.2), (D, 0.0, 0.3), (3 * D * D, 0.0, 1.5 / math.sqrt(D)), (3 * D, 0.0, 0.3), (D * D, 0.0, 6.0 / math.sqrt(D)), (D, 0.0, 0.3), (D * FF, 0.0, 1.0 / math.sqrt(D)), (FF, 0.0, 0.3), (FF * D, 0.0, 1.5 / math.sqrt(FF)), (D, 0.0, 0.3)]


def parameter_values(noise_field):
    element_ids = jnp.arange(NPARAM, dtype=jnp.int32)
    centers = jnp.zeros((NPARAM,), jnp.float32)
    scales = jnp.zeros((NPARAM,), jnp.float32)
    cursor = 0
    for number, center, spread in segment_law():
        inside = (element_ids >= cursor) & (element_ids < cursor + number)
        centers = jnp.where(inside, center, centers)
        scales = jnp.where(inside, spread, scales)
        cursor += number
    return centers + scales * noise_field


def draw_masters(key, part):
    noise_field = jax.random.truncated_normal(key, -4.0, 4.0, (NPARAM,), jnp.float32)
    return parameter_values(noise_field)


def draw_averages(key, part):
    inner_key = jax.random.fold_in(key, 7)
    noise_field = jax.random.truncated_normal(inner_key, -4.0, 4.0, (NPARAM,), jnp.float32)
    return parameter_values(noise_field)


def draw_momenta(key, part):
    inner_key = jax.random.fold_in(key, 11)
    spread = 0.4 * math.sqrt(SEQS * SEQ)
    noise_field = jax.random.truncated_normal(inner_key, -4.0, 4.0, (NPARAM,), jnp.float32)
    return spread * noise_field


def draw_lengths(key, part):
    first_key, second_key = jax.random.split(key)
    drawn_lengths = jax.random.randint(first_key, (SEQS,), SEQ // 4, SEQ + 1)
    chosen = jax.random.randint(second_key, (), 0, SEQS)
    return jnp.where(jnp.arange(SEQS, dtype=jnp.int32) == chosen, SEQ, drawn_lengths).astype(jnp.int32)


def draw_positions(key, part):
    first_key, second_key = jax.random.split(jax.random.fold_in(key, 5))
    starts = jax.random.randint(first_key, (SEQS, SEQ), 0, 64) == 0
    forced = jax.random.randint(second_key, (SEQS, 1), 1, SEQ)
    element_ids = jnp.broadcast_to(jnp.arange(SEQ, dtype=jnp.int32), (SEQS, SEQ))
    slot_ids = jnp.broadcast_to(jnp.arange(SEQS, dtype=jnp.int32)[:, None], (SEQS, SEQ))
    starts = (starts | (element_ids == forced)) & (slot_ids != 0) | (element_ids == 0)
    latest = lax.cummax(jnp.where(starts, element_ids, 0), axis=1)
    return (element_ids - latest).astype(jnp.int32)


def level_of(own_key, extent, cuts, low, high):
    loudness = 1.0
    for axis_at, parts in cuts:
        steps = jax.random.uniform(jax.random.fold_in(jax.random.fold_in(own_key, 6), axis_at), (parts,), jnp.float32, low / len(cuts), high / len(cuts))
        loudness = loudness * jnp.repeat(jnp.exp(steps), extent[axis_at] // parts).reshape((-1,) + (1,) * (len(extent) - 1 - axis_at))
    return loudness


def centred(own_key, dims, deviation, bound, cuts=(), kind=jnp.bfloat16):
    level = level_of(own_key, dims, cuts, -0.22, 0.18) if cuts else 1.0
    drawn = jax.random.normal(own_key, dims, jnp.float32) * deviation * level
    return jnp.minimum(jnp.maximum(drawn, -bound), bound).astype(kind)


def setup_inputs(seed: int = 0) -> dict:
    arg_keys = jax.random.split(jax.random.key(seed), 8)
    return {
        "residual": centred(arg_keys[0], (SEQS, SEQ, D), 1.0, 6.0, ((1, 32),)),
        "cotangent": centred(arg_keys[1], (SEQS, SEQ, D), 1.0, 6.0, ((1, 32),)),
        "lengths": draw_lengths(jax.random.fold_in(arg_keys[7], 71), 0),
        "positions": draw_positions(jax.random.fold_in(arg_keys[7], 71), 0),
        "masters": draw_masters(jax.random.fold_in(arg_keys[7], 71), 0),
        "momenta": draw_momenta(jax.random.fold_in(arg_keys[7], 71), 0),
        "averages": draw_averages(jax.random.fold_in(arg_keys[7], 71), 0),
    }


@jax.custom_vjp
def low(v):
    return lax.optimization_barrier(v.astype(jnp.bfloat16)).astype(jnp.float32)

@jax.custom_vjp
def low_back(v):
    return v

def low_keep(v):
    return (low(v), None)

def low_pass(kept, grad):
    return (grad,)

def back_keep(v):
    return (v, None)

def back_low(kept, grad):
    return (low(grad),)
low.defvjp(low_keep, low_pass)
low_back.defvjp(back_keep, back_low)
EPSILON = 1e-05
NEGATIVE = -1e+30
MOMENTUM = 0.5
LEARN_RATE = 0.05
AVERAGE_DECAY = 0.5
ROTARY_BASE = 10000.0
HIGHEST_MODE = lax.Precision.HIGHEST

def unpack(flat_vector):
    layouts = [(D,), (D,), (D,), (D,), (D, 3 * D), (3 * D,), (D, D), (D,), (D, FF), (FF,), (FF, D), (D,)]
    pieces = []
    cursor = 0
    for layout in layouts:
        number = math.prod(layout)
        pieces.append(flat_vector[cursor:cursor + number].reshape(layout))
        cursor += number
    return pieces

def layer_norm(values, gain, shift):
    centered = values - lax.optimization_barrier(jnp.mean(values, axis=-1, keepdims=True))
    variance = lax.optimization_barrier(jnp.mean(centered * centered, axis=-1, keepdims=True))
    return centered * lax.rsqrt(variance + EPSILON) * gain + shift

def rotary_tables(positions):
    half_dims = ROT // 2
    inverse = ROTARY_BASE ** (-(jnp.arange(half_dims, dtype=jnp.float32) * 2.0 / ROT))
    angles = positions.astype(jnp.float32)[..., None] * inverse
    return (jnp.cos(angles), jnp.sin(angles))

def rotate(values, cos_table, sin_table):
    half_dims = ROT // 2
    first_half = values[..., :half_dims]
    second_half = values[..., half_dims:ROT]
    return jnp.concatenate([first_half * cos_table - second_half * sin_table, second_half * cos_table + first_half * sin_table, values[..., ROT:]], axis=-1)

def query_block(inputs, keys_all, values_all, length):
    query_rows, row_start = inputs
    block_rows = query_rows.shape[0]
    scores = jnp.dot(query_rows, keys_all.T, precision=HIGHEST_MODE) * HD ** (-0.5)
    scores = low_back(scores)
    row_index = row_start + jnp.arange(block_rows, dtype=jnp.int32)
    col_index = jnp.arange(keys_all.shape[0], dtype=jnp.int32)
    allowed = (col_index[None, :] <= row_index[:, None]) & (col_index[None, :] < length)
    scores = jnp.where(allowed, scores, NEGATIVE)
    row_max = lax.optimization_barrier(jnp.max(scores, axis=-1, keepdims=True))
    exponent = jnp.exp(scores - row_max)
    attend_prob = exponent / lax.optimization_barrier(jnp.sum(exponent, axis=-1, keepdims=True))
    return jnp.dot(low(attend_prob), values_all, precision=HIGHEST_MODE)

def head_attention(inputs, length):
    queries, keys_all, values_all = inputs
    block_rows = min(SEQ, 1024)
    block_count = SEQ // block_rows
    grouped = queries.reshape(block_count, block_rows, HD)
    starts = jnp.arange(block_count, dtype=jnp.int32) * block_rows

    def one_block(block_inputs):
        return query_block(block_inputs, keys_all, values_all, length)
    mapped = lax.map(jax.checkpoint(one_block), (grouped, starts))
    return mapped.reshape(SEQ, HD)

def one_sequence(inputs, params):
    values, positions, length = inputs
    gain_one, shift_one, gain_two, shift_two, project_w, project_b, dense_w, dense_b, expand_w, expand_b, shrink_w, shrink_b = params
    normed_one = low(layer_norm(values, gain_one, shift_one))
    normed_two = low(layer_norm(values, gain_two, shift_two))
    mixed_rows = low_back(jnp.dot(normed_one, project_w, precision=HIGHEST_MODE) + project_b)
    mixed_rows = mixed_rows.reshape(SEQ, H, 3, HD)
    cos_table, sin_table = rotary_tables(positions)
    cos_table = cos_table[:, None, :]
    sin_table = sin_table[:, None, :]
    queries = low_back(low(rotate(mixed_rows[:, :, 0], cos_table, sin_table)))
    keys_all = low_back(low(rotate(mixed_rows[:, :, 1], cos_table, sin_table)))
    values_all = low_back(low(mixed_rows[:, :, 2]))

    def per_head(head_inputs):
        return head_attention(head_inputs, length)
    attended = lax.map(jax.checkpoint(per_head), (queries.transpose(1, 0, 2), keys_all.transpose(1, 0, 2), values_all.transpose(1, 0, 2)))
    attended = low_back(low(attended.transpose(1, 0, 2).reshape(SEQ, D)))
    branch_attn = low_back(jnp.dot(attended, dense_w, precision=HIGHEST_MODE) + dense_b)
    hidden_pre = low_back(jnp.dot(normed_two, expand_w, precision=HIGHEST_MODE) + expand_b)
    activated = low(jax.nn.gelu(hidden_pre, approximate=False))
    branch_feed = low_back(jnp.dot(activated, shrink_w, precision=HIGHEST_MODE) + shrink_b)
    return values + branch_attn + branch_feed

def reference(residual, cotangent, lengths, positions, masters, momenta, averages):

    def forward(values_all, flat_master):
        params = unpack(low(flat_master))

        def per_sequence(inputs):
            return one_sequence(inputs, params)
        return lax.map(jax.checkpoint(per_sequence), (values_all, positions, lengths))
    start_values = residual.astype(jnp.float32)
    outputs, pullback = jax.vjp(forward, start_values, masters)
    live_mask = (jnp.arange(SEQ, dtype=jnp.int32)[None, :] < lengths[:, None]).astype(jnp.float32)
    seed_grad = cotangent.astype(jnp.float32) * live_mask[:, :, None]
    input_grad, gradients = pullback(seed_grad)
    velocity = MOMENTUM * momenta + gradients
    step_rate = LEARN_RATE / math.sqrt(SEQS * SEQ)
    updated = masters - step_rate * (gradients + MOMENTUM * velocity)
    averaged = AVERAGE_DECAY * averages + (1.0 - AVERAGE_DECAY) * updated
    return (outputs.astype(jnp.bfloat16), input_grad.astype(jnp.bfloat16), gradients, updated, velocity, averaged)
```

```python
from functools import partial
import math

import jax
import jax.numpy as jnp
from jax import lax
from jax.experimental import pallas as pl
from jax.experimental.pallas import tpu as pltpu
from jax.sharding import Mesh, PartitionSpec as P

D = 1024
H = 16
HD = 64
ROT = 16
FF = 4096


EPSILON = 1e-05
NEGATIVE = -1e30
MOMENTUM = 0.5
LEARN_RATE = 0.05
AVERAGE_DECAY = 0.5
ROTARY_BASE = 10000.0


def passed_along(block, axis, distance):
    devices = range(lax.axis_size(axis))
    route = [((i - distance) % len(devices), i) for i in devices]
    return lax.ppermute(block, axis, route)


def unpack(flat_vector):
    layouts = [
        (D,),
        (D,),
        (D,),
        (D,),
        (D, 3 * D),
        (3 * D,),
        (D, D),
        (D,),
        (D, FF),
        (FF,),
        (FF, D),
        (D,),
    ]
    pieces = []
    cursor = 0
    for layout in layouts:
        number = math.prod(layout)
        pieces.append(flat_vector[cursor : cursor + number].reshape(layout))
        cursor += number
    return pieces


def layer_norm(values, gain, shift):
    centered = values - jnp.mean(values, axis=-1, keepdims=True)
    variance = jnp.mean(centered * centered, axis=-1, keepdims=True)
    return centered * lax.rsqrt(variance + EPSILON) * gain + shift


def rotary_tables(positions):
    half_dims = ROT // 2
    inverse = ROTARY_BASE ** (-(jnp.arange(half_dims, dtype=jnp.float32) * 2.0 / ROT))
    angles = positions.astype(jnp.float32)[..., None] * inverse
    return (jnp.cos(angles), jnp.sin(angles))


def rotate(values, cos_table, sin_table):
    half_dims = ROT // 2
    first_half = values[..., :half_dims]
    second_half = values[..., half_dims:ROT]
    return jnp.concatenate(
        [
            first_half * cos_table - second_half * sin_table,
            second_half * cos_table + first_half * sin_table,
            values[..., ROT:],
        ],
        axis=-1,
    )


def group_tokens(source, group_count, uly_count, span_rows):
    spans = jnp.arange(uly_count, dtype=jnp.int32)[:, None] * group_count + source
    return (spans * span_rows + jnp.arange(span_rows, dtype=jnp.int32)[None, :]).reshape(-1)


def block_scores(queries, keys_rows, row_tokens, col_tokens, length):
    scores = jnp.einsum(
        "qhd,khd->hqk", queries, keys_rows, preferred_element_type=jnp.float32
    ) * HD ** (-0.5)
    allowed = (col_tokens[None, :] <= row_tokens[:, None]) & (col_tokens[None, :] < length)
    return jnp.where(allowed[None], scores, NEGATIVE)


def is_live(row_tokens, col_tokens, length):
    return (col_tokens[0] <= row_tokens[-1]) & (col_tokens[0] < length)


def fold_stats(row_max, row_total, queries, key_value, lengths, row_tokens, col_tokens):

    def per_slot(inputs):
        slot_max, slot_total, slot_queries, slot_pairs, length = inputs

        def compute(current):
            prev_max, prev_total = current
            scores = block_scores(slot_queries, slot_pairs[:, :, 0], row_tokens, col_tokens, length)
            next_max = jnp.maximum(prev_max, jnp.max(scores, axis=-1))
            next_total = prev_total * jnp.exp(prev_max - next_max) + jnp.sum(
                jnp.exp(scores - next_max[..., None]), axis=-1
            )
            return (next_max, next_total)

        return lax.cond(
            is_live(row_tokens, col_tokens, length),
            compute,
            lambda current: current,
            (slot_max, slot_total),
        )

    return lax.map(per_slot, (row_max, row_total, queries, key_value, lengths))


def fold_values(attended, queries, key_value, log_total, lengths, row_tokens, col_tokens):

    def per_slot(inputs):
        slot_out, slot_queries, slot_pairs, slot_log, length = inputs

        def compute(current):
            scores = block_scores(slot_queries, slot_pairs[:, :, 0], row_tokens, col_tokens, length)
            prob_low = jnp.exp(scores - slot_log[..., None]).astype(jnp.bfloat16)
            return current + jnp.einsum(
                "hqk,khd->qhd", prob_low, slot_pairs[:, :, 1], preferred_element_type=jnp.float32
            )

        return lax.cond(
            is_live(row_tokens, col_tokens, length), compute, lambda current: current, slot_out
        )

    return lax.map(per_slot, (attended, queries, key_value, log_total, lengths))


def fold_grads(
    query_grad,
    pair_grad,
    queries,
    key_value,
    grad_out,
    log_total,
    row_delta,
    lengths,
    row_tokens,
    col_tokens,
):

    def per_slot(inputs):
        (
            slot_qgrad,
            slot_pgrad,
            slot_queries,
            slot_pairs,
            slot_gout,
            slot_log,
            slot_delta,
            length,
        ) = inputs

        def compute(current):
            cur_qgrad, cur_pgrad = current
            scores = block_scores(slot_queries, slot_pairs[:, :, 0], row_tokens, col_tokens, length)
            attend_prob = jnp.exp(scores - slot_log[..., None])
            prob_low = attend_prob.astype(jnp.bfloat16)
            prob_grad = jnp.einsum(
                "qhd,khd->hqk", slot_gout, slot_pairs[:, :, 1], preferred_element_type=jnp.float32
            )
            score_grad = (attend_prob * (prob_grad - slot_delta[..., None])).astype(jnp.bfloat16)
            cur_qgrad = cur_qgrad + jnp.einsum(
                "hqk,khd->qhd", score_grad, slot_pairs[:, :, 0], preferred_element_type=jnp.float32
            ) * HD ** (-0.5)
            key_grad = jnp.einsum(
                "hqk,qhd->khd", score_grad, slot_queries, preferred_element_type=jnp.float32
            ) * HD ** (-0.5)
            value_grad = jnp.einsum(
                "hqk,qhd->khd", prob_low, slot_gout, preferred_element_type=jnp.float32
            )
            return (cur_qgrad, cur_pgrad + jnp.stack([key_grad, value_grad], axis=2))

        return lax.cond(
            is_live(row_tokens, col_tokens, length),
            compute,
            lambda current: current,
            (slot_qgrad, slot_pgrad),
        )

    return lax.map(
        per_slot,
        (query_grad, pair_grad, queries, key_value, grad_out, log_total, row_delta, lengths),
    )


def local(residual, cotangent, lengths, positions, masters, momenta, averages):
    slot_count, span_rows, model_width = residual.shape
    group_count = lax.axis_size("blk")
    uly_count = lax.axis_size("uly")
    group_index = lax.axis_index("blk")
    uly_index = lax.axis_index("uly")
    block_rows = uly_count * span_rows
    full_rows = group_count * block_rows
    local_heads = H // uly_count
    token_rows = slot_count * span_rows
    row_tokens = group_tokens(group_index, group_count, uly_count, span_rows)

    def tokens_of(source):
        return group_tokens(source, group_count, uly_count, span_rows)

    gathered = lax.all_gather(masters.astype(jnp.bfloat16), ("blk", "uly"), axis=0, tiled=True)
    (
        gain_one,
        shift_one,
        gain_two,
        shift_two,
        project_w,
        project_b,
        dense_w,
        dense_b,
        expand_w,
        expand_b,
        shrink_w,
        shrink_b,
    ) = unpack(gathered)
    values = residual.astype(jnp.float32).reshape(token_rows, model_width)
    normed_one, norm_back_one = jax.vjp(
        layer_norm, values, gain_one.astype(jnp.float32), shift_one.astype(jnp.float32)
    )
    normed_two, norm_back_two = jax.vjp(
        layer_norm, values, gain_two.astype(jnp.float32), shift_two.astype(jnp.float32)
    )
    normed_one = normed_one.astype(jnp.bfloat16)
    normed_two = normed_two.astype(jnp.bfloat16)
    mixed_rows = jnp.dot(
        normed_one, project_w, preferred_element_type=jnp.float32
    ) + project_b.astype(jnp.float32)
    mixed_rows = mixed_rows.reshape(slot_count, span_rows, H, 3, HD)
    cos_table, sin_table = rotary_tables(positions)
    cos_table = cos_table[:, :, None, None, :]
    sin_table = sin_table[:, :, None, None, :]
    turned, turn_back = jax.vjp(
        lambda pair_rows: rotate(pair_rows, cos_table, sin_table), mixed_rows[:, :, :, 0:2]
    )
    packed = jnp.concatenate([turned, mixed_rows[:, :, :, 2:3]], axis=3).astype(jnp.bfloat16)
    packed = packed.reshape(slot_count, span_rows, 3 * model_width)
    heads_rows = lax.all_to_all(packed, "uly", split_axis=2, concat_axis=1, tiled=True).reshape(
        slot_count, block_rows, local_heads, 3, HD
    )
    queries = heads_rows[:, :, :, 0]
    key_value = heads_rows[:, :, :, 1:3]
    row_max = jnp.full((slot_count, local_heads, block_rows), NEGATIVE, jnp.float32)
    row_total = jnp.zeros((slot_count, local_heads, block_rows), jnp.float32)
    attended = jnp.zeros((slot_count, block_rows, local_heads, HD), jnp.float32)
    last_tokens = tokens_of((group_index + 1) % group_count)

    def stats_turn(turn_index, carried):
        pairs_now, cur_max, cur_total = carried
        col_tokens = tokens_of((group_index - turn_index) % group_count)
        cur_max, cur_total = fold_stats(
            cur_max, cur_total, queries, pairs_now, lengths, row_tokens, col_tokens
        )
        pairs_now = passed_along(pairs_now, "blk", 1)
        return (pairs_now, cur_max, cur_total)

    pairs_now, row_max, row_total = lax.fori_loop(
        0, group_count - 1, stats_turn, (key_value, row_max, row_total)
    )
    row_max, row_total = fold_stats(
        row_max, row_total, queries, pairs_now, lengths, row_tokens, last_tokens
    )
    log_total = row_max + jnp.log(row_total)

    def value_turn(turn_index, carried):
        pairs_now, cur_out = carried
        col_tokens = tokens_of((group_index - turn_index) % group_count)
        cur_out = fold_values(
            cur_out, queries, pairs_now, log_total, lengths, row_tokens, col_tokens
        )
        pairs_now = passed_along(pairs_now, "blk", 1)
        return (pairs_now, cur_out)

    pairs_now, attended = lax.fori_loop(0, group_count - 1, value_turn, (key_value, attended))
    attended = fold_values(
        attended, queries, pairs_now, log_total, lengths, row_tokens, last_tokens
    )
    heads_out = attended.astype(jnp.bfloat16).reshape(slot_count, block_rows, local_heads * HD)
    merged = lax.all_to_all(heads_out, "uly", split_axis=1, concat_axis=2, tiled=True).reshape(
        token_rows, model_width
    )
    branch_attn = jnp.dot(merged, dense_w, preferred_element_type=jnp.float32) + dense_b.astype(
        jnp.float32
    )
    hidden_pre = jnp.dot(
        normed_two, expand_w, preferred_element_type=jnp.float32
    ) + expand_b.astype(jnp.float32)
    activated, gelu_back = jax.vjp(partial(jax.nn.gelu, approximate=False), hidden_pre)
    activated_low = activated.astype(jnp.bfloat16)
    branch_feed = jnp.dot(
        activated_low, shrink_w, preferred_element_type=jnp.float32
    ) + shrink_b.astype(jnp.float32)
    outputs = (
        (values + branch_attn + branch_feed)
        .astype(jnp.bfloat16)
        .reshape(slot_count, span_rows, model_width)
    )
    first_token = (uly_index * group_count + group_index) * span_rows
    token_index = first_token + jnp.arange(span_rows, dtype=jnp.int32)
    live_mask = (token_index[None, :] < lengths[:, None]).astype(jnp.float32)
    seed_grad = (cotangent.astype(jnp.float32) * live_mask[:, :, None]).reshape(
        token_rows, model_width
    )
    seed_low = seed_grad.astype(jnp.bfloat16)
    dense_w_grad = jnp.einsum("ra,rb->ab", merged, seed_low, preferred_element_type=jnp.float32)
    bias_grad = jnp.sum(seed_low.astype(jnp.float32), axis=0)
    merged_grad = jnp.einsum(
        "rb,ab->ra", seed_low, dense_w, preferred_element_type=jnp.float32
    ).astype(jnp.bfloat16)
    shrink_w_grad = jnp.einsum(
        "rf,rb->fb", activated_low, seed_low, preferred_element_type=jnp.float32
    )
    activated_grad = jnp.einsum("rb,fb->rf", seed_low, shrink_w, preferred_element_type=jnp.float32)
    hidden_grad = gelu_back(activated_grad)[0].astype(jnp.bfloat16)
    expand_w_grad = jnp.einsum(
        "ra,rf->af", normed_two, hidden_grad, preferred_element_type=jnp.float32
    )
    expand_b_grad = jnp.sum(hidden_grad.astype(jnp.float32), axis=0)
    normed_two_grad = jnp.einsum(
        "rf,af->ra", hidden_grad, expand_w, preferred_element_type=jnp.float32
    )
    grad_heads = lax.all_to_all(
        merged_grad.reshape(slot_count, span_rows, model_width),
        "uly",
        split_axis=2,
        concat_axis=1,
        tiled=True,
    )
    grad_out = grad_heads.reshape(slot_count, block_rows, local_heads, HD)
    row_delta = jnp.sum(grad_out.astype(jnp.float32) * attended, axis=-1).transpose(0, 2, 1)
    query_grad = jnp.zeros((slot_count, block_rows, local_heads, HD), jnp.float32)
    pair_grad = jnp.zeros((slot_count, block_rows, local_heads, 2, HD), jnp.float32)

    def grad_turn(turn_index, carried):
        pairs_now, cur_pgrad, cur_qgrad = carried
        col_tokens = tokens_of((group_index - turn_index) % group_count)
        cur_qgrad, cur_pgrad = fold_grads(
            cur_qgrad,
            cur_pgrad,
            queries,
            pairs_now,
            grad_out,
            log_total,
            row_delta,
            lengths,
            row_tokens,
            col_tokens,
        )
        pairs_now = passed_along(pairs_now, "blk", 1)
        cur_pgrad = passed_along(cur_pgrad.astype(jnp.bfloat16), "blk", 1).astype(cur_pgrad.dtype)
        return (pairs_now, cur_pgrad, cur_qgrad)

    pairs_now, pair_grad, query_grad = lax.fori_loop(
        0, group_count - 1, grad_turn, (key_value, pair_grad, query_grad)
    )
    query_grad, pair_grad = fold_grads(
        query_grad,
        pair_grad,
        queries,
        pairs_now,
        grad_out,
        log_total,
        row_delta,
        lengths,
        row_tokens,
        last_tokens,
    )
    pair_grad = passed_along(pair_grad.astype(jnp.bfloat16), "blk", 1).astype(pair_grad.dtype)
    back_packed = jnp.concatenate(
        [query_grad.astype(jnp.bfloat16)[:, :, :, None], pair_grad.astype(jnp.bfloat16)], axis=3
    )
    back_packed = back_packed.reshape(slot_count, block_rows, local_heads * 3 * HD)
    token_grads = lax.all_to_all(
        back_packed, "uly", split_axis=1, concat_axis=2, tiled=True
    ).reshape(slot_count, span_rows, H, 3, HD)
    turned_grad = turn_back(token_grads[:, :, :, 0:2].astype(jnp.float32))[0]
    mixed_grad = jnp.concatenate(
        [turned_grad, token_grads[:, :, :, 2:3].astype(jnp.float32)], axis=3
    ).astype(jnp.bfloat16)
    mixed_grad = mixed_grad.reshape(token_rows, 3 * model_width)
    project_w_grad = jnp.einsum(
        "ra,rc->ac", normed_one, mixed_grad, preferred_element_type=jnp.float32
    )
    project_b_grad = jnp.sum(mixed_grad.astype(jnp.float32), axis=0)
    normed_one_grad = jnp.einsum(
        "rc,ac->ra", mixed_grad, project_w, preferred_element_type=jnp.float32
    )
    values_one, gain_one_grad, shift_one_grad = norm_back_one(normed_one_grad)
    values_two, gain_two_grad, shift_two_grad = norm_back_two(normed_two_grad)
    input_grad = (
        (seed_grad + values_one + values_two)
        .astype(jnp.bfloat16)
        .reshape(slot_count, span_rows, model_width)
    )
    local_grads = jnp.concatenate(
        [
            gain_one_grad,
            shift_one_grad,
            gain_two_grad,
            shift_two_grad,
            project_w_grad.reshape(-1),
            project_b_grad,
            dense_w_grad.reshape(-1),
            bias_grad,
            expand_w_grad.reshape(-1),
            expand_b_grad,
            shrink_w_grad.reshape(-1),
            bias_grad,
        ]
    )
    gradients = lax.psum_scatter(local_grads, ("blk", "uly"), scatter_dimension=0, tiled=True)
    velocity = MOMENTUM * momenta + gradients
    step_rate = LEARN_RATE / math.sqrt(slot_count * full_rows)
    updated = masters - step_rate * (gradients + MOMENTUM * velocity)
    averaged = AVERAGE_DECAY * averages + (1.0 - AVERAGE_DECAY) * updated
    return (outputs, input_grad, gradients, updated, velocity, averaged)


LANES = 128
BLOCK = 256
RING = ("core", "z", "y")
ALL = ("x", "core", "z", "y")
F32 = jnp.float32
BF16 = jnp.bfloat16


def call(body, grid, in_specs, out_specs, out_shape, scratch=(), prefetch=0, name=None):
    return pl.pallas_call(
        body,
        grid_spec=pltpu.PrefetchScalarGridSpec(
            num_scalar_prefetch=prefetch,
            grid=grid,
            in_specs=in_specs,
            out_specs=out_specs,
            scratch_shapes=scratch,
        ),
        out_shape=out_shape,
        name=name,
        compiler_params=pltpu.CompilerParams(vmem_limit_bytes=56 << 20),
    )


def whole(shape):
    return pl.BlockSpec(shape, lambda *_: (0,) * len(shape))


def shaped(shape, kind):
    return jax.ShapeDtypeStruct(shape, kind)


def mm(a, b, dims=((1,), (0,))):
    return lax.dot_general(a, b, (dims, ((), ())), preferred_element_type=F32)


def low_lanes(shape):
    return lax.broadcasted_iota(jnp.int32, shape, len(shape) - 1) < LANES // 2


def swap(a):
    return pltpu.roll(a, LANES // 2, 1)


def join(a, a_half, b, b_half):
    first = swap(a) if a_half else a
    second = b if b_half else swap(b)
    return jnp.where(low_lanes(a.shape), first, second)


OWNERS = 32
PER = (3 * D + D + FF + FF) // OWNERS
FLAT = PER * D // LANES
PIECE = FLAT // 16
LEAD = 4 * D // LANES
PROJECT, PLAIN, PLAIN_EXPAND, EXPAND, EXPAND_PLAIN = range(5)


def kind_of(c):
    return (
        PROJECT
        if c < 8
        else PLAIN
        if c < 10 or c > 21
        else PLAIN_EXPAND
        if c == 10
        else EXPAND_PLAIN
        if c == 21
        else EXPAND
    )


def plain_place(row, base, count):
    local = row - base
    half = int(local >= count // 2)
    return local - half * (count // 2), half


def dense_place(row):
    if row < 768:
        c = 8 + row // 384
        return (c, 0) + plain_place(row, 384 * (c - 8), 384)
    return (10, 0) + plain_place(row, 768, 256)


def shrink_place(row):
    if row < 256:
        return (21, 64) + plain_place(row, 0, 256)
    c = 22 + (row - 256) // 384
    return (c, 0) + plain_place(row, 256 + 384 * (c - 22), 384)


def expand_places():
    places = [(10, 128, 0, 32)]
    places += [(c, 0, 32 + 96 * (c - 11), 96) for c in range(11, 21)]
    places += [(21, 0, 992, 32)]
    return places


def shifted_rows(source, start, shift, at, rows):
    turn = (LANES - shift) % LANES
    first = pltpu.roll(source[pl.ds(start + at, rows), :], turn, 1)
    second = pltpu.roll(source[pl.ds(start + at + 1, rows), :], turn, 1)
    lane = lax.broadcasted_iota(jnp.int32, (rows, LANES), 1)
    return jnp.where(lane < LANES - shift, first, second)


SHIFT_ROWS = 3200
SEND_ROWS = PIECE + 32 + 16


def weights_out_body(scalars, source, places, out, flat):
    start, shift, kind, vector_row = scalars[0], scalars[1], scalars[2], scalars[3]

    def align(step, carry):
        at = pl.multiple_of(step * 80, 8)
        flat[pl.ds(at, 80), :] = shifted_rows(source, start, shift, at, 80)
        return carry

    lax.fori_loop(0, SHIFT_ROWS // 80, align, 0)

    def rows(first, count, stride):
        return flat[pl.ds(first, count, stride), :]

    def plain(base, count, to):
        for m in range(8):
            tile = rows(base + m, count, 8)
            a, b = tile[: count // 2], tile[count // 2 :]
            out[2 * m, to : to + count // 2] = join(a, 0, b, 0).astype(BF16)
            out[2 * m + 1, to : to + count // 2] = join(a, 1, b, 1).astype(BF16)

    def expand(base, count, to):
        for r in range(16):
            out[r, to : to + count] = rows(base + 2 * r, count, 32).astype(BF16)
            out[r, to + count : to + 2 * count] = rows(base + 2 * r + 1, count, 32).astype(BF16)

    def project(base):
        for m in range(8):
            first, middle, last = (rows(base + 3 * m + j, 128, 24) for j in range(3))
            out[2 * m, 0:128] = first.astype(BF16)
            out[2 * m, 128:192] = join(middle[:64], 0, middle[64:], 0).astype(BF16)
            out[2 * m + 1, 0:128] = join(middle, 1, last, 0).astype(BF16)
            out[2 * m + 1, 128:192] = join(last[:64], 1, last[64:], 1).astype(BF16)

    @pl.when(kind == PROJECT)
    def _():
        project(LEAD)

    @pl.when(kind == PLAIN)
    def _():
        plain(LEAD, 384, 0)

    @pl.when(kind == PLAIN_EXPAND)
    def _():
        plain(LEAD, 256, 0)
        expand(LEAD + 2048 + 8, 32, 128)

    @pl.when(kind == EXPAND)
    def _():
        expand(LEAD, 96, 0)

    @pl.when(kind == EXPAND_PLAIN)
    def _():
        expand(LEAD, 32, 0)
        plain(LEAD + 1024 + 32, 256, 64)

    vectors = flat[pl.ds(vector_row, 32), :].astype(BF16)
    for r in range(16):
        out[r, PIECE : PIECE + 32] = vectors
        out[r, PIECE + 32 :] = places[...]


def weights_in_body(scalars, got, qkv_w, expand_w, second, vectors, qkv_b, expand_b, project_rows, expand_rows):
    head = scalars[0]
    low = low_lanes((64, LANES))
    for c in range(8):
        qkv_w[128 * c : 128 * c + 128, 0:128] = got[c, 0:128]
        packed = got[c, 128:192].astype(F32)
        qkv_w[128 * c : 128 * c + 64, 128:256] = jnp.where(low, packed, 0.0).astype(BF16)
        qkv_w[128 * c + 64 : 128 * c + 128, 128:256] = jnp.where(low, swap(packed), 0.0).astype(BF16)
    for c, at, row, count in expand_places():
        expand_w[row : row + count, 0:128] = got[c, at : at + count]
        expand_w[row : row + count, 128:256] = got[c, at + count : at + 2 * count]

    for h in range(16):
        c, at, row, half = dense_place(64 * h)
        tile = got[c, at + row : at + row + 64].astype(F32)
        second[h, 0:32] = join(tile[:32], half, tile[32:], half).astype(BF16)
        for part in range(2):
            c, at, row, half = shrink_place(256 * h + 64 * part)
            tile = got[c, at + row : at + row + 64].astype(F32)
            c, at, row, other = shrink_place(256 * h + 128 + 64 * part)
            after = got[c, at + row : at + row + 64].astype(F32)
            second[h, 32 + 64 * part : 96 + 64 * part] = join(tile, half, after, other).astype(BF16)

    def vector(c, at, to):
        tile = got[c, PIECE + at : PIECE + at + 8].astype(F32)
        for j in range(8):
            vectors[to : to + 1, 128 * j : 128 * j + 128] = tile[j : j + 1]

    vectors[...] = jnp.zeros(vectors.shape, F32)
    for v in range(4):
        vector(0, 8 * v, v)
    vector(10, 0, 4)
    vector(31, 0, 5)
    project_rows[...] = got[8, PIECE + 8 : PIECE + 32].astype(F32)
    expand_rows[...] = got[21, PIECE : PIECE + 32].astype(F32)
    row = head // 2 * 3
    first, middle, last = (project_rows[pl.ds(row + j, 1), :] for j in range(3))
    odd = head % 2 == 1
    qkv_b[0:1, 0:128] = jnp.where(odd, join(middle, 1, last, 0), first)
    value = jnp.where(odd, swap(last), middle)
    qkv_b[0:1, 128:256] = jnp.where(low_lanes((1, LANES)), value, 0.0)
    expand_b[0:1, 0:128] = expand_rows[pl.ds(2 * head, 1), :]
    expand_b[0:1, 128:256] = expand_rows[pl.ds(2 * head + 1, 1), :]


def rows_in_body(got, dense_w, shrink_w):
    for m in range(8):
        even, odd = got[2 * m].astype(F32), got[2 * m + 1].astype(F32)
        columns = slice(128 * m, 128 * m + 128)
        for out, at, half in ((dense_w, 0, 32), (shrink_w, 32, 128)):
            a, b = even[at : at + half], odd[at : at + half]
            out[0:half, columns] = join(a, 0, b, 0).astype(BF16)
            out[half : 2 * half, columns] = join(a, 1, b, 1).astype(BF16)


def rows_out_body(dense_g, shrink_g, out):
    for m in range(8):
        columns = slice(128 * m, 128 * m + 128)
        for source, at, half in ((dense_g, 0, 32), (shrink_g, 32, 128)):
            a, b = source[0:half, columns], source[half : 2 * half, columns]
            out[2 * m, at : at + half] = join(a, 0, b, 0).astype(BF16)
            out[2 * m + 1, at : at + half] = join(a, 1, b, 1).astype(BF16)


BACK_ROWS = PIECE + 32


def grads_out_body(scalars, second, qkv_g, expand_g, vector_g, qkv_bg, expand_bg, out, project_rows, expand_rows):
    head = scalars[0]
    out[...] = jnp.zeros(out.shape, BF16)
    for c in range(8):
        out[c, 0:128] = qkv_g[128 * c : 128 * c + 128, 0:128].astype(BF16)
        a = qkv_g[128 * c : 128 * c + 64, 128:256]
        b = qkv_g[128 * c + 64 : 128 * c + 128, 128:256]
        out[c, 128:192] = join(a, 0, b, 0).astype(BF16)
    for c, at, row, count in expand_places():
        out[c, at : at + count] = expand_g[row : row + count, 0:128].astype(BF16)
        out[c, at + count : at + 2 * count] = expand_g[row : row + count, 128:256].astype(BF16)

    def dense_rows(row):
        packed = second[row // 64, 0:32].astype(F32)
        return jnp.concatenate([packed, swap(packed)], axis=0)

    def shrink_rows(row):
        h, part = row // 256, row % 256 // 64
        packed = second[h, 32 + part % 2 * 64 : 96 + part % 2 * 64].astype(F32)
        return swap(packed) if part >= 2 else packed

    def plain(c, to, base, count, take):
        for i in range(count // 128):
            a, b = take(base + 64 * i), take(base + count // 2 + 64 * i)
            out[c, to + 64 * i : to + 64 * i + 64] = join(a, 0, b, 0).astype(BF16)

    plain(8, 0, 0, 384, dense_rows)
    plain(9, 0, 384, 384, dense_rows)
    plain(10, 0, 768, 256, dense_rows)
    plain(21, 64, 0, 256, shrink_rows)
    for c in range(22, 32):
        plain(c, 0, 256 + 384 * (c - 22), 384, shrink_rows)

    def rows_of(row):
        return jnp.concatenate([vector_g[row : row + 1, 128 * j : 128 * j + 128] for j in range(8)], axis=0)

    gains = jnp.concatenate([rows_of(v) for v in range(4)], axis=0)
    out[0, PIECE : PIECE + 32] = gains.astype(BF16)
    bias = jnp.concatenate([rows_of(4), jnp.zeros((8, LANES), F32)], axis=0).astype(BF16)
    out[10, PIECE : PIECE + 16] = bias
    out[31, PIECE : PIECE + 16] = bias
    project_rows[...] = jnp.zeros(project_rows.shape, F32)
    expand_rows[...] = jnp.zeros(expand_rows.shape, F32)
    pair, value = qkv_bg[0:1, 0:128], qkv_bg[0:1, 128:256]
    low = low_lanes((1, LANES))
    row = 8 + head // 2 * 3
    odd = head % 2 == 1
    project_rows[pl.ds(row, 1), :] = jnp.where(odd, 0.0, pair)
    project_rows[pl.ds(row + 1, 1), :] = jnp.where(
        odd, jnp.where(low, 0.0, swap(pair)), jnp.where(low, value, 0.0)
    )
    project_rows[pl.ds(row + 2, 1), :] = jnp.where(odd, join(pair, 1, value, 0), 0.0)
    out[8, PIECE : PIECE + 32] = project_rows[...].astype(BF16)
    expand_rows[pl.ds(2 * head, 1), :] = expand_bg[0:1, 0:128]
    expand_rows[pl.ds(2 * head + 1, 1), :] = expand_bg[0:1, 128:256]
    out[21, PIECE : PIECE + 32] = expand_rows[...].astype(BF16)


TAKE_ROWS = 3120


def grads_in_body(scalars, got, out, flat):
    start, shift, kind, vector_row = scalars[0], scalars[1], scalars[2], scalars[3]
    lead = LEAD + 8

    def clear(step, carry):
        flat[pl.ds(pl.multiple_of(step * 80, 8), 80), :] = jnp.zeros((80, LANES), F32)
        return carry

    lax.fori_loop(0, SHIFT_ROWS // 80, clear, 0)

    def add_vectors(source, total):
        return total + got[source, PIECE : PIECE + 32].astype(F32)

    flat[pl.ds(vector_row + 8, 32), :] = lax.fori_loop(0, OWNERS, add_vectors, jnp.zeros((32, LANES), F32))

    def taken(r, at, count):
        return got[r, at : at + count].astype(F32) + got[16 + r, at : at + count].astype(F32)

    def plain(base, count, at):
        half = count // 2
        for m in range(8):
            a, b = taken(2 * m, at, half), taken(2 * m + 1, at, half)
            flat[pl.ds(base + m, half, 8), :] = join(a, 0, b, 0)
            flat[pl.ds(base + m + 8 * half, half, 8), :] = join(a, 1, b, 1)

    def expand(base, count, at):
        for r in range(16):
            flat[pl.ds(base + 2 * r, count, 32), :] = taken(r, at, count)
            flat[pl.ds(base + 2 * r + 1, count, 32), :] = taken(r, at + count, count)

    def project(base):
        for m in range(8):
            pair, values = taken(2 * m, 0, 128), taken(2 * m, 128, 64)
            odd_pair, odd_values = taken(2 * m + 1, 0, 128), taken(2 * m + 1, 128, 64)
            values = jnp.concatenate([values, swap(values)], axis=0)
            odd_values = jnp.concatenate([odd_values, swap(odd_values)], axis=0)
            flat[pl.ds(base + 3 * m, 128, 24), :] = pair
            flat[pl.ds(base + 3 * m + 1, 128, 24), :] = join(values, 0, odd_pair, 0)
            flat[pl.ds(base + 3 * m + 2, 128, 24), :] = join(odd_pair, 1, odd_values, 0)

    @pl.when(kind == PROJECT)
    def _():
        project(lead)

    @pl.when(kind == PLAIN)
    def _():
        plain(lead, 384, 0)

    @pl.when(kind == PLAIN_EXPAND)
    def _():
        plain(lead, 256, 0)
        expand(lead + 2048 + 8, 32, 128)

    @pl.when(kind == EXPAND)
    def _():
        expand(lead, 96, 0)

    @pl.when(kind == EXPAND_PLAIN)
    def _():
        expand(lead, 32, 0)
        plain(lead + 1024 + 32, 256, 64)

    def align(step, carry):
        at = pl.multiple_of(step * 80, 8)
        out[pl.ds(at, 80), :] = shifted_rows(flat, start, shift, at, 80)
        return carry

    lax.fori_loop(0, TAKE_ROWS // 80, align, 0)


def token_rows(ref):
    return jnp.concatenate([ref[0, 0, 0], ref[1, 0, 0], ref[0, 0, 1], ref[1, 0, 1]], axis=0)


def put_rows(ref, rows):
    step = rows.shape[0] // 4
    for i, (core, x) in enumerate(((0, 0), (1, 0), (0, 1), (1, 1))):
        ref[core, 0, x] = rows[step * i : step * i + step].astype(ref.dtype)


def normalized(values):
    centered = values - jnp.mean(values, axis=-1, keepdims=True)
    variance = jnp.mean(centered * centered, axis=-1, keepdims=True)
    return centered * lax.rsqrt(variance + EPSILON)


def turned(pair, cos, sin):
    lane = lax.broadcasted_iota(jnp.int32, pair.shape, 1) % HD
    half = ROT // 2
    other = jnp.where(
        lane < half, -pltpu.roll(pair, LANES - half, 1), jnp.where(lane < ROT, pltpu.roll(pair, half, 1), 0.0)
    )
    return pair * cos + other * sin


def mixed_body(tokens, vectors, qkv_w, qkv_b, cos, sin, one, two, query, key, value):
    unit = normalized(token_rows(tokens).astype(F32))
    first = (unit * vectors[0:1] + vectors[1:2]).astype(BF16)
    one[...] = first
    two[...] = (unit * vectors[2:3] + vectors[3:4]).astype(BF16)
    mixed = mm(first, qkv_w[...]) + qkv_b[...]
    pair = turned(mixed[:, :LANES], cos[...], sin[...])
    query[...] = pair[:, :HD].astype(BF16) * HD ** (-0.5)
    key[...] = pair[:, HD:].astype(BF16)
    value[...] = mixed[:, LANES : LANES + HD].astype(BF16)


def masked_scores(key, query_t, at, first_query, length):
    scores = mm(key, query_t)
    keys = at * BLOCK + lax.broadcasted_iota(jnp.int32, scores.shape, 0)
    queries = first_query + lax.broadcasted_iota(jnp.int32, scores.shape, 1)
    return jnp.where((keys <= queries) & (keys < length), scores, NEGATIVE)


def folded(values, op):
    parts = [values[8 * i : 8 * i + 8] for i in range(values.shape[0] // 8)]
    while len(parts) > 1:
        parts = [op(a, b) for a, b in zip(parts[::2], parts[1::2])]
    return parts[0]


def attend_body(lengths, query, key, value, low_out, full_out, log_out, scores, value_t):
    at = pl.program_id(0)
    length = lengths[0]

    @pl.when(at == 0)
    def _():
        value_t[...] = value[...].astype(F32).T.astype(BF16)

    query_t = query[...].astype(F32).T.astype(BF16)
    clear = jnp.minimum(at, length // BLOCK)
    stop = jnp.minimum(at, (length - 1) // BLOCK) + 1

    def rows(j):
        return pl.ds(pl.multiple_of(j * BLOCK, BLOCK), BLOCK)

    def score(j, top, masked):
        if masked:
            tile = masked_scores(key[rows(j), :], query_t, j, at * BLOCK, length)
        else:
            tile = mm(key[rows(j), :], query_t)
        scores[rows(j), :] = tile
        return jnp.maximum(top, folded(tile, jnp.maximum))

    top = jnp.full((8, BLOCK), NEGATIVE, F32)
    top = lax.fori_loop(0, clear, lambda j, t: score(j, t, False), top)
    top = lax.fori_loop(clear, stop, lambda j, t: score(j, t, True), top)
    top = jnp.max(top, axis=0, keepdims=True)

    def power(j, total):
        tile = jnp.exp(scores[rows(j), :] - top)
        scores[rows(j), :] = tile
        return total + folded(tile, jnp.add)

    total = lax.fori_loop(0, stop, power, jnp.zeros((8, BLOCK), F32))
    total = jnp.sum(total, axis=0, keepdims=True)
    inverse = 1.0 / total

    def weigh(j, out):
        low = (scores[rows(j), :] * inverse).astype(BF16)
        return out + mm(value_t[:, rows(j)], low)

    out = lax.fori_loop(0, stop, weigh, jnp.zeros((HD, BLOCK), F32))
    full_out[...] = out
    low_out[...] = out.T.astype(BF16)
    log_out[...] = top + jnp.log(total)


def attend_back_body(
    lengths, query, key, value, grad, full_out, log_in, query_g, key_g, value_g, key_t, key_sum, value_sum
):
    at = pl.program_id(0)
    length = lengths[0]

    @pl.when(at == 0)
    def _():
        key_t[...] = key[...].astype(F32).T.astype(BF16)
        key_sum[...] = jnp.zeros(key_sum.shape, F32)
        value_sum[...] = jnp.zeros(value_sum.shape, F32)

    query_rows, grad_rows = query[...], grad[...]
    query_t = query_rows.astype(F32).T.astype(BF16)
    grad_full_t = grad_rows.astype(F32).T
    grad_t = grad_full_t.astype(BF16)
    delta = jnp.sum(grad_full_t * full_out[...], axis=0, keepdims=True)
    log_total = log_in[...]
    clear = jnp.minimum(at, length // BLOCK)
    stop = jnp.minimum(at, (length - 1) // BLOCK) + 1
    clear, stop = (jnp.where(at * BLOCK < length, n, 0) for n in (clear, stop))

    def step(j, query_sum, masked):
        rows = pl.ds(pl.multiple_of(j * BLOCK, BLOCK), BLOCK)
        if masked:
            tile = masked_scores(key[rows, :], query_t, j, at * BLOCK, length)
        else:
            tile = mm(key[rows, :], query_t)
        probs = jnp.exp(tile - log_total)
        value_sum[rows, :] += mm(probs.astype(BF16), grad_rows)
        score_g = (probs * (mm(value[rows, :], grad_t) - delta)).astype(BF16)
        key_sum[rows, :] += mm(score_g, query_rows)
        return query_sum + mm(key_t[:, rows], score_g)

    query_sum = jnp.zeros((HD, BLOCK), F32)
    query_sum = lax.fori_loop(0, clear, lambda j, s: step(j, s, False), query_sum)
    query_sum = lax.fori_loop(clear, stop, lambda j, s: step(j, s, True), query_sum)
    query_g[...] = (query_sum * HD ** (-0.5)).T.astype(BF16)

    @pl.when(at == pl.num_programs(0) - 1)
    def _():
        key_g[...] = key_sum[...].astype(BF16)
        value_g[...] = value_sum[...].astype(BF16)


def feed_body(
    lengths, two, attended, cotangent, expand_w, expand_b, shrink_w, dense_w,
    partial_out, attended_g, hidden_g, shrink_g, dense_g, expand_g, expand_bg, bias_g,
):
    at = pl.program_id(0)

    @pl.when(at == 0)
    def _():
        for total in (shrink_g, dense_g, expand_g, expand_bg, bias_g):
            total[...] = jnp.zeros(total.shape, F32)

    normed, mixed = two[...], attended[...]
    hidden = mm(normed, expand_w[...]) + expand_b[...]
    error = lax.erf(hidden * math.sqrt(0.5))
    cumulative = 0.5 * (1.0 + error)
    active = (hidden * cumulative).astype(BF16)
    put_rows(partial_out, mm(mixed, dense_w[...]) + mm(active, shrink_w[...]))
    token = at * BLOCK + lax.broadcasted_iota(jnp.int32, (BLOCK, D), 0)
    seed = jnp.where(token < lengths[0], token_rows(cotangent).astype(F32), 0.0)
    bias_g[...] += jnp.sum(seed, axis=0, keepdims=True)
    seed = seed.astype(BF16)
    attended_g[...] = mm(seed, dense_w[...], ((1,), (1,))).astype(BF16)
    slope = cumulative + hidden * jnp.exp(-0.5 * hidden * hidden) * (1.0 / math.sqrt(2.0 * math.pi))
    back = (mm(seed, shrink_w[...], ((1,), (1,))) * slope).astype(BF16)
    hidden_g[...] = back
    expand_bg[...] += jnp.sum(back.astype(F32), axis=0, keepdims=True)
    shrink_g[...] += mm(active, seed, ((0,), (0,)))
    dense_g[...] += mm(mixed, seed, ((0,), (0,)))
    expand_g[...] += mm(normed, back, ((0,), (0,)))


def mixed_back_body(
    tokens, one, query_g, key_g, value_g, hidden_g, vectors, qkv_w, expand_w, cos, sin,
    partial_out, qkv_g, qkv_bg, vector_g,
):
    at = pl.program_id(0)

    @pl.when(at == 0)
    def _():
        for total in (qkv_g, qkv_bg, vector_g):
            total[...] = jnp.zeros(total.shape, F32)

    pair = jnp.concatenate([query_g[...].astype(F32), key_g[...].astype(F32)], axis=1)
    pair = turned(pair, cos[...], -sin[...])
    values = value_g[...].astype(F32)
    mixed_g = jnp.concatenate([pair, values, jnp.zeros_like(values)], axis=1)
    mixed_low = mixed_g.astype(BF16)
    qkv_bg[...] += jnp.sum(mixed_low.astype(F32), axis=0, keepdims=True)
    qkv_g[...] += mm(one[...], mixed_low, ((0,), (0,)))
    one_g = mm(mixed_low, qkv_w[...], ((1,), (1,)))
    two_g = mm(hidden_g[...], expand_w[...], ((1,), (1,)))
    unit = normalized(token_rows(tokens).astype(F32))
    vector_g[0:1] += jnp.sum(one_g * unit, axis=0, keepdims=True)
    vector_g[1:2] += jnp.sum(one_g, axis=0, keepdims=True)
    vector_g[2:3] += jnp.sum(two_g * unit, axis=0, keepdims=True)
    vector_g[3:4] += jnp.sum(two_g, axis=0, keepdims=True)
    put_rows(partial_out, one_g * vectors[0:1] + two_g * vectors[2:3])


def split_mesh(mesh):
    groups, members = mesh.shape["blk"], mesh.shape["uly"]
    return Mesh(mesh.devices.reshape(groups // 2, 2, members // 2, 2), ALL)


def across_x(block):
    return lax.ppermute(block, "x", [(0, 1), (1, 0)])


def by_head(residual, cotangent, lengths, positions, masters, momenta, averages):
    slots, span, width = residual.shape
    x = lax.axis_index("x")
    head = lax.axis_index("core") * 8 + lax.axis_index("z") * 2 + lax.axis_index("y")
    owner = x * 16 + head
    groups = lax.axis_size("z") * lax.axis_size("y")
    count = groups * 4 * span
    chunk = masters.shape[0]
    length = lax.dynamic_slice_in_dim(lengths, x, 1)

    def to_slot(rows):
        mine = lax.dynamic_index_in_dim(rows, x, 0, keepdims=False)
        theirs = across_x(lax.dynamic_index_in_dim(rows, 1 - x, 0, keepdims=False))
        both = jnp.where(x == 0, jnp.stack([mine, theirs]), jnp.stack([theirs, mine]))
        return lax.all_gather(both, RING, axis=0).reshape(2, groups, 2, span, width)

    def to_tokens(partial_rows):
        rows = lax.psum_scatter(partial_rows.reshape(16, 2, span, width), RING, scatter_dimension=0, tiled=True)[0]
        mine = lax.dynamic_index_in_dim(rows, x, 0, keepdims=False)
        theirs = across_x(lax.dynamic_index_in_dim(rows, 1 - x, 0, keepdims=False))
        return jnp.where(x == 0, jnp.stack([mine, theirs]), jnp.stack([theirs, mine])).astype(F32)

    onward = [(i, i + 1) for i in range(OWNERS - 1)]
    backward = [(i + 1, i) for i in range(OWNERS - 1)]
    before = lax.ppermute(masters[chunk - D :], ALL, onward)
    after = lax.ppermute(masters[: 4 * D], ALL, backward)
    total = 410 * D
    source = jnp.concatenate(
        [jnp.zeros((7 * D,), F32), before, masters, after, jnp.zeros((total - 12 * D - chunk,), F32)]
    ).reshape(total // LANES, LANES)
    skipped = jnp.where(owner < 8, 4, jnp.where(owner < 11, 7, jnp.where(owner < 22, 8, 12)))
    kind = jnp.where(
        owner < 8,
        PROJECT,
        jnp.where(
            owner == 10,
            PLAIN_EXPAND,
            jnp.where(owner == 21, EXPAND_PLAIN, jnp.where((owner > 10) & (owner < 21), EXPAND, PLAIN)),
        ),
    )
    vector_row = jnp.where(owner == 10, 2080, jnp.where(owner == 21, 1056, jnp.where(owner == 31, 3104, 0)))
    ahead = skipped * D - (chunk - PER * D) * owner
    begin = ahead + 4 * D
    scalars = jnp.stack([begin // LANES, begin % LANES, kind, vector_row]).astype(jnp.int32)
    high = (positions // 256).astype(BF16).reshape(1, 2 * span)
    rest = (positions % 256).astype(BF16).reshape(1, 2 * span)
    places = jnp.concatenate([high, rest, jnp.zeros((14, 2 * span), BF16)])
    sent = call(
        weights_out_body, (1,),
        [whole(source.shape), whole(places.shape)],
        whole((16, SEND_ROWS, LANES)),
        shaped((16, SEND_ROWS, LANES), BF16),
        [pltpu.VMEM((SHIFT_ROWS, LANES), F32)], 1, "weights_out",
    )(scalars, source, places)
    got = lax.all_to_all(jnp.concatenate([sent, sent]), ALL, 0, 0, tiled=True)
    slot_tokens = to_slot(residual)
    slot_cotangent = to_slot(cotangent)
    head_scalar = head.astype(jnp.int32).reshape(1)
    qkv_w, expand_w, second, vectors, qkv_b, expand_b = call(
        weights_in_body, (1,),
        [whole(got.shape)],
        [whole((D, 256)), whole((D, 256)), whole((16, 160, LANES)), whole((8, D)), whole((1, 256)), whole((1, 256))],
        [shaped((D, 256), BF16), shaped((D, 256), BF16), shaped((16, 160, LANES), BF16), shaped((8, D), F32),
         shaped((1, 256), F32), shaped((1, 256), F32)],
        [pltpu.VMEM((24, LANES), F32), pltpu.VMEM((32, LANES), F32)], 1, "weights_in",
    )(head_scalar, got)
    second = lax.all_to_all(second, RING, 0, 0, tiled=True)
    dense_w, shrink_w = call(
        rows_in_body, (1,), [whole(second.shape)], [whole((HD, D)), whole((256, D))],
        [shaped((HD, D), BF16), shaped((256, D), BF16)], name="rows_in",
    )(second)

    halves = got[:, PIECE + 32 : PIECE + 34].astype(F32).reshape(2, 2, groups, 2, slots, span)
    halves = lax.dynamic_index_in_dim(halves, x, 4, keepdims=False)
    place = (halves[:, :, :, 0] * 256.0 + halves[:, :, :, 1]).transpose(2, 0, 1, 3).reshape(count)
    half_dims = ROT // 2
    inverse = ROTARY_BASE ** (-(jnp.arange(half_dims, dtype=F32) * 2.0 / ROT))
    angles = place[:, None] * inverse
    cos, sin = jnp.cos(angles), jnp.sin(angles)
    flat_part = jnp.ones((count, HD - ROT), F32)
    cos = jnp.concatenate([cos, cos, flat_part] * 2, axis=1)
    sin = jnp.concatenate([sin, sin, 0.0 * flat_part] * 2, axis=1)

    steps = (count // BLOCK,)
    token_spec = pl.BlockSpec((2, 1, 2, span, width), lambda i, *_: (0, i, 0, 0, 0))
    token_shape = shaped((2, groups, 2, span, width), BF16)

    def rows_spec(columns):
        return pl.BlockSpec((BLOCK, columns), lambda i, *_: (i, 0))

    def columns_spec(rows):
        return pl.BlockSpec((rows, BLOCK), lambda i, *_: (0, i))

    narrow = shaped((count, HD), BF16)
    one, two, query, key, value = call(
        mixed_body, steps,
        [token_spec, whole((8, D)), whole((D, 256)), whole((1, 256)), rows_spec(LANES), rows_spec(LANES)],
        [rows_spec(D), rows_spec(D), rows_spec(HD), rows_spec(HD), rows_spec(HD)],
        [shaped((count, D), BF16), shaped((count, D), BF16), narrow, narrow, narrow], name="mixed",
    )(slot_tokens, vectors, qkv_w, qkv_b, cos, sin)
    attended, attended_full, log_total = call(
        attend_body, steps,
        [rows_spec(HD), whole((count, HD)), whole((count, HD))],
        [rows_spec(HD), columns_spec(HD), columns_spec(1)],
        [narrow, shaped((HD, count), F32), shaped((1, count), F32)],
        [pltpu.VMEM((count, BLOCK), F32), pltpu.VMEM((HD, count), BF16)], 1, "attend",
    )(length, query, key, value)
    partial_out, attended_g, hidden_g, shrink_g, dense_g, expand_g, expand_bg, bias_g = call(
        feed_body, steps,
        [rows_spec(D), rows_spec(HD), token_spec, whole((D, 256)), whole((1, 256)), whole((256, D)), whole((HD, D))],
        [token_spec, rows_spec(HD), rows_spec(256), whole((256, D)), whole((HD, D)), whole((D, 256)),
         whole((1, 256)), whole((1, D))],
        [token_shape, narrow, shaped((count, 256), BF16), shaped((256, D), F32), shaped((HD, D), F32),
         shaped((D, 256), F32), shaped((1, 256), F32), shaped((1, D), F32)], (), 1, "feed",
    )(length, two, attended, slot_cotangent, expand_w, expand_b, shrink_w, dense_w)
    out_rows = to_tokens(partial_out)
    query_g, key_g, value_g = call(
        attend_back_body, steps,
        [rows_spec(HD), whole((count, HD)), whole((count, HD)), rows_spec(HD), columns_spec(HD), columns_spec(1)],
        [rows_spec(HD), whole((count, HD)), whole((count, HD))],
        [narrow, narrow, narrow],
        [pltpu.VMEM((HD, count), BF16), pltpu.VMEM((count, HD), F32), pltpu.VMEM((count, HD), F32)],
        1, "attend_back",
    )(length, query, key, value, attended_g, attended_full, log_total)
    partial_in, qkv_g, qkv_bg, vector_g = call(
        mixed_back_body, steps,
        [token_spec, rows_spec(D), rows_spec(HD), rows_spec(HD), rows_spec(HD), rows_spec(256), whole((8, D)),
         whole((D, 256)), whole((D, 256)), rows_spec(LANES), rows_spec(LANES)],
        [token_spec, whole((D, 256)), whole((1, 256)), whole((8, D))],
        [token_shape, shaped((D, 256), F32), shaped((1, 256), F32), shaped((8, D), F32)], name="mixed_back",
    )(slot_tokens, one, query_g, key_g, value_g, hidden_g, vectors, qkv_w, expand_w, cos, sin)
    in_rows = to_tokens(partial_in)

    second_g = call(
        rows_out_body, (1,), [whole((HD, D)), whole((256, D))], whole((16, 160, LANES)),
        shaped((16, 160, LANES), BF16), name="rows_out",
    )(dense_g, shrink_g)
    second_g = lax.all_to_all(second_g, RING, 0, 0, tiled=True)
    bias_g = jnp.where(head == 0, bias_g, 0.0)
    vector_g = jnp.concatenate([vector_g[:4], bias_g, jnp.zeros((3, D), F32)])
    sent_g = call(
        grads_out_body, (1,),
        [whole((16, 160, LANES)), whole((D, 256)), whole((D, 256)), whole((8, D)), whole((1, 256)), whole((1, 256))],
        whole((OWNERS, BACK_ROWS, LANES)),
        shaped((OWNERS, BACK_ROWS, LANES), BF16),
        [pltpu.VMEM((32, LANES), F32), pltpu.VMEM((32, LANES), F32)], 1, "grads_out",
    )(head_scalar, second_g, qkv_g, expand_g, vector_g, qkv_bg, expand_bg)
    got_g = lax.all_to_all(sent_g, ALL, 0, 0, tiled=True)
    begin_g = (chunk - PER * D) * owner - skipped * D + 4 * D
    scalars_g = jnp.stack([begin_g // LANES, begin_g % LANES, kind, vector_row]).astype(jnp.int32)
    taken = call(
        grads_in_body, (1,), [whole(got_g.shape)], whole((TAKE_ROWS, LANES)), shaped((TAKE_ROWS, LANES), F32),
        [pltpu.VMEM((SHIFT_ROWS, LANES), F32)], 1, "grads_in",
    )(scalars_g, got_g).reshape(-1)
    from_before = lax.ppermute(taken[D + chunk : 5 * D + chunk], ALL, onward)
    from_after = lax.ppermute(taken[:D], ALL, backward)
    gradients = taken[D : D + chunk]
    gradients = gradients.at[: 4 * D].add(from_before).at[chunk - D :].add(from_after)

    values = residual.astype(F32)
    outputs = (values + out_rows + (vectors[4] + vectors[5])).astype(BF16)
    first_token = ((lax.axis_index("z") * 2 + lax.axis_index("y")) * 4 + x * 2 + lax.axis_index("core")) * span
    token = first_token + jnp.arange(span, dtype=jnp.int32)
    live = token[None, :] < lengths[:, None]
    seed = jnp.where(live[:, :, None], cotangent.astype(F32), 0.0)
    centered = values - jnp.mean(values, axis=-1, keepdims=True)
    scale = lax.rsqrt(jnp.mean(centered * centered, axis=-1, keepdims=True) + EPSILON)
    unit = centered * scale
    back = in_rows - jnp.mean(in_rows, axis=-1, keepdims=True)
    back = scale * (back - unit * jnp.mean(in_rows * unit, axis=-1, keepdims=True))
    input_grad = (seed + back).astype(BF16)

    velocity = MOMENTUM * momenta + gradients
    step_rate = LEARN_RATE / math.sqrt(slots * count)
    updated = masters - step_rate * (gradients + MOMENTUM * velocity)
    averaged = AVERAGE_DECAY * averages + (1.0 - AVERAGE_DECAY) * updated
    return (outputs, input_grad, gradients, updated, velocity, averaged)


def solution(mesh):
    def step(*args):
        slots, tokens = args[0].shape[:2]
        if mesh.size == OWNERS == slots * H and mesh.shape["blk"] == 4 and tokens == 64 * OWNERS:
            tokens_in, flat, used, body = P(None, ("z", "y", "x", "core"), None), P(ALL), split_mesh(mesh), by_head
            places = P(None, ("z", "y", "x", "core"))
        else:
            tokens_in, flat, used, body = P(None, ("uly", "blk"), None), P(("blk", "uly")), mesh, local
            places = P(None, ("uly", "blk"))
        return jax.shard_map(
            body,
            mesh=used,
            in_specs=(tokens_in, tokens_in, P(), places, flat, flat, flat),
            out_specs=(tokens_in, tokens_in, flat, flat, flat, flat),
            check_vma=False,
        )(*args)

    return step
```

```python
from functools import partial
import math

import jax
import jax.numpy as jnp
from jax import lax
from jax.experimental import pallas as pl
from jax.experimental.pallas import tpu as pltpu
from jax.sharding import Mesh, PartitionSpec as P

D = 1024
H = 16
HD = 64
ROT = 16
FF = 4096


EPSILON = 1e-05
NEGATIVE = -1e30
MOMENTUM = 0.5
LEARN_RATE = 0.05
AVERAGE_DECAY = 0.5
ROTARY_BASE = 10000.0


def passed_along(block, axis, distance):
    devices = range(lax.axis_size(axis))
    route = [((i - distance) % len(devices), i) for i in devices]
    return lax.ppermute(block, axis, route)


def unpack(flat_vector):
    layouts = [
        (D,),
        (D,),
        (D,),
        (D,),
        (D, 3 * D),
        (3 * D,),
        (D, D),
        (D,),
        (D, FF),
        (FF,),
        (FF, D),
        (D,),
    ]
    pieces = []
    cursor = 0
    for layout in layouts:
        number = math.prod(layout)
        pieces.append(flat_vector[cursor : cursor + number].reshape(layout))
        cursor += number
    return pieces


def layer_norm(values, gain, shift):
    centered = values - jnp.mean(values, axis=-1, keepdims=True)
    variance = jnp.mean(centered * centered, axis=-1, keepdims=True)
    return centered * lax.rsqrt(variance + EPSILON) * gain + shift


def rotary_tables(positions):
    half_dims = ROT // 2
    inverse = ROTARY_BASE ** (-(jnp.arange(half_dims, dtype=jnp.float32) * 2.0 / ROT))
    angles = positions.astype(jnp.float32)[..., None] * inverse
    return (jnp.cos(angles), jnp.sin(angles))


def rotate(values, cos_table, sin_table):
    half_dims = ROT // 2
    first_half = values[..., :half_dims]
    second_half = values[..., half_dims:ROT]
    return jnp.concatenate(
        [
            first_half * cos_table - second_half * sin_table,
            second_half * cos_table + first_half * sin_table,
            values[..., ROT:],
        ],
        axis=-1,
    )


def group_tokens(source, group_count, uly_count, span_rows):
    spans = jnp.arange(uly_count, dtype=jnp.int32)[:, None] * group_count + source
    return (spans * span_rows + jnp.arange(span_rows, dtype=jnp.int32)[None, :]).reshape(-1)


def block_scores(queries, keys_rows, row_tokens, col_tokens, length):
    scores = jnp.einsum(
        "qhd,khd->hqk", queries, keys_rows, preferred_element_type=jnp.float32
    ) * HD ** (-0.5)
    allowed = (col_tokens[None, :] <= row_tokens[:, None]) & (col_tokens[None, :] < length)
    return jnp.where(allowed[None], scores, NEGATIVE)


def is_live(row_tokens, col_tokens, length):
    return (col_tokens[0] <= row_tokens[-1]) & (col_tokens[0] < length)


def fold_stats(row_max, row_total, queries, key_value, lengths, row_tokens, col_tokens):

    def per_slot(inputs):
        slot_max, slot_total, slot_queries, slot_pairs, length = inputs

        def compute(current):
            prev_max, prev_total = current
            scores = block_scores(slot_queries, slot_pairs[:, :, 0], row_tokens, col_tokens, length)
            next_max = jnp.maximum(prev_max, jnp.max(scores, axis=-1))
            next_total = prev_total * jnp.exp(prev_max - next_max) + jnp.sum(
                jnp.exp(scores - next_max[..., None]), axis=-1
            )
            return (next_max, next_total)

        return lax.cond(
            is_live(row_tokens, col_tokens, length),
            compute,
            lambda current: current,
            (slot_max, slot_total),
        )

    return lax.map(per_slot, (row_max, row_total, queries, key_value, lengths))


def fold_values(attended, queries, key_value, log_total, lengths, row_tokens, col_tokens):

    def per_slot(inputs):
        slot_out, slot_queries, slot_pairs, slot_log, length = inputs

        def compute(current):
            scores = block_scores(slot_queries, slot_pairs[:, :, 0], row_tokens, col_tokens, length)
            prob_low = jnp.exp(scores - slot_log[..., None]).astype(jnp.bfloat16)
            return current + jnp.einsum(
                "hqk,khd->qhd", prob_low, slot_pairs[:, :, 1], preferred_element_type=jnp.float32
            )

        return lax.cond(
            is_live(row_tokens, col_tokens, length), compute, lambda current: current, slot_out
        )

    return lax.map(per_slot, (attended, queries, key_value, log_total, lengths))


def fold_grads(
    query_grad,
    pair_grad,
    queries,
    key_value,
    grad_out,
    log_total,
    row_delta,
    lengths,
    row_tokens,
    col_tokens,
):

    def per_slot(inputs):
        (
            slot_qgrad,
            slot_pgrad,
            slot_queries,
            slot_pairs,
            slot_gout,
            slot_log,
            slot_delta,
            length,
        ) = inputs

        def compute(current):
            cur_qgrad, cur_pgrad = current
            scores = block_scores(slot_queries, slot_pairs[:, :, 0], row_tokens, col_tokens, length)
            attend_prob = jnp.exp(scores - slot_log[..., None])
            prob_low = attend_prob.astype(jnp.bfloat16)
            prob_grad = jnp.einsum(
                "qhd,khd->hqk", slot_gout, slot_pairs[:, :, 1], preferred_element_type=jnp.float32
            )
            score_grad = (attend_prob * (prob_grad - slot_delta[..., None])).astype(jnp.bfloat16)
            cur_qgrad = cur_qgrad + jnp.einsum(
                "hqk,khd->qhd", score_grad, slot_pairs[:, :, 0], preferred_element_type=jnp.float32
            ) * HD ** (-0.5)
            key_grad = jnp.einsum(
                "hqk,qhd->khd", score_grad, slot_queries, preferred_element_type=jnp.float32
            ) * HD ** (-0.5)
            value_grad = jnp.einsum(
                "hqk,qhd->khd", prob_low, slot_gout, preferred_element_type=jnp.float32
            )
            return (cur_qgrad, cur_pgrad + jnp.stack([key_grad, value_grad], axis=2))

        return lax.cond(
            is_live(row_tokens, col_tokens, length),
            compute,
            lambda current: current,
            (slot_qgrad, slot_pgrad),
        )

    return lax.map(
        per_slot,
        (query_grad, pair_grad, queries, key_value, grad_out, log_total, row_delta, lengths),
    )


def local(residual, cotangent, lengths, positions, masters, momenta, averages):
    slot_count, span_rows, model_width = residual.shape
    group_count = lax.axis_size("blk")
    uly_count = lax.axis_size("uly")
    group_index = lax.axis_index("blk")
    uly_index = lax.axis_index("uly")
    block_rows = uly_count * span_rows
    full_rows = group_count * block_rows
    local_heads = H // uly_count
    token_rows = slot_count * span_rows
    row_tokens = group_tokens(group_index, group_count, uly_count, span_rows)

    def tokens_of(source):
        return group_tokens(source, group_count, uly_count, span_rows)

    gathered = lax.all_gather(masters.astype(jnp.bfloat16), ("blk", "uly"), axis=0, tiled=True)
    (
        gain_one,
        shift_one,
        gain_two,
        shift_two,
        project_w,
        project_b,
        dense_w,
        dense_b,
        expand_w,
        expand_b,
        shrink_w,
        shrink_b,
    ) = unpack(gathered)
    values = residual.astype(jnp.float32).reshape(token_rows, model_width)
    normed_one, norm_back_one = jax.vjp(
        layer_norm, values, gain_one.astype(jnp.float32), shift_one.astype(jnp.float32)
    )
    normed_two, norm_back_two = jax.vjp(
        layer_norm, values, gain_two.astype(jnp.float32), shift_two.astype(jnp.float32)
    )
    normed_one = normed_one.astype(jnp.bfloat16)
    normed_two = normed_two.astype(jnp.bfloat16)
    mixed_rows = jnp.dot(
        normed_one, project_w, preferred_element_type=jnp.float32
    ) + project_b.astype(jnp.float32)
    mixed_rows = mixed_rows.reshape(slot_count, span_rows, H, 3, HD)
    cos_table, sin_table = rotary_tables(positions)
    cos_table = cos_table[:, :, None, None, :]
    sin_table = sin_table[:, :, None, None, :]
    turned, turn_back = jax.vjp(
        lambda pair_rows: rotate(pair_rows, cos_table, sin_table), mixed_rows[:, :, :, 0:2]
    )
    packed = jnp.concatenate([turned, mixed_rows[:, :, :, 2:3]], axis=3).astype(jnp.bfloat16)
    packed = packed.reshape(slot_count, span_rows, 3 * model_width)
    heads_rows = lax.all_to_all(packed, "uly", split_axis=2, concat_axis=1, tiled=True).reshape(
        slot_count, block_rows, local_heads, 3, HD
    )
    queries = heads_rows[:, :, :, 0]
    key_value = heads_rows[:, :, :, 1:3]
    row_max = jnp.full((slot_count, local_heads, block_rows), NEGATIVE, jnp.float32)
    row_total = jnp.zeros((slot_count, local_heads, block_rows), jnp.float32)
    attended = jnp.zeros((slot_count, block_rows, local_heads, HD), jnp.float32)
    last_tokens = tokens_of((group_index + 1) % group_count)

    def stats_turn(turn_index, carried):
        pairs_now, cur_max, cur_total = carried
        col_tokens = tokens_of((group_index - turn_index) % group_count)
        cur_max, cur_total = fold_stats(
            cur_max, cur_total, queries, pairs_now, lengths, row_tokens, col_tokens
        )
        pairs_now = passed_along(pairs_now, "blk", 1)
        return (pairs_now, cur_max, cur_total)

    pairs_now, row_max, row_total = lax.fori_loop(
        0, group_count - 1, stats_turn, (key_value, row_max, row_total)
    )
    row_max, row_total = fold_stats(
        row_max, row_total, queries, pairs_now, lengths, row_tokens, last_tokens
    )
    log_total = row_max + jnp.log(row_total)

    def value_turn(turn_index, carried):
        pairs_now, cur_out = carried
        col_tokens = tokens_of((group_index - turn_index) % group_count)
        cur_out = fold_values(
            cur_out, queries, pairs_now, log_total, lengths, row_tokens, col_tokens
        )
        pairs_now = passed_along(pairs_now, "blk", 1)
        return (pairs_now, cur_out)

    pairs_now, attended = lax.fori_loop(0, group_count - 1, value_turn, (key_value, attended))
    attended = fold_values(
        attended, queries, pairs_now, log_total, lengths, row_tokens, last_tokens
    )
    heads_out = attended.astype(jnp.bfloat16).reshape(slot_count, block_rows, local_heads * HD)
    merged = lax.all_to_all(heads_out, "uly", split_axis=1, concat_axis=2, tiled=True).reshape(
        token_rows, model_width
    )
    branch_attn = jnp.dot(merged, dense_w, preferred_element_type=jnp.float32) + dense_b.astype(
        jnp.float32
    )
    hidden_pre = jnp.dot(
        normed_two, expand_w, preferred_element_type=jnp.float32
    ) + expand_b.astype(jnp.float32)
    activated, gelu_back = jax.vjp(partial(jax.nn.gelu, approximate=False), hidden_pre)
    activated_low = activated.astype(jnp.bfloat16)
    branch_feed = jnp.dot(
        activated_low, shrink_w, preferred_element_type=jnp.float32
    ) + shrink_b.astype(jnp.float32)
    outputs = (
        (values + branch_attn + branch_feed)
        .astype(jnp.bfloat16)
        .reshape(slot_count, span_rows, model_width)
    )
    first_token = (uly_index * group_count + group_index) * span_rows
    token_index = first_token + jnp.arange(span_rows, dtype=jnp.int32)
    live_mask = (token_index[None, :] < lengths[:, None]).astype(jnp.float32)
    seed_grad = (cotangent.astype(jnp.float32) * live_mask[:, :, None]).reshape(
        token_rows, model_width
    )
    seed_low = seed_grad.astype(jnp.bfloat16)
    dense_w_grad = jnp.einsum("ra,rb->ab", merged, seed_low, preferred_element_type=jnp.float32)
    bias_grad = jnp.sum(seed_low.astype(jnp.float32), axis=0)
    merged_grad = jnp.einsum(
        "rb,ab->ra", seed_low, dense_w, preferred_element_type=jnp.float32
    ).astype(jnp.bfloat16)
    shrink_w_grad = jnp.einsum(
        "rf,rb->fb", activated_low, seed_low, preferred_element_type=jnp.float32
    )
    activated_grad = jnp.einsum("rb,fb->rf", seed_low, shrink_w, preferred_element_type=jnp.float32)
    hidden_grad = gelu_back(activated_grad)[0].astype(jnp.bfloat16)
    expand_w_grad = jnp.einsum(
        "ra,rf->af", normed_two, hidden_grad, preferred_element_type=jnp.float32
    )
    expand_b_grad = jnp.sum(hidden_grad.astype(jnp.float32), axis=0)
    normed_two_grad = jnp.einsum(
        "rf,af->ra", hidden_grad, expand_w, preferred_element_type=jnp.float32
    )
    grad_heads = lax.all_to_all(
        merged_grad.reshape(slot_count, span_rows, model_width),
        "uly",
        split_axis=2,
        concat_axis=1,
        tiled=True,
    )
    grad_out = grad_heads.reshape(slot_count, block_rows, local_heads, HD)
    row_delta = jnp.sum(grad_out.astype(jnp.float32) * attended, axis=-1).transpose(0, 2, 1)
    query_grad = jnp.zeros((slot_count, block_rows, local_heads, HD), jnp.float32)
    pair_grad = jnp.zeros((slot_count, block_rows, local_heads, 2, HD), jnp.float32)

    def grad_turn(turn_index, carried):
        pairs_now, cur_pgrad, cur_qgrad = carried
        col_tokens = tokens_of((group_index - turn_index) % group_count)
        cur_qgrad, cur_pgrad = fold_grads(
            cur_qgrad,
            cur_pgrad,
            queries,
            pairs_now,
            grad_out,
            log_total,
            row_delta,
            lengths,
            row_tokens,
            col_tokens,
        )
        pairs_now = passed_along(pairs_now, "blk", 1)
        cur_pgrad = passed_along(cur_pgrad.astype(jnp.bfloat16), "blk", 1).astype(cur_pgrad.dtype)
        return (pairs_now, cur_pgrad, cur_qgrad)

    pairs_now, pair_grad, query_grad = lax.fori_loop(
        0, group_count - 1, grad_turn, (key_value, pair_grad, query_grad)
    )
    query_grad, pair_grad = fold_grads(
        query_grad,
        pair_grad,
        queries,
        pairs_now,
        grad_out,
        log_total,
        row_delta,
        lengths,
        row_tokens,
        last_tokens,
    )
    pair_grad = passed_along(pair_grad.astype(jnp.bfloat16), "blk", 1).astype(pair_grad.dtype)
    back_packed = jnp.concatenate(
        [query_grad.astype(jnp.bfloat16)[:, :, :, None], pair_grad.astype(jnp.bfloat16)], axis=3
    )
    back_packed = back_packed.reshape(slot_count, block_rows, local_heads * 3 * HD)
    token_grads = lax.all_to_all(
        back_packed, "uly", split_axis=1, concat_axis=2, tiled=True
    ).reshape(slot_count, span_rows, H, 3, HD)
    turned_grad = turn_back(token_grads[:, :, :, 0:2].astype(jnp.float32))[0]
    mixed_grad = jnp.concatenate(
        [turned_grad, token_grads[:, :, :, 2:3].astype(jnp.float32)], axis=3
    ).astype(jnp.bfloat16)
    mixed_grad = mixed_grad.reshape(token_rows, 3 * model_width)
    project_w_grad = jnp.einsum(
        "ra,rc->ac", normed_one, mixed_grad, preferred_element_type=jnp.float32
    )
    project_b_grad = jnp.sum(mixed_grad.astype(jnp.float32), axis=0)
    normed_one_grad = jnp.einsum(
        "rc,ac->ra", mixed_grad, project_w, preferred_element_type=jnp.float32
    )
    values_one, gain_one_grad, shift_one_grad = norm_back_one(normed_one_grad)
    values_two, gain_two_grad, shift_two_grad = norm_back_two(normed_two_grad)
    input_grad = (
        (seed_grad + values_one + values_two)
        .astype(jnp.bfloat16)
        .reshape(slot_count, span_rows, model_width)
    )
    local_grads = jnp.concatenate(
        [
            gain_one_grad,
            shift_one_grad,
            gain_two_grad,
            shift_two_grad,
            project_w_grad.reshape(-1),
            project_b_grad,
            dense_w_grad.reshape(-1),
            bias_grad,
            expand_w_grad.reshape(-1),
            expand_b_grad,
            shrink_w_grad.reshape(-1),
            bias_grad,
        ]
    )
    gradients = lax.psum_scatter(local_grads, ("blk", "uly"), scatter_dimension=0, tiled=True)
    velocity = MOMENTUM * momenta + gradients
    step_rate = LEARN_RATE / math.sqrt(slot_count * full_rows)
    updated = masters - step_rate * (gradients + MOMENTUM * velocity)
    averaged = AVERAGE_DECAY * averages + (1.0 - AVERAGE_DECAY) * updated
    return (outputs, input_grad, gradients, updated, velocity, averaged)


LANES = 128
BLOCK = 256
RING = ("core", "z", "y")
ALL = ("x", "core", "z", "y")
F32 = jnp.float32
BF16 = jnp.bfloat16


def call(body, grid, in_specs, out_specs, out_shape, scratch=(), prefetch=0, name=None, aliases=None):
    return pl.pallas_call(
        body,
        grid_spec=pltpu.PrefetchScalarGridSpec(
            num_scalar_prefetch=prefetch,
            grid=grid,
            in_specs=in_specs,
            out_specs=out_specs,
            scratch_shapes=scratch,
        ),
        out_shape=out_shape,
        name=name,
        input_output_aliases=aliases or {},
        compiler_params=pltpu.CompilerParams(vmem_limit_bytes=56 << 20),
    )


def whole(shape):
    return pl.BlockSpec(shape, lambda *_: (0,) * len(shape))


def shaped(shape, kind):
    return jax.ShapeDtypeStruct(shape, kind)


def mm(a, b, dims=((1,), (0,))):
    return lax.dot_general(a, b, (dims, ((), ())), preferred_element_type=F32)


def low_lanes(shape):
    return lax.broadcasted_iota(jnp.int32, shape, len(shape) - 1) < LANES // 2


def swap(a):
    return pltpu.roll(a, LANES // 2, 1)


def join(a, a_half, b, b_half):
    first = swap(a) if a_half else a
    second = b if b_half else swap(b)
    return jnp.where(low_lanes(a.shape), first, second)


OWNERS = 32
PER = (3 * D + D + FF + FF) // OWNERS
FLAT = PER * D // LANES
PIECE = FLAT // 16
LEAD = 4 * D // LANES
EDGE = PER * D + 13 * D // OWNERS
PROJECT, PLAIN, PLAIN_EXPAND, EXPAND, EXPAND_PLAIN = range(5)


def kind_of(c):
    return (
        PROJECT
        if c < 8
        else PLAIN
        if c < 10 or c > 21
        else PLAIN_EXPAND
        if c == 10
        else EXPAND_PLAIN
        if c == 21
        else EXPAND
    )


def plain_place(row, base, count):
    local = row - base
    half = int(local >= count // 2)
    return local - half * (count // 2), half


def dense_place(row):
    if row < 768:
        c = 8 + row // 384
        return (c, 0) + plain_place(row, 384 * (c - 8), 384)
    return (10, 0) + plain_place(row, 768, 256)


def shrink_place(row):
    if row < 256:
        return (21, 64) + plain_place(row, 0, 256)
    c = 22 + (row - 256) // 384
    return (c, 0) + plain_place(row, 256 + 384 * (c - 22), 384)


def expand_places():
    places = [(10, 128, 0, 32)]
    places += [(c, 0, 32 + 96 * (c - 11), 96) for c in range(11, 21)]
    places += [(21, 0, 992, 32)]
    return places


def shifted_rows(source, start, shift, at, rows):
    turn = (LANES - shift) % LANES
    first = pltpu.roll(source[pl.ds(start + at, rows), :], turn, 1)
    second = pltpu.roll(source[pl.ds(start + at + 1, rows), :], turn, 1)
    lane = lax.broadcasted_iota(jnp.int32, (rows, LANES), 1)
    return jnp.where(lane < LANES - shift, first, second)


SHIFT_ROWS = 3200
SEND_ROWS = PIECE + 32
OWN_ROW = 64


def weights_out_body(scalars, before, own, after, out, source, flat, tail):
    start, shift, kind, vector_row = scalars[0], scalars[1], scalars[2], scalars[3]
    count = own.shape[0]
    source[0 : OWN_ROW - 8] = jnp.zeros((OWN_ROW - 8, LANES), F32)
    source[OWN_ROW - 8 : OWN_ROW] = before[...]

    def copy(step, carry):
        at = pl.multiple_of(step * 88, 8)
        source[pl.ds(at + OWN_ROW, 88), :] = own[pl.ds(at, 88), :]
        return carry

    lax.fori_loop(0, count // 88, copy, 0)
    last = OWN_ROW + EDGE // LANES
    source[OWN_ROW + count :] = jnp.zeros((source.shape[0] - OWN_ROW - count, LANES), F32)
    edge = EDGE % LANES
    tail[...] = jnp.zeros(tail.shape, F32)
    tail[7:8] = source[last : last + 1]
    tail[8:40] = pltpu.roll(after[...], edge, 1)
    lane = lax.broadcasted_iota(jnp.int32, (40, LANES), 1)
    source[last : last + 40] = jnp.where(lane < edge, tail[7:47], tail[8:48])

    def align(step, carry):
        at = pl.multiple_of(step * 80, 8)
        flat[pl.ds(at, 80), :] = shifted_rows(source, start, shift, at, 80)
        return carry

    lax.fori_loop(0, SHIFT_ROWS // 80, align, 0)

    def rows(first, count, stride):
        return flat[pl.ds(first, count, stride), :]

    def plain(base, count, to):
        for m in range(8):
            tile = rows(base + m, count, 8)
            a, b = tile[: count // 2], tile[count // 2 :]
            out[2 * m, to : to + count // 2] = join(a, 0, b, 0).astype(BF16)
            out[2 * m + 1, to : to + count // 2] = join(a, 1, b, 1).astype(BF16)

    def expand(base, count, to):
        for r in range(16):
            out[r, to : to + count] = rows(base + 2 * r, count, 32).astype(BF16)
            out[r, to + count : to + 2 * count] = rows(base + 2 * r + 1, count, 32).astype(BF16)

    def project(base):
        for m in range(8):
            first, middle, last = (rows(base + 3 * m + j, 128, 24) for j in range(3))
            out[2 * m, 0:128] = first.astype(BF16)
            out[2 * m, 128:192] = join(middle[:64], 0, middle[64:], 0).astype(BF16)
            out[2 * m + 1, 0:128] = join(middle, 1, last, 0).astype(BF16)
            out[2 * m + 1, 128:192] = join(last[:64], 1, last[64:], 1).astype(BF16)

    @pl.when(kind == PROJECT)
    def _():
        project(LEAD)

    @pl.when(kind == PLAIN)
    def _():
        plain(LEAD, 384, 0)

    @pl.when(kind == PLAIN_EXPAND)
    def _():
        plain(LEAD, 256, 0)
        expand(LEAD + 2048 + 8, 32, 128)

    @pl.when(kind == EXPAND)
    def _():
        expand(LEAD, 96, 0)

    @pl.when(kind == EXPAND_PLAIN)
    def _():
        expand(LEAD, 32, 0)
        plain(LEAD + 1024 + 32, 256, 64)

    vectors = flat[pl.ds(vector_row, 32), :].astype(BF16)
    for r in range(16):
        out[r, PIECE : PIECE + 32] = vectors


def weights_in_body(scalars, got, qkv_w, expand_w, second, vectors, qkv_b, expand_b, project_rows, expand_rows):
    head = scalars[0]
    low = low_lanes((64, LANES))
    for c in range(8):
        qkv_w[128 * c : 128 * c + 128, 0:128] = got[c, 0:128]
        packed = got[c, 128:192].astype(F32)
        qkv_w[128 * c : 128 * c + 64, 128:256] = jnp.where(low, packed, 0.0).astype(BF16)
        qkv_w[128 * c + 64 : 128 * c + 128, 128:256] = jnp.where(low, swap(packed), 0.0).astype(BF16)
    for c, at, row, count in expand_places():
        expand_w[row : row + count, 0:128] = got[c, at : at + count]
        expand_w[row : row + count, 128:256] = got[c, at + count : at + 2 * count]

    for h in range(16):
        c, at, row, half = dense_place(64 * h)
        tile = got[c, at + row : at + row + 64].astype(F32)
        second[h, 0:32] = join(tile[:32], half, tile[32:], half).astype(BF16)
        for part in range(2):
            c, at, row, half = shrink_place(256 * h + 64 * part)
            tile = got[c, at + row : at + row + 64].astype(F32)
            c, at, row, other = shrink_place(256 * h + 128 + 64 * part)
            after = got[c, at + row : at + row + 64].astype(F32)
            second[h, 32 + 64 * part : 96 + 64 * part] = join(tile, half, after, other).astype(BF16)

    def vector(c, at, to):
        tile = got[c, PIECE + at : PIECE + at + 8].astype(F32)
        for j in range(8):
            vectors[to : to + 1, 128 * j : 128 * j + 128] = tile[j : j + 1]

    vectors[...] = jnp.zeros(vectors.shape, F32)
    for v in range(4):
        vector(0, 8 * v, v)
    vector(10, 0, 4)
    vector(31, 0, 5)
    project_rows[...] = got[8, PIECE + 8 : PIECE + 32].astype(F32)
    expand_rows[...] = got[21, PIECE : PIECE + 32].astype(F32)
    row = head // 2 * 3
    first, middle, last = (project_rows[pl.ds(row + j, 1), :] for j in range(3))
    odd = head % 2 == 1
    qkv_b[0:1, 0:128] = jnp.where(odd, join(middle, 1, last, 0), first)
    value = jnp.where(odd, swap(last), middle)
    qkv_b[0:1, 128:256] = jnp.where(low_lanes((1, LANES)), value, 0.0)
    expand_b[0:1, 0:128] = expand_rows[pl.ds(2 * head, 1), :]
    expand_b[0:1, 128:256] = expand_rows[pl.ds(2 * head + 1, 1), :]


def rows_in_body(got, dense_w, shrink_w):
    for m in range(8):
        even, odd = got[2 * m].astype(F32), got[2 * m + 1].astype(F32)
        columns = slice(128 * m, 128 * m + 128)
        for out, at, half in ((dense_w, 0, 32), (shrink_w, 32, 128)):
            a, b = even[at : at + half], odd[at : at + half]
            out[0:half, columns] = join(a, 0, b, 0).astype(BF16)
            out[half : 2 * half, columns] = join(a, 1, b, 1).astype(BF16)


def rows_out_body(dense_g, shrink_g, out):
    for m in range(8):
        columns = slice(128 * m, 128 * m + 128)
        for source, at, half in ((dense_g, 0, 32), (shrink_g, 32, 128)):
            a, b = source[0:half, columns], source[half : 2 * half, columns]
            out[2 * m, at : at + half] = join(a, 0, b, 0).astype(BF16)
            out[2 * m + 1, at : at + half] = join(a, 1, b, 1).astype(BF16)


BACK_ROWS = PIECE + 32


def grads_out_body(scalars, second, qkv_g, expand_g, vector_g, qkv_bg, expand_bg, out, project_rows, expand_rows):
    head = scalars[0]
    out[...] = jnp.zeros(out.shape, BF16)
    for c in range(8):
        out[c, 0:128] = qkv_g[128 * c : 128 * c + 128, 0:128].astype(BF16)
        a = qkv_g[128 * c : 128 * c + 64, 128:256]
        b = qkv_g[128 * c + 64 : 128 * c + 128, 128:256]
        out[c, 128:192] = join(a, 0, b, 0).astype(BF16)
    for c, at, row, count in expand_places():
        out[c, at : at + count] = expand_g[row : row + count, 0:128].astype(BF16)
        out[c, at + count : at + 2 * count] = expand_g[row : row + count, 128:256].astype(BF16)

    def dense_rows(row):
        packed = second[row // 64, 0:32].astype(F32)
        return jnp.concatenate([packed, swap(packed)], axis=0)

    def shrink_rows(row):
        h, part = row // 256, row % 256 // 64
        packed = second[h, 32 + part % 2 * 64 : 96 + part % 2 * 64].astype(F32)
        return swap(packed) if part >= 2 else packed

    def plain(c, to, base, count, take):
        for i in range(count // 128):
            a, b = take(base + 64 * i), take(base + count // 2 + 64 * i)
            out[c, to + 64 * i : to + 64 * i + 64] = join(a, 0, b, 0).astype(BF16)

    plain(8, 0, 0, 384, dense_rows)
    plain(9, 0, 384, 384, dense_rows)
    plain(10, 0, 768, 256, dense_rows)
    plain(21, 64, 0, 256, shrink_rows)
    for c in range(22, 32):
        plain(c, 0, 256 + 384 * (c - 22), 384, shrink_rows)

    def rows_of(row):
        return jnp.concatenate([vector_g[row : row + 1, 128 * j : 128 * j + 128] for j in range(8)], axis=0)

    gains = jnp.concatenate([rows_of(v) for v in range(4)], axis=0)
    out[0, PIECE : PIECE + 32] = gains.astype(BF16)
    bias = jnp.concatenate([rows_of(4), jnp.zeros((8, LANES), F32)], axis=0).astype(BF16)
    out[10, PIECE : PIECE + 16] = bias
    out[31, PIECE : PIECE + 16] = bias
    project_rows[...] = jnp.zeros(project_rows.shape, F32)
    expand_rows[...] = jnp.zeros(expand_rows.shape, F32)
    pair, value = qkv_bg[0:1, 0:128], qkv_bg[0:1, 128:256]
    low = low_lanes((1, LANES))
    row = 8 + head // 2 * 3
    odd = head % 2 == 1
    project_rows[pl.ds(row, 1), :] = jnp.where(odd, 0.0, pair)
    project_rows[pl.ds(row + 1, 1), :] = jnp.where(
        odd, jnp.where(low, 0.0, swap(pair)), jnp.where(low, value, 0.0)
    )
    project_rows[pl.ds(row + 2, 1), :] = jnp.where(odd, join(pair, 1, value, 0), 0.0)
    out[8, PIECE : PIECE + 32] = project_rows[...].astype(BF16)
    expand_rows[pl.ds(2 * head, 1), :] = expand_bg[0:1, 0:128]
    expand_rows[pl.ds(2 * head + 1, 1), :] = expand_bg[0:1, 128:256]
    out[21, PIECE : PIECE + 32] = expand_rows[...].astype(BF16)


TAKE_ROWS = 3120


def grads_in_body(scalars, got, out, flat):
    start, shift, kind, vector_row = scalars[0], scalars[1], scalars[2], scalars[3]
    lead = LEAD + 8

    def clear(step, carry):
        flat[pl.ds(pl.multiple_of(step * 80, 8), 80), :] = jnp.zeros((80, LANES), F32)
        return carry

    lax.fori_loop(0, SHIFT_ROWS // 80, clear, 0)

    def add_vectors(source, total):
        return total + got[source, PIECE : PIECE + 32].astype(F32)

    flat[pl.ds(vector_row + 8, 32), :] = lax.fori_loop(0, OWNERS, add_vectors, jnp.zeros((32, LANES), F32))

    def taken(r, at, count):
        return got[r, at : at + count].astype(F32) + got[16 + r, at : at + count].astype(F32)

    def plain(base, count, at):
        half = count // 2
        for m in range(8):
            a, b = taken(2 * m, at, half), taken(2 * m + 1, at, half)
            flat[pl.ds(base + m, half, 8), :] = join(a, 0, b, 0)
            flat[pl.ds(base + m + 8 * half, half, 8), :] = join(a, 1, b, 1)

    def expand(base, count, at):
        for r in range(16):
            flat[pl.ds(base + 2 * r, count, 32), :] = taken(r, at, count)
            flat[pl.ds(base + 2 * r + 1, count, 32), :] = taken(r, at + count, count)

    def project(base):
        for m in range(8):
            pair, values = taken(2 * m, 0, 128), taken(2 * m, 128, 64)
            odd_pair, odd_values = taken(2 * m + 1, 0, 128), taken(2 * m + 1, 128, 64)
            values = jnp.concatenate([values, swap(values)], axis=0)
            odd_values = jnp.concatenate([odd_values, swap(odd_values)], axis=0)
            flat[pl.ds(base + 3 * m, 128, 24), :] = pair
            flat[pl.ds(base + 3 * m + 1, 128, 24), :] = join(values, 0, odd_pair, 0)
            flat[pl.ds(base + 3 * m + 2, 128, 24), :] = join(odd_pair, 1, odd_values, 0)

    @pl.when(kind == PROJECT)
    def _():
        project(lead)

    @pl.when(kind == PLAIN)
    def _():
        plain(lead, 384, 0)

    @pl.when(kind == PLAIN_EXPAND)
    def _():
        plain(lead, 256, 0)
        expand(lead + 2048 + 8, 32, 128)

    @pl.when(kind == EXPAND)
    def _():
        expand(lead, 96, 0)

    @pl.when(kind == EXPAND_PLAIN)
    def _():
        expand(lead, 32, 0)
        plain(lead + 1024 + 32, 256, 64)

    def align(step, carry):
        at = pl.multiple_of(step * 80, 8)
        out[pl.ds(at, 80), :] = shifted_rows(flat, start, shift, at, 80)
        return carry

    lax.fori_loop(0, TAKE_ROWS // 80, align, 0)


def token_rows(ref):
    return jnp.concatenate([ref[0, 0, 0], ref[1, 0, 0], ref[0, 0, 1], ref[1, 0, 1]], axis=0)


def put_rows(ref, rows):
    step = rows.shape[0] // 4
    for i, (core, x) in enumerate(((0, 0), (1, 0), (0, 1), (1, 1))):
        ref[core, 0, x] = rows[step * i : step * i + step].astype(ref.dtype)


def normalized(values):
    centered = values - jnp.mean(values, axis=-1, keepdims=True)
    variance = jnp.mean(centered * centered, axis=-1, keepdims=True)
    return centered * lax.rsqrt(variance + EPSILON)


def turned(pair, cos, sin):
    lane = lax.broadcasted_iota(jnp.int32, pair.shape, 1) % HD
    half = ROT // 2
    other = jnp.where(
        lane < half, -pltpu.roll(pair, LANES - half, 1), jnp.where(lane < ROT, pltpu.roll(pair, half, 1), 0.0)
    )
    return pair * cos + other * sin


def mixed_body(tokens, vectors, qkv_w, qkv_b, cos, sin, one, two, query, key, value):
    unit = normalized(token_rows(tokens).astype(F32))
    first = (unit * vectors[0:1] + vectors[1:2]).astype(BF16)
    one[...] = first
    two[...] = (unit * vectors[2:3] + vectors[3:4]).astype(BF16)
    mixed = mm(first, qkv_w[...]) + qkv_b[...]
    pair = turned(mixed[:, :LANES], cos[...], sin[...])
    query[...] = pair[:, :HD].astype(BF16) * HD ** (-0.5)
    key[...] = pair[:, HD:].astype(BF16)
    value[...] = mixed[:, LANES : LANES + HD].astype(BF16)


def masked_scores(key, query_t, at, first_query, length):
    scores = mm(key, query_t)
    keys = at * BLOCK + lax.broadcasted_iota(jnp.int32, scores.shape, 0)
    queries = first_query + lax.broadcasted_iota(jnp.int32, scores.shape, 1)
    return jnp.where((keys <= queries) & (keys < length), scores, NEGATIVE)


def folded(values, op):
    parts = [values[8 * i : 8 * i + 8] for i in range(values.shape[0] // 8)]
    while len(parts) > 1:
        parts = [op(a, b) for a, b in zip(parts[::2], parts[1::2])]
    return parts[0]


def attend_body(lengths, query, key, value, low_out, full_out, log_out, scores, value_t):
    at = pl.program_id(0)
    length = lengths[0]

    @pl.when(at == 0)
    def _():
        value_t[...] = value[...].astype(F32).T.astype(BF16)

    query_t = query[...].astype(F32).T.astype(BF16)
    clear = jnp.minimum(at, length // BLOCK)
    stop = jnp.minimum(at, (length - 1) // BLOCK) + 1

    def rows(j):
        return pl.ds(pl.multiple_of(j * BLOCK, BLOCK), BLOCK)

    def score(j, top, masked):
        if masked:
            tile = masked_scores(key[rows(j), :], query_t, j, at * BLOCK, length)
        else:
            tile = mm(key[rows(j), :], query_t)
        scores[rows(j), :] = tile
        return jnp.maximum(top, folded(tile, jnp.maximum))

    top = jnp.full((8, BLOCK), NEGATIVE, F32)
    top = lax.fori_loop(0, clear, lambda j, t: score(j, t, False), top)
    top = lax.fori_loop(clear, stop, lambda j, t: score(j, t, True), top)
    top = jnp.max(top, axis=0, keepdims=True)

    def power(j, total):
        tile = jnp.exp(scores[rows(j), :] - top)
        scores[rows(j), :] = tile
        return total + folded(tile, jnp.add)

    total = lax.fori_loop(0, stop, power, jnp.zeros((8, BLOCK), F32))
    total = jnp.sum(total, axis=0, keepdims=True)
    inverse = 1.0 / total

    def weigh(j, out):
        low = (scores[rows(j), :] * inverse).astype(BF16)
        return out + mm(value_t[:, rows(j)], low)

    out = lax.fori_loop(0, stop, weigh, jnp.zeros((HD, BLOCK), F32))
    full_out[...] = out
    low_out[...] = out.T.astype(BF16)
    log_out[...] = top + jnp.log(total)


def attend_back_body(
    lengths, query, key, value, grad, full_out, log_in, query_g, key_g, value_g, key_t, key_sum, value_sum
):
    at = pl.program_id(0)
    length = lengths[0]

    @pl.when(at == 0)
    def _():
        key_t[...] = key[...].astype(F32).T.astype(BF16)
        key_sum[...] = jnp.zeros(key_sum.shape, F32)
        value_sum[...] = jnp.zeros(value_sum.shape, F32)

    query_rows, grad_rows = query[...], grad[...]
    query_t = query_rows.astype(F32).T.astype(BF16)
    grad_full_t = grad_rows.astype(F32).T
    grad_t = grad_full_t.astype(BF16)
    delta = jnp.sum(grad_full_t * full_out[...], axis=0, keepdims=True)
    log_total = log_in[...]
    clear = jnp.minimum(at, length // BLOCK)
    stop = jnp.minimum(at, (length - 1) // BLOCK) + 1
    clear, stop = (jnp.where(at * BLOCK < length, n, 0) for n in (clear, stop))

    def step(j, query_sum, masked):
        rows = pl.ds(pl.multiple_of(j * BLOCK, BLOCK), BLOCK)
        if masked:
            tile = masked_scores(key[rows, :], query_t, j, at * BLOCK, length)
        else:
            tile = mm(key[rows, :], query_t)
        probs = jnp.exp(tile - log_total)
        value_sum[rows, :] += mm(probs.astype(BF16), grad_rows)
        score_g = (probs * (mm(value[rows, :], grad_t) - delta)).astype(BF16)
        key_sum[rows, :] += mm(score_g, query_rows)
        return query_sum + mm(key_t[:, rows], score_g)

    query_sum = jnp.zeros((HD, BLOCK), F32)
    query_sum = lax.fori_loop(0, clear, lambda j, s: step(j, s, False), query_sum)
    query_sum = lax.fori_loop(clear, stop, lambda j, s: step(j, s, True), query_sum)
    query_g[...] = (query_sum * HD ** (-0.5)).T.astype(BF16)

    @pl.when(at == pl.num_programs(0) - 1)
    def _():
        key_g[...] = key_sum[...].astype(BF16)
        value_g[...] = value_sum[...].astype(BF16)


def feed_body(
    lengths, two, attended, cotangent, expand_w, expand_b, shrink_w, dense_w,
    partial_out, attended_g, hidden_g, shrink_g, dense_g, expand_g, expand_bg, bias_g,
):
    at = pl.program_id(0)

    @pl.when(at == 0)
    def _():
        for total in (shrink_g, dense_g, expand_g, expand_bg, bias_g):
            total[...] = jnp.zeros(total.shape, F32)

    normed, mixed = two[...], attended[...]
    hidden = mm(normed, expand_w[...]) + expand_b[...]
    error = lax.erf(hidden * math.sqrt(0.5))
    cumulative = 0.5 * (1.0 + error)
    active = (hidden * cumulative).astype(BF16)
    put_rows(partial_out, mm(mixed, dense_w[...]) + mm(active, shrink_w[...]))
    token = at * BLOCK + lax.broadcasted_iota(jnp.int32, (BLOCK, D), 0)
    seed = jnp.where(token < lengths[0], token_rows(cotangent).astype(F32), 0.0)
    bias_g[...] += jnp.sum(seed, axis=0, keepdims=True)
    seed = seed.astype(BF16)
    attended_g[...] = mm(seed, dense_w[...], ((1,), (1,))).astype(BF16)
    slope = cumulative + hidden * jnp.exp(-0.5 * hidden * hidden) * (1.0 / math.sqrt(2.0 * math.pi))
    back = (mm(seed, shrink_w[...], ((1,), (1,))) * slope).astype(BF16)
    hidden_g[...] = back
    expand_bg[...] += jnp.sum(back.astype(F32), axis=0, keepdims=True)
    shrink_g[...] += mm(active, seed, ((0,), (0,)))
    dense_g[...] += mm(mixed, seed, ((0,), (0,)))
    expand_g[...] += mm(normed, back, ((0,), (0,)))


def mixed_back_body(
    partials, tokens, one, query_g, key_g, value_g, hidden_g, vectors, qkv_w, expand_w, cos, sin,
    partial_out, qkv_g, qkv_bg, vector_g,
):
    at = pl.program_id(0)

    @pl.when(at == 0)
    def _():
        for total in (qkv_g, qkv_bg, vector_g):
            total[...] = jnp.zeros(total.shape, F32)

    pair = jnp.concatenate([query_g[...].astype(F32), key_g[...].astype(F32)], axis=1)
    pair = turned(pair, cos[...], -sin[...])
    values = value_g[...].astype(F32)
    mixed_g = jnp.concatenate([pair, values, jnp.zeros_like(values)], axis=1)
    mixed_low = mixed_g.astype(BF16)
    qkv_bg[...] += jnp.sum(mixed_low.astype(F32), axis=0, keepdims=True)
    qkv_g[...] += mm(one[...], mixed_low, ((0,), (0,)))
    one_g = mm(mixed_low, qkv_w[...], ((1,), (1,)))
    two_g = mm(hidden_g[...], expand_w[...], ((1,), (1,)))
    unit = normalized(token_rows(tokens).astype(F32))
    vector_g[0:1] += jnp.sum(one_g * unit, axis=0, keepdims=True)
    vector_g[1:2] += jnp.sum(one_g, axis=0, keepdims=True)
    vector_g[2:3] += jnp.sum(two_g * unit, axis=0, keepdims=True)
    vector_g[3:4] += jnp.sum(two_g, axis=0, keepdims=True)
    put_rows(partial_out, one_g * vectors[0:1] + two_g * vectors[2:3])


def split_mesh(mesh):
    groups, members = mesh.shape["blk"], mesh.shape["uly"]
    return Mesh(mesh.devices.reshape(groups // 2, 2, members // 2, 2), ALL)


def across_x(block):
    return lax.ppermute(block, "x", [(0, 1), (1, 0)])


def by_head(residual, cotangent, lengths, positions, masters, momenta, averages):
    slots, span, width = residual.shape
    x = lax.axis_index("x")
    head = lax.axis_index("core") * 8 + lax.axis_index("z") * 2 + lax.axis_index("y")
    owner = x * 16 + head
    groups = lax.axis_size("z") * lax.axis_size("y")
    count = groups * 4 * span
    chunk = masters.shape[0]
    length = lax.dynamic_slice_in_dim(lengths, x, 1)

    def paired(mine, theirs):
        return jnp.where(x == 0, jnp.stack([mine, theirs]), jnp.stack([theirs, mine]))

    def at_x(rows, index):
        return lax.dynamic_index_in_dim(rows, index, 0, keepdims=False)

    rows = jnp.stack([residual, cotangent], axis=1)
    rows = paired(at_x(rows, x), across_x(at_x(rows, 1 - x)))
    gathered = lax.all_gather(rows, RING, axis=0).reshape(2, groups, 2, 2, span, width)

    place = jnp.broadcast_to(positions.reshape(1, slots * span), (OWNERS, slots * span))
    place = lax.all_to_all(place, ALL, 0, 0, tiled=True).reshape(2, 2, groups, slots, span)
    place = lax.dynamic_index_in_dim(place, x, 3, keepdims=False).transpose(2, 0, 1, 3).reshape(count)
    half_dims = ROT // 2
    inverse = ROTARY_BASE ** (-(jnp.arange(half_dims, dtype=F32) * 2.0 / ROT))
    angles = place.astype(F32)[:, None] * inverse
    cos, sin = jnp.cos(angles), jnp.sin(angles)
    flat_part = jnp.ones((count, HD - ROT), F32)
    cos = jnp.concatenate([cos, cos, flat_part] * 2, axis=1)
    sin = jnp.concatenate([sin, sin, 0.0 * flat_part] * 2, axis=1)

    onward = [(i, i + 1) for i in range(OWNERS - 1)]
    backward = [(i + 1, i) for i in range(OWNERS - 1)]
    before = lax.ppermute(masters[chunk - D :], ALL, onward)
    after = lax.ppermute(masters[: 4 * D], ALL, backward)
    own_rows = -(-chunk // D) * 8
    own = jnp.pad(masters, (0, own_rows * LANES - chunk)).reshape(own_rows, LANES)
    before, after = before.reshape(8, LANES), after.reshape(32, LANES)
    skipped = jnp.where(owner < 8, 4, jnp.where(owner < 11, 7, jnp.where(owner < 22, 8, 12)))
    kind = jnp.where(
        owner < 8,
        PROJECT,
        jnp.where(
            owner == 10,
            PLAIN_EXPAND,
            jnp.where(owner == 21, EXPAND_PLAIN, jnp.where((owner > 10) & (owner < 21), EXPAND, PLAIN)),
        ),
    )
    vector_row = jnp.where(owner == 10, 2080, jnp.where(owner == 21, 1056, jnp.where(owner == 31, 3104, 0)))
    ahead = skipped * D - (chunk - PER * D) * owner
    begin = ahead + 4 * D
    scalars = jnp.stack([begin // LANES, begin % LANES, kind, vector_row]).astype(jnp.int32)
    sent = call(
        weights_out_body, (1,),
        [whole(before.shape), whole(own.shape), whole(after.shape)],
        whole((16, SEND_ROWS, LANES)),
        shaped((16, SEND_ROWS, LANES), BF16),
        [pltpu.VMEM((3280, LANES), F32), pltpu.VMEM((SHIFT_ROWS, LANES), F32), pltpu.VMEM((48, LANES), F32)],
        1, "weights_out",
    )(scalars, before, own, after)
    got = lax.all_to_all(jnp.concatenate([sent, sent]), ALL, 0, 0, tiled=True)
    head_scalar = head.astype(jnp.int32).reshape(1)
    qkv_w, expand_w, second, vectors, qkv_b, expand_b = call(
        weights_in_body, (1,),
        [whole(got.shape)],
        [whole((D, 256)), whole((D, 256)), whole((16, 160, LANES)), whole((8, D)), whole((1, 256)), whole((1, 256))],
        [shaped((D, 256), BF16), shaped((D, 256), BF16), shaped((16, 160, LANES), BF16), shaped((8, D), F32),
         shaped((1, 256), F32), shaped((1, 256), F32)],
        [pltpu.VMEM((24, LANES), F32), pltpu.VMEM((32, LANES), F32)], 1, "weights_in",
    )(head_scalar, got)
    second = lax.all_to_all(second, RING, 0, 0, tiled=True)
    dense_w, shrink_w = call(
        rows_in_body, (1,), [whole(second.shape)], [whole((HD, D)), whole((256, D))],
        [shaped((HD, D), BF16), shaped((256, D), BF16)], name="rows_in",
    )(second)

    steps = (count // BLOCK,)
    first_spec, second_spec = (
        pl.BlockSpec((2, 1, 2, None, span, width), lambda i, *_, which=which: (0, i, 0, which, 0, 0))
        for which in range(2)
    )
    token_shape = shaped(gathered.shape, BF16)

    def rows_spec(columns):
        return pl.BlockSpec((BLOCK, columns), lambda i, *_: (i, 0))

    def columns_spec(rows):
        return pl.BlockSpec((rows, BLOCK), lambda i, *_: (0, i))

    narrow = shaped((count, HD), BF16)
    one, two, query, key, value = call(
        mixed_body, steps,
        [first_spec, whole((8, D)), whole((D, 256)), whole((1, 256)), rows_spec(LANES), rows_spec(LANES)],
        [rows_spec(D), rows_spec(D), rows_spec(HD), rows_spec(HD), rows_spec(HD)],
        [shaped((count, D), BF16), shaped((count, D), BF16), narrow, narrow, narrow], name="mixed",
    )(gathered, vectors, qkv_w, qkv_b, cos, sin)
    attended, attended_full, log_total = call(
        attend_body, steps,
        [rows_spec(HD), whole((count, HD)), whole((count, HD))],
        [rows_spec(HD), columns_spec(HD), columns_spec(1)],
        [narrow, shaped((HD, count), F32), shaped((1, count), F32)],
        [pltpu.VMEM((count, BLOCK), F32), pltpu.VMEM((HD, count), BF16)], 1, "attend",
    )(length, query, key, value)
    partials, attended_g, hidden_g, shrink_g, dense_g, expand_g, expand_bg, bias_g = call(
        feed_body, steps,
        [rows_spec(D), rows_spec(HD), second_spec, whole((D, 256)), whole((1, 256)), whole((256, D)), whole((HD, D))],
        [first_spec, rows_spec(HD), rows_spec(256), whole((256, D)), whole((HD, D)), whole((D, 256)),
         whole((1, 256)), whole((1, D))],
        [token_shape, narrow, shaped((count, 256), BF16), shaped((256, D), F32), shaped((HD, D), F32),
         shaped((D, 256), F32), shaped((1, 256), F32), shaped((1, D), F32)], (), 1, "feed",
    )(length, two, attended, gathered, expand_w, expand_b, shrink_w, dense_w)
    query_g, key_g, value_g = call(
        attend_back_body, steps,
        [rows_spec(HD), whole((count, HD)), whole((count, HD)), rows_spec(HD), columns_spec(HD), columns_spec(1)],
        [rows_spec(HD), whole((count, HD)), whole((count, HD))],
        [narrow, narrow, narrow],
        [pltpu.VMEM((HD, count), BF16), pltpu.VMEM((count, HD), F32), pltpu.VMEM((count, HD), F32)],
        1, "attend_back",
    )(length, query, key, value, attended_g, attended_full, log_total)
    partials, qkv_g, qkv_bg, vector_g = call(
        mixed_back_body, steps,
        [pl.BlockSpec(memory_space=pl.ANY), first_spec, rows_spec(D), rows_spec(HD), rows_spec(HD), rows_spec(HD),
         rows_spec(256), whole((8, D)), whole((D, 256)), whole((D, 256)), rows_spec(LANES), rows_spec(LANES)],
        [second_spec, whole((D, 256)), whole((1, 256)), whole((8, D))],
        [token_shape, shaped((D, 256), F32), shaped((1, 256), F32), shaped((8, D), F32)], name="mixed_back", aliases={0: 0},
    )(partials, gathered, one, query_g, key_g, value_g, hidden_g, vectors, qkv_w, expand_w, cos, sin)
    rows = lax.psum_scatter(partials.reshape(16, 2, 2, span, width), RING, scatter_dimension=0, tiled=True)[0]
    rows = paired(at_x(rows, x), across_x(at_x(rows, 1 - x))).astype(F32)
    out_rows, in_rows = rows[:, 0], rows[:, 1]

    second_g = call(
        rows_out_body, (1,), [whole((HD, D)), whole((256, D))], whole((16, 160, LANES)),
        shaped((16, 160, LANES), BF16), name="rows_out",
    )(dense_g, shrink_g)
    second_g = lax.all_to_all(second_g, RING, 0, 0, tiled=True)
    bias_g = jnp.where(head == 0, bias_g, 0.0)
    vector_g = jnp.concatenate([vector_g[:4], bias_g, jnp.zeros((3, D), F32)])
    sent_g = call(
        grads_out_body, (1,),
        [whole((16, 160, LANES)), whole((D, 256)), whole((D, 256)), whole((8, D)), whole((1, 256)), whole((1, 256))],
        whole((OWNERS, BACK_ROWS, LANES)),
        shaped((OWNERS, BACK_ROWS, LANES), BF16),
        [pltpu.VMEM((32, LANES), F32), pltpu.VMEM((32, LANES), F32)], 1, "grads_out",
    )(head_scalar, second_g, qkv_g, expand_g, vector_g, qkv_bg, expand_bg)
    got_g = lax.all_to_all(sent_g, ALL, 0, 0, tiled=True)
    begin_g = (chunk - PER * D) * owner - skipped * D + 4 * D
    scalars_g = jnp.stack([begin_g // LANES, begin_g % LANES, kind, vector_row]).astype(jnp.int32)
    taken = call(
        grads_in_body, (1,), [whole(got_g.shape)], whole((TAKE_ROWS, LANES)), shaped((TAKE_ROWS, LANES), F32),
        [pltpu.VMEM((SHIFT_ROWS, LANES), F32)], 1, "grads_in",
    )(scalars_g, got_g).reshape(-1)
    from_before = lax.ppermute(taken[D + chunk : 5 * D + chunk], ALL, onward)
    from_after = lax.ppermute(taken[:D], ALL, backward)
    gradients = taken[D : D + chunk]
    gradients = gradients.at[: 4 * D].add(from_before).at[chunk - D :].add(from_after)

    values = residual.astype(F32)
    outputs = (values + out_rows + (vectors[4] + vectors[5])).astype(BF16)
    first_token = ((lax.axis_index("z") * 2 + lax.axis_index("y")) * 4 + x * 2 + lax.axis_index("core")) * span
    token = first_token + jnp.arange(span, dtype=jnp.int32)
    live = token[None, :] < lengths[:, None]
    seed = jnp.where(live[:, :, None], cotangent.astype(F32), 0.0)
    centered = values - jnp.mean(values, axis=-1, keepdims=True)
    scale = lax.rsqrt(jnp.mean(centered * centered, axis=-1, keepdims=True) + EPSILON)
    unit = centered * scale
    back = in_rows - jnp.mean(in_rows, axis=-1, keepdims=True)
    back = scale * (back - unit * jnp.mean(in_rows * unit, axis=-1, keepdims=True))
    input_grad = (seed + back).astype(BF16)

    velocity = MOMENTUM * momenta + gradients
    step_rate = LEARN_RATE / math.sqrt(slots * count)
    updated = masters - step_rate * (gradients + MOMENTUM * velocity)
    averaged = AVERAGE_DECAY * averages + (1.0 - AVERAGE_DECAY) * updated
    return (outputs, input_grad, gradients, updated, velocity, averaged)


def solution(mesh):
    def step(*args):
        slots, tokens = args[0].shape[:2]
        if mesh.size == OWNERS == slots * H and mesh.shape["blk"] == 4 and tokens == 64 * OWNERS:
            tokens_in, flat, used, body = P(None, ("z", "y", "x", "core"), None), P(ALL), split_mesh(mesh), by_head
            places = P(None, ("z", "y", "x", "core"))
        else:
            tokens_in, flat, used, body = P(None, ("uly", "blk"), None), P(("blk", "uly")), mesh, local
            places = P(None, ("uly", "blk"))
        return jax.shard_map(
            body,
            mesh=used,
            in_specs=(tokens_in, tokens_in, P(), places, flat, flat, flat),
            out_specs=(tokens_in, tokens_in, flat, flat, flat, flat),
            check_vma=False,
        )(*args)

    return step
```

```python
from functools import partial
import math

import jax
import jax.numpy as jnp
from jax import lax
from jax.experimental import pallas as pl
from jax.experimental.pallas import tpu as pltpu
from jax.sharding import Mesh, PartitionSpec as P

D = 1024
H = 16
HD = 64
ROT = 16
FF = 4096


EPSILON = 1e-05
NEGATIVE = -1e30
MOMENTUM = 0.5
LEARN_RATE = 0.05
AVERAGE_DECAY = 0.5
ROTARY_BASE = 10000.0


def passed_along(block, axis, distance):
    devices = range(lax.axis_size(axis))
    route = [((i - distance) % len(devices), i) for i in devices]
    return lax.ppermute(block, axis, route)


def unpack(flat_vector):
    layouts = [
        (D,),
        (D,),
        (D,),
        (D,),
        (D, 3 * D),
        (3 * D,),
        (D, D),
        (D,),
        (D, FF),
        (FF,),
        (FF, D),
        (D,),
    ]
    pieces = []
    cursor = 0
    for layout in layouts:
        number = math.prod(layout)
        pieces.append(flat_vector[cursor : cursor + number].reshape(layout))
        cursor += number
    return pieces


def layer_norm(values, gain, shift):
    centered = values - jnp.mean(values, axis=-1, keepdims=True)
    variance = jnp.mean(centered * centered, axis=-1, keepdims=True)
    return centered * lax.rsqrt(variance + EPSILON) * gain + shift


def rotary_tables(positions):
    half_dims = ROT // 2
    inverse = ROTARY_BASE ** (-(jnp.arange(half_dims, dtype=jnp.float32) * 2.0 / ROT))
    angles = positions.astype(jnp.float32)[..., None] * inverse
    return (jnp.cos(angles), jnp.sin(angles))


def rotate(values, cos_table, sin_table):
    half_dims = ROT // 2
    first_half = values[..., :half_dims]
    second_half = values[..., half_dims:ROT]
    return jnp.concatenate(
        [
            first_half * cos_table - second_half * sin_table,
            second_half * cos_table + first_half * sin_table,
            values[..., ROT:],
        ],
        axis=-1,
    )


def group_tokens(source, group_count, uly_count, span_rows):
    spans = jnp.arange(uly_count, dtype=jnp.int32)[:, None] * group_count + source
    return (spans * span_rows + jnp.arange(span_rows, dtype=jnp.int32)[None, :]).reshape(-1)


def block_scores(queries, keys_rows, row_tokens, col_tokens, length):
    scores = jnp.einsum(
        "qhd,khd->hqk", queries, keys_rows, preferred_element_type=jnp.float32
    ) * HD ** (-0.5)
    allowed = (col_tokens[None, :] <= row_tokens[:, None]) & (col_tokens[None, :] < length)
    return jnp.where(allowed[None], scores, NEGATIVE)


def is_live(row_tokens, col_tokens, length):
    return (col_tokens[0] <= row_tokens[-1]) & (col_tokens[0] < length)


def fold_stats(row_max, row_total, queries, key_value, lengths, row_tokens, col_tokens):

    def per_slot(inputs):
        slot_max, slot_total, slot_queries, slot_pairs, length = inputs

        def compute(current):
            prev_max, prev_total = current
            scores = block_scores(slot_queries, slot_pairs[:, :, 0], row_tokens, col_tokens, length)
            next_max = jnp.maximum(prev_max, jnp.max(scores, axis=-1))
            next_total = prev_total * jnp.exp(prev_max - next_max) + jnp.sum(
                jnp.exp(scores - next_max[..., None]), axis=-1
            )
            return (next_max, next_total)

        return lax.cond(
            is_live(row_tokens, col_tokens, length),
            compute,
            lambda current: current,
            (slot_max, slot_total),
        )

    return lax.map(per_slot, (row_max, row_total, queries, key_value, lengths))


def fold_values(attended, queries, key_value, log_total, lengths, row_tokens, col_tokens):

    def per_slot(inputs):
        slot_out, slot_queries, slot_pairs, slot_log, length = inputs

        def compute(current):
            scores = block_scores(slot_queries, slot_pairs[:, :, 0], row_tokens, col_tokens, length)
            prob_low = jnp.exp(scores - slot_log[..., None]).astype(jnp.bfloat16)
            return current + jnp.einsum(
                "hqk,khd->qhd", prob_low, slot_pairs[:, :, 1], preferred_element_type=jnp.float32
            )

        return lax.cond(
            is_live(row_tokens, col_tokens, length), compute, lambda current: current, slot_out
        )

    return lax.map(per_slot, (attended, queries, key_value, log_total, lengths))


def fold_grads(
    query_grad,
    pair_grad,
    queries,
    key_value,
    grad_out,
    log_total,
    row_delta,
    lengths,
    row_tokens,
    col_tokens,
):

    def per_slot(inputs):
        (
            slot_qgrad,
            slot_pgrad,
            slot_queries,
            slot_pairs,
            slot_gout,
            slot_log,
            slot_delta,
            length,
        ) = inputs

        def compute(current):
            cur_qgrad, cur_pgrad = current
            scores = block_scores(slot_queries, slot_pairs[:, :, 0], row_tokens, col_tokens, length)
            attend_prob = jnp.exp(scores - slot_log[..., None])
            prob_low = attend_prob.astype(jnp.bfloat16)
            prob_grad = jnp.einsum(
                "qhd,khd->hqk", slot_gout, slot_pairs[:, :, 1], preferred_element_type=jnp.float32
            )
            score_grad = (attend_prob * (prob_grad - slot_delta[..., None])).astype(jnp.bfloat16)
            cur_qgrad = cur_qgrad + jnp.einsum(
                "hqk,khd->qhd", score_grad, slot_pairs[:, :, 0], preferred_element_type=jnp.float32
            ) * HD ** (-0.5)
            key_grad = jnp.einsum(
                "hqk,qhd->khd", score_grad, slot_queries, preferred_element_type=jnp.float32
            ) * HD ** (-0.5)
            value_grad = jnp.einsum(
                "hqk,qhd->khd", prob_low, slot_gout, preferred_element_type=jnp.float32
            )
            return (cur_qgrad, cur_pgrad + jnp.stack([key_grad, value_grad], axis=2))

        return lax.cond(
            is_live(row_tokens, col_tokens, length),
            compute,
            lambda current: current,
            (slot_qgrad, slot_pgrad),
        )

    return lax.map(
        per_slot,
        (query_grad, pair_grad, queries, key_value, grad_out, log_total, row_delta, lengths),
    )


def local(residual, cotangent, lengths, positions, masters, momenta, averages):
    slot_count, span_rows, model_width = residual.shape
    group_count = lax.axis_size("blk")
    uly_count = lax.axis_size("uly")
    group_index = lax.axis_index("blk")
    uly_index = lax.axis_index("uly")
    block_rows = uly_count * span_rows
    full_rows = group_count * block_rows
    local_heads = H // uly_count
    token_rows = slot_count * span_rows
    row_tokens = group_tokens(group_index, group_count, uly_count, span_rows)

    def tokens_of(source):
        return group_tokens(source, group_count, uly_count, span_rows)

    gathered = lax.all_gather(masters.astype(jnp.bfloat16), ("blk", "uly"), axis=0, tiled=True)
    (
        gain_one,
        shift_one,
        gain_two,
        shift_two,
        project_w,
        project_b,
        dense_w,
        dense_b,
        expand_w,
        expand_b,
        shrink_w,
        shrink_b,
    ) = unpack(gathered)
    values = residual.astype(jnp.float32).reshape(token_rows, model_width)
    normed_one, norm_back_one = jax.vjp(
        layer_norm, values, gain_one.astype(jnp.float32), shift_one.astype(jnp.float32)
    )
    normed_two, norm_back_two = jax.vjp(
        layer_norm, values, gain_two.astype(jnp.float32), shift_two.astype(jnp.float32)
    )
    normed_one = normed_one.astype(jnp.bfloat16)
    normed_two = normed_two.astype(jnp.bfloat16)
    mixed_rows = jnp.dot(
        normed_one, project_w, preferred_element_type=jnp.float32
    ) + project_b.astype(jnp.float32)
    mixed_rows = mixed_rows.reshape(slot_count, span_rows, H, 3, HD)
    cos_table, sin_table = rotary_tables(positions)
    cos_table = cos_table[:, :, None, None, :]
    sin_table = sin_table[:, :, None, None, :]
    turned, turn_back = jax.vjp(
        lambda pair_rows: rotate(pair_rows, cos_table, sin_table), mixed_rows[:, :, :, 0:2]
    )
    packed = jnp.concatenate([turned, mixed_rows[:, :, :, 2:3]], axis=3).astype(jnp.bfloat16)
    packed = packed.reshape(slot_count, span_rows, 3 * model_width)
    heads_rows = lax.all_to_all(packed, "uly", split_axis=2, concat_axis=1, tiled=True).reshape(
        slot_count, block_rows, local_heads, 3, HD
    )
    queries = heads_rows[:, :, :, 0]
    key_value = heads_rows[:, :, :, 1:3]
    row_max = jnp.full((slot_count, local_heads, block_rows), NEGATIVE, jnp.float32)
    row_total = jnp.zeros((slot_count, local_heads, block_rows), jnp.float32)
    attended = jnp.zeros((slot_count, block_rows, local_heads, HD), jnp.float32)
    last_tokens = tokens_of((group_index + 1) % group_count)

    def stats_turn(turn_index, carried):
        pairs_now, cur_max, cur_total = carried
        col_tokens = tokens_of((group_index - turn_index) % group_count)
        cur_max, cur_total = fold_stats(
            cur_max, cur_total, queries, pairs_now, lengths, row_tokens, col_tokens
        )
        pairs_now = passed_along(pairs_now, "blk", 1)
        return (pairs_now, cur_max, cur_total)

    pairs_now, row_max, row_total = lax.fori_loop(
        0, group_count - 1, stats_turn, (key_value, row_max, row_total)
    )
    row_max, row_total = fold_stats(
        row_max, row_total, queries, pairs_now, lengths, row_tokens, last_tokens
    )
    log_total = row_max + jnp.log(row_total)

    def value_turn(turn_index, carried):
        pairs_now, cur_out = carried
        col_tokens = tokens_of((group_index - turn_index) % group_count)
        cur_out = fold_values(
            cur_out, queries, pairs_now, log_total, lengths, row_tokens, col_tokens
        )
        pairs_now = passed_along(pairs_now, "blk", 1)
        return (pairs_now, cur_out)

    pairs_now, attended = lax.fori_loop(0, group_count - 1, value_turn, (key_value, attended))
    attended = fold_values(
        attended, queries, pairs_now, log_total, lengths, row_tokens, last_tokens
    )
    heads_out = attended.astype(jnp.bfloat16).reshape(slot_count, block_rows, local_heads * HD)
    merged = lax.all_to_all(heads_out, "uly", split_axis=1, concat_axis=2, tiled=True).reshape(
        token_rows, model_width
    )
    branch_attn = jnp.dot(merged, dense_w, preferred_element_type=jnp.float32) + dense_b.astype(
        jnp.float32
    )
    hidden_pre = jnp.dot(
        normed_two, expand_w, preferred_element_type=jnp.float32
    ) + expand_b.astype(jnp.float32)
    activated, gelu_back = jax.vjp(partial(jax.nn.gelu, approximate=False), hidden_pre)
    activated_low = activated.astype(jnp.bfloat16)
    branch_feed = jnp.dot(
        activated_low, shrink_w, preferred_element_type=jnp.float32
    ) + shrink_b.astype(jnp.float32)
    outputs = (
        (values + branch_attn + branch_feed)
        .astype(jnp.bfloat16)
        .reshape(slot_count, span_rows, model_width)
    )
    first_token = (uly_index * group_count + group_index) * span_rows
    token_index = first_token + jnp.arange(span_rows, dtype=jnp.int32)
    live_mask = (token_index[None, :] < lengths[:, None]).astype(jnp.float32)
    seed_grad = (cotangent.astype(jnp.float32) * live_mask[:, :, None]).reshape(
        token_rows, model_width
    )
    seed_low = seed_grad.astype(jnp.bfloat16)
    dense_w_grad = jnp.einsum("ra,rb->ab", merged, seed_low, preferred_element_type=jnp.float32)
    bias_grad = jnp.sum(seed_low.astype(jnp.float32), axis=0)
    merged_grad = jnp.einsum(
        "rb,ab->ra", seed_low, dense_w, preferred_element_type=jnp.float32
    ).astype(jnp.bfloat16)
    shrink_w_grad = jnp.einsum(
        "rf,rb->fb", activated_low, seed_low, preferred_element_type=jnp.float32
    )
    activated_grad = jnp.einsum("rb,fb->rf", seed_low, shrink_w, preferred_element_type=jnp.float32)
    hidden_grad = gelu_back(activated_grad)[0].astype(jnp.bfloat16)
    expand_w_grad = jnp.einsum(
        "ra,rf->af", normed_two, hidden_grad, preferred_element_type=jnp.float32
    )
    expand_b_grad = jnp.sum(hidden_grad.astype(jnp.float32), axis=0)
    normed_two_grad = jnp.einsum(
        "rf,af->ra", hidden_grad, expand_w, preferred_element_type=jnp.float32
    )
    grad_heads = lax.all_to_all(
        merged_grad.reshape(slot_count, span_rows, model_width),
        "uly",
        split_axis=2,
        concat_axis=1,
        tiled=True,
    )
    grad_out = grad_heads.reshape(slot_count, block_rows, local_heads, HD)
    row_delta = jnp.sum(grad_out.astype(jnp.float32) * attended, axis=-1).transpose(0, 2, 1)
    query_grad = jnp.zeros((slot_count, block_rows, local_heads, HD), jnp.float32)
    pair_grad = jnp.zeros((slot_count, block_rows, local_heads, 2, HD), jnp.float32)

    def grad_turn(turn_index, carried):
        pairs_now, cur_pgrad, cur_qgrad = carried
        col_tokens = tokens_of((group_index - turn_index) % group_count)
        cur_qgrad, cur_pgrad = fold_grads(
            cur_qgrad,
            cur_pgrad,
            queries,
            pairs_now,
            grad_out,
            log_total,
            row_delta,
            lengths,
            row_tokens,
            col_tokens,
        )
        pairs_now = passed_along(pairs_now, "blk", 1)
        cur_pgrad = passed_along(cur_pgrad.astype(jnp.bfloat16), "blk", 1).astype(cur_pgrad.dtype)
        return (pairs_now, cur_pgrad, cur_qgrad)

    pairs_now, pair_grad, query_grad = lax.fori_loop(
        0, group_count - 1, grad_turn, (key_value, pair_grad, query_grad)
    )
    query_grad, pair_grad = fold_grads(
        query_grad,
        pair_grad,
        queries,
        pairs_now,
        grad_out,
        log_total,
        row_delta,
        lengths,
        row_tokens,
        last_tokens,
    )
    pair_grad = passed_along(pair_grad.astype(jnp.bfloat16), "blk", 1).astype(pair_grad.dtype)
    back_packed = jnp.concatenate(
        [query_grad.astype(jnp.bfloat16)[:, :, :, None], pair_grad.astype(jnp.bfloat16)], axis=3
    )
    back_packed = back_packed.reshape(slot_count, block_rows, local_heads * 3 * HD)
    token_grads = lax.all_to_all(
        back_packed, "uly", split_axis=1, concat_axis=2, tiled=True
    ).reshape(slot_count, span_rows, H, 3, HD)
    turned_grad = turn_back(token_grads[:, :, :, 0:2].astype(jnp.float32))[0]
    mixed_grad = jnp.concatenate(
        [turned_grad, token_grads[:, :, :, 2:3].astype(jnp.float32)], axis=3
    ).astype(jnp.bfloat16)
    mixed_grad = mixed_grad.reshape(token_rows, 3 * model_width)
    project_w_grad = jnp.einsum(
        "ra,rc->ac", normed_one, mixed_grad, preferred_element_type=jnp.float32
    )
    project_b_grad = jnp.sum(mixed_grad.astype(jnp.float32), axis=0)
    normed_one_grad = jnp.einsum(
        "rc,ac->ra", mixed_grad, project_w, preferred_element_type=jnp.float32
    )
    values_one, gain_one_grad, shift_one_grad = norm_back_one(normed_one_grad)
    values_two, gain_two_grad, shift_two_grad = norm_back_two(normed_two_grad)
    input_grad = (
        (seed_grad + values_one + values_two)
        .astype(jnp.bfloat16)
        .reshape(slot_count, span_rows, model_width)
    )
    local_grads = jnp.concatenate(
        [
            gain_one_grad,
            shift_one_grad,
            gain_two_grad,
            shift_two_grad,
            project_w_grad.reshape(-1),
            project_b_grad,
            dense_w_grad.reshape(-1),
            bias_grad,
            expand_w_grad.reshape(-1),
            expand_b_grad,
            shrink_w_grad.reshape(-1),
            bias_grad,
        ]
    )
    gradients = lax.psum_scatter(local_grads, ("blk", "uly"), scatter_dimension=0, tiled=True)
    velocity = MOMENTUM * momenta + gradients
    step_rate = LEARN_RATE / math.sqrt(slot_count * full_rows)
    updated = masters - step_rate * (gradients + MOMENTUM * velocity)
    averaged = AVERAGE_DECAY * averages + (1.0 - AVERAGE_DECAY) * updated
    return (outputs, input_grad, gradients, updated, velocity, averaged)


LANES = 128
BLOCK = 256
RING = ("core", "z", "y")
ALL = ("x", "core", "z", "y")
F32 = jnp.float32
BF16 = jnp.bfloat16


def call(body, grid, in_specs, out_specs, out_shape, scratch=(), prefetch=0, name=None):
    return pl.pallas_call(
        body,
        grid_spec=pltpu.PrefetchScalarGridSpec(
            num_scalar_prefetch=prefetch,
            grid=grid,
            in_specs=in_specs,
            out_specs=out_specs,
            scratch_shapes=scratch,
        ),
        out_shape=out_shape,
        name=name,
        compiler_params=pltpu.CompilerParams(vmem_limit_bytes=56 << 20),
    )


def whole(shape):
    return pl.BlockSpec(shape, lambda *_: (0,) * len(shape))


def shaped(shape, kind):
    return jax.ShapeDtypeStruct(shape, kind)


def mm(a, b, dims=((1,), (0,))):
    return lax.dot_general(a, b, (dims, ((), ())), preferred_element_type=F32)


def low_lanes(shape):
    return lax.broadcasted_iota(jnp.int32, shape, len(shape) - 1) < LANES // 2


def swap(a):
    return pltpu.roll(a, LANES // 2, 1)


def join(a, a_half, b, b_half):
    first = swap(a) if a_half else a
    second = b if b_half else swap(b)
    return jnp.where(low_lanes(a.shape), first, second)


OWNERS = 32
PER = (3 * D + D + FF + FF) // OWNERS
FLAT = PER * D // LANES
PIECE = FLAT // 16
LEAD = 4 * D // LANES
EDGE = PER * D + 13 * D // OWNERS
PROJECT, PLAIN, PLAIN_EXPAND, EXPAND, EXPAND_PLAIN = range(5)


def kind_of(c):
    return (
        PROJECT
        if c < 8
        else PLAIN
        if c < 10 or c > 21
        else PLAIN_EXPAND
        if c == 10
        else EXPAND_PLAIN
        if c == 21
        else EXPAND
    )


def plain_place(row, base, count):
    local = row - base
    half = int(local >= count // 2)
    return local - half * (count // 2), half


def dense_place(row):
    if row < 768:
        c = 8 + row // 384
        return (c, 0) + plain_place(row, 384 * (c - 8), 384)
    return (10, 0) + plain_place(row, 768, 256)


def shrink_place(row):
    if row < 256:
        return (21, 64) + plain_place(row, 0, 256)
    c = 22 + (row - 256) // 384
    return (c, 0) + plain_place(row, 256 + 384 * (c - 22), 384)


def expand_places():
    places = [(10, 128, 0, 32)]
    places += [(c, 0, 32 + 96 * (c - 11), 96) for c in range(11, 21)]
    places += [(21, 0, 992, 32)]
    return places


def shifted_rows(source, start, shift, at, rows):
    turn = (LANES - shift) % LANES
    first = pltpu.roll(source[pl.ds(start + at, rows), :], turn, 1)
    second = pltpu.roll(source[pl.ds(start + at + 1, rows), :], turn, 1)
    lane = lax.broadcasted_iota(jnp.int32, (rows, LANES), 1)
    return jnp.where(lane < LANES - shift, first, second)


SHIFT_ROWS = 3200
SEND_ROWS = PIECE + 32
OWN_ROW = 64


def weights_out_body(scalars, before, own, after, out, source, flat, tail):
    start, shift, kind, vector_row = scalars[0], scalars[1], scalars[2], scalars[3]
    count = own.shape[0]
    source[0 : OWN_ROW - 8] = jnp.zeros((OWN_ROW - 8, LANES), F32)
    source[OWN_ROW - 8 : OWN_ROW] = before[...]

    def copy(step, carry):
        at = pl.multiple_of(step * 88, 8)
        source[pl.ds(at + OWN_ROW, 88), :] = own[pl.ds(at, 88), :]
        return carry

    lax.fori_loop(0, count // 88, copy, 0)
    last = OWN_ROW + EDGE // LANES
    source[OWN_ROW + count :] = jnp.zeros((source.shape[0] - OWN_ROW - count, LANES), F32)
    edge = EDGE % LANES
    tail[...] = jnp.zeros(tail.shape, F32)
    tail[7:8] = source[last : last + 1]
    tail[8:40] = pltpu.roll(after[...], edge, 1)
    lane = lax.broadcasted_iota(jnp.int32, (40, LANES), 1)
    source[last : last + 40] = jnp.where(lane < edge, tail[7:47], tail[8:48])

    def align(step, carry):
        at = pl.multiple_of(step * 80, 8)
        flat[pl.ds(at, 80), :] = shifted_rows(source, start, shift, at, 80)
        return carry

    lax.fori_loop(0, SHIFT_ROWS // 80, align, 0)

    def rows(first, count, stride):
        return flat[pl.ds(first, count, stride), :]

    def plain(base, count, to):
        for m in range(8):
            tile = rows(base + m, count, 8)
            a, b = tile[: count // 2], tile[count // 2 :]
            out[2 * m, to : to + count // 2] = join(a, 0, b, 0).astype(BF16)
            out[2 * m + 1, to : to + count // 2] = join(a, 1, b, 1).astype(BF16)

    def expand(base, count, to):
        for r in range(16):
            out[r, to : to + count] = rows(base + 2 * r, count, 32).astype(BF16)
            out[r, to + count : to + 2 * count] = rows(base + 2 * r + 1, count, 32).astype(BF16)

    def project(base):
        for m in range(8):
            first, middle, last = (rows(base + 3 * m + j, 128, 24) for j in range(3))
            out[2 * m, 0:128] = first.astype(BF16)
            out[2 * m, 128:192] = join(middle[:64], 0, middle[64:], 0).astype(BF16)
            out[2 * m + 1, 0:128] = join(middle, 1, last, 0).astype(BF16)
            out[2 * m + 1, 128:192] = join(last[:64], 1, last[64:], 1).astype(BF16)

    @pl.when(kind == PROJECT)
    def _():
        project(LEAD)

    @pl.when(kind == PLAIN)
    def _():
        plain(LEAD, 384, 0)

    @pl.when(kind == PLAIN_EXPAND)
    def _():
        plain(LEAD, 256, 0)
        expand(LEAD + 2048 + 8, 32, 128)

    @pl.when(kind == EXPAND)
    def _():
        expand(LEAD, 96, 0)

    @pl.when(kind == EXPAND_PLAIN)
    def _():
        expand(LEAD, 32, 0)
        plain(LEAD + 1024 + 32, 256, 64)

    vectors = flat[pl.ds(vector_row, 32), :].astype(BF16)
    for r in range(16):
        out[r, PIECE : PIECE + 32] = vectors


def weights_in_body(scalars, got, qkv_w, expand_w, second, vectors, qkv_b, expand_b, project_rows, expand_rows):
    head = scalars[0]
    low = low_lanes((64, LANES))
    for c in range(8):
        qkv_w[128 * c : 128 * c + 128, 0:128] = got[c, 0:128]
        packed = got[c, 128:192].astype(F32)
        qkv_w[128 * c : 128 * c + 64, 128:256] = jnp.where(low, packed, 0.0).astype(BF16)
        qkv_w[128 * c + 64 : 128 * c + 128, 128:256] = jnp.where(low, swap(packed), 0.0).astype(BF16)
    for c, at, row, count in expand_places():
        expand_w[row : row + count, 0:128] = got[c, at : at + count]
        expand_w[row : row + count, 128:256] = got[c, at + count : at + 2 * count]

    for h in range(16):
        c, at, row, half = dense_place(64 * h)
        tile = got[c, at + row : at + row + 64].astype(F32)
        second[h, 0:32] = join(tile[:32], half, tile[32:], half).astype(BF16)
        for part in range(2):
            c, at, row, half = shrink_place(256 * h + 64 * part)
            tile = got[c, at + row : at + row + 64].astype(F32)
            c, at, row, other = shrink_place(256 * h + 128 + 64 * part)
            after = got[c, at + row : at + row + 64].astype(F32)
            second[h, 32 + 64 * part : 96 + 64 * part] = join(tile, half, after, other).astype(BF16)

    def vector(c, at, to):
        tile = got[c, PIECE + at : PIECE + at + 8].astype(F32)
        for j in range(8):
            vectors[to : to + 1, 128 * j : 128 * j + 128] = tile[j : j + 1]

    vectors[...] = jnp.zeros(vectors.shape, F32)
    for v in range(4):
        vector(0, 8 * v, v)
    vector(10, 0, 4)
    vector(31, 0, 5)
    project_rows[...] = got[8, PIECE + 8 : PIECE + 32].astype(F32)
    expand_rows[...] = got[21, PIECE : PIECE + 32].astype(F32)
    row = head // 2 * 3
    first, middle, last = (project_rows[pl.ds(row + j, 1), :] for j in range(3))
    odd = head % 2 == 1
    qkv_b[0:1, 0:128] = jnp.where(odd, join(middle, 1, last, 0), first)
    value = jnp.where(odd, swap(last), middle)
    qkv_b[0:1, 128:256] = jnp.where(low_lanes((1, LANES)), value, 0.0)
    expand_b[0:1, 0:128] = expand_rows[pl.ds(2 * head, 1), :]
    expand_b[0:1, 128:256] = expand_rows[pl.ds(2 * head + 1, 1), :]


def rows_in_body(got, dense_w, shrink_w):
    for m in range(8):
        even, odd = got[2 * m].astype(F32), got[2 * m + 1].astype(F32)
        columns = slice(128 * m, 128 * m + 128)
        for out, at, half in ((dense_w, 0, 32), (shrink_w, 32, 128)):
            a, b = even[at : at + half], odd[at : at + half]
            out[0:half, columns] = join(a, 0, b, 0).astype(BF16)
            out[half : 2 * half, columns] = join(a, 1, b, 1).astype(BF16)


def rows_out_body(dense_g, shrink_g, out):
    for m in range(8):
        columns = slice(128 * m, 128 * m + 128)
        for source, at, half in ((dense_g, 0, 32), (shrink_g, 32, 128)):
            a, b = source[0:half, columns], source[half : 2 * half, columns]
            out[2 * m, at : at + half] = join(a, 0, b, 0).astype(BF16)
            out[2 * m + 1, at : at + half] = join(a, 1, b, 1).astype(BF16)


BACK_ROWS = PIECE + 32


def grads_out_body(scalars, second, qkv_g, expand_g, vector_g, qkv_bg, expand_bg, out, project_rows, expand_rows):
    head = scalars[0]
    out[...] = jnp.zeros(out.shape, BF16)
    for c in range(8):
        out[c, 0:128] = qkv_g[128 * c : 128 * c + 128, 0:128].astype(BF16)
        a = qkv_g[128 * c : 128 * c + 64, 128:256]
        b = qkv_g[128 * c + 64 : 128 * c + 128, 128:256]
        out[c, 128:192] = join(a, 0, b, 0).astype(BF16)
    for c, at, row, count in expand_places():
        out[c, at : at + count] = expand_g[row : row + count, 0:128].astype(BF16)
        out[c, at + count : at + 2 * count] = expand_g[row : row + count, 128:256].astype(BF16)

    def dense_rows(row):
        packed = second[row // 64, 0:32].astype(F32)
        return jnp.concatenate([packed, swap(packed)], axis=0)

    def shrink_rows(row):
        h, part = row // 256, row % 256 // 64
        packed = second[h, 32 + part % 2 * 64 : 96 + part % 2 * 64].astype(F32)
        return swap(packed) if part >= 2 else packed

    def plain(c, to, base, count, take):
        for i in range(count // 128):
            a, b = take(base + 64 * i), take(base + count // 2 + 64 * i)
            out[c, to + 64 * i : to + 64 * i + 64] = join(a, 0, b, 0).astype(BF16)

    plain(8, 0, 0, 384, dense_rows)
    plain(9, 0, 384, 384, dense_rows)
    plain(10, 0, 768, 256, dense_rows)
    plain(21, 64, 0, 256, shrink_rows)
    for c in range(22, 32):
        plain(c, 0, 256 + 384 * (c - 22), 384, shrink_rows)

    def rows_of(row):
        return jnp.concatenate([vector_g[row : row + 1, 128 * j : 128 * j + 128] for j in range(8)], axis=0)

    gains = jnp.concatenate([rows_of(v) for v in range(4)], axis=0)
    out[0, PIECE : PIECE + 32] = gains.astype(BF16)
    bias = jnp.concatenate([rows_of(4), jnp.zeros((8, LANES), F32)], axis=0).astype(BF16)
    out[10, PIECE : PIECE + 16] = bias
    out[31, PIECE : PIECE + 16] = bias
    project_rows[...] = jnp.zeros(project_rows.shape, F32)
    expand_rows[...] = jnp.zeros(expand_rows.shape, F32)
    pair, value = qkv_bg[0:1, 0:128], qkv_bg[0:1, 128:256]
    low = low_lanes((1, LANES))
    row = 8 + head // 2 * 3
    odd = head % 2 == 1
    project_rows[pl.ds(row, 1), :] = jnp.where(odd, 0.0, pair)
    project_rows[pl.ds(row + 1, 1), :] = jnp.where(
        odd, jnp.where(low, 0.0, swap(pair)), jnp.where(low, value, 0.0)
    )
    project_rows[pl.ds(row + 2, 1), :] = jnp.where(odd, join(pair, 1, value, 0), 0.0)
    out[8, PIECE : PIECE + 32] = project_rows[...].astype(BF16)
    expand_rows[pl.ds(2 * head, 1), :] = expand_bg[0:1, 0:128]
    expand_rows[pl.ds(2 * head + 1, 1), :] = expand_bg[0:1, 128:256]
    out[21, PIECE : PIECE + 32] = expand_rows[...].astype(BF16)


TAKE_ROWS = 3120


def grads_in_body(scalars, got, out, flat):
    start, shift, kind, vector_row = scalars[0], scalars[1], scalars[2], scalars[3]
    lead = LEAD + 8

    def clear(step, carry):
        flat[pl.ds(pl.multiple_of(step * 80, 8), 80), :] = jnp.zeros((80, LANES), F32)
        return carry

    lax.fori_loop(0, SHIFT_ROWS // 80, clear, 0)

    def add_vectors(source, total):
        return total + got[source, PIECE : PIECE + 32].astype(F32)

    flat[pl.ds(vector_row + 8, 32), :] = lax.fori_loop(0, OWNERS, add_vectors, jnp.zeros((32, LANES), F32))

    def taken(r, at, count):
        return got[r, at : at + count].astype(F32) + got[16 + r, at : at + count].astype(F32)

    def plain(base, count, at):
        half = count // 2
        for m in range(8):
            a, b = taken(2 * m, at, half), taken(2 * m + 1, at, half)
            flat[pl.ds(base + m, half, 8), :] = join(a, 0, b, 0)
            flat[pl.ds(base + m + 8 * half, half, 8), :] = join(a, 1, b, 1)

    def expand(base, count, at):
        for r in range(16):
            flat[pl.ds(base + 2 * r, count, 32), :] = taken(r, at, count)
            flat[pl.ds(base + 2 * r + 1, count, 32), :] = taken(r, at + count, count)

    def project(base):
        for m in range(8):
            pair, values = taken(2 * m, 0, 128), taken(2 * m, 128, 64)
            odd_pair, odd_values = taken(2 * m + 1, 0, 128), taken(2 * m + 1, 128, 64)
            values = jnp.concatenate([values, swap(values)], axis=0)
            odd_values = jnp.concatenate([odd_values, swap(odd_values)], axis=0)
            flat[pl.ds(base + 3 * m, 128, 24), :] = pair
            flat[pl.ds(base + 3 * m + 1, 128, 24), :] = join(values, 0, odd_pair, 0)
            flat[pl.ds(base + 3 * m + 2, 128, 24), :] = join(odd_pair, 1, odd_values, 0)

    @pl.when(kind == PROJECT)
    def _():
        project(lead)

    @pl.when(kind == PLAIN)
    def _():
        plain(lead, 384, 0)

    @pl.when(kind == PLAIN_EXPAND)
    def _():
        plain(lead, 256, 0)
        expand(lead + 2048 + 8, 32, 128)

    @pl.when(kind == EXPAND)
    def _():
        expand(lead, 96, 0)

    @pl.when(kind == EXPAND_PLAIN)
    def _():
        expand(lead, 32, 0)
        plain(lead + 1024 + 32, 256, 64)

    def align(step, carry):
        at = pl.multiple_of(step * 80, 8)
        out[pl.ds(at, 80), :] = shifted_rows(flat, start, shift, at, 80)
        return carry

    lax.fori_loop(0, TAKE_ROWS // 80, align, 0)


def token_rows(ref):
    return jnp.concatenate([ref[0, 0, 0], ref[1, 0, 0], ref[0, 0, 1], ref[1, 0, 1]], axis=0)


def put_rows(kept, sent, rows, core):
    step = rows.shape[0] // 4
    for x in range(2):
        first, second = (rows[step * i : step * i + step].astype(kept.dtype) for i in (2 * x, 2 * x + 1))
        kept[0, x] = jnp.where(core == 0, first, second)
        sent[0, x] = jnp.where(core == 0, second, first)


def relative_place(i, here):
    y = (i & 1) ^ here[2]
    z = (i >> 1) ^ here[3]
    return y * 4 + (z & 1) * 2 + (z >> 1)


def normalized(values):
    centered = values - jnp.mean(values, axis=-1, keepdims=True)
    variance = jnp.mean(centered * centered, axis=-1, keepdims=True)
    return centered * lax.rsqrt(variance + EPSILON)


def turned(pair, cos, sin):
    lane = lax.broadcasted_iota(jnp.int32, pair.shape, 1) % HD
    half = ROT // 2
    other = jnp.where(
        lane < half, -pltpu.roll(pair, LANES - half, 1), jnp.where(lane < ROT, pltpu.roll(pair, half, 1), 0.0)
    )
    return pair * cos + other * sin


def mixed_body(tokens, vectors, qkv_w, qkv_b, cos, sin, one, two, query, key, value):
    unit = normalized(token_rows(tokens).astype(F32))
    first = (unit * vectors[0:1] + vectors[1:2]).astype(BF16)
    one[...] = first
    two[...] = (unit * vectors[2:3] + vectors[3:4]).astype(BF16)
    mixed = mm(first, qkv_w[...]) + qkv_b[...]
    pair = turned(mixed[:, :LANES], cos[...], sin[...])
    query[...] = pair[:, :HD].astype(BF16) * HD ** (-0.5)
    key[...] = pair[:, HD:].astype(BF16)
    value[...] = mixed[:, LANES : LANES + HD].astype(BF16)


def masked_scores(key, query_t, at, first_query, length):
    scores = mm(key, query_t)
    keys = at * BLOCK + lax.broadcasted_iota(jnp.int32, scores.shape, 0)
    queries = first_query + lax.broadcasted_iota(jnp.int32, scores.shape, 1)
    return jnp.where((keys <= queries) & (keys < length), scores, NEGATIVE)


def folded(values, op):
    parts = [values[8 * i : 8 * i + 8] for i in range(values.shape[0] // 8)]
    while len(parts) > 1:
        parts = [op(a, b) for a, b in zip(parts[::2], parts[1::2])]
    return parts[0]


def attend_body(lengths, query, key, value, low_out, full_out, log_out, scores, value_t):
    at = pl.program_id(0)
    length = lengths[0]

    @pl.when(at == 0)
    def _():
        value_t[...] = value[...].astype(F32).T.astype(BF16)

    query_t = query[...].astype(F32).T.astype(BF16)
    clear = jnp.minimum(at, length // BLOCK)
    stop = jnp.minimum(at, (length - 1) // BLOCK) + 1

    def rows(j):
        return pl.ds(pl.multiple_of(j * BLOCK, BLOCK), BLOCK)

    def score(j, top, masked):
        if masked:
            tile = masked_scores(key[rows(j), :], query_t, j, at * BLOCK, length)
        else:
            tile = mm(key[rows(j), :], query_t)
        scores[rows(j), :] = tile
        return jnp.maximum(top, folded(tile, jnp.maximum))

    top = jnp.full((8, BLOCK), NEGATIVE, F32)
    top = lax.fori_loop(0, clear, lambda j, t: score(j, t, False), top)
    top = lax.fori_loop(clear, stop, lambda j, t: score(j, t, True), top)
    top = jnp.max(top, axis=0, keepdims=True)

    def power(j, total):
        tile = jnp.exp(scores[rows(j), :] - top)
        scores[rows(j), :] = tile
        return total + folded(tile, jnp.add)

    total = lax.fori_loop(0, stop, power, jnp.zeros((8, BLOCK), F32))
    total = jnp.sum(total, axis=0, keepdims=True)
    inverse = 1.0 / total

    def weigh(j, out):
        low = (scores[rows(j), :] * inverse).astype(BF16)
        return out + mm(value_t[:, rows(j)], low)

    out = lax.fori_loop(0, stop, weigh, jnp.zeros((HD, BLOCK), F32))
    full_out[...] = out
    low_out[...] = out.T.astype(BF16)
    log_out[...] = top + jnp.log(total)


def attend_back_body(
    lengths, query, key, value, grad, full_out, log_in, query_g, key_g, value_g, key_t, key_sum, value_sum
):
    at = pl.program_id(0)
    length = lengths[0]

    @pl.when(at == 0)
    def _():
        key_t[...] = key[...].astype(F32).T.astype(BF16)
        key_sum[...] = jnp.zeros(key_sum.shape, F32)
        value_sum[...] = jnp.zeros(value_sum.shape, F32)

    query_rows, grad_rows = query[...], grad[...]
    query_t = query_rows.astype(F32).T.astype(BF16)
    grad_full_t = grad_rows.astype(F32).T
    grad_t = grad_full_t.astype(BF16)
    delta = jnp.sum(grad_full_t * full_out[...], axis=0, keepdims=True)
    log_total = log_in[...]
    clear = jnp.minimum(at, length // BLOCK)
    stop = jnp.minimum(at, (length - 1) // BLOCK) + 1
    clear, stop = (jnp.where(at * BLOCK < length, n, 0) for n in (clear, stop))

    def step(j, query_sum, masked):
        rows = pl.ds(pl.multiple_of(j * BLOCK, BLOCK), BLOCK)
        if masked:
            tile = masked_scores(key[rows, :], query_t, j, at * BLOCK, length)
        else:
            tile = mm(key[rows, :], query_t)
        probs = jnp.exp(tile - log_total)
        value_sum[rows, :] += mm(probs.astype(BF16), grad_rows)
        score_g = (probs * (mm(value[rows, :], grad_t) - delta)).astype(BF16)
        key_sum[rows, :] += mm(score_g, query_rows)
        return query_sum + mm(key_t[:, rows], score_g)

    query_sum = jnp.zeros((HD, BLOCK), F32)
    query_sum = lax.fori_loop(0, clear, lambda j, s: step(j, s, False), query_sum)
    query_sum = lax.fori_loop(clear, stop, lambda j, s: step(j, s, True), query_sum)
    query_g[...] = (query_sum * HD ** (-0.5)).T.astype(BF16)

    @pl.when(at == pl.num_programs(0) - 1)
    def _():
        key_g[...] = key_sum[...].astype(BF16)
        value_g[...] = value_sum[...].astype(BF16)


def feed_body(
    here, two, attended, cotangent, expand_w, expand_b, shrink_w, dense_w,
    kept, sent, attended_g, hidden_g, shrink_g, dense_g, expand_g, expand_bg, bias_g,
):
    at = pl.program_id(0)

    @pl.when(at == 0)
    def _():
        for total in (shrink_g, dense_g, expand_g, expand_bg, bias_g):
            total[...] = jnp.zeros(total.shape, F32)

    normed, mixed = two[...], attended[...]
    hidden = mm(normed, expand_w[...]) + expand_b[...]
    error = lax.erf(hidden * math.sqrt(0.5))
    cumulative = 0.5 * (1.0 + error)
    active = (hidden * cumulative).astype(BF16)
    put_rows(kept, sent, mm(mixed, dense_w[...]) + mm(active, shrink_w[...]), here[1])
    token = at * BLOCK + lax.broadcasted_iota(jnp.int32, (BLOCK, D), 0)
    seed = jnp.where(token < here[0], token_rows(cotangent).astype(F32), 0.0)
    bias_g[...] += jnp.sum(seed, axis=0, keepdims=True)
    seed = seed.astype(BF16)
    attended_g[...] = mm(seed, dense_w[...], ((1,), (1,))).astype(BF16)
    slope = cumulative + hidden * jnp.exp(-0.5 * hidden * hidden) * (1.0 / math.sqrt(2.0 * math.pi))
    back = (mm(seed, shrink_w[...], ((1,), (1,))) * slope).astype(BF16)
    hidden_g[...] = back
    expand_bg[...] += jnp.sum(back.astype(F32), axis=0, keepdims=True)
    shrink_g[...] += mm(active, seed, ((0,), (0,)))
    dense_g[...] += mm(mixed, seed, ((0,), (0,)))
    expand_g[...] += mm(normed, back, ((0,), (0,)))


def mixed_back_body(
    here, tokens, one, query_g, key_g, value_g, hidden_g, vectors, qkv_w, expand_w, cos, sin,
    kept, sent, qkv_g, qkv_bg, vector_g,
):
    at = pl.program_id(0)

    @pl.when(at == 0)
    def _():
        for total in (qkv_g, qkv_bg, vector_g):
            total[...] = jnp.zeros(total.shape, F32)

    pair = jnp.concatenate([query_g[...].astype(F32), key_g[...].astype(F32)], axis=1)
    pair = turned(pair, cos[...], -sin[...])
    values = value_g[...].astype(F32)
    mixed_g = jnp.concatenate([pair, values, jnp.zeros_like(values)], axis=1)
    mixed_low = mixed_g.astype(BF16)
    qkv_bg[...] += jnp.sum(mixed_low.astype(F32), axis=0, keepdims=True)
    qkv_g[...] += mm(one[...], mixed_low, ((0,), (0,)))
    one_g = mm(mixed_low, qkv_w[...], ((1,), (1,)))
    two_g = mm(hidden_g[...], expand_w[...], ((1,), (1,)))
    unit = normalized(token_rows(tokens).astype(F32))
    vector_g[0:1] += jnp.sum(one_g * unit, axis=0, keepdims=True)
    vector_g[1:2] += jnp.sum(one_g, axis=0, keepdims=True)
    vector_g[2:3] += jnp.sum(two_g * unit, axis=0, keepdims=True)
    vector_g[3:4] += jnp.sum(two_g, axis=0, keepdims=True)
    put_rows(kept, sent, one_g * vectors[0:1] + two_g * vectors[2:3], here[1])


def split_mesh(mesh):
    groups, members = mesh.shape["blk"], mesh.shape["uly"]
    return Mesh(mesh.devices.reshape(groups // 2, 2, members // 2, 2), ALL)


def across_x(block):
    return lax.ppermute(block, "x", [(0, 1), (1, 0)])


def by_head(residual, cotangent, lengths, positions, masters, momenta, averages):
    slots, span, width = residual.shape
    x = lax.axis_index("x")
    head = lax.axis_index("core") * 8 + lax.axis_index("z") * 2 + lax.axis_index("y")
    owner = x * 16 + head
    groups = lax.axis_size("z") * lax.axis_size("y")
    count = groups * 4 * span
    chunk = masters.shape[0]
    length = lax.dynamic_slice_in_dim(lengths, x, 1)

    def paired(mine, theirs):
        return jnp.where(x == 0, jnp.stack([mine, theirs]), jnp.stack([theirs, mine]))

    def at_x(rows, index):
        return lax.dynamic_index_in_dim(rows, index, 0, keepdims=False)

    rows = jnp.stack([residual, cotangent], axis=1)
    rows = paired(at_x(rows, x), across_x(at_x(rows, 1 - x)))
    tokens_shape = (2, groups, 2, span, width)
    slot_tokens = lax.all_gather(rows[:, 0], RING, axis=0).reshape(tokens_shape)
    later, slot_tokens = lax.optimization_barrier((rows[:, 1], slot_tokens))
    slot_cotangent = lax.all_gather(later, RING, axis=0).reshape(tokens_shape)

    place = jnp.broadcast_to(positions.reshape(1, slots * span), (OWNERS, slots * span))
    place = lax.all_to_all(place, ALL, 0, 0, tiled=True)
    known = place
    place = place.reshape(2, 2, groups, slots, span)
    place = lax.dynamic_index_in_dim(place, x, 3, keepdims=False).transpose(2, 0, 1, 3).reshape(count)
    half_dims = ROT // 2
    inverse = ROTARY_BASE ** (-(jnp.arange(half_dims, dtype=F32) * 2.0 / ROT))
    angles = place.astype(F32)[:, None] * inverse
    cos, sin = jnp.cos(angles), jnp.sin(angles)
    flat_part = jnp.ones((count, HD - ROT), F32)
    cos = jnp.concatenate([cos, cos, flat_part] * 2, axis=1)
    sin = jnp.concatenate([sin, sin, 0.0 * flat_part] * 2, axis=1)

    onward = [(i, i + 1) for i in range(OWNERS - 1)]
    backward = [(i + 1, i) for i in range(OWNERS - 1)]
    before = lax.ppermute(masters[chunk - D :], ALL, onward)
    after = lax.ppermute(masters[: 4 * D], ALL, backward)
    own_rows = -(-chunk // D) * 8
    own = jnp.pad(masters, (0, own_rows * LANES - chunk)).reshape(own_rows, LANES)
    before, after = before.reshape(8, LANES), after.reshape(32, LANES)
    skipped = jnp.where(owner < 8, 4, jnp.where(owner < 11, 7, jnp.where(owner < 22, 8, 12)))
    kind = jnp.where(
        owner < 8,
        PROJECT,
        jnp.where(
            owner == 10,
            PLAIN_EXPAND,
            jnp.where(owner == 21, EXPAND_PLAIN, jnp.where((owner > 10) & (owner < 21), EXPAND, PLAIN)),
        ),
    )
    vector_row = jnp.where(owner == 10, 2080, jnp.where(owner == 21, 1056, jnp.where(owner == 31, 3104, 0)))
    ahead = skipped * D - (chunk - PER * D) * owner
    begin = ahead + 4 * D
    scalars = jnp.stack([begin // LANES, begin % LANES, kind, vector_row]).astype(jnp.int32)
    sent = call(
        weights_out_body, (1,),
        [whole(before.shape), whole(own.shape), whole(after.shape)],
        whole((16, SEND_ROWS, LANES)),
        shaped((16, SEND_ROWS, LANES), BF16),
        [pltpu.VMEM((3280, LANES), F32), pltpu.VMEM((SHIFT_ROWS, LANES), F32), pltpu.VMEM((48, LANES), F32)],
        1, "weights_out",
    )(scalars, before, own, after)
    sent, _ = lax.optimization_barrier((jnp.concatenate([sent, sent]), known))
    got = lax.all_to_all(sent, ALL, 0, 0, tiled=True)
    head_scalar = head.astype(jnp.int32).reshape(1)
    qkv_w, expand_w, second, vectors, qkv_b, expand_b = call(
        weights_in_body, (1,),
        [whole(got.shape)],
        [whole((D, 256)), whole((D, 256)), whole((16, 160, LANES)), whole((8, D)), whole((1, 256)), whole((1, 256))],
        [shaped((D, 256), BF16), shaped((D, 256), BF16), shaped((16, 160, LANES), BF16), shaped((8, D), F32),
         shaped((1, 256), F32), shaped((1, 256), F32)],
        [pltpu.VMEM((24, LANES), F32), pltpu.VMEM((32, LANES), F32)], 1, "weights_in",
    )(head_scalar, got)
    second = lax.all_to_all(second, RING, 0, 0, tiled=True)
    steps = (count // BLOCK,)
    token_spec = pl.BlockSpec((2, 1, 2, span, width), lambda i, *_: (0, i, 0, 0, 0))
    part_spec = pl.BlockSpec((1, 2, span, width), lambda i, here: (relative_place(i, here), 0, 0, 0))
    part_shape = shaped((groups, 2, span, width), BF16)
    y, z, core = lax.axis_index("y"), lax.axis_index("z"), lax.axis_index("core")
    here = jnp.stack([length[0], core, y, z]).astype(jnp.int32)

    def summed(kept, sent):
        groups_left = kept.shape[0]
        for axis, route in (
            ("core", [(0, 1), (1, 0)]),
            ("y", [(0, 1), (1, 0)]),
            ("z", [(0, 1), (1, 0), (2, 3), (3, 2)]),
            ("z", [(0, 2), (2, 0), (1, 3), (3, 1)]),
        ):
            came = lax.ppermute(sent, axis, route)
            if groups_left == 1:
                return kept[0].astype(F32) + came[0].astype(F32)
            groups_left //= 2
            kept, sent = (
                (kept[half].astype(F32) + came[half].astype(F32)).astype(BF16)
                for half in (slice(0, groups_left), slice(groups_left, None))
            )

    def rows_spec(columns):
        return pl.BlockSpec((BLOCK, columns), lambda i, *_: (i, 0))

    def columns_spec(rows):
        return pl.BlockSpec((rows, BLOCK), lambda i, *_: (0, i))

    narrow = shaped((count, HD), BF16)
    one, two, query, key, value = call(
        mixed_body, steps,
        [token_spec, whole((8, D)), whole((D, 256)), whole((1, 256)), rows_spec(LANES), rows_spec(LANES)],
        [rows_spec(D), rows_spec(D), rows_spec(HD), rows_spec(HD), rows_spec(HD)],
        [shaped((count, D), BF16), shaped((count, D), BF16), narrow, narrow, narrow], name="mixed",
    )(slot_tokens, vectors, qkv_w, qkv_b, cos, sin)
    attended, attended_full, log_total = call(
        attend_body, steps,
        [rows_spec(HD), whole((count, HD)), whole((count, HD))],
        [rows_spec(HD), columns_spec(HD), columns_spec(1)],
        [narrow, shaped((HD, count), F32), shaped((1, count), F32)],
        [pltpu.VMEM((count, BLOCK), F32), pltpu.VMEM((HD, count), BF16)], 1, "attend",
    )(length, query, key, value)
    second, attended = lax.optimization_barrier((second, attended))
    dense_w, shrink_w = call(
        rows_in_body, (1,), [whole(second.shape)], [whole((HD, D)), whole((256, D))],
        [shaped((HD, D), BF16), shaped((256, D), BF16)], name="rows_in",
    )(second)

    kept, sent, attended_g, hidden_g, shrink_g, dense_g, expand_g, expand_bg, bias_g = call(
        feed_body, steps,
        [rows_spec(D), rows_spec(HD), token_spec, whole((D, 256)), whole((1, 256)), whole((256, D)), whole((HD, D))],
        [part_spec, part_spec, rows_spec(HD), rows_spec(256), whole((256, D)), whole((HD, D)), whole((D, 256)),
         whole((1, 256)), whole((1, D))],
        [part_shape, part_shape, narrow, shaped((count, 256), BF16), shaped((256, D), F32), shaped((HD, D), F32),
         shaped((D, 256), F32), shaped((1, 256), F32), shaped((1, D), F32)], (), 1, "feed",
    )(here, two, attended, slot_cotangent, expand_w, expand_b, shrink_w, dense_w)
    second_g = call(
        rows_out_body, (1,), [whole((HD, D)), whole((256, D))], whole((16, 160, LANES)),
        shaped((16, 160, LANES), BF16), name="rows_out",
    )(dense_g, shrink_g)
    attended_g, second_g = lax.optimization_barrier((attended_g, second_g))
    second_g = lax.all_to_all(second_g, RING, 0, 0, tiled=True)
    out_rows = summed(kept, sent)
    query_g, key_g, value_g = call(
        attend_back_body, steps,
        [rows_spec(HD), whole((count, HD)), whole((count, HD)), rows_spec(HD), columns_spec(HD), columns_spec(1)],
        [rows_spec(HD), whole((count, HD)), whole((count, HD))],
        [narrow, narrow, narrow],
        [pltpu.VMEM((HD, count), BF16), pltpu.VMEM((count, HD), F32), pltpu.VMEM((count, HD), F32)],
        1, "attend_back",
    )(length, query, key, value, attended_g, attended_full, log_total)
    kept, sent, qkv_g, qkv_bg, vector_g = call(
        mixed_back_body, steps,
        [token_spec, rows_spec(D), rows_spec(HD), rows_spec(HD), rows_spec(HD),
         rows_spec(256), whole((8, D)), whole((D, 256)), whole((D, 256)), rows_spec(LANES), rows_spec(LANES)],
        [part_spec, part_spec, whole((D, 256)), whole((1, 256)), whole((8, D))],
        [part_shape, part_shape, shaped((D, 256), F32), shaped((1, 256), F32), shaped((8, D), F32)], (), 1, "mixed_back",
    )(here, slot_tokens, one, query_g, key_g, value_g, hidden_g, vectors, qkv_w, expand_w, cos, sin)
    in_rows = summed(kept, sent)
    rows = jnp.stack([out_rows, in_rows], axis=1).astype(BF16)
    rows = paired(at_x(rows, x), across_x(at_x(rows, 1 - x))).astype(F32)
    out_rows, in_rows = rows[:, 0], rows[:, 1]

    bias_g = jnp.where(head == 0, bias_g, 0.0)
    vector_g = jnp.concatenate([vector_g[:4], bias_g, jnp.zeros((3, D), F32)])
    sent_g = call(
        grads_out_body, (1,),
        [whole((16, 160, LANES)), whole((D, 256)), whole((D, 256)), whole((8, D)), whole((1, 256)), whole((1, 256))],
        whole((OWNERS, BACK_ROWS, LANES)),
        shaped((OWNERS, BACK_ROWS, LANES), BF16),
        [pltpu.VMEM((32, LANES), F32), pltpu.VMEM((32, LANES), F32)], 1, "grads_out",
    )(head_scalar, second_g, qkv_g, expand_g, vector_g, qkv_bg, expand_bg)
    got_g = lax.all_to_all(sent_g, ALL, 0, 0, tiled=True)
    begin_g = (chunk - PER * D) * owner - skipped * D + 4 * D
    scalars_g = jnp.stack([begin_g // LANES, begin_g % LANES, kind, vector_row]).astype(jnp.int32)
    taken = call(
        grads_in_body, (1,), [whole(got_g.shape)], whole((TAKE_ROWS, LANES)), shaped((TAKE_ROWS, LANES), F32),
        [pltpu.VMEM((SHIFT_ROWS, LANES), F32)], 1, "grads_in",
    )(scalars_g, got_g).reshape(-1)
    from_before = lax.ppermute(taken[D + chunk : 5 * D + chunk], ALL, onward)
    from_after = lax.ppermute(taken[:D], ALL, backward)
    gradients = taken[D : D + chunk]
    gradients = gradients.at[: 4 * D].add(from_before).at[chunk - D :].add(from_after)

    values = residual.astype(F32)
    outputs = (values + out_rows + (vectors[4] + vectors[5])).astype(BF16)
    first_token = ((lax.axis_index("z") * 2 + lax.axis_index("y")) * 4 + x * 2 + lax.axis_index("core")) * span
    token = first_token + jnp.arange(span, dtype=jnp.int32)
    live = token[None, :] < lengths[:, None]
    seed = jnp.where(live[:, :, None], cotangent.astype(F32), 0.0)
    centered = values - jnp.mean(values, axis=-1, keepdims=True)
    scale = lax.rsqrt(jnp.mean(centered * centered, axis=-1, keepdims=True) + EPSILON)
    unit = centered * scale
    back = in_rows - jnp.mean(in_rows, axis=-1, keepdims=True)
    back = scale * (back - unit * jnp.mean(in_rows * unit, axis=-1, keepdims=True))
    input_grad = (seed + back).astype(BF16)

    velocity = MOMENTUM * momenta + gradients
    step_rate = LEARN_RATE / math.sqrt(slots * count)
    updated = masters - step_rate * (gradients + MOMENTUM * velocity)
    averaged = AVERAGE_DECAY * averages + (1.0 - AVERAGE_DECAY) * updated
    return (outputs, input_grad, gradients, updated, velocity, averaged)


def solution(mesh):
    def step(*args):
        slots, tokens = args[0].shape[:2]
        if mesh.size == OWNERS == slots * H and mesh.shape["blk"] == 4 and tokens == 64 * OWNERS:
            tokens_in, flat, used, body = P(None, ("z", "y", "x", "core"), None), P(ALL), split_mesh(mesh), by_head
            places = P(None, ("z", "y", "x", "core"))
        else:
            tokens_in, flat, used, body = P(None, ("uly", "blk"), None), P(("blk", "uly")), mesh, local
            places = P(None, ("uly", "blk"))
        return jax.shard_map(
            body,
            mesh=used,
            in_specs=(tokens_in, tokens_in, P(), places, flat, flat, flat),
            out_specs=(tokens_in, tokens_in, flat, flat, flat, flat),
            check_vma=False,
        )(*args)

    return step
```

```python
from functools import partial
import math

import jax
import jax.numpy as jnp
from jax import lax
from jax.experimental import pallas as pl
from jax.experimental.pallas import tpu as pltpu
from jax.sharding import Mesh, PartitionSpec as P

D = 1024
H = 16
HD = 64
ROT = 16
FF = 4096


EPSILON = 1e-05
NEGATIVE = -1e30
MOMENTUM = 0.5
LEARN_RATE = 0.05
AVERAGE_DECAY = 0.5
ROTARY_BASE = 10000.0


def passed_along(block, axis, distance):
    devices = range(lax.axis_size(axis))
    route = [((i - distance) % len(devices), i) for i in devices]
    return lax.ppermute(block, axis, route)


def unpack(flat_vector):
    layouts = [
        (D,),
        (D,),
        (D,),
        (D,),
        (D, 3 * D),
        (3 * D,),
        (D, D),
        (D,),
        (D, FF),
        (FF,),
        (FF, D),
        (D,),
    ]
    pieces = []
    cursor = 0
    for layout in layouts:
        number = math.prod(layout)
        pieces.append(flat_vector[cursor : cursor + number].reshape(layout))
        cursor += number
    return pieces


def layer_norm(values, gain, shift):
    centered = values - jnp.mean(values, axis=-1, keepdims=True)
    variance = jnp.mean(centered * centered, axis=-1, keepdims=True)
    return centered * lax.rsqrt(variance + EPSILON) * gain + shift


def rotary_tables(positions):
    half_dims = ROT // 2
    inverse = ROTARY_BASE ** (-(jnp.arange(half_dims, dtype=jnp.float32) * 2.0 / ROT))
    angles = positions.astype(jnp.float32)[..., None] * inverse
    return (jnp.cos(angles), jnp.sin(angles))


def rotate(values, cos_table, sin_table):
    half_dims = ROT // 2
    first_half = values[..., :half_dims]
    second_half = values[..., half_dims:ROT]
    return jnp.concatenate(
        [
            first_half * cos_table - second_half * sin_table,
            second_half * cos_table + first_half * sin_table,
            values[..., ROT:],
        ],
        axis=-1,
    )


def group_tokens(source, group_count, uly_count, span_rows):
    spans = jnp.arange(uly_count, dtype=jnp.int32)[:, None] * group_count + source
    return (spans * span_rows + jnp.arange(span_rows, dtype=jnp.int32)[None, :]).reshape(-1)


def block_scores(queries, keys_rows, row_tokens, col_tokens, length):
    scores = jnp.einsum(
        "qhd,khd->hqk", queries, keys_rows, preferred_element_type=jnp.float32
    ) * HD ** (-0.5)
    allowed = (col_tokens[None, :] <= row_tokens[:, None]) & (col_tokens[None, :] < length)
    return jnp.where(allowed[None], scores, NEGATIVE)


def is_live(row_tokens, col_tokens, length):
    return (col_tokens[0] <= row_tokens[-1]) & (col_tokens[0] < length)


def fold_stats(row_max, row_total, queries, key_value, lengths, row_tokens, col_tokens):

    def per_slot(inputs):
        slot_max, slot_total, slot_queries, slot_pairs, length = inputs

        def compute(current):
            prev_max, prev_total = current
            scores = block_scores(slot_queries, slot_pairs[:, :, 0], row_tokens, col_tokens, length)
            next_max = jnp.maximum(prev_max, jnp.max(scores, axis=-1))
            next_total = prev_total * jnp.exp(prev_max - next_max) + jnp.sum(
                jnp.exp(scores - next_max[..., None]), axis=-1
            )
            return (next_max, next_total)

        return lax.cond(
            is_live(row_tokens, col_tokens, length),
            compute,
            lambda current: current,
            (slot_max, slot_total),
        )

    return lax.map(per_slot, (row_max, row_total, queries, key_value, lengths))


def fold_values(attended, queries, key_value, log_total, lengths, row_tokens, col_tokens):

    def per_slot(inputs):
        slot_out, slot_queries, slot_pairs, slot_log, length = inputs

        def compute(current):
            scores = block_scores(slot_queries, slot_pairs[:, :, 0], row_tokens, col_tokens, length)
            prob_low = jnp.exp(scores - slot_log[..., None]).astype(jnp.bfloat16)
            return current + jnp.einsum(
                "hqk,khd->qhd", prob_low, slot_pairs[:, :, 1], preferred_element_type=jnp.float32
            )

        return lax.cond(
            is_live(row_tokens, col_tokens, length), compute, lambda current: current, slot_out
        )

    return lax.map(per_slot, (attended, queries, key_value, log_total, lengths))


def fold_grads(
    query_grad,
    pair_grad,
    queries,
    key_value,
    grad_out,
    log_total,
    row_delta,
    lengths,
    row_tokens,
    col_tokens,
):

    def per_slot(inputs):
        (
            slot_qgrad,
            slot_pgrad,
            slot_queries,
            slot_pairs,
            slot_gout,
            slot_log,
            slot_delta,
            length,
        ) = inputs

        def compute(current):
            cur_qgrad, cur_pgrad = current
            scores = block_scores(slot_queries, slot_pairs[:, :, 0], row_tokens, col_tokens, length)
            attend_prob = jnp.exp(scores - slot_log[..., None])
            prob_low = attend_prob.astype(jnp.bfloat16)
            prob_grad = jnp.einsum(
                "qhd,khd->hqk", slot_gout, slot_pairs[:, :, 1], preferred_element_type=jnp.float32
            )
            score_grad = (attend_prob * (prob_grad - slot_delta[..., None])).astype(jnp.bfloat16)
            cur_qgrad = cur_qgrad + jnp.einsum(
                "hqk,khd->qhd", score_grad, slot_pairs[:, :, 0], preferred_element_type=jnp.float32
            ) * HD ** (-0.5)
            key_grad = jnp.einsum(
                "hqk,qhd->khd", score_grad, slot_queries, preferred_element_type=jnp.float32
            ) * HD ** (-0.5)
            value_grad = jnp.einsum(
                "hqk,qhd->khd", prob_low, slot_gout, preferred_element_type=jnp.float32
            )
            return (cur_qgrad, cur_pgrad + jnp.stack([key_grad, value_grad], axis=2))

        return lax.cond(
            is_live(row_tokens, col_tokens, length),
            compute,
            lambda current: current,
            (slot_qgrad, slot_pgrad),
        )

    return lax.map(
        per_slot,
        (query_grad, pair_grad, queries, key_value, grad_out, log_total, row_delta, lengths),
    )


def local(residual, cotangent, lengths, positions, masters, momenta, averages):
    slot_count, span_rows, model_width = residual.shape
    group_count = lax.axis_size("blk")
    uly_count = lax.axis_size("uly")
    group_index = lax.axis_index("blk")
    uly_index = lax.axis_index("uly")
    block_rows = uly_count * span_rows
    full_rows = group_count * block_rows
    local_heads = H // uly_count
    token_rows = slot_count * span_rows
    row_tokens = group_tokens(group_index, group_count, uly_count, span_rows)

    def tokens_of(source):
        return group_tokens(source, group_count, uly_count, span_rows)

    gathered = lax.all_gather(masters.astype(jnp.bfloat16), ("blk", "uly"), axis=0, tiled=True)
    (
        gain_one,
        shift_one,
        gain_two,
        shift_two,
        project_w,
        project_b,
        dense_w,
        dense_b,
        expand_w,
        expand_b,
        shrink_w,
        shrink_b,
    ) = unpack(gathered)
    values = residual.astype(jnp.float32).reshape(token_rows, model_width)
    normed_one, norm_back_one = jax.vjp(
        layer_norm, values, gain_one.astype(jnp.float32), shift_one.astype(jnp.float32)
    )
    normed_two, norm_back_two = jax.vjp(
        layer_norm, values, gain_two.astype(jnp.float32), shift_two.astype(jnp.float32)
    )
    normed_one = normed_one.astype(jnp.bfloat16)
    normed_two = normed_two.astype(jnp.bfloat16)
    mixed_rows = jnp.dot(
        normed_one, project_w, preferred_element_type=jnp.float32
    ) + project_b.astype(jnp.float32)
    mixed_rows = mixed_rows.reshape(slot_count, span_rows, H, 3, HD)
    cos_table, sin_table = rotary_tables(positions)
    cos_table = cos_table[:, :, None, None, :]
    sin_table = sin_table[:, :, None, None, :]
    turned, turn_back = jax.vjp(
        lambda pair_rows: rotate(pair_rows, cos_table, sin_table), mixed_rows[:, :, :, 0:2]
    )
    packed = jnp.concatenate([turned, mixed_rows[:, :, :, 2:3]], axis=3).astype(jnp.bfloat16)
    packed = packed.reshape(slot_count, span_rows, 3 * model_width)
    heads_rows = lax.all_to_all(packed, "uly", split_axis=2, concat_axis=1, tiled=True).reshape(
        slot_count, block_rows, local_heads, 3, HD
    )
    queries = heads_rows[:, :, :, 0]
    key_value = heads_rows[:, :, :, 1:3]
    row_max = jnp.full((slot_count, local_heads, block_rows), NEGATIVE, jnp.float32)
    row_total = jnp.zeros((slot_count, local_heads, block_rows), jnp.float32)
    attended = jnp.zeros((slot_count, block_rows, local_heads, HD), jnp.float32)
    last_tokens = tokens_of((group_index + 1) % group_count)

    def stats_turn(turn_index, carried):
        pairs_now, cur_max, cur_total = carried
        col_tokens = tokens_of((group_index - turn_index) % group_count)
        cur_max, cur_total = fold_stats(
            cur_max, cur_total, queries, pairs_now, lengths, row_tokens, col_tokens
        )
        pairs_now = passed_along(pairs_now, "blk", 1)
        return (pairs_now, cur_max, cur_total)

    pairs_now, row_max, row_total = lax.fori_loop(
        0, group_count - 1, stats_turn, (key_value, row_max, row_total)
    )
    row_max, row_total = fold_stats(
        row_max, row_total, queries, pairs_now, lengths, row_tokens, last_tokens
    )
    log_total = row_max + jnp.log(row_total)

    def value_turn(turn_index, carried):
        pairs_now, cur_out = carried
        col_tokens = tokens_of((group_index - turn_index) % group_count)
        cur_out = fold_values(
            cur_out, queries, pairs_now, log_total, lengths, row_tokens, col_tokens
        )
        pairs_now = passed_along(pairs_now, "blk", 1)
        return (pairs_now, cur_out)

    pairs_now, attended = lax.fori_loop(0, group_count - 1, value_turn, (key_value, attended))
    attended = fold_values(
        attended, queries, pairs_now, log_total, lengths, row_tokens, last_tokens
    )
    heads_out = attended.astype(jnp.bfloat16).reshape(slot_count, block_rows, local_heads * HD)
    merged = lax.all_to_all(heads_out, "uly", split_axis=1, concat_axis=2, tiled=True).reshape(
        token_rows, model_width
    )
    branch_attn = jnp.dot(merged, dense_w, preferred_element_type=jnp.float32) + dense_b.astype(
        jnp.float32
    )
    hidden_pre = jnp.dot(
        normed_two, expand_w, preferred_element_type=jnp.float32
    ) + expand_b.astype(jnp.float32)
    activated, gelu_back = jax.vjp(partial(jax.nn.gelu, approximate=False), hidden_pre)
    activated_low = activated.astype(jnp.bfloat16)
    branch_feed = jnp.dot(
        activated_low, shrink_w, preferred_element_type=jnp.float32
    ) + shrink_b.astype(jnp.float32)
    outputs = (
        (values + branch_attn + branch_feed)
        .astype(jnp.bfloat16)
        .reshape(slot_count, span_rows, model_width)
    )
    first_token = (uly_index * group_count + group_index) * span_rows
    token_index = first_token + jnp.arange(span_rows, dtype=jnp.int32)
    live_mask = (token_index[None, :] < lengths[:, None]).astype(jnp.float32)
    seed_grad = (cotangent.astype(jnp.float32) * live_mask[:, :, None]).reshape(
        token_rows, model_width
    )
    seed_low = seed_grad.astype(jnp.bfloat16)
    dense_w_grad = jnp.einsum("ra,rb->ab", merged, seed_low, preferred_element_type=jnp.float32)
    bias_grad = jnp.sum(seed_low.astype(jnp.float32), axis=0)
    merged_grad = jnp.einsum(
        "rb,ab->ra", seed_low, dense_w, preferred_element_type=jnp.float32
    ).astype(jnp.bfloat16)
    shrink_w_grad = jnp.einsum(
        "rf,rb->fb", activated_low, seed_low, preferred_element_type=jnp.float32
    )
    activated_grad = jnp.einsum("rb,fb->rf", seed_low, shrink_w, preferred_element_type=jnp.float32)
    hidden_grad = gelu_back(activated_grad)[0].astype(jnp.bfloat16)
    expand_w_grad = jnp.einsum(
        "ra,rf->af", normed_two, hidden_grad, preferred_element_type=jnp.float32
    )
    expand_b_grad = jnp.sum(hidden_grad.astype(jnp.float32), axis=0)
    normed_two_grad = jnp.einsum(
        "rf,af->ra", hidden_grad, expand_w, preferred_element_type=jnp.float32
    )
    grad_heads = lax.all_to_all(
        merged_grad.reshape(slot_count, span_rows, model_width),
        "uly",
        split_axis=2,
        concat_axis=1,
        tiled=True,
    )
    grad_out = grad_heads.reshape(slot_count, block_rows, local_heads, HD)
    row_delta = jnp.sum(grad_out.astype(jnp.float32) * attended, axis=-1).transpose(0, 2, 1)
    query_grad = jnp.zeros((slot_count, block_rows, local_heads, HD), jnp.float32)
    pair_grad = jnp.zeros((slot_count, block_rows, local_heads, 2, HD), jnp.float32)

    def grad_turn(turn_index, carried):
        pairs_now, cur_pgrad, cur_qgrad = carried
        col_tokens = tokens_of((group_index - turn_index) % group_count)
        cur_qgrad, cur_pgrad = fold_grads(
            cur_qgrad,
            cur_pgrad,
            queries,
            pairs_now,
            grad_out,
            log_total,
            row_delta,
            lengths,
            row_tokens,
            col_tokens,
        )
        pairs_now = passed_along(pairs_now, "blk", 1)
        cur_pgrad = passed_along(cur_pgrad.astype(jnp.bfloat16), "blk", 1).astype(cur_pgrad.dtype)
        return (pairs_now, cur_pgrad, cur_qgrad)

    pairs_now, pair_grad, query_grad = lax.fori_loop(
        0, group_count - 1, grad_turn, (key_value, pair_grad, query_grad)
    )
    query_grad, pair_grad = fold_grads(
        query_grad,
        pair_grad,
        queries,
        pairs_now,
        grad_out,
        log_total,
        row_delta,
        lengths,
        row_tokens,
        last_tokens,
    )
    pair_grad = passed_along(pair_grad.astype(jnp.bfloat16), "blk", 1).astype(pair_grad.dtype)
    back_packed = jnp.concatenate(
        [query_grad.astype(jnp.bfloat16)[:, :, :, None], pair_grad.astype(jnp.bfloat16)], axis=3
    )
    back_packed = back_packed.reshape(slot_count, block_rows, local_heads * 3 * HD)
    token_grads = lax.all_to_all(
        back_packed, "uly", split_axis=1, concat_axis=2, tiled=True
    ).reshape(slot_count, span_rows, H, 3, HD)
    turned_grad = turn_back(token_grads[:, :, :, 0:2].astype(jnp.float32))[0]
    mixed_grad = jnp.concatenate(
        [turned_grad, token_grads[:, :, :, 2:3].astype(jnp.float32)], axis=3
    ).astype(jnp.bfloat16)
    mixed_grad = mixed_grad.reshape(token_rows, 3 * model_width)
    project_w_grad = jnp.einsum(
        "ra,rc->ac", normed_one, mixed_grad, preferred_element_type=jnp.float32
    )
    project_b_grad = jnp.sum(mixed_grad.astype(jnp.float32), axis=0)
    normed_one_grad = jnp.einsum(
        "rc,ac->ra", mixed_grad, project_w, preferred_element_type=jnp.float32
    )
    values_one, gain_one_grad, shift_one_grad = norm_back_one(normed_one_grad)
    values_two, gain_two_grad, shift_two_grad = norm_back_two(normed_two_grad)
    input_grad = (
        (seed_grad + values_one + values_two)
        .astype(jnp.bfloat16)
        .reshape(slot_count, span_rows, model_width)
    )
    local_grads = jnp.concatenate(
        [
            gain_one_grad,
            shift_one_grad,
            gain_two_grad,
            shift_two_grad,
            project_w_grad.reshape(-1),
            project_b_grad,
            dense_w_grad.reshape(-1),
            bias_grad,
            expand_w_grad.reshape(-1),
            expand_b_grad,
            shrink_w_grad.reshape(-1),
            bias_grad,
        ]
    )
    gradients = lax.psum_scatter(local_grads, ("blk", "uly"), scatter_dimension=0, tiled=True)
    velocity = MOMENTUM * momenta + gradients
    step_rate = LEARN_RATE / math.sqrt(slot_count * full_rows)
    updated = masters - step_rate * (gradients + MOMENTUM * velocity)
    averaged = AVERAGE_DECAY * averages + (1.0 - AVERAGE_DECAY) * updated
    return (outputs, input_grad, gradients, updated, velocity, averaged)


LANES = 128
BLOCK = 256
RING = ("core", "z", "y")
ALL = ("x", "core", "z", "y")
F32 = jnp.float32
BF16 = jnp.bfloat16


def call(body, grid, in_specs, out_specs, out_shape, scratch=(), prefetch=0):
    return pl.pallas_call(
        body,
        grid_spec=pltpu.PrefetchScalarGridSpec(
            num_scalar_prefetch=prefetch,
            grid=grid,
            in_specs=in_specs,
            out_specs=out_specs,
            scratch_shapes=scratch,
        ),
        out_shape=out_shape,
        compiler_params=pltpu.CompilerParams(vmem_limit_bytes=56 << 20),
    )


def whole(shape):
    return pl.BlockSpec(shape, lambda *_: (0,) * len(shape))


def shaped(shape, kind):
    return jax.ShapeDtypeStruct(shape, kind)


def mm(a, b, dims=((1,), (0,))):
    return lax.dot_general(a, b, (dims, ((), ())), preferred_element_type=F32)


def low_lanes(shape):
    return lax.broadcasted_iota(jnp.int32, shape, len(shape) - 1) < LANES // 2


def swap(a):
    return pltpu.roll(a, LANES // 2, 1)


def join(a, a_half, b, b_half):
    first = swap(a) if a_half else a
    second = b if b_half else swap(b)
    return jnp.where(low_lanes(a.shape), first, second)


OWNERS = 32
PER = (3 * D + D + FF + FF) // OWNERS
FLAT = PER * D // LANES
PIECE = FLAT // 16
LEAD = 4 * D // LANES
EDGE = PER * D + 13 * D // OWNERS
PROJECT, PLAIN, PLAIN_EXPAND, EXPAND, EXPAND_PLAIN = range(5)


def plain_place(row, base, count):
    local = row - base
    half = int(local >= count // 2)
    return local - half * (count // 2), half


def dense_place(row):
    if row < 768:
        c = 8 + row // 384
        return (c, 0) + plain_place(row, 384 * (c - 8), 384)
    return (10, 0) + plain_place(row, 768, 256)


def shrink_place(row):
    if row < 256:
        return (21, 64) + plain_place(row, 0, 256)
    c = 22 + (row - 256) // 384
    return (c, 0) + plain_place(row, 256 + 384 * (c - 22), 384)


def expand_places():
    places = [(10, 128, 0, 32)]
    places += [(c, 0, 32 + 96 * (c - 11), 96) for c in range(11, 21)]
    places += [(21, 0, 992, 32)]
    return places


def shifted_rows(source, start, shift, at, rows):
    turn = (LANES - shift) % LANES
    first = pltpu.roll(source[pl.ds(start + at, rows), :], turn, 1)
    second = pltpu.roll(source[pl.ds(start + at + 1, rows), :], turn, 1)
    lane = lax.broadcasted_iota(jnp.int32, (rows, LANES), 1)
    return jnp.where(lane < LANES - shift, first, second)


SHIFT_ROWS = 3200
SEND_ROWS = PIECE + 32
OWN_ROW = 64


def weights_out_body(scalars, before, own, after, out, source, flat, tail):
    start, shift, kind, vector_row = scalars[0], scalars[1], scalars[2], scalars[3]
    count = own.shape[0]
    source[0 : OWN_ROW - 8] = jnp.zeros((OWN_ROW - 8, LANES), F32)
    source[OWN_ROW - 8 : OWN_ROW] = before[...]

    def copy(step, carry):
        at = pl.multiple_of(step * 88, 8)
        source[pl.ds(at + OWN_ROW, 88), :] = own[pl.ds(at, 88), :]
        return carry

    lax.fori_loop(0, count // 88, copy, 0)
    last = OWN_ROW + EDGE // LANES
    source[OWN_ROW + count :] = jnp.zeros((source.shape[0] - OWN_ROW - count, LANES), F32)
    edge = EDGE % LANES
    tail[...] = jnp.zeros(tail.shape, F32)
    tail[7:8] = source[last : last + 1]
    tail[8:40] = pltpu.roll(after[...], edge, 1)
    lane = lax.broadcasted_iota(jnp.int32, (40, LANES), 1)
    source[last : last + 40] = jnp.where(lane < edge, tail[7:47], tail[8:48])

    def align(step, carry):
        at = pl.multiple_of(step * 80, 8)
        flat[pl.ds(at, 80), :] = shifted_rows(source, start, shift, at, 80)
        return carry

    lax.fori_loop(0, SHIFT_ROWS // 80, align, 0)

    def rows(first, count, stride):
        return flat[pl.ds(first, count, stride), :]

    def plain(base, count, to):
        for m in range(8):
            tile = rows(base + m, count, 8)
            a, b = tile[: count // 2], tile[count // 2 :]
            out[2 * m, to : to + count // 2] = join(a, 0, b, 0).astype(BF16)
            out[2 * m + 1, to : to + count // 2] = join(a, 1, b, 1).astype(BF16)

    def expand(base, count, to):
        for r in range(16):
            out[r, to : to + count] = rows(base + 2 * r, count, 32).astype(BF16)
            out[r, to + count : to + 2 * count] = rows(base + 2 * r + 1, count, 32).astype(BF16)

    def project(base):
        for m in range(8):
            first, middle, last = (rows(base + 3 * m + j, 128, 24) for j in range(3))
            out[2 * m, 0:128] = first.astype(BF16)
            out[2 * m, 128:192] = join(middle[:64], 0, middle[64:], 0).astype(BF16)
            out[2 * m + 1, 0:128] = join(middle, 1, last, 0).astype(BF16)
            out[2 * m + 1, 128:192] = join(last[:64], 1, last[64:], 1).astype(BF16)

    @pl.when(kind == PROJECT)
    def _():
        project(LEAD)

    @pl.when(kind == PLAIN)
    def _():
        plain(LEAD, 384, 0)

    @pl.when(kind == PLAIN_EXPAND)
    def _():
        plain(LEAD, 256, 0)
        expand(LEAD + 2048 + 8, 32, 128)

    @pl.when(kind == EXPAND)
    def _():
        expand(LEAD, 96, 0)

    @pl.when(kind == EXPAND_PLAIN)
    def _():
        expand(LEAD, 32, 0)
        plain(LEAD + 1024 + 32, 256, 64)

    vectors = flat[pl.ds(vector_row, 32), :].astype(BF16)
    for r in range(16):
        out[r, PIECE : PIECE + 32] = vectors


def weights_in_body(scalars, got, qkv_w, expand_w, second, vectors, qkv_b, expand_b, project_rows, expand_rows):
    head = scalars[0]
    low = low_lanes((64, LANES))
    for c in range(8):
        qkv_w[128 * c : 128 * c + 128, 0:128] = got[c, 0:128]
        packed = got[c, 128:192].astype(F32)
        qkv_w[128 * c : 128 * c + 64, 128:256] = jnp.where(low, packed, 0.0).astype(BF16)
        qkv_w[128 * c + 64 : 128 * c + 128, 128:256] = jnp.where(low, swap(packed), 0.0).astype(BF16)
    for c, at, row, count in expand_places():
        expand_w[row : row + count, 0:128] = got[c, at : at + count]
        expand_w[row : row + count, 128:256] = got[c, at + count : at + 2 * count]

    for h in range(16):
        c, at, row, half = dense_place(64 * h)
        tile = got[c, at + row : at + row + 64].astype(F32)
        second[h, 0:32] = join(tile[:32], half, tile[32:], half).astype(BF16)
        for part in range(2):
            c, at, row, half = shrink_place(256 * h + 64 * part)
            tile = got[c, at + row : at + row + 64].astype(F32)
            c, at, row, other = shrink_place(256 * h + 128 + 64 * part)
            after = got[c, at + row : at + row + 64].astype(F32)
            second[h, 32 + 64 * part : 96 + 64 * part] = join(tile, half, after, other).astype(BF16)

    def vector(c, at, to):
        tile = got[c, PIECE + at : PIECE + at + 8].astype(F32)
        for j in range(8):
            vectors[to : to + 1, 128 * j : 128 * j + 128] = tile[j : j + 1]

    vectors[...] = jnp.zeros(vectors.shape, F32)
    for v in range(4):
        vector(0, 8 * v, v)
    vector(10, 0, 4)
    vector(31, 0, 5)
    project_rows[...] = got[8, PIECE + 8 : PIECE + 32].astype(F32)
    expand_rows[...] = got[21, PIECE : PIECE + 32].astype(F32)
    row = head // 2 * 3
    first, middle, last = (project_rows[pl.ds(row + j, 1), :] for j in range(3))
    odd = head % 2 == 1
    qkv_b[0:1, 0:128] = jnp.where(odd, join(middle, 1, last, 0), first)
    value = jnp.where(odd, swap(last), middle)
    qkv_b[0:1, 128:256] = jnp.where(low_lanes((1, LANES)), value, 0.0)
    expand_b[0:1, 0:128] = expand_rows[pl.ds(2 * head, 1), :]
    expand_b[0:1, 128:256] = expand_rows[pl.ds(2 * head + 1, 1), :]


def rows_in_body(got, dense_w, shrink_w):
    for m in range(8):
        even, odd = got[2 * m].astype(F32), got[2 * m + 1].astype(F32)
        columns = slice(128 * m, 128 * m + 128)
        for out, at, half in ((dense_w, 0, 32), (shrink_w, 32, 128)):
            a, b = even[at : at + half], odd[at : at + half]
            out[0:half, columns] = join(a, 0, b, 0).astype(BF16)
            out[half : 2 * half, columns] = join(a, 1, b, 1).astype(BF16)


def rows_out_body(dense_g, shrink_g, out):
    for m in range(8):
        columns = slice(128 * m, 128 * m + 128)
        for source, at, half in ((dense_g, 0, 32), (shrink_g, 32, 128)):
            a, b = source[0:half, columns], source[half : 2 * half, columns]
            out[2 * m, at : at + half] = join(a, 0, b, 0).astype(BF16)
            out[2 * m + 1, at : at + half] = join(a, 1, b, 1).astype(BF16)


BACK_ROWS = PIECE + 32


def grads_out_body(scalars, second, qkv_g, expand_g, vector_g, qkv_bg, expand_bg, out, project_rows, expand_rows):
    head = scalars[0]
    out[...] = jnp.zeros(out.shape, BF16)
    for c in range(8):
        out[c, 0:128] = qkv_g[128 * c : 128 * c + 128, 0:128].astype(BF16)
        a = qkv_g[128 * c : 128 * c + 64, 128:256]
        b = qkv_g[128 * c + 64 : 128 * c + 128, 128:256]
        out[c, 128:192] = join(a, 0, b, 0).astype(BF16)
    for c, at, row, count in expand_places():
        out[c, at : at + count] = expand_g[row : row + count, 0:128].astype(BF16)
        out[c, at + count : at + 2 * count] = expand_g[row : row + count, 128:256].astype(BF16)

    def dense_rows(row):
        packed = second[row // 64, 0:32].astype(F32)
        return jnp.concatenate([packed, swap(packed)], axis=0)

    def shrink_rows(row):
        h, part = row // 256, row % 256 // 64
        packed = second[h, 32 + part % 2 * 64 : 96 + part % 2 * 64].astype(F32)
        return swap(packed) if part >= 2 else packed

    def plain(c, to, base, count, take):
        for i in range(count // 128):
            a, b = take(base + 64 * i), take(base + count // 2 + 64 * i)
            out[c, to + 64 * i : to + 64 * i + 64] = join(a, 0, b, 0).astype(BF16)

    plain(8, 0, 0, 384, dense_rows)
    plain(9, 0, 384, 384, dense_rows)
    plain(10, 0, 768, 256, dense_rows)
    plain(21, 64, 0, 256, shrink_rows)
    for c in range(22, 32):
        plain(c, 0, 256 + 384 * (c - 22), 384, shrink_rows)

    def rows_of(row):
        return jnp.concatenate([vector_g[row : row + 1, 128 * j : 128 * j + 128] for j in range(8)], axis=0)

    gains = jnp.concatenate([rows_of(v) for v in range(4)], axis=0)
    out[0, PIECE : PIECE + 32] = gains.astype(BF16)
    bias = jnp.concatenate([rows_of(4), jnp.zeros((8, LANES), F32)], axis=0).astype(BF16)
    out[10, PIECE : PIECE + 16] = bias
    out[31, PIECE : PIECE + 16] = bias
    project_rows[...] = jnp.zeros(project_rows.shape, F32)
    expand_rows[...] = jnp.zeros(expand_rows.shape, F32)
    pair, value = qkv_bg[0:1, 0:128], qkv_bg[0:1, 128:256]
    low = low_lanes((1, LANES))
    row = 8 + head // 2 * 3
    odd = head % 2 == 1
    project_rows[pl.ds(row, 1), :] = jnp.where(odd, 0.0, pair)
    project_rows[pl.ds(row + 1, 1), :] = jnp.where(
        odd, jnp.where(low, 0.0, swap(pair)), jnp.where(low, value, 0.0)
    )
    project_rows[pl.ds(row + 2, 1), :] = jnp.where(odd, join(pair, 1, value, 0), 0.0)
    out[8, PIECE : PIECE + 32] = project_rows[...].astype(BF16)
    expand_rows[pl.ds(2 * head, 1), :] = expand_bg[0:1, 0:128]
    expand_rows[pl.ds(2 * head + 1, 1), :] = expand_bg[0:1, 128:256]
    out[21, PIECE : PIECE + 32] = expand_rows[...].astype(BF16)


TAKE_ROWS = 3120


def grads_in_body(scalars, got, out, flat):
    start, shift, kind, vector_row = scalars[0], scalars[1], scalars[2], scalars[3]
    lead = LEAD + 8

    def clear(step, carry):
        flat[pl.ds(pl.multiple_of(step * 80, 8), 80), :] = jnp.zeros((80, LANES), F32)
        return carry

    lax.fori_loop(0, SHIFT_ROWS // 80, clear, 0)

    def add_vectors(source, total):
        return total + got[source, PIECE : PIECE + 32].astype(F32)

    flat[pl.ds(vector_row + 8, 32), :] = lax.fori_loop(0, OWNERS, add_vectors, jnp.zeros((32, LANES), F32))

    def taken(r, at, count):
        return got[r, at : at + count].astype(F32) + got[16 + r, at : at + count].astype(F32)

    def plain(base, count, at):
        half = count // 2
        for m in range(8):
            a, b = taken(2 * m, at, half), taken(2 * m + 1, at, half)
            flat[pl.ds(base + m, half, 8), :] = join(a, 0, b, 0)
            flat[pl.ds(base + m + 8 * half, half, 8), :] = join(a, 1, b, 1)

    def expand(base, count, at):
        for r in range(16):
            flat[pl.ds(base + 2 * r, count, 32), :] = taken(r, at, count)
            flat[pl.ds(base + 2 * r + 1, count, 32), :] = taken(r, at + count, count)

    def project(base):
        for m in range(8):
            pair, values = taken(2 * m, 0, 128), taken(2 * m, 128, 64)
            odd_pair, odd_values = taken(2 * m + 1, 0, 128), taken(2 * m + 1, 128, 64)
            values = jnp.concatenate([values, swap(values)], axis=0)
            odd_values = jnp.concatenate([odd_values, swap(odd_values)], axis=0)
            flat[pl.ds(base + 3 * m, 128, 24), :] = pair
            flat[pl.ds(base + 3 * m + 1, 128, 24), :] = join(values, 0, odd_pair, 0)
            flat[pl.ds(base + 3 * m + 2, 128, 24), :] = join(odd_pair, 1, odd_values, 0)

    @pl.when(kind == PROJECT)
    def _():
        project(lead)

    @pl.when(kind == PLAIN)
    def _():
        plain(lead, 384, 0)

    @pl.when(kind == PLAIN_EXPAND)
    def _():
        plain(lead, 256, 0)
        expand(lead + 2048 + 8, 32, 128)

    @pl.when(kind == EXPAND)
    def _():
        expand(lead, 96, 0)

    @pl.when(kind == EXPAND_PLAIN)
    def _():
        expand(lead, 32, 0)
        plain(lead + 1024 + 32, 256, 64)

    def align(step, carry):
        at = pl.multiple_of(step * 80, 8)
        out[pl.ds(at, 80), :] = shifted_rows(flat, start, shift, at, 80)
        return carry

    lax.fori_loop(0, TAKE_ROWS // 80, align, 0)


def token_rows(ref):
    return jnp.concatenate([ref[0, 0, 0], ref[1, 0, 0], ref[0, 0, 1], ref[1, 0, 1]], axis=0)


def put_rows(kept, sent, rows, core):
    step = rows.shape[0] // 4
    for x in range(2):
        first, second = (rows[step * i : step * i + step].astype(kept.dtype) for i in (2 * x, 2 * x + 1))
        kept[0, x] = jnp.where(core == 0, first, second)
        sent[0, x] = jnp.where(core == 0, second, first)


def relative_place(i, here):
    y = (i & 1) ^ here[2]
    z = (i >> 1) ^ here[3]
    return y * 4 + (z & 1) * 2 + (z >> 1)


def normalized(values):
    centered = values - jnp.mean(values, axis=-1, keepdims=True)
    variance = jnp.mean(centered * centered, axis=-1, keepdims=True)
    return centered * lax.rsqrt(variance + EPSILON)


def turned(pair, cos, sin):
    lane = lax.broadcasted_iota(jnp.int32, pair.shape, 1) % HD
    half = ROT // 2
    other = jnp.where(
        lane < half, -pltpu.roll(pair, LANES - half, 1), jnp.where(lane < ROT, pltpu.roll(pair, half, 1), 0.0)
    )
    return pair * cos + other * sin


def mixed_body(tokens, vectors, qkv_w, qkv_b, cos, sin, one, two, query, key, value):
    unit = normalized(token_rows(tokens).astype(F32))
    first = (unit * vectors[0:1] + vectors[1:2]).astype(BF16)
    one[...] = first
    two[...] = (unit * vectors[2:3] + vectors[3:4]).astype(BF16)
    mixed = mm(first, qkv_w[...]) + qkv_b[...]
    pair = turned(mixed[:, :LANES], cos[...], sin[...])
    query[...] = pair[:, :HD].astype(BF16) * HD ** (-0.5)
    key[...] = pair[:, HD:].astype(BF16)
    value[...] = mixed[:, LANES : LANES + HD].astype(BF16)


def masked_scores(key, query_t, at, first_query, length):
    scores = mm(key, query_t)
    keys = at * BLOCK + lax.broadcasted_iota(jnp.int32, scores.shape, 0)
    queries = first_query + lax.broadcasted_iota(jnp.int32, scores.shape, 1)
    return jnp.where((keys <= queries) & (keys < length), scores, NEGATIVE)


def folded(values, op):
    parts = [values[8 * i : 8 * i + 8] for i in range(values.shape[0] // 8)]
    while len(parts) > 1:
        parts = [op(a, b) for a, b in zip(parts[::2], parts[1::2])]
    return parts[0]


def attend_body(lengths, query, key, value, low_out, full_out, log_out, scores, value_t):
    at = pl.program_id(0)
    length = lengths[0]

    @pl.when(at == 0)
    def _():
        value_t[...] = value[...].astype(F32).T.astype(BF16)

    query_t = query[...].astype(F32).T.astype(BF16)
    clear = jnp.minimum(at, length // BLOCK)
    stop = jnp.minimum(at, (length - 1) // BLOCK) + 1

    def rows(j):
        return pl.ds(pl.multiple_of(j * BLOCK, BLOCK), BLOCK)

    def score(j, top, masked):
        if masked:
            tile = masked_scores(key[rows(j), :], query_t, j, at * BLOCK, length)
        else:
            tile = mm(key[rows(j), :], query_t)
        scores[rows(j), :] = tile
        return jnp.maximum(top, folded(tile, jnp.maximum))

    top = jnp.full((8, BLOCK), NEGATIVE, F32)
    top = lax.fori_loop(0, clear, lambda j, t: score(j, t, False), top)
    top = lax.fori_loop(clear, stop, lambda j, t: score(j, t, True), top)
    top = jnp.max(top, axis=0, keepdims=True)

    def power(j, total):
        tile = jnp.exp(scores[rows(j), :] - top)
        scores[rows(j), :] = tile
        return total + folded(tile, jnp.add)

    total = lax.fori_loop(0, stop, power, jnp.zeros((8, BLOCK), F32))
    total = jnp.sum(total, axis=0, keepdims=True)
    inverse = 1.0 / total

    def weigh(j, out):
        low = (scores[rows(j), :] * inverse).astype(BF16)
        return out + mm(value_t[:, rows(j)], low)

    out = lax.fori_loop(0, stop, weigh, jnp.zeros((HD, BLOCK), F32))
    full_out[...] = out
    low_out[...] = out.T.astype(BF16)
    log_out[...] = top + jnp.log(total)


def attend_back_body(
    lengths, query, key, value, grad, full_out, log_in, query_g, key_g, value_g, key_t, key_sum, value_sum
):
    at = pl.program_id(0)
    length = lengths[0]

    @pl.when(at == 0)
    def _():
        key_t[...] = key[...].astype(F32).T.astype(BF16)
        key_sum[...] = jnp.zeros(key_sum.shape, F32)
        value_sum[...] = jnp.zeros(value_sum.shape, F32)

    query_rows, grad_rows = query[...], grad[...]
    query_t = query_rows.astype(F32).T.astype(BF16)
    grad_full_t = grad_rows.astype(F32).T
    grad_t = grad_full_t.astype(BF16)
    delta = jnp.sum(grad_full_t * full_out[...], axis=0, keepdims=True)
    log_total = log_in[...]
    clear = jnp.minimum(at, length // BLOCK)
    stop = jnp.minimum(at, (length - 1) // BLOCK) + 1
    clear, stop = (jnp.where(at * BLOCK < length, n, 0) for n in (clear, stop))

    def step(j, query_sum, masked):
        rows = pl.ds(pl.multiple_of(j * BLOCK, BLOCK), BLOCK)
        if masked:
            tile = masked_scores(key[rows, :], query_t, j, at * BLOCK, length)
        else:
            tile = mm(key[rows, :], query_t)
        probs = jnp.exp(tile - log_total)
        value_sum[rows, :] += mm(probs.astype(BF16), grad_rows)
        score_g = (probs * (mm(value[rows, :], grad_t) - delta)).astype(BF16)
        key_sum[rows, :] += mm(score_g, query_rows)
        return query_sum + mm(key_t[:, rows], score_g)

    query_sum = jnp.zeros((HD, BLOCK), F32)
    query_sum = lax.fori_loop(0, clear, lambda j, s: step(j, s, False), query_sum)
    query_sum = lax.fori_loop(clear, stop, lambda j, s: step(j, s, True), query_sum)
    query_g[...] = (query_sum * HD ** (-0.5)).T.astype(BF16)

    @pl.when(at == pl.num_programs(0) - 1)
    def _():
        key_g[...] = key_sum[...].astype(BF16)
        value_g[...] = value_sum[...].astype(BF16)


def feed_body(
    here, two, attended, cotangent, expand_w, expand_b, shrink_w, dense_w,
    kept, sent, attended_g, hidden_g, shrink_g, dense_g, expand_g, expand_bg, bias_g,
):
    at = pl.program_id(0)

    @pl.when(at == 0)
    def _():
        for total in (shrink_g, dense_g, expand_g, expand_bg, bias_g):
            total[...] = jnp.zeros(total.shape, F32)

    normed, mixed = two[...], attended[...]
    hidden = mm(normed, expand_w[...]) + expand_b[...]
    error = lax.erf(hidden * math.sqrt(0.5))
    cumulative = 0.5 * (1.0 + error)
    active = (hidden * cumulative).astype(BF16)
    put_rows(kept, sent, mm(mixed, dense_w[...]) + mm(active, shrink_w[...]), here[1])
    token = at * BLOCK + lax.broadcasted_iota(jnp.int32, (BLOCK, D), 0)
    seed = jnp.where(token < here[0], token_rows(cotangent).astype(F32), 0.0)
    bias_g[...] += jnp.sum(seed, axis=0, keepdims=True)
    seed = seed.astype(BF16)
    attended_g[...] = mm(seed, dense_w[...], ((1,), (1,))).astype(BF16)
    slope = cumulative + hidden * jnp.exp(-0.5 * hidden * hidden) * (1.0 / math.sqrt(2.0 * math.pi))
    back = (mm(seed, shrink_w[...], ((1,), (1,))) * slope).astype(BF16)
    hidden_g[...] = back
    expand_bg[...] += jnp.sum(back.astype(F32), axis=0, keepdims=True)
    shrink_g[...] += mm(active, seed, ((0,), (0,)))
    dense_g[...] += mm(mixed, seed, ((0,), (0,)))
    expand_g[...] += mm(normed, back, ((0,), (0,)))


def mixed_back_body(
    here, tokens, one, query_g, key_g, value_g, hidden_g, vectors, qkv_w, expand_w, cos, sin,
    kept, sent, qkv_g, qkv_bg, vector_g,
):
    at = pl.program_id(0)

    @pl.when(at == 0)
    def _():
        for total in (qkv_g, qkv_bg, vector_g):
            total[...] = jnp.zeros(total.shape, F32)

    pair = jnp.concatenate([query_g[...].astype(F32), key_g[...].astype(F32)], axis=1)
    pair = turned(pair, cos[...], -sin[...])
    values = value_g[...].astype(F32)
    mixed_g = jnp.concatenate([pair, values, jnp.zeros_like(values)], axis=1)
    mixed_low = mixed_g.astype(BF16)
    qkv_bg[...] += jnp.sum(mixed_low.astype(F32), axis=0, keepdims=True)
    qkv_g[...] += mm(one[...], mixed_low, ((0,), (0,)))
    one_g = mm(mixed_low, qkv_w[...], ((1,), (1,)))
    two_g = mm(hidden_g[...], expand_w[...], ((1,), (1,)))
    unit = normalized(token_rows(tokens).astype(F32))
    vector_g[0:1] += jnp.sum(one_g * unit, axis=0, keepdims=True)
    vector_g[1:2] += jnp.sum(one_g, axis=0, keepdims=True)
    vector_g[2:3] += jnp.sum(two_g * unit, axis=0, keepdims=True)
    vector_g[3:4] += jnp.sum(two_g, axis=0, keepdims=True)
    put_rows(kept, sent, one_g * vectors[0:1] + two_g * vectors[2:3], here[1])


def split_mesh(mesh):
    groups, members = mesh.shape["blk"], mesh.shape["uly"]
    return Mesh(mesh.devices.reshape(groups // 2, 2, members // 2, 2), ALL)


def across_x(block):
    return lax.ppermute(block, "x", [(0, 1), (1, 0)])


def by_head(residual, cotangent, lengths, positions, masters, momenta, averages):
    slots, span, width = residual.shape
    x = lax.axis_index("x")
    head = lax.axis_index("core") * 8 + lax.axis_index("z") * 2 + lax.axis_index("y")
    owner = x * 16 + head
    groups = lax.axis_size("z") * lax.axis_size("y")
    count = groups * 4 * span
    chunk = masters.shape[0]
    length = lax.dynamic_slice_in_dim(lengths, x, 1)

    def paired(mine, theirs):
        return jnp.where(x == 0, jnp.stack([mine, theirs]), jnp.stack([theirs, mine]))

    def at_x(rows, index):
        return lax.dynamic_index_in_dim(rows, index, 0, keepdims=False)

    rows = jnp.stack([residual, cotangent], axis=1)
    rows = paired(at_x(rows, x), across_x(at_x(rows, 1 - x)))
    tokens_shape = (2, groups, 2, span, width)
    slot_tokens = lax.all_gather(rows[:, 0], RING, axis=0).reshape(tokens_shape)

    place = jnp.broadcast_to(positions.reshape(1, slots * span), (OWNERS, slots * span))
    place = lax.all_to_all(place, ALL, 0, 0, tiled=True)
    place = place.reshape(2, 2, groups, slots, span)
    place = lax.dynamic_index_in_dim(place, x, 3, keepdims=False).transpose(2, 0, 1, 3).reshape(count)
    half_dims = ROT // 2
    inverse = ROTARY_BASE ** (-(jnp.arange(half_dims, dtype=F32) * 2.0 / ROT))
    angles = place.astype(F32)[:, None] * inverse
    cos, sin = jnp.cos(angles), jnp.sin(angles)
    flat_part = jnp.ones((count, HD - ROT), F32)
    cos = jnp.concatenate([cos, cos, flat_part] * 2, axis=1)
    sin = jnp.concatenate([sin, sin, 0.0 * flat_part] * 2, axis=1)

    onward = [(i, i + 1) for i in range(OWNERS - 1)]
    backward = [(i + 1, i) for i in range(OWNERS - 1)]
    before = lax.ppermute(masters[chunk - D :], ALL, onward)
    after = lax.ppermute(masters[: 4 * D], ALL, backward)
    own_rows = -(-chunk // D) * 8
    own = jnp.pad(masters, (0, own_rows * LANES - chunk)).reshape(own_rows, LANES)
    before, after = before.reshape(8, LANES), after.reshape(32, LANES)
    skipped = jnp.where(owner < 8, 4, jnp.where(owner < 11, 7, jnp.where(owner < 22, 8, 12)))
    kind = jnp.where(
        owner < 8,
        PROJECT,
        jnp.where(
            owner == 10,
            PLAIN_EXPAND,
            jnp.where(owner == 21, EXPAND_PLAIN, jnp.where((owner > 10) & (owner < 21), EXPAND, PLAIN)),
        ),
    )
    vector_row = jnp.where(owner == 10, 2080, jnp.where(owner == 21, 1056, jnp.where(owner == 31, 3104, 0)))
    ahead = skipped * D - (chunk - PER * D) * owner
    begin = ahead + 4 * D
    scalars = jnp.stack([begin // LANES, begin % LANES, kind, vector_row]).astype(jnp.int32)
    sent = call(
        weights_out_body, (1,),
        [whole(before.shape), whole(own.shape), whole(after.shape)],
        whole((16, SEND_ROWS, LANES)),
        shaped((16, SEND_ROWS, LANES), BF16),
        [pltpu.VMEM((3280, LANES), F32), pltpu.VMEM((SHIFT_ROWS, LANES), F32), pltpu.VMEM((48, LANES), F32)],
        1,
    )(scalars, before, own, after)
    sent = jnp.concatenate([sent, sent])
    got = lax.all_to_all(sent, ALL, 0, 0, tiled=True)
    later, got = lax.optimization_barrier((rows[:, 1], got))
    slot_cotangent = lax.all_gather(later, RING, axis=0).reshape(tokens_shape)
    head_scalar = head.astype(jnp.int32).reshape(1)
    qkv_w, expand_w, second, vectors, qkv_b, expand_b = call(
        weights_in_body, (1,),
        [whole(got.shape)],
        [whole((D, 256)), whole((D, 256)), whole((16, 160, LANES)), whole((8, D)), whole((1, 256)), whole((1, 256))],
        [shaped((D, 256), BF16), shaped((D, 256), BF16), shaped((16, 160, LANES), BF16), shaped((8, D), F32),
         shaped((1, 256), F32), shaped((1, 256), F32)],
        [pltpu.VMEM((24, LANES), F32), pltpu.VMEM((32, LANES), F32)], 1,
    )(head_scalar, got)
    second = lax.all_to_all(second, RING, 0, 0, tiled=True)
    steps = (count // BLOCK,)
    token_spec = pl.BlockSpec((2, 1, 2, span, width), lambda i, *_: (0, i, 0, 0, 0))
    part_spec = pl.BlockSpec((1, 2, span, width), lambda i, here: (relative_place(i, here), 0, 0, 0))
    part_shape = shaped((groups, 2, span, width), BF16)
    y, z, core = lax.axis_index("y"), lax.axis_index("z"), lax.axis_index("core")
    here = jnp.stack([length[0], core, y, z]).astype(jnp.int32)

    def summed(kept, sent):
        groups_left = kept.shape[0]
        for axis, route in (
            ("core", [(0, 1), (1, 0)]),
            ("y", [(0, 1), (1, 0)]),
            ("z", [(0, 1), (1, 0), (2, 3), (3, 2)]),
            ("z", [(0, 2), (2, 0), (1, 3), (3, 1)]),
        ):
            came = lax.ppermute(sent, axis, route)
            if groups_left == 1:
                return kept[0].astype(F32) + came[0].astype(F32)
            groups_left //= 2
            kept, sent = (
                (kept[half].astype(F32) + came[half].astype(F32)).astype(BF16)
                for half in (slice(0, groups_left), slice(groups_left, None))
            )

    def rows_spec(columns):
        return pl.BlockSpec((BLOCK, columns), lambda i, *_: (i, 0))

    def columns_spec(rows):
        return pl.BlockSpec((rows, BLOCK), lambda i, *_: (0, i))

    narrow = shaped((count, HD), BF16)
    one, two, query, key, value = call(
        mixed_body, steps,
        [token_spec, whole((8, D)), whole((D, 256)), whole((1, 256)), rows_spec(LANES), rows_spec(LANES)],
        [rows_spec(D), rows_spec(D), rows_spec(HD), rows_spec(HD), rows_spec(HD)],
        [shaped((count, D), BF16), shaped((count, D), BF16), narrow, narrow, narrow],
    )(slot_tokens, vectors, qkv_w, qkv_b, cos, sin)
    attended, attended_full, log_total = call(
        attend_body, steps,
        [rows_spec(HD), whole((count, HD)), whole((count, HD))],
        [rows_spec(HD), columns_spec(HD), columns_spec(1)],
        [narrow, shaped((HD, count), F32), shaped((1, count), F32)],
        [pltpu.VMEM((count, BLOCK), F32), pltpu.VMEM((HD, count), BF16)], 1,
    )(length, query, key, value)
    second, attended = lax.optimization_barrier((second, attended))
    dense_w, shrink_w = call(
        rows_in_body, (1,), [whole(second.shape)], [whole((HD, D)), whole((256, D))],
        [shaped((HD, D), BF16), shaped((256, D), BF16)],
    )(second)

    kept, sent, attended_g, hidden_g, shrink_g, dense_g, expand_g, expand_bg, bias_g = call(
        feed_body, steps,
        [rows_spec(D), rows_spec(HD), token_spec, whole((D, 256)), whole((1, 256)), whole((256, D)), whole((HD, D))],
        [part_spec, part_spec, rows_spec(HD), rows_spec(256), whole((256, D)), whole((HD, D)), whole((D, 256)),
         whole((1, 256)), whole((1, D))],
        [part_shape, part_shape, narrow, shaped((count, 256), BF16), shaped((256, D), F32), shaped((HD, D), F32),
         shaped((D, 256), F32), shaped((1, 256), F32), shaped((1, D), F32)], (), 1,
    )(here, two, attended, slot_cotangent, expand_w, expand_b, shrink_w, dense_w)
    second_g = call(
        rows_out_body, (1,), [whole((HD, D)), whole((256, D))], whole((16, 160, LANES)),
        shaped((16, 160, LANES), BF16),
    )(dense_g, shrink_g)
    attended_g, second_g = lax.optimization_barrier((attended_g, second_g))
    second_g = lax.all_to_all(second_g, RING, 0, 0, tiled=True)
    out_rows = summed(kept, sent)
    query_g, key_g, value_g = call(
        attend_back_body, steps,
        [rows_spec(HD), whole((count, HD)), whole((count, HD)), rows_spec(HD), columns_spec(HD), columns_spec(1)],
        [rows_spec(HD), whole((count, HD)), whole((count, HD))],
        [narrow, narrow, narrow],
        [pltpu.VMEM((HD, count), BF16), pltpu.VMEM((count, HD), F32), pltpu.VMEM((count, HD), F32)],
        1,
    )(length, query, key, value, attended_g, attended_full, log_total)
    kept, sent, qkv_g, qkv_bg, vector_g = call(
        mixed_back_body, steps,
        [token_spec, rows_spec(D), rows_spec(HD), rows_spec(HD), rows_spec(HD),
         rows_spec(256), whole((8, D)), whole((D, 256)), whole((D, 256)), rows_spec(LANES), rows_spec(LANES)],
        [part_spec, part_spec, whole((D, 256)), whole((1, 256)), whole((8, D))],
        [part_shape, part_shape, shaped((D, 256), F32), shaped((1, 256), F32), shaped((8, D), F32)], (), 1,
    )(here, slot_tokens, one, query_g, key_g, value_g, hidden_g, vectors, qkv_w, expand_w, cos, sin)
    in_rows = summed(kept, sent)
    rows = jnp.stack([out_rows, in_rows], axis=1).astype(BF16)
    rows = paired(at_x(rows, x), across_x(at_x(rows, 1 - x))).astype(F32)
    out_rows, in_rows = rows[:, 0], rows[:, 1]

    bias_g = jnp.where(head == 0, bias_g, 0.0)
    vector_g = jnp.concatenate([vector_g[:4], bias_g, jnp.zeros((3, D), F32)])
    sent_g = call(
        grads_out_body, (1,),
        [whole((16, 160, LANES)), whole((D, 256)), whole((D, 256)), whole((8, D)), whole((1, 256)), whole((1, 256))],
        whole((OWNERS, BACK_ROWS, LANES)),
        shaped((OWNERS, BACK_ROWS, LANES), BF16),
        [pltpu.VMEM((32, LANES), F32), pltpu.VMEM((32, LANES), F32)], 1,
    )(head_scalar, second_g, qkv_g, expand_g, vector_g, qkv_bg, expand_bg)
    got_g = lax.all_to_all(sent_g, ALL, 0, 0, tiled=True)
    begin_g = (chunk - PER * D) * owner - skipped * D + 4 * D
    scalars_g = jnp.stack([begin_g // LANES, begin_g % LANES, kind, vector_row]).astype(jnp.int32)
    taken = call(
        grads_in_body, (1,), [whole(got_g.shape)], whole((TAKE_ROWS, LANES)), shaped((TAKE_ROWS, LANES), F32),
        [pltpu.VMEM((SHIFT_ROWS, LANES), F32)], 1,
    )(scalars_g, got_g).reshape(-1)
    from_before = lax.ppermute(taken[D + chunk : 5 * D + chunk], ALL, onward)
    from_after = lax.ppermute(taken[:D], ALL, backward)
    gradients = taken[D : D + chunk]
    gradients = gradients.at[: 4 * D].add(from_before).at[chunk - D :].add(from_after)

    values = residual.astype(F32)
    outputs = (values + out_rows + (vectors[4] + vectors[5])).astype(BF16)
    first_token = ((lax.axis_index("z") * 2 + lax.axis_index("y")) * 4 + x * 2 + lax.axis_index("core")) * span
    token = first_token + jnp.arange(span, dtype=jnp.int32)
    live = token[None, :] < lengths[:, None]
    seed = jnp.where(live[:, :, None], cotangent.astype(F32), 0.0)
    centered = values - jnp.mean(values, axis=-1, keepdims=True)
    scale = lax.rsqrt(jnp.mean(centered * centered, axis=-1, keepdims=True) + EPSILON)
    unit = centered * scale
    back = in_rows - jnp.mean(in_rows, axis=-1, keepdims=True)
    back = scale * (back - unit * jnp.mean(in_rows * unit, axis=-1, keepdims=True))
    input_grad = (seed + back).astype(BF16)

    velocity = MOMENTUM * momenta + gradients
    step_rate = LEARN_RATE / math.sqrt(slots * count)
    updated = masters - step_rate * (gradients + MOMENTUM * velocity)
    averaged = AVERAGE_DECAY * averages + (1.0 - AVERAGE_DECAY) * updated
    return (outputs, input_grad, gradients, updated, velocity, averaged)


def solution(mesh):
    fits = mesh.size == OWNERS and mesh.shape["blk"] == 4

    def step(*args):
        slots, tokens = args[0].shape[:2]
        if fits and slots * H == OWNERS and tokens == 64 * OWNERS:
            tokens_in, flat, used, body = P(None, ("z", "y", "x", "core"), None), P(ALL), split_mesh(mesh), by_head
            places = P(None, ("z", "y", "x", "core"))
        else:
            tokens_in, flat, used, body = P(None, ("uly", "blk"), None), P(("blk", "uly")), mesh, local
            places = P(None, ("uly", "blk"))
        return jax.shard_map(
            body,
            mesh=used,
            in_specs=(tokens_in, tokens_in, P(), places, flat, flat, flat),
            out_specs=(tokens_in, tokens_in, flat, flat, flat, flat),
            check_vma=False,
        )(*args)

    return step
```

```python
from functools import partial
import math

import jax
import jax.numpy as jnp
from jax import lax
from jax.experimental import pallas as pl
from jax.experimental.pallas import tpu as pltpu
from jax.sharding import Mesh, PartitionSpec as P

D = 1024
H = 16
HD = 64
ROT = 16
FF = 4096


EPSILON = 1e-05
NEGATIVE = -1e30
MOMENTUM = 0.5
LEARN_RATE = 0.05
AVERAGE_DECAY = 0.5
ROTARY_BASE = 10000.0


def passed_along(block, axis, distance):
    devices = range(lax.axis_size(axis))
    route = [((i - distance) % len(devices), i) for i in devices]
    return lax.ppermute(block, axis, route)


def unpack(flat_vector):
    layouts = [
        (D,),
        (D,),
        (D,),
        (D,),
        (D, 3 * D),
        (3 * D,),
        (D, D),
        (D,),
        (D, FF),
        (FF,),
        (FF, D),
        (D,),
    ]
    pieces = []
    cursor = 0
    for layout in layouts:
        number = math.prod(layout)
        pieces.append(flat_vector[cursor : cursor + number].reshape(layout))
        cursor += number
    return pieces


def layer_norm(values, gain, shift):
    centered = values - jnp.mean(values, axis=-1, keepdims=True)
    variance = jnp.mean(centered * centered, axis=-1, keepdims=True)
    return centered * lax.rsqrt(variance + EPSILON) * gain + shift


def rotary_tables(positions):
    half_dims = ROT // 2
    inverse = ROTARY_BASE ** (-(jnp.arange(half_dims, dtype=jnp.float32) * 2.0 / ROT))
    angles = positions.astype(jnp.float32)[..., None] * inverse
    return (jnp.cos(angles), jnp.sin(angles))


def rotate(values, cos_table, sin_table):
    half_dims = ROT // 2
    first_half = values[..., :half_dims]
    second_half = values[..., half_dims:ROT]
    return jnp.concatenate(
        [
            first_half * cos_table - second_half * sin_table,
            second_half * cos_table + first_half * sin_table,
            values[..., ROT:],
        ],
        axis=-1,
    )


def group_tokens(source, group_count, uly_count, span_rows):
    spans = jnp.arange(uly_count, dtype=jnp.int32)[:, None] * group_count + source
    return (spans * span_rows + jnp.arange(span_rows, dtype=jnp.int32)[None, :]).reshape(-1)


def block_scores(queries, keys_rows, row_tokens, col_tokens, length):
    scores = jnp.einsum(
        "qhd,khd->hqk", queries, keys_rows, preferred_element_type=jnp.float32
    ) * HD ** (-0.5)
    allowed = (col_tokens[None, :] <= row_tokens[:, None]) & (col_tokens[None, :] < length)
    return jnp.where(allowed[None], scores, NEGATIVE)


def is_live(row_tokens, col_tokens, length):
    return (col_tokens[0] <= row_tokens[-1]) & (col_tokens[0] < length)


def fold_stats(row_max, row_total, queries, key_value, lengths, row_tokens, col_tokens):

    def per_slot(inputs):
        slot_max, slot_total, slot_queries, slot_pairs, length = inputs

        def compute(current):
            prev_max, prev_total = current
            scores = block_scores(slot_queries, slot_pairs[:, :, 0], row_tokens, col_tokens, length)
            next_max = jnp.maximum(prev_max, jnp.max(scores, axis=-1))
            next_total = prev_total * jnp.exp(prev_max - next_max) + jnp.sum(
                jnp.exp(scores - next_max[..., None]), axis=-1
            )
            return (next_max, next_total)

        return lax.cond(
            is_live(row_tokens, col_tokens, length),
            compute,
            lambda current: current,
            (slot_max, slot_total),
        )

    return lax.map(per_slot, (row_max, row_total, queries, key_value, lengths))


def fold_values(attended, queries, key_value, log_total, lengths, row_tokens, col_tokens):

    def per_slot(inputs):
        slot_out, slot_queries, slot_pairs, slot_log, length = inputs

        def compute(current):
            scores = block_scores(slot_queries, slot_pairs[:, :, 0], row_tokens, col_tokens, length)
            prob_low = jnp.exp(scores - slot_log[..., None]).astype(jnp.bfloat16)
            return current + jnp.einsum(
                "hqk,khd->qhd", prob_low, slot_pairs[:, :, 1], preferred_element_type=jnp.float32
            )

        return lax.cond(
            is_live(row_tokens, col_tokens, length), compute, lambda current: current, slot_out
        )

    return lax.map(per_slot, (attended, queries, key_value, log_total, lengths))


def fold_grads(
    query_grad,
    pair_grad,
    queries,
    key_value,
    grad_out,
    log_total,
    row_delta,
    lengths,
    row_tokens,
    col_tokens,
):

    def per_slot(inputs):
        (
            slot_qgrad,
            slot_pgrad,
            slot_queries,
            slot_pairs,
            slot_gout,
            slot_log,
            slot_delta,
            length,
        ) = inputs

        def compute(current):
            cur_qgrad, cur_pgrad = current
            scores = block_scores(slot_queries, slot_pairs[:, :, 0], row_tokens, col_tokens, length)
            attend_prob = jnp.exp(scores - slot_log[..., None])
            prob_low = attend_prob.astype(jnp.bfloat16)
            prob_grad = jnp.einsum(
                "qhd,khd->hqk", slot_gout, slot_pairs[:, :, 1], preferred_element_type=jnp.float32
            )
            score_grad = (attend_prob * (prob_grad - slot_delta[..., None])).astype(jnp.bfloat16)
            cur_qgrad = cur_qgrad + jnp.einsum(
                "hqk,khd->qhd", score_grad, slot_pairs[:, :, 0], preferred_element_type=jnp.float32
            ) * HD ** (-0.5)
            key_grad = jnp.einsum(
                "hqk,qhd->khd", score_grad, slot_queries, preferred_element_type=jnp.float32
            ) * HD ** (-0.5)
            value_grad = jnp.einsum(
                "hqk,qhd->khd", prob_low, slot_gout, preferred_element_type=jnp.float32
            )
            return (cur_qgrad, cur_pgrad + jnp.stack([key_grad, value_grad], axis=2))

        return lax.cond(
            is_live(row_tokens, col_tokens, length),
            compute,
            lambda current: current,
            (slot_qgrad, slot_pgrad),
        )

    return lax.map(
        per_slot,
        (query_grad, pair_grad, queries, key_value, grad_out, log_total, row_delta, lengths),
    )


def local(residual, cotangent, lengths, positions, masters, momenta, averages):
    slot_count, span_rows, model_width = residual.shape
    group_count = lax.axis_size("blk")
    uly_count = lax.axis_size("uly")
    group_index = lax.axis_index("blk")
    uly_index = lax.axis_index("uly")
    block_rows = uly_count * span_rows
    full_rows = group_count * block_rows
    local_heads = H // uly_count
    token_rows = slot_count * span_rows
    row_tokens = group_tokens(group_index, group_count, uly_count, span_rows)

    def tokens_of(source):
        return group_tokens(source, group_count, uly_count, span_rows)

    gathered = lax.all_gather(masters.astype(jnp.bfloat16), ("blk", "uly"), axis=0, tiled=True)
    (
        gain_one,
        shift_one,
        gain_two,
        shift_two,
        project_w,
        project_b,
        dense_w,
        dense_b,
        expand_w,
        expand_b,
        shrink_w,
        shrink_b,
    ) = unpack(gathered)
    values = residual.astype(jnp.float32).reshape(token_rows, model_width)
    normed_one, norm_back_one = jax.vjp(
        layer_norm, values, gain_one.astype(jnp.float32), shift_one.astype(jnp.float32)
    )
    normed_two, norm_back_two = jax.vjp(
        layer_norm, values, gain_two.astype(jnp.float32), shift_two.astype(jnp.float32)
    )
    normed_one = normed_one.astype(jnp.bfloat16)
    normed_two = normed_two.astype(jnp.bfloat16)
    mixed_rows = jnp.dot(
        normed_one, project_w, preferred_element_type=jnp.float32
    ) + project_b.astype(jnp.float32)
    mixed_rows = mixed_rows.reshape(slot_count, span_rows, H, 3, HD)
    cos_table, sin_table = rotary_tables(positions)
    cos_table = cos_table[:, :, None, None, :]
    sin_table = sin_table[:, :, None, None, :]
    turned, turn_back = jax.vjp(
        lambda pair_rows: rotate(pair_rows, cos_table, sin_table), mixed_rows[:, :, :, 0:2]
    )
    packed = jnp.concatenate([turned, mixed_rows[:, :, :, 2:3]], axis=3).astype(jnp.bfloat16)
    packed = packed.reshape(slot_count, span_rows, 3 * model_width)
    heads_rows = lax.all_to_all(packed, "uly", split_axis=2, concat_axis=1, tiled=True).reshape(
        slot_count, block_rows, local_heads, 3, HD
    )
    queries = heads_rows[:, :, :, 0]
    key_value = heads_rows[:, :, :, 1:3]
    row_max = jnp.full((slot_count, local_heads, block_rows), NEGATIVE, jnp.float32)
    row_total = jnp.zeros((slot_count, local_heads, block_rows), jnp.float32)
    attended = jnp.zeros((slot_count, block_rows, local_heads, HD), jnp.float32)
    last_tokens = tokens_of((group_index + 1) % group_count)

    def stats_turn(turn_index, carried):
        pairs_now, cur_max, cur_total = carried
        col_tokens = tokens_of((group_index - turn_index) % group_count)
        cur_max, cur_total = fold_stats(
            cur_max, cur_total, queries, pairs_now, lengths, row_tokens, col_tokens
        )
        pairs_now = passed_along(pairs_now, "blk", 1)
        return (pairs_now, cur_max, cur_total)

    pairs_now, row_max, row_total = lax.fori_loop(
        0, group_count - 1, stats_turn, (key_value, row_max, row_total)
    )
    row_max, row_total = fold_stats(
        row_max, row_total, queries, pairs_now, lengths, row_tokens, last_tokens
    )
    log_total = row_max + jnp.log(row_total)

    def value_turn(turn_index, carried):
        pairs_now, cur_out = carried
        col_tokens = tokens_of((group_index - turn_index) % group_count)
        cur_out = fold_values(
            cur_out, queries, pairs_now, log_total, lengths, row_tokens, col_tokens
        )
        pairs_now = passed_along(pairs_now, "blk", 1)
        return (pairs_now, cur_out)

    pairs_now, attended = lax.fori_loop(0, group_count - 1, value_turn, (key_value, attended))
    attended = fold_values(
        attended, queries, pairs_now, log_total, lengths, row_tokens, last_tokens
    )
    heads_out = attended.astype(jnp.bfloat16).reshape(slot_count, block_rows, local_heads * HD)
    merged = lax.all_to_all(heads_out, "uly", split_axis=1, concat_axis=2, tiled=True).reshape(
        token_rows, model_width
    )
    branch_attn = jnp.dot(merged, dense_w, preferred_element_type=jnp.float32) + dense_b.astype(
        jnp.float32
    )
    hidden_pre = jnp.dot(
        normed_two, expand_w, preferred_element_type=jnp.float32
    ) + expand_b.astype(jnp.float32)
    activated, gelu_back = jax.vjp(partial(jax.nn.gelu, approximate=False), hidden_pre)
    activated_low = activated.astype(jnp.bfloat16)
    branch_feed = jnp.dot(
        activated_low, shrink_w, preferred_element_type=jnp.float32
    ) + shrink_b.astype(jnp.float32)
    outputs = (
        (values + branch_attn + branch_feed)
        .astype(jnp.bfloat16)
        .reshape(slot_count, span_rows, model_width)
    )
    first_token = (uly_index * group_count + group_index) * span_rows
    token_index = first_token + jnp.arange(span_rows, dtype=jnp.int32)
    live_mask = (token_index[None, :] < lengths[:, None]).astype(jnp.float32)
    seed_grad = (cotangent.astype(jnp.float32) * live_mask[:, :, None]).reshape(
        token_rows, model_width
    )
    seed_low = seed_grad.astype(jnp.bfloat16)
    dense_w_grad = jnp.einsum("ra,rb->ab", merged, seed_low, preferred_element_type=jnp.float32)
    bias_grad = jnp.sum(seed_low.astype(jnp.float32), axis=0)
    merged_grad = jnp.einsum(
        "rb,ab->ra", seed_low, dense_w, preferred_element_type=jnp.float32
    ).astype(jnp.bfloat16)
    shrink_w_grad = jnp.einsum(
        "rf,rb->fb", activated_low, seed_low, preferred_element_type=jnp.float32
    )
    activated_grad = jnp.einsum("rb,fb->rf", seed_low, shrink_w, preferred_element_type=jnp.float32)
    hidden_grad = gelu_back(activated_grad)[0].astype(jnp.bfloat16)
    expand_w_grad = jnp.einsum(
        "ra,rf->af", normed_two, hidden_grad, preferred_element_type=jnp.float32
    )
    expand_b_grad = jnp.sum(hidden_grad.astype(jnp.float32), axis=0)
    normed_two_grad = jnp.einsum(
        "rf,af->ra", hidden_grad, expand_w, preferred_element_type=jnp.float32
    )
    grad_heads = lax.all_to_all(
        merged_grad.reshape(slot_count, span_rows, model_width),
        "uly",
        split_axis=2,
        concat_axis=1,
        tiled=True,
    )
    grad_out = grad_heads.reshape(slot_count, block_rows, local_heads, HD)
    row_delta = jnp.sum(grad_out.astype(jnp.float32) * attended, axis=-1).transpose(0, 2, 1)
    query_grad = jnp.zeros((slot_count, block_rows, local_heads, HD), jnp.float32)
    pair_grad = jnp.zeros((slot_count, block_rows, local_heads, 2, HD), jnp.float32)

    def grad_turn(turn_index, carried):
        pairs_now, cur_pgrad, cur_qgrad = carried
        col_tokens = tokens_of((group_index - turn_index) % group_count)
        cur_qgrad, cur_pgrad = fold_grads(
            cur_qgrad,
            cur_pgrad,
            queries,
            pairs_now,
            grad_out,
            log_total,
            row_delta,
            lengths,
            row_tokens,
            col_tokens,
        )
        pairs_now = passed_along(pairs_now, "blk", 1)
        cur_pgrad = passed_along(cur_pgrad.astype(jnp.bfloat16), "blk", 1).astype(cur_pgrad.dtype)
        return (pairs_now, cur_pgrad, cur_qgrad)

    pairs_now, pair_grad, query_grad = lax.fori_loop(
        0, group_count - 1, grad_turn, (key_value, pair_grad, query_grad)
    )
    query_grad, pair_grad = fold_grads(
        query_grad,
        pair_grad,
        queries,
        pairs_now,
        grad_out,
        log_total,
        row_delta,
        lengths,
        row_tokens,
        last_tokens,
    )
    pair_grad = passed_along(pair_grad.astype(jnp.bfloat16), "blk", 1).astype(pair_grad.dtype)
    back_packed = jnp.concatenate(
        [query_grad.astype(jnp.bfloat16)[:, :, :, None], pair_grad.astype(jnp.bfloat16)], axis=3
    )
    back_packed = back_packed.reshape(slot_count, block_rows, local_heads * 3 * HD)
    token_grads = lax.all_to_all(
        back_packed, "uly", split_axis=1, concat_axis=2, tiled=True
    ).reshape(slot_count, span_rows, H, 3, HD)
    turned_grad = turn_back(token_grads[:, :, :, 0:2].astype(jnp.float32))[0]
    mixed_grad = jnp.concatenate(
        [turned_grad, token_grads[:, :, :, 2:3].astype(jnp.float32)], axis=3
    ).astype(jnp.bfloat16)
    mixed_grad = mixed_grad.reshape(token_rows, 3 * model_width)
    project_w_grad = jnp.einsum(
        "ra,rc->ac", normed_one, mixed_grad, preferred_element_type=jnp.float32
    )
    project_b_grad = jnp.sum(mixed_grad.astype(jnp.float32), axis=0)
    normed_one_grad = jnp.einsum(
        "rc,ac->ra", mixed_grad, project_w, preferred_element_type=jnp.float32
    )
    values_one, gain_one_grad, shift_one_grad = norm_back_one(normed_one_grad)
    values_two, gain_two_grad, shift_two_grad = norm_back_two(normed_two_grad)
    input_grad = (
        (seed_grad + values_one + values_two)
        .astype(jnp.bfloat16)
        .reshape(slot_count, span_rows, model_width)
    )
    local_grads = jnp.concatenate(
        [
            gain_one_grad,
            shift_one_grad,
            gain_two_grad,
            shift_two_grad,
            project_w_grad.reshape(-1),
            project_b_grad,
            dense_w_grad.reshape(-1),
            bias_grad,
            expand_w_grad.reshape(-1),
            expand_b_grad,
            shrink_w_grad.reshape(-1),
            bias_grad,
        ]
    )
    gradients = lax.psum_scatter(local_grads, ("blk", "uly"), scatter_dimension=0, tiled=True)
    velocity = MOMENTUM * momenta + gradients
    step_rate = LEARN_RATE / math.sqrt(slot_count * full_rows)
    updated = masters - step_rate * (gradients + MOMENTUM * velocity)
    averaged = AVERAGE_DECAY * averages + (1.0 - AVERAGE_DECAY) * updated
    return (outputs, input_grad, gradients, updated, velocity, averaged)


LANES = 128
BLOCK = 256
RING = ("core", "z", "y")
ALL = ("x", "core", "z", "y")
F32 = jnp.float32
BF16 = jnp.bfloat16


def call(body, grid, in_specs, out_specs, out_shape, scratch=(), prefetch=0):
    return pl.pallas_call(
        body,
        grid_spec=pltpu.PrefetchScalarGridSpec(
            num_scalar_prefetch=prefetch,
            grid=grid,
            in_specs=in_specs,
            out_specs=out_specs,
            scratch_shapes=scratch,
        ),
        out_shape=out_shape,
        compiler_params=pltpu.CompilerParams(vmem_limit_bytes=56 << 20),
    )


def whole(shape):
    return pl.BlockSpec(shape, lambda *_: (0,) * len(shape))


def shaped(shape, kind):
    return jax.ShapeDtypeStruct(shape, kind)


def mm(a, b, dims=((1,), (0,))):
    return lax.dot_general(a, b, (dims, ((), ())), preferred_element_type=F32)


def low_lanes(shape):
    return lax.broadcasted_iota(jnp.int32, shape, len(shape) - 1) < LANES // 2


def swap(a):
    return pltpu.roll(a, LANES // 2, 1)


def join(a, a_half, b, b_half):
    first = swap(a) if a_half else a
    second = b if b_half else swap(b)
    return jnp.where(low_lanes(a.shape), first, second)


OWNERS = 32
PER = (3 * D + D + FF + FF) // OWNERS
FLAT = PER * D // LANES
PIECE = FLAT // 16
LEAD = 4 * D // LANES
EDGE = PER * D + 13 * D // OWNERS
PROJECT, PLAIN, PLAIN_EXPAND, EXPAND, EXPAND_PLAIN = range(5)


def plain_place(row, base, count):
    local = row - base
    half = int(local >= count // 2)
    return local - half * (count // 2), half


def dense_place(row):
    if row < 768:
        c = 8 + row // 384
        return (c, 0) + plain_place(row, 384 * (c - 8), 384)
    return (10, 0) + plain_place(row, 768, 256)


def shrink_place(row):
    if row < 256:
        return (21, 64) + plain_place(row, 0, 256)
    c = 22 + (row - 256) // 384
    return (c, 0) + plain_place(row, 256 + 384 * (c - 22), 384)


def expand_places():
    places = [(10, 128, 0, 32)]
    places += [(c, 0, 32 + 96 * (c - 11), 96) for c in range(11, 21)]
    places += [(21, 0, 992, 32)]
    return places


def shifted_rows(source, start, shift, at, rows):
    turn = (LANES - shift) % LANES
    first = pltpu.roll(source[pl.ds(start + at, rows), :], turn, 1)
    second = pltpu.roll(source[pl.ds(start + at + 1, rows), :], turn, 1)
    lane = lax.broadcasted_iota(jnp.int32, (rows, LANES), 1)
    return jnp.where(lane < LANES - shift, first, second)


SHIFT_ROWS = 3200
SEND_ROWS = PIECE + 32 + 16
OWN_ROW = 64


def weights_out_body(scalars, before, own, after, places, out, source, flat, tail):
    start, shift, kind, vector_row = scalars[0], scalars[1], scalars[2], scalars[3]
    count = own.shape[0]
    source[0 : OWN_ROW - 8] = jnp.zeros((OWN_ROW - 8, LANES), F32)
    source[OWN_ROW - 8 : OWN_ROW] = before[...]

    def copy(step, carry):
        at = pl.multiple_of(step * 88, 8)
        source[pl.ds(at + OWN_ROW, 88), :] = own[pl.ds(at, 88), :]
        return carry

    lax.fori_loop(0, count // 88, copy, 0)
    last = OWN_ROW + EDGE // LANES
    source[OWN_ROW + count :] = jnp.zeros((source.shape[0] - OWN_ROW - count, LANES), F32)
    edge = EDGE % LANES
    tail[...] = jnp.zeros(tail.shape, F32)
    tail[7:8] = source[last : last + 1]
    tail[8:40] = pltpu.roll(after[...], edge, 1)
    lane = lax.broadcasted_iota(jnp.int32, (40, LANES), 1)
    source[last : last + 40] = jnp.where(lane < edge, tail[7:47], tail[8:48])

    def align(step, carry):
        at = pl.multiple_of(step * 80, 8)
        flat[pl.ds(at, 80), :] = shifted_rows(source, start, shift, at, 80)
        return carry

    lax.fori_loop(0, SHIFT_ROWS // 80, align, 0)

    def rows(first, count, stride):
        return flat[pl.ds(first, count, stride), :]

    def plain(base, count, to):
        for m in range(8):
            tile = rows(base + m, count, 8)
            a, b = tile[: count // 2], tile[count // 2 :]
            out[2 * m, to : to + count // 2] = join(a, 0, b, 0).astype(BF16)
            out[2 * m + 1, to : to + count // 2] = join(a, 1, b, 1).astype(BF16)

    def expand(base, count, to):
        for r in range(16):
            out[r, to : to + count] = rows(base + 2 * r, count, 32).astype(BF16)
            out[r, to + count : to + 2 * count] = rows(base + 2 * r + 1, count, 32).astype(BF16)

    def project(base):
        for m in range(8):
            first, middle, last = (rows(base + 3 * m + j, 128, 24) for j in range(3))
            out[2 * m, 0:128] = first.astype(BF16)
            out[2 * m, 128:192] = join(middle[:64], 0, middle[64:], 0).astype(BF16)
            out[2 * m + 1, 0:128] = join(middle, 1, last, 0).astype(BF16)
            out[2 * m + 1, 128:192] = join(last[:64], 1, last[64:], 1).astype(BF16)

    @pl.when(kind == PROJECT)
    def _():
        project(LEAD)

    @pl.when(kind == PLAIN)
    def _():
        plain(LEAD, 384, 0)

    @pl.when(kind == PLAIN_EXPAND)
    def _():
        plain(LEAD, 256, 0)
        expand(LEAD + 2048 + 8, 32, 128)

    @pl.when(kind == EXPAND)
    def _():
        expand(LEAD, 96, 0)

    @pl.when(kind == EXPAND_PLAIN)
    def _():
        expand(LEAD, 32, 0)
        plain(LEAD + 1024 + 32, 256, 64)

    vectors = flat[pl.ds(vector_row, 32), :].astype(BF16)
    for r in range(16):
        out[r, PIECE : PIECE + 32] = vectors
        out[r, PIECE + 32 :] = places[...]


def spread(source, at, vectors, to):
    tile = source[pl.ds(at, 8), :].astype(F32)
    for j in range(8):
        vectors[to : to + 1, 128 * j : 128 * j + 128] = tile[j : j + 1]


def project_in_body(scalars, own, came, qkv_w, vectors, qkv_b, project_rows):
    head = scalars[0]
    low = low_lanes((64, LANES))
    vectors[...] = jnp.zeros(vectors.shape, F32)

    def take(got):
        for c in range(8):
            qkv_w[128 * c : 128 * c + 128, 0:128] = got[c, 0:128]
            packed = got[c, 128:192].astype(F32)
            qkv_w[128 * c : 128 * c + 64, 128:256] = jnp.where(low, packed, 0.0).astype(BF16)
            qkv_w[128 * c + 64 : 128 * c + 128, 128:256] = jnp.where(low, swap(packed), 0.0).astype(BF16)
        project_rows[0:32] = got[0, PIECE : PIECE + 32].astype(F32)
        for v in range(4):
            spread(project_rows, 8 * v, vectors, v)
        project_rows[0:24] = got[8, PIECE + 8 : PIECE + 32].astype(F32)

    pl.when(scalars[1] == 0)(lambda: take(own))
    pl.when(scalars[1] != 0)(lambda: take(came))
    row = head // 2 * 3
    first, middle, last = (project_rows[pl.ds(row + j, 1), :] for j in range(3))
    odd = head % 2 == 1
    qkv_b[0:1, 0:128] = jnp.where(odd, join(middle, 1, last, 0), first)
    value = jnp.where(odd, swap(last), middle)
    qkv_b[0:1, 128:256] = jnp.where(low_lanes((1, LANES)), value, 0.0)


def rest_in_body(scalars, own, came, expand_w, second, biases, expand_b, rows):
    head = scalars[0]
    biases[...] = jnp.zeros(biases.shape, F32)

    def take(lower, upper):
        def block(c, at, count):
            return (lower if c < 16 else upper)[c % 16, at : at + count]

        for c, at, row, count in expand_places():
            expand_w[row : row + count, 0:128] = block(c, at, count)
            expand_w[row : row + count, 128:256] = block(c, at + count, count)

        def tile(place):
            c, at, row, half = place
            return block(c, at + row, 64).astype(F32), half

        for h in range(16):
            a, half = tile(dense_place(64 * h))
            second[h, 0:32] = join(a[:32], half, a[32:], half).astype(BF16)
            for part in range(2):
                a, half = tile(shrink_place(256 * h + 64 * part))
                b, other = tile(shrink_place(256 * h + 128 + 64 * part))
                second[h, 32 + 64 * part : 96 + 64 * part] = join(a, half, b, other).astype(BF16)
        for to, c in enumerate((10, 31)):
            rows[0:16] = block(c, PIECE, 16).astype(F32)
            spread(rows, 0, biases, to)
        rows[...] = block(21, PIECE, 32).astype(F32)

    pl.when(scalars[1] == 0)(lambda: take(own, came))
    pl.when(scalars[1] != 0)(lambda: take(came, own))
    expand_b[0:1, 0:128] = rows[pl.ds(2 * head, 1), :]
    expand_b[0:1, 128:256] = rows[pl.ds(2 * head + 1, 1), :]


def rows_in_body(got, dense_w, shrink_w):
    for m in range(8):
        even, odd = got[2 * m].astype(F32), got[2 * m + 1].astype(F32)
        columns = slice(128 * m, 128 * m + 128)
        for out, at, half in ((dense_w, 0, 32), (shrink_w, 32, 128)):
            a, b = even[at : at + half], odd[at : at + half]
            out[0:half, columns] = join(a, 0, b, 0).astype(BF16)
            out[half : 2 * half, columns] = join(a, 1, b, 1).astype(BF16)


def rows_out_body(dense_g, shrink_g, out):
    for m in range(8):
        columns = slice(128 * m, 128 * m + 128)
        for source, at, half in ((dense_g, 0, 32), (shrink_g, 32, 128)):
            a, b = source[0:half, columns], source[half : 2 * half, columns]
            out[2 * m, at : at + half] = join(a, 0, b, 0).astype(BF16)
            out[2 * m + 1, at : at + half] = join(a, 1, b, 1).astype(BF16)


def early_body(scalars, second, expand_g, bias_g, expand_bg, own, other, expand_rows):
    head = scalars[0]
    expand_rows[...] = jnp.zeros(expand_rows.shape, F32)
    expand_rows[pl.ds(2 * head, 1), :] = expand_bg[0:1, 0:128]
    expand_rows[pl.ds(2 * head + 1, 1), :] = expand_bg[0:1, 128:256]
    rows = [bias_g[0:1, 128 * j : 128 * j + 128] for j in range(8)]
    bias = jnp.concatenate(rows + [jnp.zeros((8, LANES), F32)], axis=0).astype(BF16)

    def dense_rows(row):
        packed = second[row // 64, 0:32].astype(F32)
        return jnp.concatenate([packed, swap(packed)], axis=0)

    def shrink_rows(row):
        h, part = row // 256, row % 256 // 64
        packed = second[h, 32 + part % 2 * 64 : 96 + part % 2 * 64].astype(F32)
        return swap(packed) if part >= 2 else packed

    def put(lower, upper):
        def store(c, at, tile):
            (lower if c < 16 else upper)[c % 16, at : at + tile.shape[0]] = tile

        def plain(c, to, base, count, take):
            for i in range(count // 128):
                a, b = take(base + 64 * i), take(base + count // 2 + 64 * i)
                store(c, to + 64 * i, join(a, 0, b, 0).astype(BF16))

        for c in range(8):
            store(c, 0, jnp.zeros((PIECE, LANES), BF16))
        for c in range(OWNERS):
            store(c, PIECE, jnp.zeros((32, LANES), BF16))
        for c, at, row, count in expand_places():
            store(c, at, expand_g[row : row + count, 0:128].astype(BF16))
            store(c, at + count, expand_g[row : row + count, 128:256].astype(BF16))
        plain(8, 0, 0, 384, dense_rows)
        plain(9, 0, 384, 384, dense_rows)
        plain(10, 0, 768, 256, dense_rows)
        plain(21, 64, 0, 256, shrink_rows)
        for c in range(22, 32):
            plain(c, 0, 256 + 384 * (c - 22), 384, shrink_rows)
        store(10, PIECE, bias)
        store(31, PIECE, bias)
        store(21, PIECE, expand_rows[...].astype(BF16))

    pl.when(scalars[1] == 0)(lambda: put(own, other))
    pl.when(scalars[1] != 0)(lambda: put(other, own))


LATE_ROWS = 8 * PIECE + 64


def late_body(scalars, qkv_g, vector_g, qkv_bg, out, project_rows):
    head = scalars[0]
    for c in range(8):
        at = PIECE * c
        out[at : at + 128] = qkv_g[128 * c : 128 * c + 128, 0:128].astype(BF16)
        a = qkv_g[128 * c : 128 * c + 64, 128:256]
        b = qkv_g[128 * c + 64 : 128 * c + 128, 128:256]
        out[at + 128 : at + 192] = join(a, 0, b, 0).astype(BF16)
    gains = [vector_g[v : v + 1, 128 * j : 128 * j + 128] for v in range(4) for j in range(8)]
    out[8 * PIECE : 8 * PIECE + 32] = jnp.concatenate(gains, axis=0).astype(BF16)
    project_rows[...] = jnp.zeros(project_rows.shape, F32)
    pair, value = qkv_bg[0:1, 0:128], qkv_bg[0:1, 128:256]
    low = low_lanes((1, LANES))
    row = 8 + head // 2 * 3
    odd = head % 2 == 1
    project_rows[pl.ds(row, 1), :] = jnp.where(odd, 0.0, pair)
    project_rows[pl.ds(row + 1, 1), :] = jnp.where(
        odd, jnp.where(low, 0.0, swap(pair)), jnp.where(low, value, 0.0)
    )
    project_rows[pl.ds(row + 2, 1), :] = jnp.where(odd, join(pair, 1, value, 0), 0.0)
    out[8 * PIECE + 32 :] = project_rows[...].astype(BF16)


def both_body(scalars, early, early_came, late, late_came, out):
    def add(r, carry):
        out[r] = (early[r].astype(F32) + early_came[r].astype(F32)).astype(BF16)
        return carry

    lax.fori_loop(0, 16, add, 0)

    @pl.when(scalars[0] == 0)
    def _():
        def total(at, count):
            return (late[at : at + count].astype(F32) + late_came[at : at + count].astype(F32)).astype(BF16)

        for c in range(8):
            out[c, 0:PIECE] = total(PIECE * c, PIECE)
        out[0, PIECE : PIECE + 32] = total(8 * PIECE, 32)
        out[8, PIECE : PIECE + 32] = total(8 * PIECE + 32, 32)


BACK_ROWS = PIECE + 32
TAKE_ROWS = 3120


def grads_in_body(scalars, got, out, flat):
    start, shift, kind, vector_row = scalars[0], scalars[1], scalars[2], scalars[3]
    lead = LEAD + 8

    def clear(step, carry):
        flat[pl.ds(pl.multiple_of(step * 80, 8), 80), :] = jnp.zeros((80, LANES), F32)
        return carry

    lax.fori_loop(0, SHIFT_ROWS // 80, clear, 0)

    def add_vectors(source, total):
        return total + got[source, PIECE : PIECE + 32].astype(F32)

    flat[pl.ds(vector_row + 8, 32), :] = lax.fori_loop(0, 16, add_vectors, jnp.zeros((32, LANES), F32))

    def taken(r, at, count):
        return got[r, at : at + count].astype(F32)

    def plain(base, count, at):
        half = count // 2
        for m in range(8):
            a, b = taken(2 * m, at, half), taken(2 * m + 1, at, half)
            flat[pl.ds(base + m, half, 8), :] = join(a, 0, b, 0)
            flat[pl.ds(base + m + 8 * half, half, 8), :] = join(a, 1, b, 1)

    def expand(base, count, at):
        for r in range(16):
            flat[pl.ds(base + 2 * r, count, 32), :] = taken(r, at, count)
            flat[pl.ds(base + 2 * r + 1, count, 32), :] = taken(r, at + count, count)

    def project(base):
        for m in range(8):
            pair, values = taken(2 * m, 0, 128), taken(2 * m, 128, 64)
            odd_pair, odd_values = taken(2 * m + 1, 0, 128), taken(2 * m + 1, 128, 64)
            values = jnp.concatenate([values, swap(values)], axis=0)
            odd_values = jnp.concatenate([odd_values, swap(odd_values)], axis=0)
            flat[pl.ds(base + 3 * m, 128, 24), :] = pair
            flat[pl.ds(base + 3 * m + 1, 128, 24), :] = join(values, 0, odd_pair, 0)
            flat[pl.ds(base + 3 * m + 2, 128, 24), :] = join(odd_pair, 1, odd_values, 0)

    @pl.when(kind == PROJECT)
    def _():
        project(lead)

    @pl.when(kind == PLAIN)
    def _():
        plain(lead, 384, 0)

    @pl.when(kind == PLAIN_EXPAND)
    def _():
        plain(lead, 256, 0)
        expand(lead + 2048 + 8, 32, 128)

    @pl.when(kind == EXPAND)
    def _():
        expand(lead, 96, 0)

    @pl.when(kind == EXPAND_PLAIN)
    def _():
        expand(lead, 32, 0)
        plain(lead + 1024 + 32, 256, 64)

    def align(step, carry):
        at = pl.multiple_of(step * 80, 8)
        out[pl.ds(at, 80), :] = shifted_rows(flat, start, shift, at, 80)
        return carry

    lax.fori_loop(0, TAKE_ROWS // 80, align, 0)


def token_rows(ref):
    return jnp.concatenate([ref[0, 0, 0], ref[1, 0, 0], ref[0, 0, 1], ref[1, 0, 1]], axis=0)


def put_rows(kept, sent, rows, core):
    step = rows.shape[0] // 4
    for x in range(2):
        first, second = (rows[step * i : step * i + step].astype(BF16) for i in (2 * x, 2 * x + 1))
        kept[0, x] = jnp.where(core == 0, first, second)
        sent[0, x] = jnp.where(core == 0, second, first)


def relative_place(i, here):
    y = (i & 1) ^ here[2]
    z = (i >> 1) ^ here[3]
    return y * 4 + (z & 1) * 2 + (z >> 1)


def normalized(values):
    centered = values - jnp.mean(values, axis=-1, keepdims=True)
    variance = jnp.mean(centered * centered, axis=-1, keepdims=True)
    return centered * lax.rsqrt(variance + EPSILON)


def turned(pair, cos, sin):
    lane = lax.broadcasted_iota(jnp.int32, pair.shape, 1) % HD
    half = ROT // 2
    other = jnp.where(
        lane < half, -pltpu.roll(pair, LANES - half, 1), jnp.where(lane < ROT, pltpu.roll(pair, half, 1), 0.0)
    )
    return pair * cos + other * sin


def mixed_body(tokens, place, vectors, qkv_w, qkv_b, inverse, one, two, query, key, value, cos, sin):
    unit = normalized(token_rows(tokens).astype(F32))
    angles = place[...] * inverse[...]
    cos[...] = jnp.cos(angles)
    sin[...] = jnp.sin(angles)
    first = (unit * vectors[0:1] + vectors[1:2]).astype(BF16)
    one[...] = first
    two[...] = (unit * vectors[2:3] + vectors[3:4]).astype(BF16)
    mixed = mm(first, qkv_w[...]) + qkv_b[...]
    pair = turned(mixed[:, :LANES], cos[...], sin[...])
    query[...] = pair[:, :HD].astype(BF16) * HD ** (-0.5)
    key[...] = pair[:, HD:].astype(BF16)
    value[...] = mixed[:, LANES : LANES + HD].astype(BF16)


def masked_scores(key, query_t, at, first_query, length):
    scores = mm(key, query_t)
    keys = at * BLOCK + lax.broadcasted_iota(jnp.int32, scores.shape, 0)
    queries = first_query + lax.broadcasted_iota(jnp.int32, scores.shape, 1)
    return jnp.where((keys <= queries) & (keys < length), scores, NEGATIVE)


def folded(values, op):
    parts = [values[8 * i : 8 * i + 8] for i in range(values.shape[0] // 8)]
    while len(parts) > 1:
        parts = [op(a, b) for a, b in zip(parts[::2], parts[1::2])]
    return parts[0]


def attend_body(lengths, query, key, value, low_out, full_out, log_out, scores, value_t):
    at = pl.program_id(0)
    length = lengths[0]

    @pl.when(at == 0)
    def _():
        value_t[...] = value[...].astype(F32).T.astype(BF16)

    query_t = query[...].astype(F32).T.astype(BF16)
    clear = jnp.minimum(at, length // BLOCK)
    stop = jnp.minimum(at, (length - 1) // BLOCK) + 1

    def rows(j):
        return pl.ds(pl.multiple_of(j * BLOCK, BLOCK), BLOCK)

    def score(j, top, masked):
        if masked:
            tile = masked_scores(key[rows(j), :], query_t, j, at * BLOCK, length)
        else:
            tile = mm(key[rows(j), :], query_t)
        scores[rows(j), :] = tile
        return jnp.maximum(top, folded(tile, jnp.maximum))

    top = jnp.full((8, BLOCK), NEGATIVE, F32)
    top = lax.fori_loop(0, clear, lambda j, t: score(j, t, False), top)
    top = lax.fori_loop(clear, stop, lambda j, t: score(j, t, True), top)
    top = jnp.max(top, axis=0, keepdims=True)

    def weigh(j, carried):
        total, out = carried
        tile = jnp.exp(scores[rows(j), :] - top)
        return total + folded(tile, jnp.add), out + mm(value_t[:, rows(j)], tile.astype(BF16))

    start = (jnp.zeros((8, BLOCK), F32), jnp.zeros((HD, BLOCK), F32))
    total, out = lax.fori_loop(0, stop, weigh, start)
    total = jnp.sum(total, axis=0, keepdims=True)
    out = out * (1.0 / total)
    full_out[...] = out
    low_out[...] = out.T.astype(BF16)
    log_out[...] = top + jnp.log(total)


def attend_back_body(
    lengths, query, key, value, grad, full_out, log_in, query_g, key_g, value_g, key_t, key_sum, value_sum
):
    at = pl.program_id(0)
    length = lengths[0]

    @pl.when(at == 0)
    def _():
        key_t[...] = key[...].astype(F32).T.astype(BF16)
        key_sum[...] = jnp.zeros(key_sum.shape, F32)
        value_sum[...] = jnp.zeros(value_sum.shape, F32)

    query_rows, grad_rows = query[...], grad[...]
    query_t = query_rows.astype(F32).T.astype(BF16)
    grad_full_t = grad_rows.astype(F32).T
    grad_t = grad_full_t.astype(BF16)
    delta = jnp.sum(grad_full_t * full_out[...], axis=0, keepdims=True)
    log_total = log_in[...]
    clear = jnp.minimum(at, length // BLOCK)
    stop = jnp.minimum(at, (length - 1) // BLOCK) + 1
    clear, stop = (jnp.where(at * BLOCK < length, n, 0) for n in (clear, stop))

    def step(j, query_sum, masked):
        rows = pl.ds(pl.multiple_of(j * BLOCK, BLOCK), BLOCK)
        if masked:
            tile = masked_scores(key[rows, :], query_t, j, at * BLOCK, length)
        else:
            tile = mm(key[rows, :], query_t)
        probs = jnp.exp(tile - log_total)
        value_sum[rows, :] += mm(probs.astype(BF16), grad_rows)
        score_g = (probs * (mm(value[rows, :], grad_t) - delta)).astype(BF16)
        key_sum[rows, :] += mm(score_g, query_rows)
        return query_sum + mm(key_t[:, rows], score_g)

    query_sum = jnp.zeros((HD, BLOCK), F32)
    query_sum = lax.fori_loop(0, clear, lambda j, s: step(j, s, False), query_sum)
    query_sum = lax.fori_loop(clear, stop, lambda j, s: step(j, s, True), query_sum)
    query_g[...] = (query_sum * HD ** (-0.5)).T.astype(BF16)

    @pl.when(at == pl.num_programs(0) - 1)
    def _():
        key_g[...] = key_sum[...].astype(BF16)
        value_g[...] = value_sum[...].astype(BF16)


def feed_body(
    here, two, attended, cotangent, expand_w, expand_b, shrink_w, dense_w,
    partial_out, attended_g, hidden_g, shrink_g, dense_g, expand_g, expand_bg, bias_g,
):
    at = pl.program_id(0)

    @pl.when(at == 0)
    def _():
        for total in (shrink_g, dense_g, expand_g, expand_bg, bias_g):
            total[...] = jnp.zeros(total.shape, F32)

    normed, mixed = two[...], attended[...]
    hidden = mm(normed, expand_w[...]) + expand_b[...]
    error = lax.erf(hidden * math.sqrt(0.5))
    cumulative = 0.5 * (1.0 + error)
    active = (hidden * cumulative).astype(BF16)
    partial = mm(mixed, dense_w[...]) + mm(active, shrink_w[...])
    step = BLOCK // 4
    for i, (core, x) in enumerate(((0, 0), (1, 0), (0, 1), (1, 1))):
        partial_out[core, 0, x] = partial[step * i : step * i + step].astype(BF16)
    token = at * BLOCK + lax.broadcasted_iota(jnp.int32, (BLOCK, D), 0)
    seed = jnp.where(token < here[0], token_rows(cotangent).astype(F32), 0.0)
    bias_g[...] += jnp.sum(seed, axis=0, keepdims=True)
    seed = seed.astype(BF16)
    attended_g[...] = mm(seed, dense_w[...], ((1,), (1,))).astype(BF16)
    slope = cumulative + hidden * jnp.exp(-0.5 * hidden * hidden) * (1.0 / math.sqrt(2.0 * math.pi))
    back = (mm(seed, shrink_w[...], ((1,), (1,))) * slope).astype(BF16)
    hidden_g[...] = back
    expand_bg[...] += jnp.sum(back.astype(F32), axis=0, keepdims=True)
    shrink_g[...] += mm(active, seed, ((0,), (0,)))
    dense_g[...] += mm(mixed, seed, ((0,), (0,)))
    expand_g[...] += mm(normed, back, ((0,), (0,)))


def mixed_back_body(
    here, tokens, one, query_g, key_g, value_g, hidden_g, vectors, qkv_w, expand_w, cos, sin,
    kept, sent, qkv_g, qkv_bg, vector_g,
):
    at = pl.program_id(0)

    @pl.when(at == 0)
    def _():
        for total in (qkv_g, qkv_bg, vector_g):
            total[...] = jnp.zeros(total.shape, F32)

    pair = jnp.concatenate([query_g[...].astype(F32), key_g[...].astype(F32)], axis=1)
    pair = turned(pair, cos[...], -sin[...])
    values = value_g[...].astype(F32)
    mixed_g = jnp.concatenate([pair, values, jnp.zeros_like(values)], axis=1)
    mixed_low = mixed_g.astype(BF16)
    qkv_bg[...] += jnp.sum(mixed_low.astype(F32), axis=0, keepdims=True)
    qkv_g[...] += mm(one[...], mixed_low, ((0,), (0,)))
    one_g = mm(mixed_low, qkv_w[...], ((1,), (1,)))
    two_g = mm(hidden_g[...], expand_w[...], ((1,), (1,)))
    unit = normalized(token_rows(tokens).astype(F32))
    vector_g[0:1] += jnp.sum(one_g * unit, axis=0, keepdims=True)
    vector_g[1:2] += jnp.sum(one_g, axis=0, keepdims=True)
    vector_g[2:3] += jnp.sum(two_g * unit, axis=0, keepdims=True)
    vector_g[3:4] += jnp.sum(two_g, axis=0, keepdims=True)
    put_rows(kept, sent, one_g * vectors[0:1] + two_g * vectors[2:3], here[1])


def split_mesh(mesh):
    groups, members = mesh.shape["blk"], mesh.shape["uly"]
    return Mesh(mesh.devices.reshape(groups // 2, 2, members // 2, 2), ALL)


def across_x(block):
    return lax.ppermute(block, "x", [(0, 1), (1, 0)])


def by_head(residual, cotangent, lengths, positions, masters, momenta, averages):
    slots, span, width = residual.shape
    x = lax.axis_index("x")
    head = lax.axis_index("core") * 8 + lax.axis_index("z") * 2 + lax.axis_index("y")
    owner = x * 16 + head
    groups = lax.axis_size("z") * lax.axis_size("y")
    count = groups * 4 * span
    chunk = masters.shape[0]
    length = lax.dynamic_slice_in_dim(lengths, x, 1)

    def paired(mine, theirs):
        return jnp.where(x == 0, jnp.stack([mine, theirs]), jnp.stack([theirs, mine]))

    def at_x(rows, index):
        return lax.dynamic_index_in_dim(rows, index, 0, keepdims=False)

    rows = jnp.stack([residual, cotangent], axis=1)
    rows = paired(at_x(rows, x), across_x(at_x(rows, 1 - x)))
    places = paired(at_x(positions, x), across_x(at_x(positions, 1 - x))).reshape(1, 2 * span)
    tokens_shape = (2, groups, 2, span, width)
    slot_tokens = lax.all_gather(rows[:, 0], RING, axis=0).reshape(tokens_shape)
    slot_cotangent = lax.all_gather(rows[:, 1], RING, axis=0).reshape(tokens_shape)
    high, rest = (places // 256).astype(BF16), (places % 256).astype(BF16)
    places = jnp.concatenate([high, rest, jnp.zeros((14, 2 * span), BF16)])
    lane = jnp.arange(LANES, dtype=jnp.int32) % HD
    inverse = ROTARY_BASE ** (-((lane % (ROT // 2)).astype(F32) * 2.0 / ROT))
    inverse = jnp.where(lane < ROT, inverse, 0.0)[None, :]

    onward = [(i, i + 1) for i in range(OWNERS - 1)]
    backward = [(i + 1, i) for i in range(OWNERS - 1)]
    before = lax.ppermute(masters[chunk - D :], ALL, onward)
    after = lax.ppermute(masters[: 4 * D], ALL, backward)
    own_rows = -(-chunk // D) * 8
    own = jnp.pad(masters, (0, own_rows * LANES - chunk)).reshape(own_rows, LANES)
    before, after = before.reshape(8, LANES), after.reshape(32, LANES)
    skipped = jnp.where(owner < 8, 4, jnp.where(owner < 11, 7, jnp.where(owner < 22, 8, 12)))
    kind = jnp.where(
        owner < 8,
        PROJECT,
        jnp.where(
            owner == 10,
            PLAIN_EXPAND,
            jnp.where(owner == 21, EXPAND_PLAIN, jnp.where((owner > 10) & (owner < 21), EXPAND, PLAIN)),
        ),
    )
    vector_row = jnp.where(owner == 10, 2080, jnp.where(owner == 21, 1056, jnp.where(owner == 31, 3104, 0)))
    ahead = skipped * D - (chunk - PER * D) * owner
    begin = ahead + 4 * D
    scalars = jnp.stack([begin // LANES, begin % LANES, kind, vector_row]).astype(jnp.int32)
    sent = call(
        weights_out_body, (1,),
        [whole(before.shape), whole(own.shape), whole(after.shape), whole(places.shape)],
        whole((16, SEND_ROWS, LANES)),
        shaped((16, SEND_ROWS, LANES), BF16),
        [pltpu.VMEM((3280, LANES), F32), pltpu.VMEM((SHIFT_ROWS, LANES), F32), pltpu.VMEM((48, LANES), F32)],
        1,
    )(scalars, before, own, after, places)
    got = lax.all_to_all(sent, RING, 0, 0, tiled=True)
    head_scalar = jnp.stack([head, x]).astype(jnp.int32)
    place = got[:, PIECE + 32 : PIECE + 34].astype(F32).reshape(2, groups, 2, 2, span)
    place = (place[:, :, 0] * 256.0 + place[:, :, 1]).transpose(1, 2, 0, 3).reshape(count, 1)
    came = lax.ppermute(got[:9], "x", [(0, 1)])
    qkv_w, vectors, qkv_b = call(
        project_in_body, (1,),
        [whole((9, SEND_ROWS, LANES)), whole((9, SEND_ROWS, LANES))],
        [whole((D, 256)), whole((8, D)), whole((1, 256))],
        [shaped((D, 256), BF16), shaped((8, D), F32), shaped((1, 256), F32)],
        [pltpu.VMEM((32, LANES), F32)], 1,
    )(head_scalar, got, came)
    came = across_x(got)
    expand_w, second, biases, expand_b = call(
        rest_in_body, (1,),
        [whole(got.shape), whole(got.shape)],
        [whole((D, 256)), whole((16, 160, LANES)), whole((8, D)), whole((1, 256))],
        [shaped((D, 256), BF16), shaped((16, 160, LANES), BF16), shaped((8, D), F32), shaped((1, 256), F32)],
        [pltpu.VMEM((32, LANES), F32)], 1,
    )(head_scalar, got, came)
    second = lax.all_to_all(second, RING, 0, 0, tiled=True)
    steps = (count // BLOCK,)
    token_spec = pl.BlockSpec((2, 1, 2, span, width), lambda i, *_: (0, i, 0, 0, 0))
    part_spec = pl.BlockSpec((1, 2, span, width), lambda i, here: (relative_place(i, here), 0, 0, 0))
    part_shape = shaped((groups, 2, span, width), BF16)
    y, z, core = lax.axis_index("y"), lax.axis_index("z"), lax.axis_index("core")
    here = jnp.stack([length[0], core, y, z]).astype(jnp.int32)

    swap_pair, far_pairs = [(0, 1), (1, 0)], [(0, 2), (2, 0), (1, 3), (3, 1)]

    def summed(kept, sent):
        left = kept.shape[0]
        for axis, route in (
            ("core", swap_pair), ("y", swap_pair), ("z", swap_pair + [(2, 3), (3, 2)]), ("z", far_pairs)
        ):
            came = lax.ppermute(sent, axis, route)
            if left == 1:
                return (kept[0].astype(F32) + came[0].astype(F32)).astype(BF16)
            left //= 2
            kept, sent = [
                (kept[half].astype(F32) + came[half].astype(F32)).astype(BF16)
                for half in (slice(0, left), slice(left, None))
            ]

    def to_owner(rows):
        mine, theirs = at_x(rows, x), at_x(rows, 1 - x)
        return paired(mine, across_x(theirs)).astype(F32)

    def rows_spec(columns):
        return pl.BlockSpec((BLOCK, columns), lambda i, *_: (i, 0))

    def columns_spec(rows):
        return pl.BlockSpec((rows, BLOCK), lambda i, *_: (0, i))

    narrow = shaped((count, HD), BF16)
    table = shaped((count, LANES), F32)
    one, two, query, key, value, cos, sin = call(
        mixed_body, steps,
        [token_spec, rows_spec(1), whole((8, D)), whole((D, 256)), whole((1, 256)), whole((1, LANES))],
        [rows_spec(D), rows_spec(D), rows_spec(HD), rows_spec(HD), rows_spec(HD), rows_spec(LANES), rows_spec(LANES)],
        [shaped((count, D), BF16), shaped((count, D), BF16), narrow, narrow, narrow, table, table],
    )(slot_tokens, place, vectors, qkv_w, qkv_b, inverse)
    attended, attended_full, log_total = call(
        attend_body, steps,
        [rows_spec(HD), whole((count, HD)), whole((count, HD))],
        [rows_spec(HD), columns_spec(HD), columns_spec(1)],
        [narrow, shaped((HD, count), F32), shaped((1, count), F32)],
        [pltpu.VMEM((count, BLOCK), F32), pltpu.VMEM((HD, count), BF16)], 1,
    )(length, query, key, value)
    second, attended = lax.optimization_barrier((second, attended))
    dense_w, shrink_w = call(
        rows_in_body, (1,), [whole(second.shape)], [whole((HD, D)), whole((256, D))],
        [shaped((HD, D), BF16), shaped((256, D), BF16)],
    )(second)

    partial_out, attended_g, hidden_g, shrink_g, dense_g, expand_g, expand_bg, bias_g = call(
        feed_body, steps,
        [rows_spec(D), rows_spec(HD), token_spec, whole((D, 256)), whole((1, 256)), whole((256, D)), whole((HD, D))],
        [token_spec, rows_spec(HD), rows_spec(256), whole((256, D)), whole((HD, D)), whole((D, 256)),
         whole((1, 256)), whole((1, D))],
        [shaped(tokens_shape, BF16), narrow, shaped((count, 256), BF16), shaped((256, D), F32), shaped((HD, D), F32),
         shaped((D, 256), F32), shaped((1, 256), F32), shaped((1, D), F32)], (), 1,
    )(here, two, attended, slot_cotangent, expand_w, expand_b, shrink_w, dense_w)
    second_g = call(
        rows_out_body, (1,), [whole((HD, D)), whole((256, D))], whole((16, 160, LANES)),
        shaped((16, 160, LANES), BF16),
    )(dense_g, shrink_g)
    attended_g, second_g = lax.optimization_barrier((attended_g, second_g))
    second_g = lax.all_to_all(second_g, RING, 0, 0, tiled=True)
    out_rows = lax.psum_scatter(
        partial_out.reshape(16, 2, span, width), RING, scatter_dimension=0, tiled=True
    )[0]
    out_rows = to_owner(out_rows)
    query_g, key_g, value_g = call(
        attend_back_body, steps,
        [rows_spec(HD), whole((count, HD)), whole((count, HD)), rows_spec(HD), columns_spec(HD), columns_spec(1)],
        [rows_spec(HD), whole((count, HD)), whole((count, HD))],
        [narrow, narrow, narrow],
        [pltpu.VMEM((HD, count), BF16), pltpu.VMEM((count, HD), F32), pltpu.VMEM((count, HD), F32)],
        1,
    )(length, query, key, value, attended_g, attended_full, log_total)
    bias_g = jnp.where(head == 0, bias_g, 0.0)
    plane = (16, BACK_ROWS, LANES)
    early, early_other = call(
        early_body, (1,),
        [whole((16, 160, LANES)), whole((D, 256)), whole((1, D)), whole((1, 256))],
        [whole(plane), whole(plane)],
        [shaped(plane, BF16), shaped(plane, BF16)],
        [pltpu.VMEM((32, LANES), F32)], 1,
    )(head_scalar, second_g, expand_g, bias_g, expand_bg)
    early_came = across_x(early_other)
    kept, sent, qkv_g, qkv_bg, vector_g = call(
        mixed_back_body, steps,
        [token_spec, rows_spec(D), rows_spec(HD), rows_spec(HD), rows_spec(HD),
         rows_spec(256), whole((8, D)), whole((D, 256)), whole((D, 256)), rows_spec(LANES), rows_spec(LANES)],
        [part_spec, part_spec, whole((D, 256)), whole((1, 256)), whole((8, D))],
        [part_shape, part_shape, shaped((D, 256), F32), shaped((1, 256), F32), shaped((8, D), F32)], (), 1,
    )(here, slot_tokens, one, query_g, key_g, value_g, hidden_g, vectors, qkv_w, expand_w, cos, sin)
    in_rows = to_owner(summed(kept, sent))

    values = residual.astype(F32)
    middle = jnp.mean(values, axis=-1, keepdims=True)
    scale = lax.rsqrt(jnp.mean((values - middle) ** 2, axis=-1, keepdims=True) + EPSILON)
    middle, scale = lax.optimization_barrier((middle, scale))

    late = call(
        late_body, (1,), [whole((D, 256)), whole((8, D)), whole((1, 256))], whole((LATE_ROWS, LANES)),
        shaped((LATE_ROWS, LANES), BF16), [pltpu.VMEM((32, LANES), F32)], 1,
    )(head_scalar, qkv_g, vector_g, qkv_bg)
    late_came = lax.ppermute(late, "x", [(1, 0)])
    x_scalar = x.astype(jnp.int32).reshape(1)
    sent_g = call(
        both_body, (1,),
        [whole(plane), whole(plane), whole((LATE_ROWS, LANES)), whole((LATE_ROWS, LANES))],
        whole(plane), shaped(plane, BF16), (), 1,
    )(x_scalar, early, early_came, late, late_came)
    got_g = lax.all_to_all(sent_g, RING, 0, 0, tiled=True)
    begin_g = (chunk - PER * D) * owner - skipped * D + 4 * D
    scalars_g = jnp.stack([begin_g // LANES, begin_g % LANES, kind, vector_row]).astype(jnp.int32)
    taken = call(
        grads_in_body, (1,), [whole(got_g.shape)], whole((TAKE_ROWS, LANES)), shaped((TAKE_ROWS, LANES), F32),
        [pltpu.VMEM((SHIFT_ROWS, LANES), F32)], 1,
    )(scalars_g, got_g).reshape(-1)
    from_before = lax.ppermute(taken[D + chunk : 5 * D + chunk], ALL, onward)
    from_after = lax.ppermute(taken[:D], ALL, backward)
    gradients = (
        taken[D : D + chunk]
        + jnp.pad(from_before, (0, chunk - 4 * D))
        + jnp.pad(from_after, (chunk - D, 0))
    )

    outputs = (values + out_rows + (biases[0] + biases[1])).astype(BF16)
    first_token = ((lax.axis_index("z") * 2 + lax.axis_index("y")) * 4 + x * 2 + lax.axis_index("core")) * span
    token = first_token + jnp.arange(span, dtype=jnp.int32)
    live = token[None, :] < lengths[:, None]
    seed = jnp.where(live[:, :, None], cotangent.astype(F32), 0.0)
    unit = (values - middle) * scale
    back = in_rows - jnp.mean(in_rows, axis=-1, keepdims=True)
    back = scale * (back - unit * jnp.mean(in_rows * unit, axis=-1, keepdims=True))
    input_grad = (seed + back).astype(BF16)

    velocity = MOMENTUM * momenta + gradients
    step_rate = LEARN_RATE / math.sqrt(slots * count)
    updated = masters - step_rate * (gradients + MOMENTUM * velocity)
    averaged = AVERAGE_DECAY * averages + (1.0 - AVERAGE_DECAY) * updated
    return (outputs, input_grad, gradients, updated, velocity, averaged)


def solution(mesh):
    fits = mesh.size == OWNERS and mesh.shape["blk"] == 4

    def step(*args):
        slots, tokens = args[0].shape[:2]
        if fits and slots * H == OWNERS and tokens == 64 * OWNERS:
            tokens_in, flat, used, body = P(None, ("z", "y", "x", "core"), None), P(ALL), split_mesh(mesh), by_head
            places = P(None, ("z", "y", "x", "core"))
        else:
            tokens_in, flat, used, body = P(None, ("uly", "blk"), None), P(("blk", "uly")), mesh, local
            places = P(None, ("uly", "blk"))
        return jax.shard_map(
            body,
            mesh=used,
            in_specs=(tokens_in, tokens_in, P(), places, flat, flat, flat),
            out_specs=(tokens_in, tokens_in, flat, flat, flat, flat),
            check_vma=False,
        )(*args)

    return step
```

```python
from functools import partial
import math

import jax
import jax.numpy as jnp
from jax import lax
from jax.experimental import pallas as pl
from jax.experimental.pallas import tpu as pltpu
from jax.sharding import Mesh, PartitionSpec as P

D = 1024
H = 16
HD = 64
ROT = 16
FF = 4096


EPSILON = 1e-05
NEGATIVE = -1e30
MOMENTUM = 0.5
LEARN_RATE = 0.05
AVERAGE_DECAY = 0.5
ROTARY_BASE = 10000.0


def passed_along(block, axis, distance):
    devices = range(lax.axis_size(axis))
    route = [((i - distance) % len(devices), i) for i in devices]
    return lax.ppermute(block, axis, route)


def unpack(flat_vector):
    layouts = [
        (D,),
        (D,),
        (D,),
        (D,),
        (D, 3 * D),
        (3 * D,),
        (D, D),
        (D,),
        (D, FF),
        (FF,),
        (FF, D),
        (D,),
    ]
    pieces = []
    cursor = 0
    for layout in layouts:
        number = math.prod(layout)
        pieces.append(flat_vector[cursor : cursor + number].reshape(layout))
        cursor += number
    return pieces


def layer_norm(values, gain, shift):
    centered = values - jnp.mean(values, axis=-1, keepdims=True)
    variance = jnp.mean(centered * centered, axis=-1, keepdims=True)
    return centered * lax.rsqrt(variance + EPSILON) * gain + shift


def rotary_tables(positions):
    half_dims = ROT // 2
    inverse = ROTARY_BASE ** (-(jnp.arange(half_dims, dtype=jnp.float32) * 2.0 / ROT))
    angles = positions.astype(jnp.float32)[..., None] * inverse
    return (jnp.cos(angles), jnp.sin(angles))


def rotate(values, cos_table, sin_table):
    half_dims = ROT // 2
    first_half = values[..., :half_dims]
    second_half = values[..., half_dims:ROT]
    return jnp.concatenate(
        [
            first_half * cos_table - second_half * sin_table,
            second_half * cos_table + first_half * sin_table,
            values[..., ROT:],
        ],
        axis=-1,
    )


def group_tokens(source, group_count, uly_count, span_rows):
    spans = jnp.arange(uly_count, dtype=jnp.int32)[:, None] * group_count + source
    return (spans * span_rows + jnp.arange(span_rows, dtype=jnp.int32)[None, :]).reshape(-1)


def block_scores(queries, keys_rows, row_tokens, col_tokens, length):
    scores = jnp.einsum(
        "qhd,khd->hqk", queries, keys_rows, preferred_element_type=jnp.float32
    ) * HD ** (-0.5)
    allowed = (col_tokens[None, :] <= row_tokens[:, None]) & (col_tokens[None, :] < length)
    return jnp.where(allowed[None], scores, NEGATIVE)


def is_live(row_tokens, col_tokens, length):
    return (col_tokens[0] <= row_tokens[-1]) & (col_tokens[0] < length)


def fold_stats(row_max, row_total, queries, key_value, lengths, row_tokens, col_tokens):

    def per_slot(inputs):
        slot_max, slot_total, slot_queries, slot_pairs, length = inputs

        def compute(current):
            prev_max, prev_total = current
            scores = block_scores(slot_queries, slot_pairs[:, :, 0], row_tokens, col_tokens, length)
            next_max = jnp.maximum(prev_max, jnp.max(scores, axis=-1))
            next_total = prev_total * jnp.exp(prev_max - next_max) + jnp.sum(
                jnp.exp(scores - next_max[..., None]), axis=-1
            )
            return (next_max, next_total)

        return lax.cond(
            is_live(row_tokens, col_tokens, length),
            compute,
            lambda current: current,
            (slot_max, slot_total),
        )

    return lax.map(per_slot, (row_max, row_total, queries, key_value, lengths))


def fold_values(attended, queries, key_value, log_total, lengths, row_tokens, col_tokens):

    def per_slot(inputs):
        slot_out, slot_queries, slot_pairs, slot_log, length = inputs

        def compute(current):
            scores = block_scores(slot_queries, slot_pairs[:, :, 0], row_tokens, col_tokens, length)
            prob_low = jnp.exp(scores - slot_log[..., None]).astype(jnp.bfloat16)
            return current + jnp.einsum(
                "hqk,khd->qhd", prob_low, slot_pairs[:, :, 1], preferred_element_type=jnp.float32
            )

        return lax.cond(
            is_live(row_tokens, col_tokens, length), compute, lambda current: current, slot_out
        )

    return lax.map(per_slot, (attended, queries, key_value, log_total, lengths))


def fold_grads(
    query_grad,
    pair_grad,
    queries,
    key_value,
    grad_out,
    log_total,
    row_delta,
    lengths,
    row_tokens,
    col_tokens,
):

    def per_slot(inputs):
        (
            slot_qgrad,
            slot_pgrad,
            slot_queries,
            slot_pairs,
            slot_gout,
            slot_log,
            slot_delta,
            length,
        ) = inputs

        def compute(current):
            cur_qgrad, cur_pgrad = current
            scores = block_scores(slot_queries, slot_pairs[:, :, 0], row_tokens, col_tokens, length)
            attend_prob = jnp.exp(scores - slot_log[..., None])
            prob_low = attend_prob.astype(jnp.bfloat16)
            prob_grad = jnp.einsum(
                "qhd,khd->hqk", slot_gout, slot_pairs[:, :, 1], preferred_element_type=jnp.float32
            )
            score_grad = (attend_prob * (prob_grad - slot_delta[..., None])).astype(jnp.bfloat16)
            cur_qgrad = cur_qgrad + jnp.einsum(
                "hqk,khd->qhd", score_grad, slot_pairs[:, :, 0], preferred_element_type=jnp.float32
            ) * HD ** (-0.5)
            key_grad = jnp.einsum(
                "hqk,qhd->khd", score_grad, slot_queries, preferred_element_type=jnp.float32
            ) * HD ** (-0.5)
            value_grad = jnp.einsum(
                "hqk,qhd->khd", prob_low, slot_gout, preferred_element_type=jnp.float32
            )
            return (cur_qgrad, cur_pgrad + jnp.stack([key_grad, value_grad], axis=2))

        return lax.cond(
            is_live(row_tokens, col_tokens, length),
            compute,
            lambda current: current,
            (slot_qgrad, slot_pgrad),
        )

    return lax.map(
        per_slot,
        (query_grad, pair_grad, queries, key_value, grad_out, log_total, row_delta, lengths),
    )


def local(residual, cotangent, lengths, positions, masters, momenta, averages):
    slot_count, span_rows, model_width = residual.shape
    group_count = lax.axis_size("blk")
    uly_count = lax.axis_size("uly")
    group_index = lax.axis_index("blk")
    uly_index = lax.axis_index("uly")
    block_rows = uly_count * span_rows
    full_rows = group_count * block_rows
    local_heads = H // uly_count
    token_rows = slot_count * span_rows
    row_tokens = group_tokens(group_index, group_count, uly_count, span_rows)

    def tokens_of(source):
        return group_tokens(source, group_count, uly_count, span_rows)

    gathered = lax.all_gather(masters.astype(jnp.bfloat16), ("blk", "uly"), axis=0, tiled=True)
    (
        gain_one,
        shift_one,
        gain_two,
        shift_two,
        project_w,
        project_b,
        dense_w,
        dense_b,
        expand_w,
        expand_b,
        shrink_w,
        shrink_b,
    ) = unpack(gathered)
    values = residual.astype(jnp.float32).reshape(token_rows, model_width)
    normed_one, norm_back_one = jax.vjp(
        layer_norm, values, gain_one.astype(jnp.float32), shift_one.astype(jnp.float32)
    )
    normed_two, norm_back_two = jax.vjp(
        layer_norm, values, gain_two.astype(jnp.float32), shift_two.astype(jnp.float32)
    )
    normed_one = normed_one.astype(jnp.bfloat16)
    normed_two = normed_two.astype(jnp.bfloat16)
    mixed_rows = jnp.dot(
        normed_one, project_w, preferred_element_type=jnp.float32
    ) + project_b.astype(jnp.float32)
    mixed_rows = mixed_rows.reshape(slot_count, span_rows, H, 3, HD)
    cos_table, sin_table = rotary_tables(positions)
    cos_table = cos_table[:, :, None, None, :]
    sin_table = sin_table[:, :, None, None, :]
    turned, turn_back = jax.vjp(
        lambda pair_rows: rotate(pair_rows, cos_table, sin_table), mixed_rows[:, :, :, 0:2]
    )
    packed = jnp.concatenate([turned, mixed_rows[:, :, :, 2:3]], axis=3).astype(jnp.bfloat16)
    packed = packed.reshape(slot_count, span_rows, 3 * model_width)
    heads_rows = lax.all_to_all(packed, "uly", split_axis=2, concat_axis=1, tiled=True).reshape(
        slot_count, block_rows, local_heads, 3, HD
    )
    queries = heads_rows[:, :, :, 0]
    key_value = heads_rows[:, :, :, 1:3]
    row_max = jnp.full((slot_count, local_heads, block_rows), NEGATIVE, jnp.float32)
    row_total = jnp.zeros((slot_count, local_heads, block_rows), jnp.float32)
    attended = jnp.zeros((slot_count, block_rows, local_heads, HD), jnp.float32)
    last_tokens = tokens_of((group_index + 1) % group_count)

    def stats_turn(turn_index, carried):
        pairs_now, cur_max, cur_total = carried
        col_tokens = tokens_of((group_index - turn_index) % group_count)
        cur_max, cur_total = fold_stats(
            cur_max, cur_total, queries, pairs_now, lengths, row_tokens, col_tokens
        )
        pairs_now = passed_along(pairs_now, "blk", 1)
        return (pairs_now, cur_max, cur_total)

    pairs_now, row_max, row_total = lax.fori_loop(
        0, group_count - 1, stats_turn, (key_value, row_max, row_total)
    )
    row_max, row_total = fold_stats(
        row_max, row_total, queries, pairs_now, lengths, row_tokens, last_tokens
    )
    log_total = row_max + jnp.log(row_total)

    def value_turn(turn_index, carried):
        pairs_now, cur_out = carried
        col_tokens = tokens_of((group_index - turn_index) % group_count)
        cur_out = fold_values(
            cur_out, queries, pairs_now, log_total, lengths, row_tokens, col_tokens
        )
        pairs_now = passed_along(pairs_now, "blk", 1)
        return (pairs_now, cur_out)

    pairs_now, attended = lax.fori_loop(0, group_count - 1, value_turn, (key_value, attended))
    attended = fold_values(
        attended, queries, pairs_now, log_total, lengths, row_tokens, last_tokens
    )
    heads_out = attended.astype(jnp.bfloat16).reshape(slot_count, block_rows, local_heads * HD)
    merged = lax.all_to_all(heads_out, "uly", split_axis=1, concat_axis=2, tiled=True).reshape(
        token_rows, model_width
    )
    branch_attn = jnp.dot(merged, dense_w, preferred_element_type=jnp.float32) + dense_b.astype(
        jnp.float32
    )
    hidden_pre = jnp.dot(
        normed_two, expand_w, preferred_element_type=jnp.float32
    ) + expand_b.astype(jnp.float32)
    activated, gelu_back = jax.vjp(partial(jax.nn.gelu, approximate=False), hidden_pre)
    activated_low = activated.astype(jnp.bfloat16)
    branch_feed = jnp.dot(
        activated_low, shrink_w, preferred_element_type=jnp.float32
    ) + shrink_b.astype(jnp.float32)
    outputs = (
        (values + branch_attn + branch_feed)
        .astype(jnp.bfloat16)
        .reshape(slot_count, span_rows, model_width)
    )
    first_token = (uly_index * group_count + group_index) * span_rows
    token_index = first_token + jnp.arange(span_rows, dtype=jnp.int32)
    live_mask = (token_index[None, :] < lengths[:, None]).astype(jnp.float32)
    seed_grad = (cotangent.astype(jnp.float32) * live_mask[:, :, None]).reshape(
        token_rows, model_width
    )
    seed_low = seed_grad.astype(jnp.bfloat16)
    dense_w_grad = jnp.einsum("ra,rb->ab", merged, seed_low, preferred_element_type=jnp.float32)
    bias_grad = jnp.sum(seed_low.astype(jnp.float32), axis=0)
    merged_grad = jnp.einsum(
        "rb,ab->ra", seed_low, dense_w, preferred_element_type=jnp.float32
    ).astype(jnp.bfloat16)
    shrink_w_grad = jnp.einsum(
        "rf,rb->fb", activated_low, seed_low, preferred_element_type=jnp.float32
    )
    activated_grad = jnp.einsum("rb,fb->rf", seed_low, shrink_w, preferred_element_type=jnp.float32)
    hidden_grad = gelu_back(activated_grad)[0].astype(jnp.bfloat16)
    expand_w_grad = jnp.einsum(
        "ra,rf->af", normed_two, hidden_grad, preferred_element_type=jnp.float32
    )
    expand_b_grad = jnp.sum(hidden_grad.astype(jnp.float32), axis=0)
    normed_two_grad = jnp.einsum(
        "rf,af->ra", hidden_grad, expand_w, preferred_element_type=jnp.float32
    )
    grad_heads = lax.all_to_all(
        merged_grad.reshape(slot_count, span_rows, model_width),
        "uly",
        split_axis=2,
        concat_axis=1,
        tiled=True,
    )
    grad_out = grad_heads.reshape(slot_count, block_rows, local_heads, HD)
    row_delta = jnp.sum(grad_out.astype(jnp.float32) * attended, axis=-1).transpose(0, 2, 1)
    query_grad = jnp.zeros((slot_count, block_rows, local_heads, HD), jnp.float32)
    pair_grad = jnp.zeros((slot_count, block_rows, local_heads, 2, HD), jnp.float32)

    def grad_turn(turn_index, carried):
        pairs_now, cur_pgrad, cur_qgrad = carried
        col_tokens = tokens_of((group_index - turn_index) % group_count)
        cur_qgrad, cur_pgrad = fold_grads(
            cur_qgrad,
            cur_pgrad,
            queries,
            pairs_now,
            grad_out,
            log_total,
            row_delta,
            lengths,
            row_tokens,
            col_tokens,
        )
        pairs_now = passed_along(pairs_now, "blk", 1)
        cur_pgrad = passed_along(cur_pgrad.astype(jnp.bfloat16), "blk", 1).astype(cur_pgrad.dtype)
        return (pairs_now, cur_pgrad, cur_qgrad)

    pairs_now, pair_grad, query_grad = lax.fori_loop(
        0, group_count - 1, grad_turn, (key_value, pair_grad, query_grad)
    )
    query_grad, pair_grad = fold_grads(
        query_grad,
        pair_grad,
        queries,
        pairs_now,
        grad_out,
        log_total,
        row_delta,
        lengths,
        row_tokens,
        last_tokens,
    )
    pair_grad = passed_along(pair_grad.astype(jnp.bfloat16), "blk", 1).astype(pair_grad.dtype)
    back_packed = jnp.concatenate(
        [query_grad.astype(jnp.bfloat16)[:, :, :, None], pair_grad.astype(jnp.bfloat16)], axis=3
    )
    back_packed = back_packed.reshape(slot_count, block_rows, local_heads * 3 * HD)
    token_grads = lax.all_to_all(
        back_packed, "uly", split_axis=1, concat_axis=2, tiled=True
    ).reshape(slot_count, span_rows, H, 3, HD)
    turned_grad = turn_back(token_grads[:, :, :, 0:2].astype(jnp.float32))[0]
    mixed_grad = jnp.concatenate(
        [turned_grad, token_grads[:, :, :, 2:3].astype(jnp.float32)], axis=3
    ).astype(jnp.bfloat16)
    mixed_grad = mixed_grad.reshape(token_rows, 3 * model_width)
    project_w_grad = jnp.einsum(
        "ra,rc->ac", normed_one, mixed_grad, preferred_element_type=jnp.float32
    )
    project_b_grad = jnp.sum(mixed_grad.astype(jnp.float32), axis=0)
    normed_one_grad = jnp.einsum(
        "rc,ac->ra", mixed_grad, project_w, preferred_element_type=jnp.float32
    )
    values_one, gain_one_grad, shift_one_grad = norm_back_one(normed_one_grad)
    values_two, gain_two_grad, shift_two_grad = norm_back_two(normed_two_grad)
    input_grad = (
        (seed_grad + values_one + values_two)
        .astype(jnp.bfloat16)
        .reshape(slot_count, span_rows, model_width)
    )
    local_grads = jnp.concatenate(
        [
            gain_one_grad,
            shift_one_grad,
            gain_two_grad,
            shift_two_grad,
            project_w_grad.reshape(-1),
            project_b_grad,
            dense_w_grad.reshape(-1),
            bias_grad,
            expand_w_grad.reshape(-1),
            expand_b_grad,
            shrink_w_grad.reshape(-1),
            bias_grad,
        ]
    )
    gradients = lax.psum_scatter(local_grads, ("blk", "uly"), scatter_dimension=0, tiled=True)
    velocity = MOMENTUM * momenta + gradients
    step_rate = LEARN_RATE / math.sqrt(slot_count * full_rows)
    updated = masters - step_rate * (gradients + MOMENTUM * velocity)
    averaged = AVERAGE_DECAY * averages + (1.0 - AVERAGE_DECAY) * updated
    return (outputs, input_grad, gradients, updated, velocity, averaged)


LANES = 128
BLOCK = 256
RING = ("core", "z", "y")
ALL = ("x", "core", "z", "y")
F32 = jnp.float32
BF16 = jnp.bfloat16


def call(body, grid, in_specs, out_specs, out_shape, scratch=(), prefetch=0):
    return pl.pallas_call(
        body,
        grid_spec=pltpu.PrefetchScalarGridSpec(
            num_scalar_prefetch=prefetch,
            grid=grid,
            in_specs=in_specs,
            out_specs=out_specs,
            scratch_shapes=scratch,
        ),
        out_shape=out_shape,
        compiler_params=pltpu.CompilerParams(vmem_limit_bytes=56 << 20),
    )


def whole(shape):
    return pl.BlockSpec(shape, lambda *_: (0,) * len(shape))


def shaped(shape, kind):
    return jax.ShapeDtypeStruct(shape, kind)


def mm(a, b, dims=((1,), (0,))):
    return lax.dot_general(a, b, (dims, ((), ())), preferred_element_type=F32)


def low_lanes(shape):
    return lax.broadcasted_iota(jnp.int32, shape, len(shape) - 1) < LANES // 2


def swap(a):
    return pltpu.roll(a, LANES // 2, 1)


def join(a, a_half, b, b_half):
    first = swap(a) if a_half else a
    second = b if b_half else swap(b)
    return jnp.where(low_lanes(a.shape), first, second)


OWNERS = 32
PER = (3 * D + D + FF + FF) // OWNERS
FLAT = PER * D // LANES
PIECE = FLAT // 16
LEAD = 4 * D // LANES
EDGE = PER * D + 13 * D // OWNERS
PROJECT, PLAIN, PLAIN_EXPAND, EXPAND, EXPAND_PLAIN = range(5)


def plain_place(row, base, count):
    local = row - base
    half = int(local >= count // 2)
    return local - half * (count // 2), half


def dense_place(row):
    if row < 768:
        c = 8 + row // 384
        return (c, 0) + plain_place(row, 384 * (c - 8), 384)
    return (10, 0) + plain_place(row, 768, 256)


def shrink_place(row):
    if row < 256:
        return (21, 64) + plain_place(row, 0, 256)
    c = 22 + (row - 256) // 384
    return (c, 0) + plain_place(row, 256 + 384 * (c - 22), 384)


def expand_places():
    places = [(10, 128, 0, 32)]
    places += [(c, 0, 32 + 96 * (c - 11), 96) for c in range(11, 21)]
    places += [(21, 0, 992, 32)]
    return places


def shifted_rows(source, start, shift, at, rows):
    turn = (LANES - shift) % LANES
    first = pltpu.roll(source[pl.ds(start + at, rows), :], turn, 1)
    second = pltpu.roll(source[pl.ds(start + at + 1, rows), :], turn, 1)
    lane = lax.broadcasted_iota(jnp.int32, (rows, LANES), 1)
    return jnp.where(lane < LANES - shift, first, second)


SHIFT_ROWS = 3200
START, SHIFT, KIND, VECTOR, START_BACK, SHIFT_BACK, HEAD, X, LENGTH, CORE, Y, Z = range(12)
SEND_ROWS = PIECE + 32 + 16
OWN_ROW = 64


def weights_out_body(scalars, before, own, after, places, out, source, flat, tail):
    start, shift, kind, vector_row = scalars[START], scalars[SHIFT], scalars[KIND], scalars[VECTOR]
    count = own.shape[0]
    source[0 : OWN_ROW - 8] = jnp.zeros((OWN_ROW - 8, LANES), F32)
    source[OWN_ROW - 8 : OWN_ROW] = before[...]

    def copy(step, carry):
        at = pl.multiple_of(step * 88, 8)
        source[pl.ds(at + OWN_ROW, 88), :] = own[pl.ds(at, 88), :]
        return carry

    lax.fori_loop(0, count // 88, copy, 0)
    last = OWN_ROW + EDGE // LANES
    source[OWN_ROW + count :] = jnp.zeros((source.shape[0] - OWN_ROW - count, LANES), F32)
    edge = EDGE % LANES
    tail[...] = jnp.zeros(tail.shape, F32)
    tail[7:8] = source[last : last + 1]
    tail[8:40] = pltpu.roll(after[...], edge, 1)
    lane = lax.broadcasted_iota(jnp.int32, (40, LANES), 1)
    source[last : last + 40] = jnp.where(lane < edge, tail[7:47], tail[8:48])

    def align(step, carry):
        at = pl.multiple_of(step * 80, 8)
        flat[pl.ds(at, 80), :] = shifted_rows(source, start, shift, at, 80)
        return carry

    lax.fori_loop(0, SHIFT_ROWS // 80, align, 0)

    def rows(first, count, stride):
        return flat[pl.ds(first, count, stride), :]

    def plain(base, count, to):
        for m in range(8):
            tile = rows(base + m, count, 8)
            a, b = tile[: count // 2], tile[count // 2 :]
            out[2 * m, to : to + count // 2] = join(a, 0, b, 0).astype(BF16)
            out[2 * m + 1, to : to + count // 2] = join(a, 1, b, 1).astype(BF16)

    def expand(base, count, to):
        for r in range(16):
            out[r, to : to + count] = rows(base + 2 * r, count, 32).astype(BF16)
            out[r, to + count : to + 2 * count] = rows(base + 2 * r + 1, count, 32).astype(BF16)

    def project(base):
        for m in range(8):
            first, middle, last = (rows(base + 3 * m + j, 128, 24) for j in range(3))
            out[2 * m, 0:128] = first.astype(BF16)
            out[2 * m, 128:192] = join(middle[:64], 0, middle[64:], 0).astype(BF16)
            out[2 * m + 1, 0:128] = join(middle, 1, last, 0).astype(BF16)
            out[2 * m + 1, 128:192] = join(last[:64], 1, last[64:], 1).astype(BF16)

    @pl.when(kind == PROJECT)
    def _():
        project(LEAD)

    @pl.when(kind == PLAIN)
    def _():
        plain(LEAD, 384, 0)

    @pl.when(kind == PLAIN_EXPAND)
    def _():
        plain(LEAD, 256, 0)
        expand(LEAD + 2048 + 8, 32, 128)

    @pl.when(kind == EXPAND)
    def _():
        expand(LEAD, 96, 0)

    @pl.when(kind == EXPAND_PLAIN)
    def _():
        expand(LEAD, 32, 0)
        plain(LEAD + 1024 + 32, 256, 64)

    vectors = flat[pl.ds(vector_row, 32), :].astype(BF16)
    for r in range(16):
        out[r, PIECE : PIECE + 32] = vectors
        out[r, PIECE + 32 :] = places[...]


def spread(source, at, vectors, to):
    tile = source[pl.ds(at, 8), :].astype(F32)
    for j in range(8):
        vectors[to : to + 1, 128 * j : 128 * j + 128] = tile[j : j + 1]


def weights_in_body(facts, own, came, qkv_w, expand_w, second, vectors, qkv_b, expand_b, places, held, rows):
    head = facts[HEAD]
    low = low_lanes((64, LANES))
    vectors[...] = jnp.zeros(vectors.shape, F32)

    def take(lower, upper, slot):
        def block(c, at, count):
            return (lower if c < 16 else upper)[c % 16, at : at + count]

        for c in range(8):
            qkv_w[128 * c : 128 * c + 128, 0:128] = block(c, 0, 128)
            packed = block(c, 128, 64).astype(F32)
            qkv_w[128 * c : 128 * c + 64, 128:256] = jnp.where(low, packed, 0.0).astype(BF16)
            qkv_w[128 * c + 64 : 128 * c + 128, 128:256] = jnp.where(low, swap(packed), 0.0).astype(BF16)
        for c, at, row, count in expand_places():
            expand_w[row : row + count, 0:128] = block(c, at, count)
            expand_w[row : row + count, 128:256] = block(c, at + count, count)

        def tile(place):
            c, at, row, half = place
            return block(c, at + row, 64).astype(F32), half

        for h in range(16):
            a, half = tile(dense_place(64 * h))
            second[h, 0:32] = join(a[:32], half, a[32:], half).astype(BF16)
            for part in range(2):
                a, half = tile(shrink_place(256 * h + 64 * part))
                b, other = tile(shrink_place(256 * h + 128 + 64 * part))
                second[h, 32 + 64 * part : 96 + 64 * part] = join(a, half, b, other).astype(BF16)
        for group in range(8):
            for x in range(2):
                a, b = (block(16 * x + 8 * core + group, PIECE + 32, 16).astype(F32) for core in range(2))
                a, b = (t[0:1] * 256.0 + t[1:2] for t in (a, b))
                row = 2 * group + x
                places[row : row + 1] = join(a, slot, b, slot)
        held[...] = block(0, PIECE, 32).astype(F32)
        for v in range(4):
            spread(held, 8 * v, vectors, v)
        for to, c in ((4, 10), (5, 31)):
            rows[0:16] = block(c, PIECE, 16).astype(F32)
            spread(rows, 0, vectors, to)
        held[0:24] = block(8, PIECE, 32)[8:].astype(F32)
        rows[...] = block(21, PIECE, 32).astype(F32)

    pl.when(facts[X] == 0)(lambda: take(own, came, 0))
    pl.when(facts[X] != 0)(lambda: take(came, own, 1))
    row = head // 2 * 3
    first, middle, last = (held[pl.ds(row + j, 1), :] for j in range(3))
    odd = head % 2 == 1
    qkv_b[0:1, 0:128] = jnp.where(odd, join(middle, 1, last, 0), first)
    value = jnp.where(odd, swap(last), middle)
    qkv_b[0:1, 128:256] = jnp.where(low_lanes((1, LANES)), value, 0.0)
    expand_b[0:1, 0:128] = rows[pl.ds(2 * head, 1), :]
    expand_b[0:1, 128:256] = rows[pl.ds(2 * head + 1, 1), :]


def rows_in_body(got, dense_w, shrink_w):
    for m in range(8):
        even, odd = got[2 * m].astype(F32), got[2 * m + 1].astype(F32)
        columns = slice(128 * m, 128 * m + 128)
        for out, at, half in ((dense_w, 0, 32), (shrink_w, 32, 128)):
            a, b = even[at : at + half], odd[at : at + half]
            out[0:half, columns] = join(a, 0, b, 0).astype(BF16)
            out[half : 2 * half, columns] = join(a, 1, b, 1).astype(BF16)


def rows_out_body(dense_g, shrink_g, out):
    for m in range(8):
        columns = slice(128 * m, 128 * m + 128)
        for source, at, half in ((dense_g, 0, 32), (shrink_g, 32, 128)):
            a, b = source[0:half, columns], source[half : 2 * half, columns]
            out[2 * m, at : at + half] = join(a, 0, b, 0).astype(BF16)
            out[2 * m + 1, at : at + half] = join(a, 1, b, 1).astype(BF16)


def early_body(scalars, second, expand_g, bias_g, expand_bg, own, other, expand_rows):
    head = scalars[HEAD]
    expand_rows[...] = jnp.zeros(expand_rows.shape, F32)
    expand_rows[pl.ds(2 * head, 1), :] = expand_bg[0:1, 0:128]
    expand_rows[pl.ds(2 * head + 1, 1), :] = expand_bg[0:1, 128:256]
    rows = [bias_g[0:1, 128 * j : 128 * j + 128] for j in range(8)]
    bias = jnp.concatenate(rows + [jnp.zeros((8, LANES), F32)], axis=0).astype(BF16)

    def dense_rows(row):
        packed = second[row // 64, 0:32].astype(F32)
        return jnp.concatenate([packed, swap(packed)], axis=0)

    def shrink_rows(row):
        h, part = row // 256, row % 256 // 64
        packed = second[h, 32 + part % 2 * 64 : 96 + part % 2 * 64].astype(F32)
        return swap(packed) if part >= 2 else packed

    def put(lower, upper):
        def store(c, at, tile):
            (lower if c < 16 else upper)[c % 16, at : at + tile.shape[0]] = tile

        def plain(c, to, base, count, take):
            for i in range(count // 128):
                a, b = take(base + 64 * i), take(base + count // 2 + 64 * i)
                store(c, to + 64 * i, join(a, 0, b, 0).astype(BF16))

        for c in range(8):
            store(c, 0, jnp.zeros((PIECE, LANES), BF16))
        for c in range(OWNERS):
            store(c, PIECE, jnp.zeros((32, LANES), BF16))
        for c, at, row, count in expand_places():
            store(c, at, expand_g[row : row + count, 0:128].astype(BF16))
            store(c, at + count, expand_g[row : row + count, 128:256].astype(BF16))
        plain(8, 0, 0, 384, dense_rows)
        plain(9, 0, 384, 384, dense_rows)
        plain(10, 0, 768, 256, dense_rows)
        plain(21, 64, 0, 256, shrink_rows)
        for c in range(22, 32):
            plain(c, 0, 256 + 384 * (c - 22), 384, shrink_rows)
        store(10, PIECE, bias)
        store(31, PIECE, bias)
        store(21, PIECE, expand_rows[...].astype(BF16))

    pl.when(scalars[X] == 0)(lambda: put(own, other))
    pl.when(scalars[X] != 0)(lambda: put(other, own))


LATE_ROWS = 8 * PIECE + 64


def late_body(scalars, qkv_g, vector_g, qkv_bg, out, project_rows):
    head = scalars[HEAD]
    for c in range(8):
        at = PIECE * c
        out[at : at + 128] = qkv_g[128 * c : 128 * c + 128, 0:128].astype(BF16)
        a = qkv_g[128 * c : 128 * c + 64, 128:256]
        b = qkv_g[128 * c + 64 : 128 * c + 128, 128:256]
        out[at + 128 : at + 192] = join(a, 0, b, 0).astype(BF16)
    gains = [vector_g[v : v + 1, 128 * j : 128 * j + 128] for v in range(4) for j in range(8)]
    out[8 * PIECE : 8 * PIECE + 32] = jnp.concatenate(gains, axis=0).astype(BF16)
    project_rows[...] = jnp.zeros(project_rows.shape, F32)
    pair, value = qkv_bg[0:1, 0:128], qkv_bg[0:1, 128:256]
    low = low_lanes((1, LANES))
    row = 8 + head // 2 * 3
    odd = head % 2 == 1
    project_rows[pl.ds(row, 1), :] = jnp.where(odd, 0.0, pair)
    project_rows[pl.ds(row + 1, 1), :] = jnp.where(
        odd, jnp.where(low, 0.0, swap(pair)), jnp.where(low, value, 0.0)
    )
    project_rows[pl.ds(row + 2, 1), :] = jnp.where(odd, join(pair, 1, value, 0), 0.0)
    out[8 * PIECE + 32 :] = project_rows[...].astype(BF16)


def both_body(scalars, early, early_came, late, late_came, out):
    def add(r, carry):
        out[r] = (early[r].astype(F32) + early_came[r].astype(F32)).astype(BF16)
        return carry

    lax.fori_loop(0, 16, add, 0)

    @pl.when(scalars[X] == 0)
    def _():
        def total(at, count):
            return (late[at : at + count].astype(F32) + late_came[at : at + count].astype(F32)).astype(BF16)

        for c in range(8):
            out[c, 0:PIECE] = total(PIECE * c, PIECE)
        out[0, PIECE : PIECE + 32] = total(8 * PIECE, 32)
        out[8, PIECE : PIECE + 32] = total(8 * PIECE + 32, 32)


BACK_ROWS = PIECE + 32
TAKE_ROWS = 3120


def grads_in_body(scalars, got, out, flat):
    start, shift, kind, vector_row = scalars[START_BACK], scalars[SHIFT_BACK], scalars[KIND], scalars[VECTOR]
    lead = LEAD + 8

    def clear(step, carry):
        flat[pl.ds(pl.multiple_of(step * 80, 8), 80), :] = jnp.zeros((80, LANES), F32)
        return carry

    lax.fori_loop(0, SHIFT_ROWS // 80, clear, 0)

    def add_vectors(source, total):
        return total + got[source, PIECE : PIECE + 32].astype(F32)

    flat[pl.ds(vector_row + 8, 32), :] = lax.fori_loop(0, 16, add_vectors, jnp.zeros((32, LANES), F32))

    def taken(r, at, count):
        return got[r, at : at + count].astype(F32)

    def plain(base, count, at):
        half = count // 2
        for m in range(8):
            a, b = taken(2 * m, at, half), taken(2 * m + 1, at, half)
            flat[pl.ds(base + m, half, 8), :] = join(a, 0, b, 0)
            flat[pl.ds(base + m + 8 * half, half, 8), :] = join(a, 1, b, 1)

    def expand(base, count, at):
        for r in range(16):
            flat[pl.ds(base + 2 * r, count, 32), :] = taken(r, at, count)
            flat[pl.ds(base + 2 * r + 1, count, 32), :] = taken(r, at + count, count)

    def project(base):
        for m in range(8):
            pair, values = taken(2 * m, 0, 128), taken(2 * m, 128, 64)
            odd_pair, odd_values = taken(2 * m + 1, 0, 128), taken(2 * m + 1, 128, 64)
            values = jnp.concatenate([values, swap(values)], axis=0)
            odd_values = jnp.concatenate([odd_values, swap(odd_values)], axis=0)
            flat[pl.ds(base + 3 * m, 128, 24), :] = pair
            flat[pl.ds(base + 3 * m + 1, 128, 24), :] = join(values, 0, odd_pair, 0)
            flat[pl.ds(base + 3 * m + 2, 128, 24), :] = join(odd_pair, 1, odd_values, 0)

    @pl.when(kind == PROJECT)
    def _():
        project(lead)

    @pl.when(kind == PLAIN)
    def _():
        plain(lead, 384, 0)

    @pl.when(kind == PLAIN_EXPAND)
    def _():
        plain(lead, 256, 0)
        expand(lead + 2048 + 8, 32, 128)

    @pl.when(kind == EXPAND)
    def _():
        expand(lead, 96, 0)

    @pl.when(kind == EXPAND_PLAIN)
    def _():
        expand(lead, 32, 0)
        plain(lead + 1024 + 32, 256, 64)

    def align(step, carry):
        at = pl.multiple_of(step * 80, 8)
        out[pl.ds(at, 80), :] = shifted_rows(flat, start, shift, at, 80)
        return carry

    lax.fori_loop(0, TAKE_ROWS // 80, align, 0)


def token_rows(ref):
    return jnp.concatenate([ref[0, 0, 0], ref[1, 0, 0], ref[0, 0, 1], ref[1, 0, 1]], axis=0)


def put_rows(kept, sent, rows, core):
    step = rows.shape[0] // 4
    for x in range(2):
        first, second = (rows[step * i : step * i + step].astype(BF16) for i in (2 * x, 2 * x + 1))
        kept[0, x] = jnp.where(core == 0, first, second)
        sent[0, x] = jnp.where(core == 0, second, first)


def relative_place(i, here):
    y = (i & 1) ^ here[Y]
    z = (i >> 1) ^ here[Z]
    return y * 4 + (z & 1) * 2 + (z >> 1)


def normalized(values):
    centered = values - jnp.mean(values, axis=-1, keepdims=True)
    variance = jnp.mean(centered * centered, axis=-1, keepdims=True)
    return centered * lax.rsqrt(variance + EPSILON)


def turned(pair, cos, sin):
    lane = lax.broadcasted_iota(jnp.int32, pair.shape, 1) % HD
    half = ROT // 2
    other = jnp.where(
        lane < half, -pltpu.roll(pair, LANES - half, 1), jnp.where(lane < ROT, pltpu.roll(pair, half, 1), 0.0)
    )
    return pair * cos + other * sin


def mixed_body(tokens, places, vectors, qkv_w, qkv_b, inverse, one, two, query, key, value, cos, sin):
    unit = normalized(token_rows(tokens).astype(F32))
    at = 2 * pl.program_id(0)
    place = [jnp.broadcast_to(places[pl.ds(at + x, 1), :], (LANES, LANES)).T for x in range(2)]
    angles = jnp.concatenate(place, axis=0) * inverse[...]
    cos[...] = jnp.cos(angles)
    sin[...] = jnp.sin(angles)
    first = (unit * vectors[0:1] + vectors[1:2]).astype(BF16)
    one[...] = first
    two[...] = (unit * vectors[2:3] + vectors[3:4]).astype(BF16)
    mixed = mm(first, qkv_w[...]) + qkv_b[...]
    pair = turned(mixed[:, :LANES], cos[...], sin[...])
    query[...] = pair[:, :HD].astype(BF16) * HD ** (-0.5)
    key[...] = pair[:, HD:].astype(BF16)
    value[...] = mixed[:, LANES : LANES + HD].astype(BF16)


def masked_scores(key, query_t, at, first_query, length):
    scores = mm(key, query_t)
    keys = at * BLOCK + lax.broadcasted_iota(jnp.int32, scores.shape, 0)
    queries = first_query + lax.broadcasted_iota(jnp.int32, scores.shape, 1)
    return jnp.where((keys <= queries) & (keys < length), scores, NEGATIVE)


def folded(values, op):
    parts = [values[8 * i : 8 * i + 8] for i in range(values.shape[0] // 8)]
    while len(parts) > 1:
        parts = [op(a, b) for a, b in zip(parts[::2], parts[1::2])]
    return parts[0]


def attend_body(lengths, query, key, value, low_out, full_out, log_out, scores, value_t):
    at = pl.program_id(0)
    length = lengths[LENGTH]

    @pl.when(at == 0)
    def _():
        value_t[...] = value[...].astype(F32).T.astype(BF16)

    query_t = query[...].astype(F32).T.astype(BF16)
    clear = jnp.minimum(at, length // BLOCK)
    stop = jnp.minimum(at, (length - 1) // BLOCK) + 1

    def rows(j):
        return pl.ds(pl.multiple_of(j * BLOCK, BLOCK), BLOCK)

    def score(j, top, masked):
        if masked:
            tile = masked_scores(key[rows(j), :], query_t, j, at * BLOCK, length)
        else:
            tile = mm(key[rows(j), :], query_t)
        scores[rows(j), :] = tile
        return jnp.maximum(top, folded(tile, jnp.maximum))

    top = jnp.full((8, BLOCK), NEGATIVE, F32)
    top = lax.fori_loop(0, clear, lambda j, t: score(j, t, False), top)
    top = lax.fori_loop(clear, stop, lambda j, t: score(j, t, True), top)
    top = jnp.max(top, axis=0, keepdims=True)

    def weigh(j, carried):
        total, out = carried
        tile = jnp.exp(scores[rows(j), :] - top)
        return total + folded(tile, jnp.add), out + mm(value_t[:, rows(j)], tile.astype(BF16))

    start = (jnp.zeros((8, BLOCK), F32), jnp.zeros((HD, BLOCK), F32))
    total, out = lax.fori_loop(0, stop, weigh, start)
    total = jnp.sum(total, axis=0, keepdims=True)
    out = out * (1.0 / total)
    full_out[...] = out
    low_out[...] = out.T.astype(BF16)
    log_out[...] = top + jnp.log(total)


def attend_back_body(
    lengths, query, key, value, grad, full_out, log_in, query_g, key_g, value_g, key_t, key_sum, value_sum
):
    at = pl.program_id(0)
    length = lengths[LENGTH]

    @pl.when(at == 0)
    def _():
        key_t[...] = key[...].astype(F32).T.astype(BF16)
        key_sum[...] = jnp.zeros(key_sum.shape, F32)
        value_sum[...] = jnp.zeros(value_sum.shape, F32)

    query_rows, grad_rows = query[...], grad[...]
    query_t = query_rows.astype(F32).T.astype(BF16)
    grad_full_t = grad_rows.astype(F32).T
    grad_t = grad_full_t.astype(BF16)
    delta = jnp.sum(grad_full_t * full_out[...], axis=0, keepdims=True)
    log_total = log_in[...]
    clear = jnp.minimum(at, length // BLOCK)
    stop = jnp.minimum(at, (length - 1) // BLOCK) + 1
    clear, stop = (jnp.where(at * BLOCK < length, n, 0) for n in (clear, stop))

    def step(j, query_sum, masked):
        rows = pl.ds(pl.multiple_of(j * BLOCK, BLOCK), BLOCK)
        if masked:
            tile = masked_scores(key[rows, :], query_t, j, at * BLOCK, length)
        else:
            tile = mm(key[rows, :], query_t)
        probs = jnp.exp(tile - log_total)
        value_sum[rows, :] += mm(probs.astype(BF16), grad_rows)
        score_g = (probs * (mm(value[rows, :], grad_t) - delta)).astype(BF16)
        key_sum[rows, :] += mm(score_g, query_rows)
        return query_sum + mm(key_t[:, rows], score_g)

    query_sum = jnp.zeros((HD, BLOCK), F32)
    query_sum = lax.fori_loop(0, clear, lambda j, s: step(j, s, False), query_sum)
    query_sum = lax.fori_loop(clear, stop, lambda j, s: step(j, s, True), query_sum)
    query_g[...] = (query_sum * HD ** (-0.5)).T.astype(BF16)

    @pl.when(at == pl.num_programs(0) - 1)
    def _():
        key_g[...] = key_sum[...].astype(BF16)
        value_g[...] = value_sum[...].astype(BF16)


def feed_body(
    here, two, attended, cotangent, expand_w, expand_b, shrink_w, dense_w,
    partial_out, attended_g, hidden_g, shrink_g, dense_g, expand_g, expand_bg, bias_g,
):
    at = pl.program_id(0)

    @pl.when(at == 0)
    def _():
        for total in (shrink_g, dense_g, expand_g, expand_bg, bias_g):
            total[...] = jnp.zeros(total.shape, F32)

    normed, mixed = two[...], attended[...]
    hidden = mm(normed, expand_w[...]) + expand_b[...]
    error = lax.erf(hidden * math.sqrt(0.5))
    cumulative = 0.5 * (1.0 + error)
    active = (hidden * cumulative).astype(BF16)
    partial = mm(mixed, dense_w[...]) + mm(active, shrink_w[...])
    step = BLOCK // 4
    for i, (core, x) in enumerate(((0, 0), (1, 0), (0, 1), (1, 1))):
        partial_out[core, 0, x] = partial[step * i : step * i + step].astype(BF16)
    token = at * BLOCK + lax.broadcasted_iota(jnp.int32, (BLOCK, D), 0)
    seed = jnp.where(token < here[LENGTH], token_rows(cotangent).astype(F32), 0.0)
    bias_g[...] += jnp.sum(seed, axis=0, keepdims=True)
    seed = seed.astype(BF16)
    attended_g[...] = mm(seed, dense_w[...], ((1,), (1,))).astype(BF16)
    slope = cumulative + hidden * jnp.exp(-0.5 * hidden * hidden) * (1.0 / math.sqrt(2.0 * math.pi))
    back = (mm(seed, shrink_w[...], ((1,), (1,))) * slope).astype(BF16)
    hidden_g[...] = back
    expand_bg[...] += jnp.sum(back.astype(F32), axis=0, keepdims=True)
    shrink_g[...] += mm(active, seed, ((0,), (0,)))
    dense_g[...] += mm(mixed, seed, ((0,), (0,)))
    expand_g[...] += mm(normed, back, ((0,), (0,)))


def mixed_back_body(
    here, tokens, one, query_g, key_g, value_g, hidden_g, vectors, qkv_w, expand_w, cos, sin,
    kept, sent, qkv_g, qkv_bg, vector_g,
):
    at = pl.program_id(0)

    @pl.when(at == 0)
    def _():
        for total in (qkv_g, qkv_bg, vector_g):
            total[...] = jnp.zeros(total.shape, F32)

    pair = jnp.concatenate([query_g[...].astype(F32), key_g[...].astype(F32)], axis=1)
    pair = turned(pair, cos[...], -sin[...])
    values = value_g[...].astype(F32)
    mixed_g = jnp.concatenate([pair, values, jnp.zeros_like(values)], axis=1)
    mixed_low = mixed_g.astype(BF16)
    qkv_bg[...] += jnp.sum(mixed_low.astype(F32), axis=0, keepdims=True)
    qkv_g[...] += mm(one[...], mixed_low, ((0,), (0,)))
    one_g = mm(mixed_low, qkv_w[...], ((1,), (1,)))
    two_g = mm(hidden_g[...], expand_w[...], ((1,), (1,)))
    unit = normalized(token_rows(tokens).astype(F32))
    vector_g[0:1] += jnp.sum(one_g * unit, axis=0, keepdims=True)
    vector_g[1:2] += jnp.sum(one_g, axis=0, keepdims=True)
    vector_g[2:3] += jnp.sum(two_g * unit, axis=0, keepdims=True)
    vector_g[3:4] += jnp.sum(two_g, axis=0, keepdims=True)
    put_rows(kept, sent, one_g * vectors[0:1] + two_g * vectors[2:3], here[CORE])


def split_mesh(mesh):
    groups, members = mesh.shape["blk"], mesh.shape["uly"]
    return Mesh(mesh.devices.reshape(groups // 2, 2, members // 2, 2), ALL)


def across_x(block):
    return lax.ppermute(block, "x", [(0, 1), (1, 0)])


def by_head(residual, cotangent, lengths, positions, masters, momenta, averages):
    slots, span, width = residual.shape
    x = lax.axis_index("x")
    head = lax.axis_index("core") * 8 + lax.axis_index("z") * 2 + lax.axis_index("y")
    owner = x * 16 + head
    groups = lax.axis_size("z") * lax.axis_size("y")
    count = groups * 4 * span
    chunk = masters.shape[0]
    length = lax.dynamic_slice_in_dim(lengths, x, 1)

    def paired(mine, theirs):
        return jnp.where(x == 0, jnp.stack([mine, theirs]), jnp.stack([theirs, mine]))

    def at_x(rows, index):
        return lax.dynamic_index_in_dim(rows, index, 0, keepdims=False)

    rows = jnp.stack([residual, cotangent], axis=1)
    rows = paired(at_x(rows, x), across_x(at_x(rows, 1 - x)))
    places = positions.reshape(1, 2 * span)
    tokens_shape = (2, groups, 2, span, width)
    slot_tokens = lax.all_gather(rows[:, 0], RING, axis=0).reshape(tokens_shape)
    slot_cotangent = lax.all_gather(rows[:, 1], RING, axis=0).reshape(tokens_shape)
    high, rest = (places // 256).astype(BF16), (places % 256).astype(BF16)
    places = jnp.concatenate([high, rest, jnp.zeros((14, 2 * span), BF16)])
    lane = jnp.arange(LANES, dtype=jnp.int32) % HD
    inverse = ROTARY_BASE ** (-((lane % (ROT // 2)).astype(F32) * 2.0 / ROT))
    inverse = jnp.where(lane < ROT, inverse, 0.0)[None, :]

    onward = [(i, i + 1) for i in range(OWNERS - 1)]
    backward = [(i + 1, i) for i in range(OWNERS - 1)]
    before = lax.ppermute(masters[chunk - D :], ALL, onward)
    after = lax.ppermute(masters[: 4 * D], ALL, backward)
    own_rows = -(-chunk // D) * 8
    own = jnp.pad(masters, (0, own_rows * LANES - chunk)).reshape(own_rows, LANES)
    before, after = before.reshape(8, LANES), after.reshape(32, LANES)
    skipped = jnp.where(owner < 8, 4, jnp.where(owner < 11, 7, jnp.where(owner < 22, 8, 12)))
    kind = jnp.where(
        owner < 8,
        PROJECT,
        jnp.where(
            owner == 10,
            PLAIN_EXPAND,
            jnp.where(owner == 21, EXPAND_PLAIN, jnp.where((owner > 10) & (owner < 21), EXPAND, PLAIN)),
        ),
    )
    vector_row = jnp.where(owner == 10, 2080, jnp.where(owner == 21, 1056, jnp.where(owner == 31, 3104, 0)))
    ahead = skipped * D - (chunk - PER * D) * owner
    begin = ahead + 4 * D
    begin_g = (chunk - PER * D) * owner - skipped * D + 4 * D
    y, z, core = lax.axis_index("y"), lax.axis_index("z"), lax.axis_index("core")
    facts = [begin // LANES, begin % LANES, kind, vector_row, begin_g // LANES, begin_g % LANES]
    facts = jnp.stack(facts + [head, x, length[0], core, y, z]).astype(jnp.int32)
    sent = call(
        weights_out_body, (1,),
        [whole(before.shape), whole(own.shape), whole(after.shape), whole(places.shape)],
        whole((16, SEND_ROWS, LANES)),
        shaped((16, SEND_ROWS, LANES), BF16),
        [pltpu.VMEM((3280, LANES), F32), pltpu.VMEM((SHIFT_ROWS, LANES), F32), pltpu.VMEM((48, LANES), F32)],
        1,
    )(facts, before, own, after, places)
    got = lax.all_to_all(sent, RING, 0, 0, tiled=True)
    came = across_x(got)
    qkv_w, expand_w, second, vectors, qkv_b, expand_b, places = call(
        weights_in_body, (1,),
        [whole(got.shape), whole(got.shape)],
        [whole((D, 256)), whole((D, 256)), whole((16, 160, LANES)), whole((8, D)), whole((1, 256)), whole((1, 256)),
         whole((16, LANES))],
        [shaped((D, 256), BF16), shaped((D, 256), BF16), shaped((16, 160, LANES), BF16), shaped((8, D), F32),
         shaped((1, 256), F32), shaped((1, 256), F32), shaped((16, LANES), F32)],
        [pltpu.VMEM((32, LANES), F32), pltpu.VMEM((32, LANES), F32)], 1,
    )(facts, got, came)
    second = lax.all_to_all(second, RING, 0, 0, tiled=True)
    steps = (count // BLOCK,)
    token_spec = pl.BlockSpec((2, 1, 2, span, width), lambda i, *_: (0, i, 0, 0, 0))
    part_spec = pl.BlockSpec((1, 2, span, width), lambda i, here: (relative_place(i, here), 0, 0, 0))
    part_shape = shaped((groups, 2, span, width), BF16)
    swap_pair, far_pairs = [(0, 1), (1, 0)], [(0, 2), (2, 0), (1, 3), (3, 1)]

    def summed(kept, sent):
        left = kept.shape[0]
        for axis, route in (
            ("core", swap_pair), ("y", swap_pair), ("z", swap_pair + [(2, 3), (3, 2)]), ("z", far_pairs)
        ):
            came = lax.ppermute(sent, axis, route)
            if left == 1:
                return (kept[0].astype(F32) + came[0].astype(F32)).astype(BF16)
            left //= 2
            kept, sent = [
                (kept[half].astype(F32) + came[half].astype(F32)).astype(BF16)
                for half in (slice(0, left), slice(left, None))
            ]

    def to_owner(rows):
        mine, theirs = at_x(rows, x), at_x(rows, 1 - x)
        return paired(mine, across_x(theirs)).astype(F32)

    def rows_spec(columns):
        return pl.BlockSpec((BLOCK, columns), lambda i, *_: (i, 0))

    def columns_spec(rows):
        return pl.BlockSpec((rows, BLOCK), lambda i, *_: (0, i))

    narrow = shaped((count, HD), BF16)
    table = shaped((count, LANES), F32)
    one, two, query, key, value, cos, sin = call(
        mixed_body, steps,
        [token_spec, whole((16, LANES)), whole((8, D)), whole((D, 256)), whole((1, 256)), whole((1, LANES))],
        [rows_spec(D), rows_spec(D), rows_spec(HD), rows_spec(HD), rows_spec(HD), rows_spec(LANES), rows_spec(LANES)],
        [shaped((count, D), BF16), shaped((count, D), BF16), narrow, narrow, narrow, table, table],
    )(slot_tokens, places, vectors, qkv_w, qkv_b, inverse)
    attended, attended_full, log_total = call(
        attend_body, steps,
        [rows_spec(HD), whole((count, HD)), whole((count, HD))],
        [rows_spec(HD), columns_spec(HD), columns_spec(1)],
        [narrow, shaped((HD, count), F32), shaped((1, count), F32)],
        [pltpu.VMEM((count, BLOCK), F32), pltpu.VMEM((HD, count), BF16)], 1,
    )(facts, query, key, value)
    second, attended = lax.optimization_barrier((second, attended))
    dense_w, shrink_w = call(
        rows_in_body, (1,), [whole(second.shape)], [whole((HD, D)), whole((256, D))],
        [shaped((HD, D), BF16), shaped((256, D), BF16)],
    )(second)

    partial_out, attended_g, hidden_g, shrink_g, dense_g, expand_g, expand_bg, bias_g = call(
        feed_body, steps,
        [rows_spec(D), rows_spec(HD), token_spec, whole((D, 256)), whole((1, 256)), whole((256, D)), whole((HD, D))],
        [token_spec, rows_spec(HD), rows_spec(256), whole((256, D)), whole((HD, D)), whole((D, 256)),
         whole((1, 256)), whole((1, D))],
        [shaped(tokens_shape, BF16), narrow, shaped((count, 256), BF16), shaped((256, D), F32), shaped((HD, D), F32),
         shaped((D, 256), F32), shaped((1, 256), F32), shaped((1, D), F32)], (), 1,
    )(facts, two, attended, slot_cotangent, expand_w, expand_b, shrink_w, dense_w)
    second_g = call(
        rows_out_body, (1,), [whole((HD, D)), whole((256, D))], whole((16, 160, LANES)),
        shaped((16, 160, LANES), BF16),
    )(dense_g, shrink_g)
    attended_g, second_g = lax.optimization_barrier((attended_g, second_g))
    second_g = lax.all_to_all(second_g, RING, 0, 0, tiled=True)
    out_rows = lax.psum_scatter(
        partial_out.reshape(16, 2, span, width), RING, scatter_dimension=0, tiled=True
    )[0]
    out_rows = to_owner(out_rows)
    query_g, key_g, value_g = call(
        attend_back_body, steps,
        [rows_spec(HD), whole((count, HD)), whole((count, HD)), rows_spec(HD), columns_spec(HD), columns_spec(1)],
        [rows_spec(HD), whole((count, HD)), whole((count, HD))],
        [narrow, narrow, narrow],
        [pltpu.VMEM((HD, count), BF16), pltpu.VMEM((count, HD), F32), pltpu.VMEM((count, HD), F32)],
        1,
    )(facts, query, key, value, attended_g, attended_full, log_total)
    bias_g = jnp.where(head == 0, bias_g, 0.0)
    plane = (16, BACK_ROWS, LANES)
    early, early_other = call(
        early_body, (1,),
        [whole((16, 160, LANES)), whole((D, 256)), whole((1, D)), whole((1, 256))],
        [whole(plane), whole(plane)],
        [shaped(plane, BF16), shaped(plane, BF16)],
        [pltpu.VMEM((32, LANES), F32)], 1,
    )(facts, second_g, expand_g, bias_g, expand_bg)
    early_came = across_x(early_other)
    kept, sent, qkv_g, qkv_bg, vector_g = call(
        mixed_back_body, steps,
        [token_spec, rows_spec(D), rows_spec(HD), rows_spec(HD), rows_spec(HD),
         rows_spec(256), whole((8, D)), whole((D, 256)), whole((D, 256)), rows_spec(LANES), rows_spec(LANES)],
        [part_spec, part_spec, whole((D, 256)), whole((1, 256)), whole((8, D))],
        [part_shape, part_shape, shaped((D, 256), F32), shaped((1, 256), F32), shaped((8, D), F32)], (), 1,
    )(facts, slot_tokens, one, query_g, key_g, value_g, hidden_g, vectors, qkv_w, expand_w, cos, sin)
    in_rows = to_owner(summed(kept, sent))

    values = residual.astype(F32)
    middle = jnp.mean(values, axis=-1, keepdims=True)
    scale = lax.rsqrt(jnp.mean((values - middle) ** 2, axis=-1, keepdims=True) + EPSILON)
    middle, scale = lax.optimization_barrier((middle, scale))

    late = call(
        late_body, (1,), [whole((D, 256)), whole((8, D)), whole((1, 256))], whole((LATE_ROWS, LANES)),
        shaped((LATE_ROWS, LANES), BF16), [pltpu.VMEM((32, LANES), F32)], 1,
    )(facts, qkv_g, vector_g, qkv_bg)
    late_came = lax.ppermute(late, "x", [(1, 0)])
    sent_g = call(
        both_body, (1,),
        [whole(plane), whole(plane), whole((LATE_ROWS, LANES)), whole((LATE_ROWS, LANES))],
        whole(plane), shaped(plane, BF16), (), 1,
    )(facts, early, early_came, late, late_came)
    got_g = lax.all_to_all(sent_g, RING, 0, 0, tiled=True)
    taken = call(
        grads_in_body, (1,), [whole(got_g.shape)], whole((TAKE_ROWS, LANES)), shaped((TAKE_ROWS, LANES), F32),
        [pltpu.VMEM((SHIFT_ROWS, LANES), F32)], 1,
    )(facts, got_g).reshape(-1)
    from_before = lax.ppermute(taken[D + chunk : 5 * D + chunk], ALL, onward)
    from_after = lax.ppermute(taken[:D], ALL, backward)
    gradients = (
        taken[D : D + chunk]
        + jnp.pad(from_before, (0, chunk - 4 * D))
        + jnp.pad(from_after, (chunk - D, 0))
    )

    outputs = (values + out_rows + (vectors[4] + vectors[5])).astype(BF16)
    first_token = ((lax.axis_index("z") * 2 + lax.axis_index("y")) * 4 + x * 2 + lax.axis_index("core")) * span
    token = first_token + jnp.arange(span, dtype=jnp.int32)
    live = token[None, :] < lengths[:, None]
    seed = jnp.where(live[:, :, None], cotangent.astype(F32), 0.0)
    unit = (values - middle) * scale
    back = in_rows - jnp.mean(in_rows, axis=-1, keepdims=True)
    back = scale * (back - unit * jnp.mean(in_rows * unit, axis=-1, keepdims=True))
    input_grad = (seed + back).astype(BF16)

    velocity = MOMENTUM * momenta + gradients
    step_rate = LEARN_RATE / math.sqrt(slots * count)
    updated = masters - step_rate * (gradients + MOMENTUM * velocity)
    averaged = AVERAGE_DECAY * averages + (1.0 - AVERAGE_DECAY) * updated
    return (outputs, input_grad, gradients, updated, velocity, averaged)


def solution(mesh):
    fits = mesh.size == OWNERS and mesh.shape["blk"] == 4

    def step(*args):
        slots, tokens = args[0].shape[:2]
        if fits and slots * H == OWNERS and tokens == 64 * OWNERS:
            tokens_in, flat, used, body = P(None, ("z", "y", "x", "core"), None), P(ALL), split_mesh(mesh), by_head
            places = P(None, ("z", "y", "x", "core"))
        else:
            tokens_in, flat, used, body = P(None, ("uly", "blk"), None), P(("blk", "uly")), mesh, local
            places = P(None, ("uly", "blk"))
        return jax.shard_map(
            body,
            mesh=used,
            in_specs=(tokens_in, tokens_in, P(), places, flat, flat, flat),
            out_specs=(tokens_in, tokens_in, flat, flat, flat, flat),
            check_vma=False,
        )(*args)

    return step
```

```python
from functools import partial
import math

import jax
import jax.numpy as jnp
from jax import lax
from jax.experimental import pallas as pl
from jax.experimental.pallas import tpu as pltpu
from jax.sharding import Mesh, PartitionSpec as P

D = 1024
H = 16
HD = 64
ROT = 16
FF = 4096


EPSILON = 1e-05
NEGATIVE = -1e30
MOMENTUM = 0.5
LEARN_RATE = 0.05
AVERAGE_DECAY = 0.5
ROTARY_BASE = 10000.0


def passed_along(block, axis, distance):
    devices = range(lax.axis_size(axis))
    route = [((i - distance) % len(devices), i) for i in devices]
    return lax.ppermute(block, axis, route)


def unpack(flat_vector):
    layouts = [
        (D,),
        (D,),
        (D,),
        (D,),
        (D, 3 * D),
        (3 * D,),
        (D, D),
        (D,),
        (D, FF),
        (FF,),
        (FF, D),
        (D,),
    ]
    pieces = []
    cursor = 0
    for layout in layouts:
        number = math.prod(layout)
        pieces.append(flat_vector[cursor : cursor + number].reshape(layout))
        cursor += number
    return pieces


def layer_norm(values, gain, shift):
    centered = values - jnp.mean(values, axis=-1, keepdims=True)
    variance = jnp.mean(centered * centered, axis=-1, keepdims=True)
    return centered * lax.rsqrt(variance + EPSILON) * gain + shift


def rotary_tables(positions):
    half_dims = ROT // 2
    inverse = ROTARY_BASE ** (-(jnp.arange(half_dims, dtype=jnp.float32) * 2.0 / ROT))
    angles = positions.astype(jnp.float32)[..., None] * inverse
    return (jnp.cos(angles), jnp.sin(angles))


def rotate(values, cos_table, sin_table):
    half_dims = ROT // 2
    first_half = values[..., :half_dims]
    second_half = values[..., half_dims:ROT]
    return jnp.concatenate(
        [
            first_half * cos_table - second_half * sin_table,
            second_half * cos_table + first_half * sin_table,
            values[..., ROT:],
        ],
        axis=-1,
    )


def group_tokens(source, group_count, uly_count, span_rows):
    spans = jnp.arange(uly_count, dtype=jnp.int32)[:, None] * group_count + source
    return (spans * span_rows + jnp.arange(span_rows, dtype=jnp.int32)[None, :]).reshape(-1)


def block_scores(queries, keys_rows, row_tokens, col_tokens, length):
    scores = jnp.einsum(
        "qhd,khd->hqk", queries, keys_rows, preferred_element_type=jnp.float32
    ) * HD ** (-0.5)
    allowed = (col_tokens[None, :] <= row_tokens[:, None]) & (col_tokens[None, :] < length)
    return jnp.where(allowed[None], scores, NEGATIVE)


def is_live(row_tokens, col_tokens, length):
    return (col_tokens[0] <= row_tokens[-1]) & (col_tokens[0] < length)


def fold_stats(row_max, row_total, queries, key_value, lengths, row_tokens, col_tokens):

    def per_slot(inputs):
        slot_max, slot_total, slot_queries, slot_pairs, length = inputs

        def compute(current):
            prev_max, prev_total = current
            scores = block_scores(slot_queries, slot_pairs[:, :, 0], row_tokens, col_tokens, length)
            next_max = jnp.maximum(prev_max, jnp.max(scores, axis=-1))
            next_total = prev_total * jnp.exp(prev_max - next_max) + jnp.sum(
                jnp.exp(scores - next_max[..., None]), axis=-1
            )
            return (next_max, next_total)

        return lax.cond(
            is_live(row_tokens, col_tokens, length),
            compute,
            lambda current: current,
            (slot_max, slot_total),
        )

    return lax.map(per_slot, (row_max, row_total, queries, key_value, lengths))


def fold_values(attended, queries, key_value, log_total, lengths, row_tokens, col_tokens):

    def per_slot(inputs):
        slot_out, slot_queries, slot_pairs, slot_log, length = inputs

        def compute(current):
            scores = block_scores(slot_queries, slot_pairs[:, :, 0], row_tokens, col_tokens, length)
            prob_low = jnp.exp(scores - slot_log[..., None]).astype(jnp.bfloat16)
            return current + jnp.einsum(
                "hqk,khd->qhd", prob_low, slot_pairs[:, :, 1], preferred_element_type=jnp.float32
            )

        return lax.cond(
            is_live(row_tokens, col_tokens, length), compute, lambda current: current, slot_out
        )

    return lax.map(per_slot, (attended, queries, key_value, log_total, lengths))


def fold_grads(
    query_grad,
    pair_grad,
    queries,
    key_value,
    grad_out,
    log_total,
    row_delta,
    lengths,
    row_tokens,
    col_tokens,
):

    def per_slot(inputs):
        (
            slot_qgrad,
            slot_pgrad,
            slot_queries,
            slot_pairs,
            slot_gout,
            slot_log,
            slot_delta,
            length,
        ) = inputs

        def compute(current):
            cur_qgrad, cur_pgrad = current
            scores = block_scores(slot_queries, slot_pairs[:, :, 0], row_tokens, col_tokens, length)
            attend_prob = jnp.exp(scores - slot_log[..., None])
            prob_low = attend_prob.astype(jnp.bfloat16)
            prob_grad = jnp.einsum(
                "qhd,khd->hqk", slot_gout, slot_pairs[:, :, 1], preferred_element_type=jnp.float32
            )
            score_grad = (attend_prob * (prob_grad - slot_delta[..., None])).astype(jnp.bfloat16)
            cur_qgrad = cur_qgrad + jnp.einsum(
                "hqk,khd->qhd", score_grad, slot_pairs[:, :, 0], preferred_element_type=jnp.float32
            ) * HD ** (-0.5)
            key_grad = jnp.einsum(
                "hqk,qhd->khd", score_grad, slot_queries, preferred_element_type=jnp.float32
            ) * HD ** (-0.5)
            value_grad = jnp.einsum(
                "hqk,qhd->khd", prob_low, slot_gout, preferred_element_type=jnp.float32
            )
            return (cur_qgrad, cur_pgrad + jnp.stack([key_grad, value_grad], axis=2))

        return lax.cond(
            is_live(row_tokens, col_tokens, length),
            compute,
            lambda current: current,
            (slot_qgrad, slot_pgrad),
        )

    return lax.map(
        per_slot,
        (query_grad, pair_grad, queries, key_value, grad_out, log_total, row_delta, lengths),
    )


def local(residual, cotangent, lengths, positions, masters, momenta, averages):
    slot_count, span_rows, model_width = residual.shape
    group_count = lax.axis_size("blk")
    uly_count = lax.axis_size("uly")
    group_index = lax.axis_index("blk")
    uly_index = lax.axis_index("uly")
    block_rows = uly_count * span_rows
    full_rows = group_count * block_rows
    local_heads = H // uly_count
    token_rows = slot_count * span_rows
    row_tokens = group_tokens(group_index, group_count, uly_count, span_rows)

    def tokens_of(source):
        return group_tokens(source, group_count, uly_count, span_rows)

    gathered = lax.all_gather(masters.astype(jnp.bfloat16), ("blk", "uly"), axis=0, tiled=True)
    (
        gain_one,
        shift_one,
        gain_two,
        shift_two,
        project_w,
        project_b,
        dense_w,
        dense_b,
        expand_w,
        expand_b,
        shrink_w,
        shrink_b,
    ) = unpack(gathered)
    values = residual.astype(jnp.float32).reshape(token_rows, model_width)
    normed_one, norm_back_one = jax.vjp(
        layer_norm, values, gain_one.astype(jnp.float32), shift_one.astype(jnp.float32)
    )
    normed_two, norm_back_two = jax.vjp(
        layer_norm, values, gain_two.astype(jnp.float32), shift_two.astype(jnp.float32)
    )
    normed_one = normed_one.astype(jnp.bfloat16)
    normed_two = normed_two.astype(jnp.bfloat16)
    mixed_rows = jnp.dot(
        normed_one, project_w, preferred_element_type=jnp.float32
    ) + project_b.astype(jnp.float32)
    mixed_rows = mixed_rows.reshape(slot_count, span_rows, H, 3, HD)
    cos_table, sin_table = rotary_tables(positions)
    cos_table = cos_table[:, :, None, None, :]
    sin_table = sin_table[:, :, None, None, :]
    turned, turn_back = jax.vjp(
        lambda pair_rows: rotate(pair_rows, cos_table, sin_table), mixed_rows[:, :, :, 0:2]
    )
    packed = jnp.concatenate([turned, mixed_rows[:, :, :, 2:3]], axis=3).astype(jnp.bfloat16)
    packed = packed.reshape(slot_count, span_rows, 3 * model_width)
    heads_rows = lax.all_to_all(packed, "uly", split_axis=2, concat_axis=1, tiled=True).reshape(
        slot_count, block_rows, local_heads, 3, HD
    )
    queries = heads_rows[:, :, :, 0]
    key_value = heads_rows[:, :, :, 1:3]
    row_max = jnp.full((slot_count, local_heads, block_rows), NEGATIVE, jnp.float32)
    row_total = jnp.zeros((slot_count, local_heads, block_rows), jnp.float32)
    attended = jnp.zeros((slot_count, block_rows, local_heads, HD), jnp.float32)
    last_tokens = tokens_of((group_index + 1) % group_count)

    def stats_turn(turn_index, carried):
        pairs_now, cur_max, cur_total = carried
        col_tokens = tokens_of((group_index - turn_index) % group_count)
        cur_max, cur_total = fold_stats(
            cur_max, cur_total, queries, pairs_now, lengths, row_tokens, col_tokens
        )
        pairs_now = passed_along(pairs_now, "blk", 1)
        return (pairs_now, cur_max, cur_total)

    pairs_now, row_max, row_total = lax.fori_loop(
        0, group_count - 1, stats_turn, (key_value, row_max, row_total)
    )
    row_max, row_total = fold_stats(
        row_max, row_total, queries, pairs_now, lengths, row_tokens, last_tokens
    )
    log_total = row_max + jnp.log(row_total)

    def value_turn(turn_index, carried):
        pairs_now, cur_out = carried
        col_tokens = tokens_of((group_index - turn_index) % group_count)
        cur_out = fold_values(
            cur_out, queries, pairs_now, log_total, lengths, row_tokens, col_tokens
        )
        pairs_now = passed_along(pairs_now, "blk", 1)
        return (pairs_now, cur_out)

    pairs_now, attended = lax.fori_loop(0, group_count - 1, value_turn, (key_value, attended))
    attended = fold_values(
        attended, queries, pairs_now, log_total, lengths, row_tokens, last_tokens
    )
    heads_out = attended.astype(jnp.bfloat16).reshape(slot_count, block_rows, local_heads * HD)
    merged = lax.all_to_all(heads_out, "uly", split_axis=1, concat_axis=2, tiled=True).reshape(
        token_rows, model_width
    )
    branch_attn = jnp.dot(merged, dense_w, preferred_element_type=jnp.float32) + dense_b.astype(
        jnp.float32
    )
    hidden_pre = jnp.dot(
        normed_two, expand_w, preferred_element_type=jnp.float32
    ) + expand_b.astype(jnp.float32)
    activated, gelu_back = jax.vjp(partial(jax.nn.gelu, approximate=False), hidden_pre)
    activated_low = activated.astype(jnp.bfloat16)
    branch_feed = jnp.dot(
        activated_low, shrink_w, preferred_element_type=jnp.float32
    ) + shrink_b.astype(jnp.float32)
    outputs = (
        (values + branch_attn + branch_feed)
        .astype(jnp.bfloat16)
        .reshape(slot_count, span_rows, model_width)
    )
    first_token = (uly_index * group_count + group_index) * span_rows
    token_index = first_token + jnp.arange(span_rows, dtype=jnp.int32)
    live_mask = (token_index[None, :] < lengths[:, None]).astype(jnp.float32)
    seed_grad = (cotangent.astype(jnp.float32) * live_mask[:, :, None]).reshape(
        token_rows, model_width
    )
    seed_low = seed_grad.astype(jnp.bfloat16)
    dense_w_grad = jnp.einsum("ra,rb->ab", merged, seed_low, preferred_element_type=jnp.float32)
    bias_grad = jnp.sum(seed_low.astype(jnp.float32), axis=0)
    merged_grad = jnp.einsum(
        "rb,ab->ra", seed_low, dense_w, preferred_element_type=jnp.float32
    ).astype(jnp.bfloat16)
    shrink_w_grad = jnp.einsum(
        "rf,rb->fb", activated_low, seed_low, preferred_element_type=jnp.float32
    )
    activated_grad = jnp.einsum("rb,fb->rf", seed_low, shrink_w, preferred_element_type=jnp.float32)
    hidden_grad = gelu_back(activated_grad)[0].astype(jnp.bfloat16)
    expand_w_grad = jnp.einsum(
        "ra,rf->af", normed_two, hidden_grad, preferred_element_type=jnp.float32
    )
    expand_b_grad = jnp.sum(hidden_grad.astype(jnp.float32), axis=0)
    normed_two_grad = jnp.einsum(
        "rf,af->ra", hidden_grad, expand_w, preferred_element_type=jnp.float32
    )
    grad_heads = lax.all_to_all(
        merged_grad.reshape(slot_count, span_rows, model_width),
        "uly",
        split_axis=2,
        concat_axis=1,
        tiled=True,
    )
    grad_out = grad_heads.reshape(slot_count, block_rows, local_heads, HD)
    row_delta = jnp.sum(grad_out.astype(jnp.float32) * attended, axis=-1).transpose(0, 2, 1)
    query_grad = jnp.zeros((slot_count, block_rows, local_heads, HD), jnp.float32)
    pair_grad = jnp.zeros((slot_count, block_rows, local_heads, 2, HD), jnp.float32)

    def grad_turn(turn_index, carried):
        pairs_now, cur_pgrad, cur_qgrad = carried
        col_tokens = tokens_of((group_index - turn_index) % group_count)
        cur_qgrad, cur_pgrad = fold_grads(
            cur_qgrad,
            cur_pgrad,
            queries,
            pairs_now,
            grad_out,
            log_total,
            row_delta,
            lengths,
            row_tokens,
            col_tokens,
        )
        pairs_now = passed_along(pairs_now, "blk", 1)
        cur_pgrad = passed_along(cur_pgrad.astype(jnp.bfloat16), "blk", 1).astype(cur_pgrad.dtype)
        return (pairs_now, cur_pgrad, cur_qgrad)

    pairs_now, pair_grad, query_grad = lax.fori_loop(
        0, group_count - 1, grad_turn, (key_value, pair_grad, query_grad)
    )
    query_grad, pair_grad = fold_grads(
        query_grad,
        pair_grad,
        queries,
        pairs_now,
        grad_out,
        log_total,
        row_delta,
        lengths,
        row_tokens,
        last_tokens,
    )
    pair_grad = passed_along(pair_grad.astype(jnp.bfloat16), "blk", 1).astype(pair_grad.dtype)
    back_packed = jnp.concatenate(
        [query_grad.astype(jnp.bfloat16)[:, :, :, None], pair_grad.astype(jnp.bfloat16)], axis=3
    )
    back_packed = back_packed.reshape(slot_count, block_rows, local_heads * 3 * HD)
    token_grads = lax.all_to_all(
        back_packed, "uly", split_axis=1, concat_axis=2, tiled=True
    ).reshape(slot_count, span_rows, H, 3, HD)
    turned_grad = turn_back(token_grads[:, :, :, 0:2].astype(jnp.float32))[0]
    mixed_grad = jnp.concatenate(
        [turned_grad, token_grads[:, :, :, 2:3].astype(jnp.float32)], axis=3
    ).astype(jnp.bfloat16)
    mixed_grad = mixed_grad.reshape(token_rows, 3 * model_width)
    project_w_grad = jnp.einsum(
        "ra,rc->ac", normed_one, mixed_grad, preferred_element_type=jnp.float32
    )
    project_b_grad = jnp.sum(mixed_grad.astype(jnp.float32), axis=0)
    normed_one_grad = jnp.einsum(
        "rc,ac->ra", mixed_grad, project_w, preferred_element_type=jnp.float32
    )
    values_one, gain_one_grad, shift_one_grad = norm_back_one(normed_one_grad)
    values_two, gain_two_grad, shift_two_grad = norm_back_two(normed_two_grad)
    input_grad = (
        (seed_grad + values_one + values_two)
        .astype(jnp.bfloat16)
        .reshape(slot_count, span_rows, model_width)
    )
    local_grads = jnp.concatenate(
        [
            gain_one_grad,
            shift_one_grad,
            gain_two_grad,
            shift_two_grad,
            project_w_grad.reshape(-1),
            project_b_grad,
            dense_w_grad.reshape(-1),
            bias_grad,
            expand_w_grad.reshape(-1),
            expand_b_grad,
            shrink_w_grad.reshape(-1),
            bias_grad,
        ]
    )
    gradients = lax.psum_scatter(local_grads, ("blk", "uly"), scatter_dimension=0, tiled=True)
    velocity = MOMENTUM * momenta + gradients
    step_rate = LEARN_RATE / math.sqrt(slot_count * full_rows)
    updated = masters - step_rate * (gradients + MOMENTUM * velocity)
    averaged = AVERAGE_DECAY * averages + (1.0 - AVERAGE_DECAY) * updated
    return (outputs, input_grad, gradients, updated, velocity, averaged)


LANES = 128
BLOCK = 256
RING = ("core", "z", "y")
ALL = ("x", "core", "z", "y")
F32 = jnp.float32
BF16 = jnp.bfloat16


def call(body, grid, in_specs, out_specs, out_shape, scratch=(), prefetch=0):
    return pl.pallas_call(
        body,
        grid_spec=pltpu.PrefetchScalarGridSpec(
            num_scalar_prefetch=prefetch,
            grid=grid,
            in_specs=in_specs,
            out_specs=out_specs,
            scratch_shapes=scratch,
        ),
        out_shape=out_shape,
        compiler_params=pltpu.CompilerParams(vmem_limit_bytes=56 << 20),
    )


def whole(shape):
    return pl.BlockSpec(shape, lambda *_: (0,) * len(shape))


def shaped(shape, kind):
    return jax.ShapeDtypeStruct(shape, kind)


def mm(a, b, dims=((1,), (0,))):
    return lax.dot_general(a, b, (dims, ((), ())), preferred_element_type=F32)


def low_lanes(shape):
    return lax.broadcasted_iota(jnp.int32, shape, len(shape) - 1) < LANES // 2


def swap(a):
    return pltpu.roll(a, LANES // 2, 1)


def join(a, a_half, b, b_half):
    first = swap(a) if a_half else a
    second = b if b_half else swap(b)
    return jnp.where(low_lanes(a.shape), first, second)


OWNERS = 32
PER = (3 * D + D + FF + FF) // OWNERS
FLAT = PER * D // LANES
PIECE = FLAT // 16
LEAD = 4 * D // LANES
EDGE = PER * D + 13 * D // OWNERS
PROJECT, PLAIN, PLAIN_EXPAND, EXPAND, EXPAND_PLAIN = range(5)


def plain_place(row, base, count):
    local = row - base
    half = int(local >= count // 2)
    return local - half * (count // 2), half


def dense_place(row):
    if row < 768:
        c = 8 + row // 384
        return (c, 0) + plain_place(row, 384 * (c - 8), 384)
    return (10, 0) + plain_place(row, 768, 256)


def shrink_place(row):
    if row < 256:
        return (21, 64) + plain_place(row, 0, 256)
    c = 22 + (row - 256) // 384
    return (c, 0) + plain_place(row, 256 + 384 * (c - 22), 384)


def expand_places():
    places = [(10, 128, 0, 32)]
    places += [(c, 0, 32 + 96 * (c - 11), 96) for c in range(11, 21)]
    places += [(21, 0, 992, 32)]
    return places


def shifted_rows(source, start, shift, at, rows):
    turn = (LANES - shift) % LANES
    first = pltpu.roll(source[pl.ds(start + at, rows), :], turn, 1)
    second = pltpu.roll(source[pl.ds(start + at + 1, rows), :], turn, 1)
    lane = lax.broadcasted_iota(jnp.int32, (rows, LANES), 1)
    return jnp.where(lane < LANES - shift, first, second)


SHIFT_ROWS = 3200
START, SHIFT, KIND, VECTOR, START_BACK, SHIFT_BACK, HEAD, X, LENGTH, CORE, Y, Z = range(12)
SEND_ROWS = PIECE + 32 + 16
OWN_ROW = 64


def weights_out_body(scalars, before, own, after, places, out, source, flat, tail):
    start, shift, kind, vector_row = scalars[START], scalars[SHIFT], scalars[KIND], scalars[VECTOR]
    count = own.shape[0]
    source[0 : OWN_ROW - 8] = jnp.zeros((OWN_ROW - 8, LANES), F32)
    source[OWN_ROW - 8 : OWN_ROW] = before[...]

    def copy(step, carry):
        at = pl.multiple_of(step * 88, 8)
        source[pl.ds(at + OWN_ROW, 88), :] = own[pl.ds(at, 88), :]
        return carry

    lax.fori_loop(0, count // 88, copy, 0)
    last = OWN_ROW + EDGE // LANES
    source[OWN_ROW + count :] = jnp.zeros((source.shape[0] - OWN_ROW - count, LANES), F32)
    edge = EDGE % LANES
    tail[...] = jnp.zeros(tail.shape, F32)
    tail[7:8] = source[last : last + 1]
    tail[8:40] = pltpu.roll(after[...], edge, 1)
    lane = lax.broadcasted_iota(jnp.int32, (40, LANES), 1)
    source[last : last + 40] = jnp.where(lane < edge, tail[7:47], tail[8:48])

    def align(step, carry):
        at = pl.multiple_of(step * 80, 8)
        flat[pl.ds(at, 80), :] = shifted_rows(source, start, shift, at, 80)
        return carry

    lax.fori_loop(0, SHIFT_ROWS // 80, align, 0)

    def rows(first, count, stride):
        return flat[pl.ds(first, count, stride), :]

    def plain(base, count, to):
        for m in range(8):
            tile = rows(base + m, count, 8)
            a, b = tile[: count // 2], tile[count // 2 :]
            out[2 * m, to : to + count // 2] = join(a, 0, b, 0).astype(BF16)
            out[2 * m + 1, to : to + count // 2] = join(a, 1, b, 1).astype(BF16)

    def expand(base, count, to):
        for r in range(16):
            out[r, to : to + count] = rows(base + 2 * r, count, 32).astype(BF16)
            out[r, to + count : to + 2 * count] = rows(base + 2 * r + 1, count, 32).astype(BF16)

    def project(base):
        for m in range(8):
            first, middle, last = (rows(base + 3 * m + j, 128, 24) for j in range(3))
            out[2 * m, 0:128] = first.astype(BF16)
            out[2 * m, 128:192] = join(middle[:64], 0, middle[64:], 0).astype(BF16)
            out[2 * m + 1, 0:128] = join(middle, 1, last, 0).astype(BF16)
            out[2 * m + 1, 128:192] = join(last[:64], 1, last[64:], 1).astype(BF16)

    @pl.when(kind == PROJECT)
    def _():
        project(LEAD)

    @pl.when(kind == PLAIN)
    def _():
        plain(LEAD, 384, 0)

    @pl.when(kind == PLAIN_EXPAND)
    def _():
        plain(LEAD, 256, 0)
        expand(LEAD + 2048 + 8, 32, 128)

    @pl.when(kind == EXPAND)
    def _():
        expand(LEAD, 96, 0)

    @pl.when(kind == EXPAND_PLAIN)
    def _():
        expand(LEAD, 32, 0)
        plain(LEAD + 1024 + 32, 256, 64)

    vectors = flat[pl.ds(vector_row, 32), :].astype(BF16)
    for r in range(16):
        out[r, PIECE : PIECE + 32] = vectors
        out[r, PIECE + 32 :] = places[...]


def spread(source, at, vectors, to):
    tile = source[pl.ds(at, 8), :].astype(F32)
    for j in range(8):
        vectors[to : to + 1, 128 * j : 128 * j + 128] = tile[j : j + 1]


def weights_in_body(facts, own, came, qkv_w, expand_w, second, vectors, qkv_b, expand_b, places, held, rows):
    head = facts[HEAD]
    low = low_lanes((64, LANES))
    vectors[...] = jnp.zeros(vectors.shape, F32)

    def take(lower, upper, slot):
        def block(c, at, count):
            return (lower if c < 16 else upper)[c % 16, at : at + count]

        for c in range(8):
            qkv_w[128 * c : 128 * c + 128, 0:128] = block(c, 0, 128)
            packed = block(c, 128, 64).astype(F32)
            qkv_w[128 * c : 128 * c + 64, 128:256] = jnp.where(low, packed, 0.0).astype(BF16)
            qkv_w[128 * c + 64 : 128 * c + 128, 128:256] = jnp.where(low, swap(packed), 0.0).astype(BF16)
        for c, at, row, count in expand_places():
            expand_w[row : row + count, 0:128] = block(c, at, count)
            expand_w[row : row + count, 128:256] = block(c, at + count, count)

        def tile(place):
            c, at, row, half = place
            return block(c, at + row, 64).astype(F32), half

        for h in range(16):
            a, half = tile(dense_place(64 * h))
            second[h, 0:32] = join(a[:32], half, a[32:], half).astype(BF16)
            for part in range(2):
                a, half = tile(shrink_place(256 * h + 64 * part))
                b, other = tile(shrink_place(256 * h + 128 + 64 * part))
                second[h, 32 + 64 * part : 96 + 64 * part] = join(a, half, b, other).astype(BF16)
        for group in range(8):
            for x in range(2):
                a, b = (block(16 * x + 8 * core + group, PIECE + 32, 16).astype(F32) for core in range(2))
                a, b = (t[0:1] * 256.0 + t[1:2] for t in (a, b))
                row = 2 * group + x
                places[row : row + 1] = join(a, slot, b, slot)
        held[...] = block(0, PIECE, 32).astype(F32)
        for v in range(4):
            spread(held, 8 * v, vectors, v)
        for to, c in ((4, 10), (5, 31)):
            rows[0:16] = block(c, PIECE, 16).astype(F32)
            spread(rows, 0, vectors, to)
        held[0:24] = block(8, PIECE, 32)[8:].astype(F32)
        rows[...] = block(21, PIECE, 32).astype(F32)

    pl.when(facts[X] == 0)(lambda: take(own, came, 0))
    pl.when(facts[X] != 0)(lambda: take(came, own, 1))
    row = head // 2 * 3
    first, middle, last = (held[pl.ds(row + j, 1), :] for j in range(3))
    odd = head % 2 == 1
    qkv_b[0:1, 0:128] = jnp.where(odd, join(middle, 1, last, 0), first)
    value = jnp.where(odd, swap(last), middle)
    qkv_b[0:1, 128:256] = jnp.where(low_lanes((1, LANES)), value, 0.0)
    expand_b[0:1, 0:128] = rows[pl.ds(2 * head, 1), :]
    expand_b[0:1, 128:256] = rows[pl.ds(2 * head + 1, 1), :]


def rows_in_body(got, dense_w, shrink_w):
    for m in range(8):
        even, odd = got[2 * m].astype(F32), got[2 * m + 1].astype(F32)
        columns = slice(128 * m, 128 * m + 128)
        for out, at, half in ((dense_w, 0, 32), (shrink_w, 32, 128)):
            a, b = even[at : at + half], odd[at : at + half]
            out[0:half, columns] = join(a, 0, b, 0).astype(BF16)
            out[half : 2 * half, columns] = join(a, 1, b, 1).astype(BF16)


def rows_out_body(dense_g, shrink_g, out):
    for m in range(8):
        columns = slice(128 * m, 128 * m + 128)
        for source, at, half in ((dense_g, 0, 32), (shrink_g, 32, 128)):
            a, b = source[0:half, columns], source[half : 2 * half, columns]
            out[2 * m, at : at + half] = join(a, 0, b, 0).astype(BF16)
            out[2 * m + 1, at : at + half] = join(a, 1, b, 1).astype(BF16)


def early_body(scalars, second, expand_g, bias_g, expand_bg, own, other, expand_rows):
    head = scalars[HEAD]
    expand_rows[...] = jnp.zeros(expand_rows.shape, F32)
    expand_rows[pl.ds(2 * head, 1), :] = expand_bg[0:1, 0:128]
    expand_rows[pl.ds(2 * head + 1, 1), :] = expand_bg[0:1, 128:256]
    rows = [bias_g[0:1, 128 * j : 128 * j + 128] for j in range(8)]
    bias = jnp.concatenate(rows + [jnp.zeros((8, LANES), F32)], axis=0).astype(BF16)

    def dense_rows(row):
        packed = second[row // 64, 0:32].astype(F32)
        return jnp.concatenate([packed, swap(packed)], axis=0)

    def shrink_rows(row):
        h, part = row // 256, row % 256 // 64
        packed = second[h, 32 + part % 2 * 64 : 96 + part % 2 * 64].astype(F32)
        return swap(packed) if part >= 2 else packed

    def put(lower, upper):
        def store(c, at, tile):
            (lower if c < 16 else upper)[c % 16, at : at + tile.shape[0]] = tile

        def plain(c, to, base, count, take):
            for i in range(count // 128):
                a, b = take(base + 64 * i), take(base + count // 2 + 64 * i)
                store(c, to + 64 * i, join(a, 0, b, 0).astype(BF16))

        for c in range(8):
            store(c, 0, jnp.zeros((PIECE, LANES), BF16))
        for c in range(OWNERS):
            store(c, PIECE, jnp.zeros((32, LANES), BF16))
        for c, at, row, count in expand_places():
            store(c, at, expand_g[row : row + count, 0:128].astype(BF16))
            store(c, at + count, expand_g[row : row + count, 128:256].astype(BF16))
        plain(8, 0, 0, 384, dense_rows)
        plain(9, 0, 384, 384, dense_rows)
        plain(10, 0, 768, 256, dense_rows)
        plain(21, 64, 0, 256, shrink_rows)
        for c in range(22, 32):
            plain(c, 0, 256 + 384 * (c - 22), 384, shrink_rows)
        store(10, PIECE, bias)
        store(31, PIECE, bias)
        store(21, PIECE, expand_rows[...].astype(BF16))

    pl.when(scalars[X] == 0)(lambda: put(own, other))
    pl.when(scalars[X] != 0)(lambda: put(other, own))


LATE_ROWS = 8 * PIECE + 64


def late_body(scalars, qkv_g, vector_g, qkv_bg, out, project_rows):
    head = scalars[HEAD]
    for c in range(8):
        at = PIECE * c
        out[at : at + 128] = qkv_g[128 * c : 128 * c + 128, 0:128].astype(BF16)
        a = qkv_g[128 * c : 128 * c + 64, 128:256]
        b = qkv_g[128 * c + 64 : 128 * c + 128, 128:256]
        out[at + 128 : at + 192] = join(a, 0, b, 0).astype(BF16)
    gains = [vector_g[v : v + 1, 128 * j : 128 * j + 128] for v in range(4) for j in range(8)]
    out[8 * PIECE : 8 * PIECE + 32] = jnp.concatenate(gains, axis=0).astype(BF16)
    project_rows[...] = jnp.zeros(project_rows.shape, F32)
    pair, value = qkv_bg[0:1, 0:128], qkv_bg[0:1, 128:256]
    low = low_lanes((1, LANES))
    row = 8 + head // 2 * 3
    odd = head % 2 == 1
    project_rows[pl.ds(row, 1), :] = jnp.where(odd, 0.0, pair)
    project_rows[pl.ds(row + 1, 1), :] = jnp.where(
        odd, jnp.where(low, 0.0, swap(pair)), jnp.where(low, value, 0.0)
    )
    project_rows[pl.ds(row + 2, 1), :] = jnp.where(odd, join(pair, 1, value, 0), 0.0)
    out[8 * PIECE + 32 :] = project_rows[...].astype(BF16)


def both_body(scalars, early, early_came, late, late_came, out):
    def add(r, carry):
        out[r] = (early[r].astype(F32) + early_came[r].astype(F32)).astype(BF16)
        return carry

    lax.fori_loop(0, 16, add, 0)

    @pl.when(scalars[X] == 0)
    def _():
        def total(at, count):
            return (late[at : at + count].astype(F32) + late_came[at : at + count].astype(F32)).astype(BF16)

        for c in range(8):
            out[c, 0:PIECE] = total(PIECE * c, PIECE)
        out[0, PIECE : PIECE + 32] = total(8 * PIECE, 32)
        out[8, PIECE : PIECE + 32] = total(8 * PIECE + 32, 32)


BACK_ROWS = PIECE + 32
TAKE_ROWS = 3120


def grads_in_body(scalars, got, out, flat):
    start, shift, kind, vector_row = scalars[START_BACK], scalars[SHIFT_BACK], scalars[KIND], scalars[VECTOR]
    lead = LEAD + 8

    def clear(step, carry):
        flat[pl.ds(pl.multiple_of(step * 80, 8), 80), :] = jnp.zeros((80, LANES), F32)
        return carry

    lax.fori_loop(0, SHIFT_ROWS // 80, clear, 0)

    def add_vectors(source, total):
        return total + got[source, PIECE : PIECE + 32].astype(F32)

    flat[pl.ds(vector_row + 8, 32), :] = lax.fori_loop(0, 16, add_vectors, jnp.zeros((32, LANES), F32))

    def taken(r, at, count):
        return got[r, at : at + count].astype(F32)

    def plain(base, count, at):
        half = count // 2
        for m in range(8):
            a, b = taken(2 * m, at, half), taken(2 * m + 1, at, half)
            flat[pl.ds(base + m, half, 8), :] = join(a, 0, b, 0)
            flat[pl.ds(base + m + 8 * half, half, 8), :] = join(a, 1, b, 1)

    def expand(base, count, at):
        for r in range(16):
            flat[pl.ds(base + 2 * r, count, 32), :] = taken(r, at, count)
            flat[pl.ds(base + 2 * r + 1, count, 32), :] = taken(r, at + count, count)

    def project(base):
        for m in range(8):
            pair, values = taken(2 * m, 0, 128), taken(2 * m, 128, 64)
            odd_pair, odd_values = taken(2 * m + 1, 0, 128), taken(2 * m + 1, 128, 64)
            values = jnp.concatenate([values, swap(values)], axis=0)
            odd_values = jnp.concatenate([odd_values, swap(odd_values)], axis=0)
            flat[pl.ds(base + 3 * m, 128, 24), :] = pair
            flat[pl.ds(base + 3 * m + 1, 128, 24), :] = join(values, 0, odd_pair, 0)
            flat[pl.ds(base + 3 * m + 2, 128, 24), :] = join(odd_pair, 1, odd_values, 0)

    @pl.when(kind == PROJECT)
    def _():
        project(lead)

    @pl.when(kind == PLAIN)
    def _():
        plain(lead, 384, 0)

    @pl.when(kind == PLAIN_EXPAND)
    def _():
        plain(lead, 256, 0)
        expand(lead + 2048 + 8, 32, 128)

    @pl.when(kind == EXPAND)
    def _():
        expand(lead, 96, 0)

    @pl.when(kind == EXPAND_PLAIN)
    def _():
        expand(lead, 32, 0)
        plain(lead + 1024 + 32, 256, 64)

    def align(step, carry):
        at = pl.multiple_of(step * 80, 8)
        out[pl.ds(at, 80), :] = shifted_rows(flat, start, shift, at, 80)
        return carry

    lax.fori_loop(0, TAKE_ROWS // 80, align, 0)


def token_rows(ref):
    return jnp.concatenate([ref[0, 0, 0], ref[1, 0, 0], ref[0, 0, 1], ref[1, 0, 1]], axis=0)


def put_rows(kept, sent, rows, core):
    step = rows.shape[0] // 4
    for x in range(2):
        first, second = (rows[step * i : step * i + step].astype(BF16) for i in (2 * x, 2 * x + 1))
        kept[0, x] = jnp.where(core == 0, first, second)
        sent[0, x] = jnp.where(core == 0, second, first)


def relative_place(i, here):
    y = (i & 1) ^ here[Y]
    z = (i >> 1) ^ here[Z]
    return y * 4 + (z & 1) * 2 + (z >> 1)


def normalized(values):
    centered = values - jnp.mean(values, axis=-1, keepdims=True)
    variance = jnp.mean(centered * centered, axis=-1, keepdims=True)
    return centered * lax.rsqrt(variance + EPSILON)


def turned(pair, cos, sin):
    lane = lax.broadcasted_iota(jnp.int32, pair.shape, 1) % HD
    half = ROT // 2
    other = jnp.where(
        lane < half, -pltpu.roll(pair, LANES - half, 1), jnp.where(lane < ROT, pltpu.roll(pair, half, 1), 0.0)
    )
    return pair * cos + other * sin


def mixed_body(tokens, places, vectors, qkv_w, qkv_b, inverse, one, two, query, key, value, cos, sin):
    unit = normalized(token_rows(tokens).astype(F32))
    at = 2 * pl.program_id(0)
    place = [jnp.broadcast_to(places[pl.ds(at + x, 1), :], (LANES, LANES)).T for x in range(2)]
    angles = jnp.concatenate(place, axis=0) * inverse[...]
    cos[...] = jnp.cos(angles)
    sin[...] = jnp.sin(angles)
    first = (unit * vectors[0:1] + vectors[1:2]).astype(BF16)
    one[...] = first
    two[...] = (unit * vectors[2:3] + vectors[3:4]).astype(BF16)
    mixed = mm(first, qkv_w[...]) + qkv_b[...]
    pair = turned(mixed[:, :LANES], cos[...], sin[...])
    query[...] = pair[:, :HD].astype(BF16) * HD ** (-0.5)
    key[...] = pair[:, HD:].astype(BF16)
    value[...] = mixed[:, LANES : LANES + HD].astype(BF16)


def masked_scores(key, query_t, at, first_query, length):
    scores = mm(key, query_t)
    keys = at * BLOCK + lax.broadcasted_iota(jnp.int32, scores.shape, 0)
    queries = first_query + lax.broadcasted_iota(jnp.int32, scores.shape, 1)
    return jnp.where((keys <= queries) & (keys < length), scores, NEGATIVE)


def folded(values, op):
    parts = [values[8 * i : 8 * i + 8] for i in range(values.shape[0] // 8)]
    while len(parts) > 1:
        parts = [op(a, b) for a, b in zip(parts[::2], parts[1::2])]
    return parts[0]


def attend_body(lengths, query, key, value, low_out, full_out, log_out, scores, value_t):
    at = pl.program_id(0)
    length = lengths[LENGTH]

    @pl.when(at == 0)
    def _():
        value_t[...] = value[...].astype(F32).T.astype(BF16)

    query_t = query[...].astype(F32).T.astype(BF16)
    clear = jnp.minimum(at, length // BLOCK)
    stop = jnp.minimum(at, (length - 1) // BLOCK) + 1

    def rows(j):
        return pl.ds(pl.multiple_of(j * BLOCK, BLOCK), BLOCK)

    def score(j, top, masked):
        if masked:
            tile = masked_scores(key[rows(j), :], query_t, j, at * BLOCK, length)
        else:
            tile = mm(key[rows(j), :], query_t)
        scores[rows(j), :] = tile
        return jnp.maximum(top, folded(tile, jnp.maximum))

    top = jnp.full((8, BLOCK), NEGATIVE, F32)
    top = lax.fori_loop(0, clear, lambda j, t: score(j, t, False), top)
    top = lax.fori_loop(clear, stop, lambda j, t: score(j, t, True), top)
    top = jnp.max(top, axis=0, keepdims=True)

    def weigh(j, carried):
        total, out = carried
        tile = jnp.exp(scores[rows(j), :] - top)
        return total + folded(tile, jnp.add), out + mm(value_t[:, rows(j)], tile.astype(BF16))

    start = (jnp.zeros((8, BLOCK), F32), jnp.zeros((HD, BLOCK), F32))
    total, out = lax.fori_loop(0, stop, weigh, start)
    total = jnp.sum(total, axis=0, keepdims=True)
    out = out * (1.0 / total)
    full_out[...] = out
    low_out[...] = out.T.astype(BF16)
    log_out[...] = top + jnp.log(total)


def attend_back_body(
    lengths, query, key, value, grad, full_out, log_in, query_g, key_g, value_g, key_t, key_sum, value_sum
):
    at = pl.program_id(0)
    length = lengths[LENGTH]

    @pl.when(at == 0)
    def _():
        key_t[...] = key[...].astype(F32).T.astype(BF16)
        key_sum[...] = jnp.zeros(key_sum.shape, F32)
        value_sum[...] = jnp.zeros(value_sum.shape, F32)

    query_rows, grad_rows = query[...], grad[...]
    query_t = query_rows.astype(F32).T.astype(BF16)
    grad_full_t = grad_rows.astype(F32).T
    grad_t = grad_full_t.astype(BF16)
    delta = jnp.sum(grad_full_t * full_out[...], axis=0, keepdims=True)
    log_total = log_in[...]
    clear = jnp.minimum(at, length // BLOCK)
    stop = jnp.minimum(at, (length - 1) // BLOCK) + 1
    clear, stop = (jnp.where(at * BLOCK < length, n, 0) for n in (clear, stop))

    def step(j, query_sum, masked):
        rows = pl.ds(pl.multiple_of(j * BLOCK, BLOCK), BLOCK)
        if masked:
            tile = masked_scores(key[rows, :], query_t, j, at * BLOCK, length)
        else:
            tile = mm(key[rows, :], query_t)
        probs = jnp.exp(tile - log_total)
        value_sum[rows, :] += mm(probs.astype(BF16), grad_rows)
        score_g = (probs * (mm(value[rows, :], grad_t) - delta)).astype(BF16)
        key_sum[rows, :] += mm(score_g, query_rows)
        return query_sum + mm(key_t[:, rows], score_g)

    query_sum = jnp.zeros((HD, BLOCK), F32)
    query_sum = lax.fori_loop(0, clear, lambda j, s: step(j, s, False), query_sum)
    query_sum = lax.fori_loop(clear, stop, lambda j, s: step(j, s, True), query_sum)
    query_g[...] = (query_sum * HD ** (-0.5)).T.astype(BF16)

    @pl.when(at == pl.num_programs(0) - 1)
    def _():
        key_g[...] = key_sum[...].astype(BF16)
        value_g[...] = value_sum[...].astype(BF16)


def feed_body(two, attended, expand_w, expand_b, shrink_w, dense_w, partial_out, active_out, slope_out):
    hidden = mm(two[...], expand_w[...]) + expand_b[...]
    error = lax.erf(hidden * math.sqrt(0.5))
    cumulative = 0.5 * (1.0 + error)
    active = (hidden * cumulative).astype(BF16)
    active_out[...] = active
    slope_out[...] = cumulative + hidden * jnp.exp(-0.5 * hidden * hidden) * (1.0 / math.sqrt(2.0 * math.pi))
    partial = mm(attended[...], dense_w[...]) + mm(active, shrink_w[...])
    step = BLOCK // 4
    for i, (core, x) in enumerate(((0, 0), (1, 0), (0, 1), (1, 1))):
        partial_out[core, 0, x] = partial[step * i : step * i + step].astype(BF16)


def feed_back_body(
    here, two, attended, cotangent, active, slope, shrink_w, dense_w,
    attended_g, hidden_g, shrink_g, dense_g, expand_g, expand_bg, bias_g,
):
    at = pl.program_id(0)

    @pl.when(at == 0)
    def _():
        for total in (shrink_g, dense_g, expand_g, expand_bg, bias_g):
            total[...] = jnp.zeros(total.shape, F32)

    token = at * BLOCK + lax.broadcasted_iota(jnp.int32, (BLOCK, D), 0)
    seed = jnp.where(token < here[LENGTH], token_rows(cotangent).astype(F32), 0.0)
    bias_g[...] += jnp.sum(seed, axis=0, keepdims=True)
    seed = seed.astype(BF16)
    attended_g[...] = mm(seed, dense_w[...], ((1,), (1,))).astype(BF16)
    back = (mm(seed, shrink_w[...], ((1,), (1,))) * slope[...]).astype(BF16)
    hidden_g[...] = back
    expand_bg[...] += jnp.sum(back.astype(F32), axis=0, keepdims=True)
    shrink_g[...] += mm(active[...], seed, ((0,), (0,)))
    dense_g[...] += mm(attended[...], seed, ((0,), (0,)))
    expand_g[...] += mm(two[...], back, ((0,), (0,)))


def mixed_back_body(
    here, tokens, one, query_g, key_g, value_g, hidden_g, vectors, qkv_w, expand_w, cos, sin,
    kept, sent, qkv_g, qkv_bg, vector_g,
):
    at = pl.program_id(0)

    @pl.when(at == 0)
    def _():
        for total in (qkv_g, qkv_bg, vector_g):
            total[...] = jnp.zeros(total.shape, F32)

    pair = jnp.concatenate([query_g[...].astype(F32), key_g[...].astype(F32)], axis=1)
    pair = turned(pair, cos[...], -sin[...])
    values = value_g[...].astype(F32)
    mixed_g = jnp.concatenate([pair, values, jnp.zeros_like(values)], axis=1)
    mixed_low = mixed_g.astype(BF16)
    qkv_bg[...] += jnp.sum(mixed_low.astype(F32), axis=0, keepdims=True)
    qkv_g[...] += mm(one[...], mixed_low, ((0,), (0,)))
    one_g = mm(mixed_low, qkv_w[...], ((1,), (1,)))
    two_g = mm(hidden_g[...], expand_w[...], ((1,), (1,)))
    unit = normalized(token_rows(tokens).astype(F32))
    vector_g[0:1] += jnp.sum(one_g * unit, axis=0, keepdims=True)
    vector_g[1:2] += jnp.sum(one_g, axis=0, keepdims=True)
    vector_g[2:3] += jnp.sum(two_g * unit, axis=0, keepdims=True)
    vector_g[3:4] += jnp.sum(two_g, axis=0, keepdims=True)
    put_rows(kept, sent, one_g * vectors[0:1] + two_g * vectors[2:3], here[CORE])


def split_mesh(mesh):
    groups, members = mesh.shape["blk"], mesh.shape["uly"]
    return Mesh(mesh.devices.reshape(groups // 2, 2, members // 2, 2), ALL)


def across_x(block):
    return lax.ppermute(block, "x", [(0, 1), (1, 0)])


def by_head(residual, cotangent, lengths, positions, masters, momenta, averages):
    slots, span, width = residual.shape
    x = lax.axis_index("x")
    head = lax.axis_index("core") * 8 + lax.axis_index("z") * 2 + lax.axis_index("y")
    owner = x * 16 + head
    groups = lax.axis_size("z") * lax.axis_size("y")
    count = groups * 4 * span
    chunk = masters.shape[0]
    length = lax.dynamic_slice_in_dim(lengths, x, 1)

    def paired(mine, theirs):
        return jnp.where(x == 0, jnp.stack([mine, theirs]), jnp.stack([theirs, mine]))

    def at_x(rows, index):
        return lax.dynamic_index_in_dim(rows, index, 0, keepdims=False)

    rows = jnp.stack([residual, cotangent], axis=1)
    rows = paired(at_x(rows, x), across_x(at_x(rows, 1 - x)))
    places = positions.reshape(1, 2 * span)
    tokens_shape = (2, groups, 2, span, width)
    slot_tokens = lax.all_gather(rows[:, 0], RING, axis=0).reshape(tokens_shape)
    slot_cotangent = lax.all_gather(rows[:, 1], RING, axis=0).reshape(tokens_shape)
    high, rest = (places // 256).astype(BF16), (places % 256).astype(BF16)
    places = jnp.concatenate([high, rest, jnp.zeros((14, 2 * span), BF16)])
    lane = jnp.arange(LANES, dtype=jnp.int32) % HD
    inverse = ROTARY_BASE ** (-((lane % (ROT // 2)).astype(F32) * 2.0 / ROT))
    inverse = jnp.where(lane < ROT, inverse, 0.0)[None, :]

    onward = [(i, i + 1) for i in range(OWNERS - 1)]
    backward = [(i + 1, i) for i in range(OWNERS - 1)]
    before = lax.ppermute(masters[chunk - D :], ALL, onward)
    after = lax.ppermute(masters[: 4 * D], ALL, backward)
    own_rows = -(-chunk // D) * 8
    own = jnp.pad(masters, (0, own_rows * LANES - chunk)).reshape(own_rows, LANES)
    before, after = before.reshape(8, LANES), after.reshape(32, LANES)
    skipped = jnp.where(owner < 8, 4, jnp.where(owner < 11, 7, jnp.where(owner < 22, 8, 12)))
    kind = jnp.where(
        owner < 8,
        PROJECT,
        jnp.where(
            owner == 10,
            PLAIN_EXPAND,
            jnp.where(owner == 21, EXPAND_PLAIN, jnp.where((owner > 10) & (owner < 21), EXPAND, PLAIN)),
        ),
    )
    vector_row = jnp.where(owner == 10, 2080, jnp.where(owner == 21, 1056, jnp.where(owner == 31, 3104, 0)))
    ahead = skipped * D - (chunk - PER * D) * owner
    begin = ahead + 4 * D
    begin_g = (chunk - PER * D) * owner - skipped * D + 4 * D
    y, z, core = lax.axis_index("y"), lax.axis_index("z"), lax.axis_index("core")
    facts = [begin // LANES, begin % LANES, kind, vector_row, begin_g // LANES, begin_g % LANES]
    facts = jnp.stack(facts + [head, x, length[0], core, y, z]).astype(jnp.int32)
    sent = call(
        weights_out_body, (1,),
        [whole(before.shape), whole(own.shape), whole(after.shape), whole(places.shape)],
        whole((16, SEND_ROWS, LANES)),
        shaped((16, SEND_ROWS, LANES), BF16),
        [pltpu.VMEM((3280, LANES), F32), pltpu.VMEM((SHIFT_ROWS, LANES), F32), pltpu.VMEM((48, LANES), F32)],
        1,
    )(facts, before, own, after, places)
    got = lax.all_to_all(sent, RING, 0, 0, tiled=True)
    came = across_x(got)
    qkv_w, expand_w, second, vectors, qkv_b, expand_b, places = call(
        weights_in_body, (1,),
        [whole(got.shape), whole(got.shape)],
        [whole((D, 256)), whole((D, 256)), whole((16, 160, LANES)), whole((8, D)), whole((1, 256)), whole((1, 256)),
         whole((16, LANES))],
        [shaped((D, 256), BF16), shaped((D, 256), BF16), shaped((16, 160, LANES), BF16), shaped((8, D), F32),
         shaped((1, 256), F32), shaped((1, 256), F32), shaped((16, LANES), F32)],
        [pltpu.VMEM((32, LANES), F32), pltpu.VMEM((32, LANES), F32)], 1,
    )(facts, got, came)
    second = lax.all_to_all(second, RING, 0, 0, tiled=True)
    steps = (count // BLOCK,)
    token_spec = pl.BlockSpec((2, 1, 2, span, width), lambda i, *_: (0, i, 0, 0, 0))
    part_spec = pl.BlockSpec((1, 2, span, width), lambda i, here: (relative_place(i, here), 0, 0, 0))
    part_shape = shaped((groups, 2, span, width), BF16)
    swap_pair, far_pairs = [(0, 1), (1, 0)], [(0, 2), (2, 0), (1, 3), (3, 1)]

    def summed(kept, sent):
        left = kept.shape[0]
        for axis, route in (
            ("core", swap_pair), ("y", swap_pair), ("z", swap_pair + [(2, 3), (3, 2)]), ("z", far_pairs)
        ):
            came = lax.ppermute(sent, axis, route)
            if left == 1:
                return (kept[0].astype(F32) + came[0].astype(F32)).astype(BF16)
            left //= 2
            kept, sent = [
                (kept[half].astype(F32) + came[half].astype(F32)).astype(BF16)
                for half in (slice(0, left), slice(left, None))
            ]

    def to_owner(rows):
        mine, theirs = at_x(rows, x), at_x(rows, 1 - x)
        return paired(mine, across_x(theirs)).astype(F32)

    def rows_spec(columns):
        return pl.BlockSpec((BLOCK, columns), lambda i, *_: (i, 0))

    def columns_spec(rows):
        return pl.BlockSpec((rows, BLOCK), lambda i, *_: (0, i))

    narrow = shaped((count, HD), BF16)
    table = shaped((count, LANES), F32)
    one, two, query, key, value, cos, sin = call(
        mixed_body, steps,
        [token_spec, whole((16, LANES)), whole((8, D)), whole((D, 256)), whole((1, 256)), whole((1, LANES))],
        [rows_spec(D), rows_spec(D), rows_spec(HD), rows_spec(HD), rows_spec(HD), rows_spec(LANES), rows_spec(LANES)],
        [shaped((count, D), BF16), shaped((count, D), BF16), narrow, narrow, narrow, table, table],
    )(slot_tokens, places, vectors, qkv_w, qkv_b, inverse)
    attended, attended_full, log_total = call(
        attend_body, steps,
        [rows_spec(HD), whole((count, HD)), whole((count, HD))],
        [rows_spec(HD), columns_spec(HD), columns_spec(1)],
        [narrow, shaped((HD, count), F32), shaped((1, count), F32)],
        [pltpu.VMEM((count, BLOCK), F32), pltpu.VMEM((HD, count), BF16)], 1,
    )(facts, query, key, value)
    second, attended = lax.optimization_barrier((second, attended))
    dense_w, shrink_w = call(
        rows_in_body, (1,), [whole(second.shape)], [whole((HD, D)), whole((256, D))],
        [shaped((HD, D), BF16), shaped((256, D), BF16)],
    )(second)

    partial_out, active, slope = call(
        feed_body, steps,
        [rows_spec(D), rows_spec(HD), whole((D, 256)), whole((1, 256)), whole((256, D)), whole((HD, D))],
        [token_spec, rows_spec(256), rows_spec(256)],
        [shaped(tokens_shape, BF16), shaped((count, 256), BF16), shaped((count, 256), F32)],
    )(two, attended, expand_w, expand_b, shrink_w, dense_w)
    out_rows = lax.psum_scatter(
        partial_out.reshape(16, 2, span, width), RING, scatter_dimension=0, tiled=True
    )[0]
    out_rows = to_owner(out_rows)
    attended_g, hidden_g, shrink_g, dense_g, expand_g, expand_bg, bias_g = call(
        feed_back_body, steps,
        [rows_spec(D), rows_spec(HD), token_spec, rows_spec(256), rows_spec(256), whole((256, D)), whole((HD, D))],
        [rows_spec(HD), rows_spec(256), whole((256, D)), whole((HD, D)), whole((D, 256)), whole((1, 256)),
         whole((1, D))],
        [narrow, shaped((count, 256), BF16), shaped((256, D), F32), shaped((HD, D), F32),
         shaped((D, 256), F32), shaped((1, 256), F32), shaped((1, D), F32)], (), 1,
    )(facts, two, attended, slot_cotangent, active, slope, shrink_w, dense_w)
    second_g = call(
        rows_out_body, (1,), [whole((HD, D)), whole((256, D))], whole((16, 160, LANES)),
        shaped((16, 160, LANES), BF16),
    )(dense_g, shrink_g)
    attended_g, second_g = lax.optimization_barrier((attended_g, second_g))
    second_g = lax.all_to_all(second_g, RING, 0, 0, tiled=True)
    query_g, key_g, value_g = call(
        attend_back_body, steps,
        [rows_spec(HD), whole((count, HD)), whole((count, HD)), rows_spec(HD), columns_spec(HD), columns_spec(1)],
        [rows_spec(HD), whole((count, HD)), whole((count, HD))],
        [narrow, narrow, narrow],
        [pltpu.VMEM((HD, count), BF16), pltpu.VMEM((count, HD), F32), pltpu.VMEM((count, HD), F32)],
        1,
    )(facts, query, key, value, attended_g, attended_full, log_total)
    bias_g = jnp.where(head == 0, bias_g, 0.0)
    plane = (16, BACK_ROWS, LANES)
    early, early_other = call(
        early_body, (1,),
        [whole((16, 160, LANES)), whole((D, 256)), whole((1, D)), whole((1, 256))],
        [whole(plane), whole(plane)],
        [shaped(plane, BF16), shaped(plane, BF16)],
        [pltpu.VMEM((32, LANES), F32)], 1,
    )(facts, second_g, expand_g, bias_g, expand_bg)
    early_came = across_x(early_other)
    kept, sent, qkv_g, qkv_bg, vector_g = call(
        mixed_back_body, steps,
        [token_spec, rows_spec(D), rows_spec(HD), rows_spec(HD), rows_spec(HD),
         rows_spec(256), whole((8, D)), whole((D, 256)), whole((D, 256)), rows_spec(LANES), rows_spec(LANES)],
        [part_spec, part_spec, whole((D, 256)), whole((1, 256)), whole((8, D))],
        [part_shape, part_shape, shaped((D, 256), F32), shaped((1, 256), F32), shaped((8, D), F32)], (), 1,
    )(facts, slot_tokens, one, query_g, key_g, value_g, hidden_g, vectors, qkv_w, expand_w, cos, sin)
    in_rows = to_owner(summed(kept, sent))

    values = residual.astype(F32)
    middle = jnp.mean(values, axis=-1, keepdims=True)
    scale = lax.rsqrt(jnp.mean((values - middle) ** 2, axis=-1, keepdims=True) + EPSILON)
    middle, scale = lax.optimization_barrier((middle, scale))

    late = call(
        late_body, (1,), [whole((D, 256)), whole((8, D)), whole((1, 256))], whole((LATE_ROWS, LANES)),
        shaped((LATE_ROWS, LANES), BF16), [pltpu.VMEM((32, LANES), F32)], 1,
    )(facts, qkv_g, vector_g, qkv_bg)
    late_came = lax.ppermute(late, "x", [(1, 0)])
    sent_g = call(
        both_body, (1,),
        [whole(plane), whole(plane), whole((LATE_ROWS, LANES)), whole((LATE_ROWS, LANES))],
        whole(plane), shaped(plane, BF16), (), 1,
    )(facts, early, early_came, late, late_came)
    got_g = lax.all_to_all(sent_g, RING, 0, 0, tiled=True)
    taken = call(
        grads_in_body, (1,), [whole(got_g.shape)], whole((TAKE_ROWS, LANES)), shaped((TAKE_ROWS, LANES), F32),
        [pltpu.VMEM((SHIFT_ROWS, LANES), F32)], 1,
    )(facts, got_g).reshape(-1)
    from_before = lax.ppermute(taken[D + chunk : 5 * D + chunk], ALL, onward)
    from_after = lax.ppermute(taken[:D], ALL, backward)
    gradients = (
        taken[D : D + chunk]
        + jnp.pad(from_before, (0, chunk - 4 * D))
        + jnp.pad(from_after, (chunk - D, 0))
    )

    outputs = (values + out_rows + (vectors[4] + vectors[5])).astype(BF16)
    first_token = ((lax.axis_index("z") * 2 + lax.axis_index("y")) * 4 + x * 2 + lax.axis_index("core")) * span
    token = first_token + jnp.arange(span, dtype=jnp.int32)
    live = token[None, :] < lengths[:, None]
    seed = jnp.where(live[:, :, None], cotangent.astype(F32), 0.0)
    unit = (values - middle) * scale
    back = in_rows - jnp.mean(in_rows, axis=-1, keepdims=True)
    back = scale * (back - unit * jnp.mean(in_rows * unit, axis=-1, keepdims=True))
    input_grad = (seed + back).astype(BF16)

    velocity = MOMENTUM * momenta + gradients
    step_rate = LEARN_RATE / math.sqrt(slots * count)
    updated = masters - step_rate * (gradients + MOMENTUM * velocity)
    averaged = AVERAGE_DECAY * averages + (1.0 - AVERAGE_DECAY) * updated
    return (outputs, input_grad, gradients, updated, velocity, averaged)


def solution(mesh):
    fits = mesh.size == OWNERS and mesh.shape["blk"] == 4

    def step(*args):
        slots, tokens = args[0].shape[:2]
        if fits and slots * H == OWNERS and tokens == 64 * OWNERS:
            tokens_in, flat, used, body = P(None, ("z", "y", "x", "core"), None), P(ALL), split_mesh(mesh), by_head
            places = P(None, ("z", "y", "x", "core"))
        else:
            tokens_in, flat, used, body = P(None, ("uly", "blk"), None), P(("blk", "uly")), mesh, local
            places = P(None, ("uly", "blk"))
        return jax.shard_map(
            body,
            mesh=used,
            in_specs=(tokens_in, tokens_in, P(), places, flat, flat, flat),
            out_specs=(tokens_in, tokens_in, flat, flat, flat, flat),
            check_vma=False,
        )(*args)

    return step
```
